32 devices in a mesh: dp: 16 (over z, y, x), tensor: 2 (over core).
Axes of the slice: x: 2, y: 2, z: 4, core: 2. Of those that a mesh axis runs over, the one named last changes fastest.
Arguments:
- tokens: bfloat16 [4096, 1024], P(('dp', 'tensor')), may hold values from -6 to 6
- segment_ids: int32 [16, 256], P('dp'), may hold values from 0 to 3, never falling along the last dimension, each value on 1 to 128 neighbouring positions
- valid: int32 [16, 256], P('dp'), may hold values from 0 to 1, as said below
- expert_ids: int32 [4096, 8], P('dp'), may hold values from 0 to 15, all different within a row; in each aligned block of 256 rows (0 to 255, 256 to 511, ...) at most 136 rows name the same one
- teacher: bfloat16 [4096, 1024], P('dp'), may hold values from -6 to 6
- attn_gain: bfloat16 [1024], P('dp'), may hold values from 0.5 to 1.5
- w_query: bfloat16 [1024, 1024], P('dp', 'tensor'), may hold values from -0.75 to 0.75
- key_projection: bfloat16 [1024, 512], P('dp', 'tensor'), may hold values from -0.75 to 0.75
- value_projection: bfloat16 [1024, 512], P('dp', 'tensor'), may hold values from -0.1875 to 0.1875
- w_out: bfloat16 [1024, 1024], P('dp', 'tensor'), may hold values from -1 to 1
- moe_gain: bfloat16 [1024], P('dp'), may hold values from 0.5 to 1.5
- w_router: bfloat16 [1024, 16], P('dp'), may hold values from -0.09375 to 0.09375
- w_gate: bfloat16 [1024, 16, 512], P('dp', None, 'tensor'), may hold values from -0.1875 to 0.1875
- w_up: bfloat16 [1024, 16, 512], P('dp', None, 'tensor'), may hold values from -0.1875 to 0.1875
- w_down: bfloat16 [1024, 16, 512], P('dp', None, 'tensor'), may hold values from -1 to 1
Outputs:
- loss: float32 [], replicated
- output: bfloat16 [4096, 1024], P(('dp', 'tensor'))
- input_grad: bfloat16 [4096, 1024], P(('dp', 'tensor'))
- attn_gain_grad: float32 [1024], P('dp')
- query_grad: float32 [1024, 1024], P('dp', 'tensor')
- key_grad: float32 [1024, 512], P('dp', 'tensor')
- value_grad: float32 [1024, 512], P('dp', 'tensor')
- out_grad: float32 [1024, 1024], P('dp', 'tensor')
- moe_gain_grad: float32 [1024], P('dp')
- router_grad: float32 [1024, 16], P('dp')
- gate_grad: float32 [1024, 16, 512], P('dp', None, 'tensor')
- up_grad: float32 [1024, 16, 512], P('dp', None, 'tensor')
- down_grad: float32 [1024, 16, 512], P('dp', None, 'tensor')
The draws below stay inside these ranges and needn't reach their ends.
Inputs may be any that keep to these rules, and one draw needn't show every extreme that they name: `segment_ids`: within each sequence the ids never fall; each document has 1 to 128 tokens. `valid`: each sequence is a run of 1 followed by a run of 0; a quarter of each sequence or more is 1. `expert_ids`: each row names 8 different experts; within the 256 rows of one sequence no expert is named by more than 136 rows.
All inputs are finite; a program needn't handle non-finite values.
Results may differ from the reference program's by a relative error of at most 0.014.
The reference program's roundings to bfloat16 on the way count: a program that leaves them out, or rounds other values in their place, can miss the bound.
Values may be sent and summed in bfloat16 or wider, within the bound.
No kernel may reach another device: no remote copies, remote signals or barrier semaphores. Data moves between devices by JAX's collectives and lax.ppermute only.
A program may use at most 192 MiB of HBM per device.

```python
import math
import jax
import jax.numpy as jnp
import numpy as np
from jax import lax

MODEL_WIDTH = 1024
QUERY_HEADS = 16
KEY_VALUE_HEADS = 8
HEAD_SIZE = 64
FF = 512
TOPK = 8
EXPERTS = 16
PACKED_TOKENS = 256
SEQS = 16
TOKENS = 4096
C = 136


def draw_valid(key, part):
    rows = jnp.arange(SEQS, dtype=jnp.int32)
    ramp = (SEQS - 1 - rows) * (2 * PACKED_TOKENS // 3) // max(SEQS - 1, 1)
    extra = jax.random.randint(key, (SEQS,), 0, PACKED_TOKENS // 16 + 1, dtype=jnp.int32)
    keep_len = PACKED_TOKENS - ramp - extra
    places = jnp.arange(PACKED_TOKENS, dtype=jnp.int32)
    return (places[None, :] < keep_len[:, None]).astype(jnp.int32)


def level_of(rng, dims, split, low, top_value):
    def one(position, parts):
        draws = jax.random.uniform(jax.random.fold_in(jax.random.fold_in(rng, 6), position), (parts,), jnp.float32, low / len(split), top_value / len(split))
        return jnp.repeat(jnp.exp(draws), dims[position] // parts).reshape((-1,) + (1,) * (len(dims) - position - 1))

    factor_of = one(*split[0])
    for cut in split[1:]:
        factor_of = factor_of * one(*cut)
    return factor_of


def length_profile(number_of, total, most, skew):
    weights = [(1 << 20) // math.isqrt(standing ** skew) + 1 for standing in range(2, number_of + 1)]
    spare, counts = total - most - (number_of - 1), [1] * (number_of - 1)
    while spare > 0:
        free = [i for i in range(number_of - 1) if counts[i] < most]
        whole, budget = sum([weights[i] for i in free]), spare
        for i in free:
            addition = min(most - counts[i], max(1, budget * weights[i] // whole), spare)
            counts[i] = counts[i] + addition
            spare = spare - addition
    return np.array([most] + counts)


def uneven(own_key, amount, total, reach, slope):
    if amount == 2:
        one = jax.random.randint(own_key, (), max(1, total - reach), min(reach, total - 1) + 1)
        return jnp.stack([one, total - one])
    lengths = jnp.asarray(length_profile(amount, total, reach, slope), jnp.int32)
    couples = (amount - 1) // 2
    donor, sink = lengths[1:1 + 2 * couples:2], lengths[2:2 + 2 * couples:2]
    slack = jnp.minimum(donor - 1, reach - sink)
    passed = jax.random.randint(jax.random.fold_in(own_key, 1), (couples,), 0, 1 << 20) % (slack + 1)
    lengths = lengths.at[1:1 + 2 * couples:2].set(donor - passed).at[2:2 + 2 * couples:2].set(sink + passed)
    return lengths[jax.random.permutation(jax.random.fold_in(own_key, 2), amount)]


def routed_block(stream_key, own, number, rows, count, top, bound, skew):
    ranking = jax.random.permutation(stream_key, count)
    heavy_load, common = load_shares(count, rows * top, bound, skew, True), load_shares(count, rows * top, bound, skew, False)
    places = jnp.arange(count)

    def named(sizes, rotation):
        used = int((sizes > 0).sum())
        fixed = max(1, used // 4)
        passed = fixed + (places - fixed + rotation * (used - fixed)) % max(1, count - fixed)
        return jnp.zeros((count,), jnp.int32).at[ranking[jnp.where(places < fixed, places, passed)]].set(jnp.asarray(sizes, jnp.int32))

    sizes = jnp.where(number % 4 == 0, named(heavy_load, number // 4), named(common, number - number // 4 - 1))
    mixed = jax.random.permutation(jax.random.fold_in(own, 3), count)
    giver, taker = mixed[0:count // 2 * 2:2], mixed[1:count // 2 * 2:2]
    margin = jnp.minimum(sizes[giver] - 1, bound - sizes[taker]) // 2
    margin = jnp.where((giver == ranking[0]) | (taker == ranking[0]) | (sizes[taker] == 0), 0, jnp.maximum(margin, 0))
    passed = jax.random.randint(jax.random.fold_in(own, 4), (count // 2,), 0, 1 << 20) % (margin + 1)
    sizes = sizes.at[giver].add(-passed).at[taker].add(passed)
    labels = jnp.searchsorted(jnp.cumsum(sizes), jnp.arange(rows * top), side="right").astype(jnp.int32)
    table = labels.reshape(top, rows).T
    table = table[jax.random.permutation(jax.random.fold_in(own, 1), rows)]
    rotation = jax.random.randint(jax.random.fold_in(own, 2), (rows, 1), 0, top)
    return jnp.take_along_axis(table, (jnp.arange(top)[None, :] + rotation) % top, axis=1)


def load_shares(amount, total, reach, skew, full):
    weights = [(1 << 20) // math.isqrt(standing ** skew) + 1 for standing in range(1, amount + 1)]
    largest = reach if full else min(reach, max(-(-total // amount), total * weights[0] // sum(weights)))
    least = 1 if total - largest >= amount - 1 else 0
    given, rest = [largest] + [least] * (amount - 1), total - largest - least * (amount - 1)
    while rest > 0:
        movable = [i for i in range(1, amount) if given[i] < largest] or [i for i in range(1, amount) if given[i] < reach]
        whole, left = sum([weights[i] for i in movable]), rest
        for i in movable:
            more = min(reach - given[i], max(1, left * weights[i] // whole), rest)
            given[i] = given[i] + more
            rest = rest - more
    return np.array(given)


def centred(own_key, shape, spread, limit, pieces=(), kind=jnp.bfloat16):
    values = spread * jax.random.normal(own_key, shape, jnp.float32)
    if pieces:
        values = values * level_of(own_key, shape, pieces, -0.22, 0.18)
    return jnp.clip(values, -limit, limit).astype(kind)


def setup_inputs(seed: int = 0) -> dict:
    streams_of = jax.random.split(jax.random.key(seed), 16)
    tokens = centred(streams_of[0], (TOKENS, MODEL_WIDTH), 1.0, 6.0, ((0, 32),))
    segment_ids = jax.vmap(lambda own: jnp.searchsorted(jnp.cumsum(uneven(own, max(PACKED_TOKENS // 128, 4), PACKED_TOKENS, PACKED_TOKENS // 2, 1)), jnp.arange(PACKED_TOKENS), side="right"))(jax.random.split(streams_of[1], SEQS)).reshape((SEQS, PACKED_TOKENS)).astype(jnp.int32)
    valid = draw_valid(jax.random.fold_in(streams_of[15], 71), 0)
    expert_ids_keys = jax.random.split(jax.random.fold_in(streams_of[3], 1), TOKENS // PACKED_TOKENS)
    expert_ids_turns = jax.random.permutation(jax.random.fold_in(streams_of[3], 3), TOKENS // PACKED_TOKENS)
    expert_ids = jax.vmap(lambda own, number: routed_block(jax.random.fold_in(streams_of[3], 2), own, number, PACKED_TOKENS, EXPERTS, TOPK, C, 1))(expert_ids_keys, expert_ids_turns).reshape((TOKENS, TOPK))
    teacher = centred(streams_of[4], (TOKENS, MODEL_WIDTH), 1.0, 6.0, ((0, 16),))
    attn_gain = jnp.clip(1.0 + 0.1 * jax.random.normal(streams_of[5], (MODEL_WIDTH,), jnp.float32), 0.5, 1.5).astype(jnp.bfloat16)
    w_query = centred(streams_of[6], (MODEL_WIDTH, QUERY_HEADS * HEAD_SIZE), (MODEL_WIDTH // 16) ** -0.5, 0.75, ((0, 16), (1, 2)))
    key_projection = centred(streams_of[7], (MODEL_WIDTH, KEY_VALUE_HEADS * HEAD_SIZE), (MODEL_WIDTH // 16) ** -0.5, 0.75, ((0, 16), (1, 2)))
    value_projection = centred(streams_of[8], (MODEL_WIDTH, KEY_VALUE_HEADS * HEAD_SIZE), MODEL_WIDTH ** -0.5, 0.1875, ((0, 16), (1, 2)))
    w_out = centred(streams_of[9], (MODEL_WIDTH, QUERY_HEADS * HEAD_SIZE), (HEAD_SIZE // 2) ** -0.5, 1.0, ((0, 16), (1, 2)))
    moe_gain = jnp.clip(1.0 + 0.1 * jax.random.normal(streams_of[10], (MODEL_WIDTH,), jnp.float32), 0.5, 1.5).astype(jnp.bfloat16)
    w_router = centred(streams_of[11], (MODEL_WIDTH, EXPERTS), (4 * MODEL_WIDTH) ** -0.5, 0.09375, ((0, 16),))
    w_gate = centred(streams_of[12], (MODEL_WIDTH, EXPERTS, FF), MODEL_WIDTH ** -0.5, 0.1875, ((0, 16), (2, 2)))
    w_up = centred(streams_of[13], (MODEL_WIDTH, EXPERTS, FF), MODEL_WIDTH ** -0.5, 0.1875, ((0, 16), (2, 2)))
    w_down = centred(streams_of[14], (MODEL_WIDTH, EXPERTS, FF), (FF // 16) ** -0.5, 1.0, ((0, 16), (2, 2)))
    return {"tokens": tokens, "segment_ids": segment_ids, "valid": valid, "expert_ids": expert_ids, "teacher": teacher, "attn_gain": attn_gain, "w_query": w_query, "key_projection": key_projection, "value_projection": value_projection, "w_out": w_out, "moe_gain": moe_gain, "w_router": w_router, "w_gate": w_gate, "w_up": w_up, "w_down": w_down}


@jax.custom_vjp
def lowered_rows(v):
    return lax.optimization_barrier(v.astype(jnp.bfloat16)).astype(jnp.float32)

@jax.custom_vjp
def lowered_backward(v):
    return v

def low_keep(v):
    return (lowered_rows(v), None)

def low_pass(kept, grad):
    return (grad,)

def back_keep(v):
    return (v, None)

def back_low(kept, grad):
    return (lowered_rows(grad),)
lowered_rows.defvjp(low_keep, low_pass)
lowered_backward.defvjp(back_keep, back_low)
epsilon = 1e-06
negative = -1e+30
rope_base = 10000.0

def rope_tables(length):
    places = jnp.arange(length).astype(jnp.float32)
    freqs = rope_base ** (-2.0 * jnp.arange(HEAD_SIZE // 2).astype(jnp.float32) / HEAD_SIZE)
    angles = places[:, None] * freqs[None, :]
    return (jnp.cos(angles), jnp.sin(angles))

def apply_rotary(values, cosine_table, sine_table):
    first = values[..., :HEAD_SIZE // 2]
    second = values[..., HEAD_SIZE // 2:]
    cos_part = cosine_table[:, None, :]
    sin_part = sine_table[:, None, :]
    return jnp.concatenate([first * cos_part - second * sin_part, second * cos_part + first * sin_part], -1)

def rms_norm(values, gain):
    return values * lax.rsqrt(lax.optimization_barrier(jnp.mean(values * values, -1, keepdims=True)) + epsilon) * gain

def slot_tables(routes):
    flat = routes.reshape(-1).astype(jnp.int32)
    one_hot = (flat[:, None] == jnp.arange(EXPERTS, dtype=jnp.int32)[None, :]).astype(jnp.int32)
    ranks = lax.optimization_barrier(jnp.sum((jnp.cumsum(one_hot, 0) - one_hot) * one_hot, 1))
    slots = (flat * C + ranks).astype(jnp.int32)
    owners = jnp.full((EXPERTS * C,), PACKED_TOKENS, jnp.int32).at[slots].set(jnp.arange(PACKED_TOKENS * TOPK, dtype=jnp.int32) // TOPK)
    return (slots, owners)

def sequence(inputs, segs, lives, routes, targets, params):
    gain_one, query_w, key_matrix, value_matrix, out_w, gain_two, router_w, gate_w, up_w, down_w = params
    best_experts = lax.Precision.HIGHEST
    attention_hidden = lowered_rows(rms_norm(inputs, gain_one))
    query_unrotated = lowered_backward(jnp.dot(attention_hidden, query_w, precision=best_experts)).reshape(PACKED_TOKENS, QUERY_HEADS, HEAD_SIZE)
    key_unrotated = lowered_backward(jnp.dot(attention_hidden, key_matrix, precision=best_experts)).reshape(PACKED_TOKENS, KEY_VALUE_HEADS, HEAD_SIZE)
    value_matrix_rows = lowered_rows(lowered_backward(jnp.dot(attention_hidden, value_matrix, precision=best_experts))).reshape(PACKED_TOKENS, KEY_VALUE_HEADS, HEAD_SIZE)
    cosine_table, sine_table = rope_tables(PACKED_TOKENS)
    query_rotated = lowered_rows(apply_rotary(query_unrotated, cosine_table, sine_table)).reshape(PACKED_TOKENS, KEY_VALUE_HEADS, QUERY_HEADS // KEY_VALUE_HEADS, HEAD_SIZE)
    key_rot = lowered_rows(apply_rotary(key_unrotated, cosine_table, sine_table))
    scores = lowered_backward(jnp.einsum('qkgd,skd->kgqs', query_rotated, key_rot, precision=best_experts) * (1.0 / HEAD_SIZE))
    places = jnp.arange(PACKED_TOKENS)
    allowed = (segs[:, None] == segs[None, :]) & (places[None, :] <= places[:, None]) & (lives[None, :] > 0) | (places[:, None] == places[None, :])
    scores = jnp.where(allowed[None, None], scores, negative)
    top_score = lax.optimization_barrier(jnp.max(scores, -1, keepdims=True))
    exp_scores = jnp.exp(scores - top_score)
    probs = exp_scores / lax.optimization_barrier(jnp.sum(exp_scores, -1, keepdims=True))
    attn_out = lowered_rows(lowered_backward(jnp.einsum('kgqs,skd->qkgd', lowered_rows(probs), value_matrix_rows, precision=best_experts))).reshape(PACKED_TOKENS, QUERY_HEADS * HEAD_SIZE)
    proj = lowered_backward(jnp.dot(attn_out, out_w.T, precision=best_experts))
    resid_one = inputs + proj
    hidden_moe = lowered_rows(rms_norm(resid_one, gain_two))
    logits = lowered_backward(jnp.dot(hidden_moe, router_w, precision=best_experts))
    picked = jnp.take_along_axis(logits, routes, 1)
    gate_probs = jax.nn.softmax(picked, -1)
    slots, owners = slot_tables(routes)
    padded = jnp.concatenate([hidden_moe, jnp.zeros((1, MODEL_WIDTH), hidden_moe.dtype)], 0)
    buffer = padded[owners].reshape(EXPERTS, C, MODEL_WIDTH)
    gate_pre = lowered_backward(jnp.einsum('ecd,def->ecf', buffer, gate_w, precision=best_experts))
    up_pre = lowered_backward(jnp.einsum('ecd,def->ecf', buffer, up_w, precision=best_experts))
    hidden = lowered_rows(jax.nn.silu(gate_pre) * up_pre)
    expert_out = lowered_backward(jnp.einsum('ecf,def->ecd', hidden, down_w, precision=best_experts)).reshape(EXPERTS * C, MODEL_WIDTH)
    mixed = lax.optimization_barrier(jnp.sum(gate_probs[:, :, None] * expert_out[slots].reshape(PACKED_TOKENS, TOPK, MODEL_WIDTH), 1))
    result = resid_one + mixed
    differ = result - targets
    errors = jnp.sum(lives.astype(result.dtype)[:, None] * differ * differ)
    return (result, errors)

def reference(tokens, segment_ids, valid, expert_ids, teacher, attn_gain, w_query, key_projection, value_projection, w_out, moe_gain, w_router, w_gate, w_up, w_down):
    params = tuple((item.astype(jnp.float32) for item in (attn_gain, w_query, key_projection, value_projection, w_out, moe_gain, w_router, w_gate, w_up, w_down)))
    inputs = tokens.astype(jnp.float32).reshape(SEQS, PACKED_TOKENS, MODEL_WIDTH)
    targets = teacher.astype(jnp.float32).reshape(SEQS, PACKED_TOKENS, MODEL_WIDTH)
    routes = expert_ids.reshape(SEQS, PACKED_TOKENS, TOPK)
    count = jnp.sum(valid).astype(jnp.float32)

    def total(seq_inputs, weights):

        def one_step(carry, item):
            rows, segs, lives, picks, goals = item
            result, errors = sequence(rows, segs, lives, picks, goals, weights)
            return (carry + errors, result)
        err_sum, results = lax.scan(jax.checkpoint(one_step), jnp.zeros((), jnp.float32), (seq_inputs, segment_ids, valid, routes, targets))
        return (TOKENS * err_sum / (2.0 * count), (results, err_sum))
    objective, back_fn, extras = jax.vjp(total, inputs, params, has_aux=True)
    grad_inputs, grad_params = back_fn(jnp.ones_like(objective))
    results, err_sum = extras
    loss = err_sum / (2.0 * MODEL_WIDTH * count)
    return (loss, results.reshape(TOKENS, MODEL_WIDTH).astype(jnp.bfloat16), grad_inputs.reshape(TOKENS, MODEL_WIDTH).astype(jnp.bfloat16), grad_params[0], grad_params[1], grad_params[2], grad_params[3], grad_params[4], grad_params[5], grad_params[6], grad_params[7], grad_params[8], grad_params[9])
```

```python
import jax
import jax.numpy as jnp
from jax import lax
from jax.sharding import PartitionSpec as P

MODEL_WIDTH = 1024
HEAD_SIZE = 64
TOPK = 8
EXPERTS = 16
GROUP = 4
MISC = 128

epsilon = 1e-06
negative = -1e30
rope_base = 10000.0
f32 = jnp.float32
bf16 = jnp.bfloat16

INNER = (((1,), (1,)), ((), ()))
OUTER = (((0,), (0,)), ((), ()))


def dot(a, b):
    return jnp.dot(a, b, preferred_element_type=f32)


def dot_t(a, b):
    return lax.dot_general(a, b, INNER, preferred_element_type=f32)


def dot_o(a, b):
    return lax.dot_general(a, b, OUTER, preferred_element_type=f32)


def rope_tables(length, width):
    half = HEAD_SIZE // 2
    places = jnp.arange(length).astype(f32)
    freqs = rope_base ** (-2.0 * jnp.arange(half).astype(f32) / HEAD_SIZE)
    angles = places[:, None] * freqs[None, :]
    cosine, sine = jnp.cos(angles), jnp.sin(angles)
    reps = width // HEAD_SIZE
    return (
        jnp.tile(jnp.concatenate([cosine, cosine], 1), (1, reps)),
        jnp.tile(jnp.concatenate([-sine, sine], 1), (1, reps)),
    )


def swap_halves(u):
    half = HEAD_SIZE // 2
    low = (jnp.arange(u.shape[1]) % HEAD_SIZE) < half
    return jnp.where(low[None, :], jnp.roll(u, -half, 1), jnp.roll(u, half, 1))


class Comm:
    def __init__(self):
        self.n = lax.axis_size("dp")
        self.me = lax.axis_index("dp")
        self.core = lax.axis_index("tensor")
        self.reps = self.n // GROUP
        self.ep = self.me // self.reps
        self.rep = self.me % self.reps
        self.bits = [1 << k for k in range(self.reps.bit_length() - 1)]

    def swap(self, v, mask):
        return lax.ppermute(v, "dp", [(i, i ^ mask) for i in range(self.n)])

    def other(self, v):
        return lax.ppermute(v, "tensor", [(0, 1), (1, 0)])

    def bit(self, b):
        return (self.rep // b) % 2

    def gather_reps(self, z, last_first):
        rows, cols = z.shape[1:]
        k = len(self.bits)
        out = jnp.zeros((GROUP,) + (2,) * k + (rows, cols), z.dtype)
        zero = jnp.int32(0)
        order = list(self.bits)
        if last_first:
            order = order[::-1]
        done = set()

        def place(block, flipped):
            start = [zero]
            for b in reversed(self.bits):
                if b in done:
                    start.append(zero)
                elif b == flipped:
                    start.append(1 - self.bit(b))
                else:
                    start.append(self.bit(b))
            return start + [zero, zero]

        cur = z.reshape((GROUP,) + (1,) * k + (rows, cols))
        out = lax.dynamic_update_slice(out, cur, place(cur, None))
        for b in order:
            got = self.swap(cur, b)
            out = lax.dynamic_update_slice(out, got, place(got, b))
            done.add(b)
            if len(done) < k:
                start = place(out, None)
                shape = [GROUP] + [2 if c in done else 1 for c in reversed(self.bits)]
                cur = lax.dynamic_slice(out, start, shape + [rows, cols])
        return out.reshape(GROUP * self.reps * rows, cols)

    def stack_group(self, parts, axis=0):
        parts = jnp.stack(parts, 0)
        idx = self.ep ^ jnp.arange(GROUP)
        return jnp.concatenate(
            [lax.dynamic_index_in_dim(parts, idx[j], 0, keepdims=True) for j in range(GROUP)], 0
        )

    def gather_group(self, v):
        return [v] + [self.swap(v, self.reps * k) for k in range(1, GROUP)]

    def block(self, v, k):
        return lax.dynamic_index_in_dim(v, self.ep ^ k, 0, keepdims=False)

    def all_to_group(self, v):
        return [self.block(v, 0)] + [
            self.swap(self.block(v, k), self.reps * k) for k in range(1, GROUP)
        ]

    def scatter_reps(self, s, last_first):
        cols = s.shape[1]
        k = len(self.bits)
        rows = s.shape[0] // (GROUP * self.reps)
        s = s.reshape((GROUP,) + (2,) * k + (rows, cols))
        order = list(self.bits)
        if last_first:
            order = order[::-1]
        for b in order:
            axis = 1 + list(reversed(self.bits)).index(b)
            mine = self.bit(b)
            send = lax.dynamic_slice_in_dim(s, 1 - mine, 1, axis).astype(bf16)
            keep = lax.dynamic_slice_in_dim(s, mine, 1, axis)
            s = keep + self.swap(send, b).astype(f32)
        return s.reshape(GROUP, rows, cols)


def shards(
    tokens,
    segment_ids,
    valid,
    expert_ids,
    teacher,
    attn_gain,
    w_query,
    key_projection,
    value_projection,
    w_out,
    moe_gain,
    w_router,
    w_gate,
    w_up,
    w_down,
):
    c = Comm()
    half = tokens.shape[0]
    seq_len = expert_ids.shape[0]
    rows = w_query.shape[0]
    qw, kw = w_query.shape[1], key_projection.shape[1]
    ff = w_gate.shape[2]
    local_experts = EXPERTS // GROUP
    ew = local_experts * ff
    heads = qw // HEAD_SIZE
    kv_heads = kw // HEAD_SIZE
    per = heads // kv_heads
    scale = 1.0 / HEAD_SIZE
    first_core = c.core == 0

    def join_rows(own, other):
        return jnp.where(
            first_core, jnp.concatenate([own, other], 0), jnp.concatenate([other, own], 0)
        )

    def my_half(v):
        return lax.dynamic_slice_in_dim(v, c.core * half, half, 0)

    live_row = valid[0]
    live_count = jnp.sum(live_row).astype(f32)
    misc = jnp.concatenate(
        [
            w_router,
            attn_gain[:, None],
            moe_gain[:, None],
            jnp.broadcast_to(live_count.astype(bf16), (rows, 1)),
            jnp.zeros((rows, MISC - EXPERTS - 3), bf16),
        ],
        1,
    )
    front = jnp.concatenate([w_query, key_projection, value_projection, misc], 1)
    inputs_low = join_rows(tokens, c.other(tokens))

    def gather_attention(v):
        z = c.stack_group(c.gather_group(v))
        mid = z.shape[2] // 2
        return jnp.concatenate(
            [c.gather_reps(z[:, :, :mid], False), c.gather_reps(z[:, :, mid:], True)], 1
        )

    front_w = gather_attention(front)
    out_w = gather_attention(w_out)
    ids_half = my_half(expert_ids)
    ids_group = jnp.concatenate(c.gather_group(ids_half), 0)

    gate_up = jnp.concatenate(
        [w_gate.reshape(rows, GROUP, ew), w_up.reshape(rows, GROUP, ew)], 2
    ).transpose(1, 0, 2)
    gate_up_z = c.stack_group(c.all_to_group(gate_up))
    down_z = c.stack_group(c.all_to_group(w_down.reshape(rows, GROUP, ew).transpose(1, 0, 2)))
    gate_w = c.gather_reps(gate_up_z[:, :, :ew], False)
    up_w = c.gather_reps(gate_up_z[:, :, ew:], True)
    down_w = jnp.concatenate(
        [
            c.gather_reps(down_z[:, :, : ew // 2], False),
            c.gather_reps(down_z[:, :, ew // 2 :], True),
        ],
        1,
    )
    gate_ws = (gate_w, c.other(gate_w))
    up_ws = (up_w, c.other(up_w))
    down_ws = (down_w, c.other(down_w))

    pw = qw + 2 * kw
    proj_w = front_w[:, :pw]
    router_w = front_w[:, pw : pw + EXPERTS]
    gain_one = front_w[:, pw + EXPERTS].astype(f32)[None, :]
    gain_two = front_w[:, pw + EXPERTS + 1].astype(f32)[None, :]
    counts = front_w[:, pw + EXPERTS + 2].astype(f32).reshape(c.n, rows)[:, 0]
    live_total = jnp.sum(counts)

    inputs = inputs_low.astype(f32)
    inv_one = lax.rsqrt(jnp.mean(inputs * inputs, -1, keepdims=True) + epsilon)
    normed_one = inputs * inv_one
    attention_hidden = (normed_one * gain_one).astype(bf16)
    cosine, sine = rope_tables(seq_len, qw + kw)
    qkv = dot(attention_hidden, proj_w)
    qk_raw = qkv[:, : qw + kw]
    qk = (qk_raw * cosine + swap_halves(qk_raw) * sine).astype(bf16)
    q = qk[:, :qw].reshape(seq_len, kv_heads, per, HEAD_SIZE)
    k = qk[:, qw:].reshape(seq_len, kv_heads, HEAD_SIZE)
    v = qkv[:, qw + kw :].astype(bf16).reshape(seq_len, kv_heads, HEAD_SIZE)
    seg_row = segment_ids[0]
    places = jnp.arange(seq_len)
    allowed = (seg_row[:, None] == seg_row[None, :]) & (places[None, :] <= places[:, None]) & (
        live_row[None, :] > 0
    ) | (places[None, :] == places[:, None])
    scores = jnp.einsum("qkgd,skd->kgqs", q, k, preferred_element_type=f32) * scale
    scores = jnp.where(allowed[None, None], scores, negative)
    top_score = jnp.max(scores, -1, keepdims=True)
    exp_scores = jnp.exp(scores - top_score)
    probs = exp_scores / jnp.sum(exp_scores, -1, keepdims=True)
    probs_low = probs.astype(bf16)
    attn_out = (
        jnp.einsum("kgqs,skd->qkgd", probs_low, v, preferred_element_type=f32)
        .astype(bf16)
        .reshape(seq_len, qw)
    )
    proj_part = dot_t(attn_out, out_w)
    theirs = lax.dynamic_slice_in_dim(proj_part, (1 - c.core) * half, half, 0)
    inputs_half = tokens.astype(f32)
    resid = inputs_half + (my_half(proj_part) + c.other(theirs))
    inv_two = lax.rsqrt(jnp.mean(resid * resid, -1, keepdims=True) + epsilon)
    normed_two = resid * inv_two
    hidden_moe = (normed_two * gain_two).astype(bf16)

    hm = jnp.concatenate(c.gather_group(hidden_moe), 0)
    logits = dot(hm, router_w)
    named = jnp.any(ids_group[:, :, None] == jnp.arange(EXPERTS)[None, None, :], 1)
    masked = jnp.where(named, logits, negative)
    shifted = jnp.where(named, jnp.exp(logits - jnp.max(masked, -1, keepdims=True)), 0.0)
    gates = shifted / jnp.sum(shifted, -1, keepdims=True)
    my_gates = lax.dynamic_slice_in_dim(gates, c.ep * local_experts, local_experts, 1)
    wide = jnp.repeat(my_gates, ff, axis=1)

    kept = []
    mixed = 0.0
    for gw, uw, dw in zip(gate_ws, up_ws, down_ws):
        a = dot(hm, gw)
        b = dot(hm, uw)
        sigma = jax.nn.sigmoid(a)
        h = (a * sigma * b).astype(bf16)
        hs = (h.astype(f32) * wide).astype(bf16)
        mixed = mixed + dot_t(hs, dw)
        kept.append((a, b, h, hs))
    mixed = mixed.reshape(GROUP, half, MODEL_WIDTH)
    mix = mixed[0]
    for j in range(1, GROUP):
        mix = mix + c.swap(mixed[j].astype(bf16), c.reps * j).astype(f32)
    result = resid + mix

    live = my_half(live_row).astype(f32)[:, None]
    differ = result - my_half(teacher).astype(f32)
    err_cols = jnp.sum(live * differ * differ, 0)
    grad_out = seq_len * c.n / live_total * live * differ
    go = jnp.concatenate(c.gather_group(grad_out.astype(bf16)), 0)

    grad_hm = 0.0
    grad_gates = 0.0
    low = []
    for (a, b, h, hs), gw, uw, dw in zip(kept, gate_ws, up_ws, down_ws):
        u = dot(go, dw)
        grad_gates = grad_gates + jnp.sum(
            (h.astype(f32) * u).reshape(GROUP * half, local_experts, ff), -1
        )
        gh = u * wide
        sigma = jax.nn.sigmoid(a)
        ga = (gh * b * sigma * (1.0 + a * (1.0 - sigma))).astype(bf16)
        gb = (gh * a * sigma).astype(bf16)
        grad_hm = grad_hm + dot_t(ga, gw) + dot_t(gb, uw)
        low.append((ga, gb))
    gg = jnp.zeros((GROUP * half, MISC), f32)
    gg = lax.dynamic_update_slice_in_dim(gg, grad_gates, c.ep * local_experts, 1)
    back = jnp.concatenate([grad_hm, gg], 1).reshape(GROUP, half, MODEL_WIDTH + MISC)
    back_sum = back[0]
    for j in range(1, GROUP):
        back_sum = back_sum + c.swap(back[j].astype(bf16), c.reps * j).astype(f32)

    weight_sums = []
    for own, other in (
        ((hm, low[0][0]), (hm, low[1][0])),
        ((hm, low[0][1]), (hm, low[1][1])),
        ((go, kept[0][3]), (go, kept[1][3])),
    ):
        away = dot_o(*other).astype(bf16)
        weight_sums.append(dot_o(*own) + c.other(away).astype(f32))
    gate_s = c.scatter_reps(weight_sums[0], False)
    up_s = c.scatter_reps(weight_sums[1], True)
    down_s = jnp.concatenate(
        [
            c.scatter_reps(weight_sums[2][:, : ew // 2], False),
            c.scatter_reps(weight_sums[2][:, ew // 2 :], True),
        ],
        2,
    )
    sums = jnp.concatenate([gate_s, up_s, down_s], 2)
    sums_low = sums.astype(bf16)
    parts = [c.block(sums, 0)] + [
        c.swap(c.block(sums_low, k), c.reps * k).astype(f32) for k in range(1, GROUP)
    ]
    finished = c.stack_group(parts)

    def expert_grad(j):
        g = finished[:, :, j * ew : (j + 1) * ew].transpose(1, 0, 2)
        return g.reshape(rows, EXPERTS, ff)

    grad_probs = back_sum[:, MODEL_WIDTH : MODEL_WIDTH + EXPERTS]
    gate_probs = gates[:half]
    grad_logits = (
        gate_probs * (grad_probs - jnp.sum(gate_probs * grad_probs, -1, keepdims=True))
    ).astype(bf16)
    grad_hidden = back_sum[:, :MODEL_WIDTH] + dot_t(grad_logits, router_w)
    router_part = dot_o(hidden_moe, grad_logits)
    gain_two_part = jnp.sum(grad_hidden * normed_two, 0)
    scaled_two = grad_hidden * gain_two
    grad_resid = grad_out + inv_two * (
        scaled_two - normed_two * jnp.mean(scaled_two * normed_two, -1, keepdims=True)
    )
    gy_half = grad_resid.astype(bf16)
    gy = join_rows(gy_half, c.other(gy_half))

    out_part = dot_o(gy, attn_out)
    grad_attn = dot(gy, out_w).astype(bf16).reshape(seq_len, kv_heads, per, HEAD_SIZE)
    gp = jnp.einsum("qkgd,skd->kgqs", grad_attn, v, preferred_element_type=f32)
    gs = (probs * (gp - jnp.sum(probs * gp, -1, keepdims=True))).astype(bf16)
    gq = jnp.einsum("kgqs,skd->qkgd", gs, k, preferred_element_type=f32) * scale
    gk = jnp.einsum("kgqs,qkgd->skd", gs, q, preferred_element_type=f32) * scale
    gv = jnp.einsum("kgqs,qkgd->skd", probs_low, grad_attn, preferred_element_type=f32)
    gqk = jnp.concatenate([gq.reshape(seq_len, qw), gk.reshape(seq_len, kw)], 1)
    gqk = gqk * cosine - swap_halves(gqk) * sine
    gqkv = jnp.concatenate([gqk.astype(bf16), gv.astype(bf16).reshape(seq_len, kw)], 1)
    ghn_part = dot_t(gqkv, proj_w)
    ghn_low = ghn_part.astype(bf16)
    ghn = my_half(ghn_part) + c.other(
        lax.dynamic_slice_in_dim(ghn_low, (1 - c.core) * half, half, 0)
    ).astype(f32)
    proj_part_grad = dot_o(attention_hidden, gqkv)
    normed_half = my_half(normed_one)
    gain_one_part = jnp.sum(ghn * normed_half, 0)
    scaled_one = ghn * gain_one
    grad_input = grad_resid + my_half(inv_one) * (
        scaled_one - normed_half * jnp.mean(scaled_one * normed_half, -1, keepdims=True)
    )

    err_rows = jnp.sum(err_cols.reshape(MODEL_WIDTH // rows, rows), 0)
    misc_part = jnp.concatenate(
        [
            router_part,
            gain_one_part[:, None],
            gain_two_part[:, None],
            jnp.tile(err_rows, c.n)[:, None],
            jnp.zeros((MODEL_WIDTH, MISC - EXPERTS - 3), f32),
        ],
        1,
    )
    back_w = jnp.concatenate([proj_part_grad, out_part, misc_part], 1)
    mid = (back_w.shape[1] // 256) * 128
    attn_s = jnp.concatenate(
        [c.scatter_reps(back_w[:, :mid], False), c.scatter_reps(back_w[:, mid:], True)], 2
    )
    attn_low = attn_s.astype(bf16)
    own_w = c.block(attn_s, 0)
    for k_ in range(1, GROUP):
        own_w = own_w + c.swap(c.block(attn_low, k_), c.reps * k_).astype(f32)
    misc_own = own_w[:, pw + qw :]
    misc_own = misc_own + c.other(misc_own)
    loss = jnp.sum(misc_own[:, EXPERTS + 2]) / (2.0 * MODEL_WIDTH * live_total)

    return (
        loss,
        result.astype(bf16),
        grad_input.astype(bf16),
        misc_own[:, EXPERTS],
        own_w[:, :qw],
        own_w[:, qw : qw + kw],
        own_w[:, qw + kw : pw],
        own_w[:, pw : pw + qw],
        misc_own[:, EXPERTS + 1],
        misc_own[:, :EXPERTS],
        expert_grad(0),
        expert_grad(1),
        expert_grad(2),
    )


def solution(mesh):
    placed = (
        P(("dp", "tensor"), None),
        P("dp", None),
        P("dp", None),
        P("dp", None),
        P("dp", None),
        P("dp"),
        P("dp", "tensor"),
        P("dp", "tensor"),
        P("dp", "tensor"),
        P("dp", "tensor"),
        P("dp"),
        P("dp", None),
        P("dp", None, "tensor"),
        P("dp", None, "tensor"),
        P("dp", None, "tensor"),
    )
    return jax.shard_map(
        shards,
        mesh=mesh,
        in_specs=placed,
        out_specs=(
            P(),
            P(("dp", "tensor"), None),
            P(("dp", "tensor"), None),
            P("dp"),
            P("dp", "tensor"),
            P("dp", "tensor"),
            P("dp", "tensor"),
            P("dp", "tensor"),
            P("dp"),
            P("dp", None),
            P("dp", None, "tensor"),
            P("dp", None, "tensor"),
            P("dp", None, "tensor"),
        ),
        check_vma=False,
    )
```

```python
import jax
import jax.numpy as jnp
from jax import lax
from jax.experimental import pallas as pl
from jax.experimental.pallas import tpu as pltpu
from jax.sharding import PartitionSpec as P

MODEL_WIDTH = 1024
HEAD_SIZE = 64
TOPK = 8
EXPERTS = 16
GROUP = 4
MISC = 128
VMEM_BYTES = 48 << 20

epsilon = 1e-06
negative = -1e30
rope_base = 10000.0
f32 = jnp.float32
bf16 = jnp.bfloat16

INNER = (((1,), (1,)), ((), ()))
OUTER = (((0,), (0,)), ((), ()))


def dot(a, b):
    return jnp.dot(a, b, preferred_element_type=f32)


def dot_t(a, b):
    return lax.dot_general(a, b, INNER, preferred_element_type=f32)


def dot_o(a, b):
    return lax.dot_general(a, b, OUTER, preferred_element_type=f32)


def tie(v, *after):
    return lax.optimization_barrier((v, after))[0]


def rope_tables(length, width):
    half = HEAD_SIZE // 2
    places = jnp.arange(length).astype(f32)
    freqs = rope_base ** (-2.0 * jnp.arange(half).astype(f32) / HEAD_SIZE)
    angles = places[:, None] * freqs[None, :]
    cosine, sine = jnp.cos(angles), jnp.sin(angles)
    reps = width // HEAD_SIZE
    return (
        jnp.tile(jnp.concatenate([cosine, cosine], 1), (1, reps)),
        jnp.tile(jnp.concatenate([-sine, sine], 1), (1, reps)),
    )


def swap_halves(u):
    half = HEAD_SIZE // 2
    low = (jnp.arange(u.shape[1]) % HEAD_SIZE) < half
    return jnp.where(low[None, :], jnp.roll(u, -half, 1), jnp.roll(u, half, 1))


class Comm:
    def __init__(self):
        self.n = lax.axis_size("dp")
        self.me = lax.axis_index("dp")
        self.core = lax.axis_index("tensor")
        self.reps = self.n // GROUP
        self.ep = self.me // self.reps
        self.rep = self.me % self.reps
        self.bits = [1 << k for k in range(self.reps.bit_length() - 1)]

    def swap(self, v, mask):
        return lax.ppermute(v, "dp", [(i, i ^ mask) for i in range(self.n)])

    def other(self, v):
        return lax.ppermute(v, "tensor", [(0, 1), (1, 0)])

    def bit(self, b):
        return (self.rep // b) % 2

    def gather_reps(self, z, last_first):
        rows, cols = z.shape[1:]
        k = len(self.bits)
        out = jnp.zeros((GROUP,) + (2,) * k + (rows, cols), z.dtype)
        zero = jnp.int32(0)
        order = list(self.bits)
        if last_first:
            order = order[::-1]
        done = set()

        def place(block, flipped):
            start = [zero]
            for b in reversed(self.bits):
                if b in done:
                    start.append(zero)
                elif b == flipped:
                    start.append(1 - self.bit(b))
                else:
                    start.append(self.bit(b))
            return start + [zero, zero]

        cur = z.reshape((GROUP,) + (1,) * k + (rows, cols))
        out = lax.dynamic_update_slice(out, cur, place(cur, None))
        for b in order:
            got = self.swap(cur, b)
            out = lax.dynamic_update_slice(out, got, place(got, b))
            done.add(b)
            if len(done) < k:
                start = place(out, None)
                shape = [GROUP] + [2 if c in done else 1 for c in reversed(self.bits)]
                cur = lax.dynamic_slice(out, start, shape + [rows, cols])
        return out.reshape(GROUP * self.reps * rows, cols)

    def stack_group(self, parts, axis=0):
        parts = jnp.stack(parts, 0)
        idx = self.ep ^ jnp.arange(GROUP)
        return jnp.concatenate(
            [lax.dynamic_index_in_dim(parts, idx[j], 0, keepdims=True) for j in range(GROUP)], 0
        )

    def gather_group(self, v):
        return [v] + [self.swap(v, self.reps * k) for k in range(1, GROUP)]

    def block(self, v, k):
        return lax.dynamic_index_in_dim(v, self.ep ^ k, 0, keepdims=False)

    def all_to_group(self, v):
        return [self.block(v, 0)] + [
            self.swap(self.block(v, k), self.reps * k) for k in range(1, GROUP)
        ]

    def scatter_reps(self, s, last_first):
        cols = s.shape[1]
        k = len(self.bits)
        rows = s.shape[0] // (GROUP * self.reps)
        s = s.reshape((GROUP,) + (2,) * k + (rows, cols))
        order = list(self.bits)
        if last_first:
            order = order[::-1]
        for b in order:
            axis = 1 + list(reversed(self.bits)).index(b)
            mine = self.bit(b)
            send = lax.dynamic_slice_in_dim(s, 1 - mine, 1, axis).astype(bf16)
            keep = lax.dynamic_slice_in_dim(s, mine, 1, axis)
            s = keep + self.swap(send, b).astype(f32)
        return s.reshape(GROUP, rows, cols)


VM = pltpu.VMEM
ANY = pl.ANY


def vmem():
    return pl.BlockSpec(memory_space=pltpu.VMEM)


def anym():
    return pl.BlockSpec(memory_space=pl.ANY)


def smem():
    return pl.BlockSpec(memory_space=pltpu.SMEM)


def sds(shape, dtype):
    return jax.ShapeDtypeStruct(shape, dtype)


def kernel_call(body, out_shape, in_specs, name, scratch=(), out_specs=None, flops=0, moved=0):
    if out_specs is None:
        out_specs = jax.tree.map(lambda _: vmem(), out_shape)
    return pl.pallas_call(
        body,
        out_shape=out_shape,
        in_specs=in_specs,
        out_specs=out_specs,
        scratch_shapes=list(scratch),
        compiler_params=pltpu.CompilerParams(vmem_limit_bytes=VMEM_BYTES),
        cost_estimate=pl.CostEstimate(flops=flops, bytes_accessed=moved, transcendentals=0),
        name=name,
    )


def place(row):
    return row


def piece_copies(pieces, dst, sem, ep, rep, cols=None, first=0):
    copies = []
    for j, piece in enumerate(pieces):
        m, h = j // 2, j % 2
        for i in range(2):
            at = (ep ^ (2 * h + i)) * 4 + (rep ^ m)
            src, to = piece.at[pl.ds(64 * i, 64)], dst.at[at]
            if cols is not None:
                src, to = src.at[:, pl.ds(*cols)], to.at[:, pl.ds(*cols)]
            copies.append(pltpu.make_async_copy(src, to, sem.at[first + 2 * j + i]))
    return copies


def pack_front_body(wq, wk, wv, wr, g1, g2, valid, out):
    qw, kw = wq.shape[1], wk.shape[1]
    n = wq.shape[0]
    out[:, 0:qw] = wq[...]
    out[:, qw : qw + kw] = wk[...]
    out[:, qw + kw : qw + 2 * kw] = wv[...]
    count = jnp.sum(valid[...].astype(f32), axis=1, keepdims=True)
    base = jnp.concatenate([wr[...].astype(f32), jnp.zeros((MISC - EXPERTS, n), f32)], 0)
    row = lax.broadcasted_iota(jnp.int32, (MISC, n), 0)
    base = jnp.where(row == EXPERTS, g1[...].astype(f32), base)
    base = jnp.where(row == EXPERTS + 1, g2[...].astype(f32), base)
    base = jnp.where(row == EXPERTS + 2, count, base)
    eye = lax.broadcasted_iota(jnp.int32, (n, n), 0) == lax.broadcasted_iota(jnp.int32, (n, n), 1)
    misc = dot_t(eye.astype(f32).astype(bf16), base.astype(bf16))
    out[:, qw + 2 * kw :] = misc.astype(bf16)


def pack_front(wq, wk, wv, wr, g1, g2, valid):
    n = wq.shape[0]
    width = wq.shape[1] + 2 * wk.shape[1] + MISC
    return kernel_call(pack_front_body, sds((n, width), bf16), [vmem()] * 7, "pack_front")(
        wq, wk, wv, wr.T, g1[None, :], g2[None, :], valid
    )


def pack_experts_body(sc, wg, wu, wd, out0, out1, out2, out3, wide):
    ep = sc[0]
    n, e, f = wg.shape
    per = e // GROUP
    for j, w in enumerate((wg, wu, wd)):
        for l in range(f // 128):
            wide[l] = w[:, :, 128 * l : 128 * (l + 1)].astype(f32).reshape(n * e, 128)
        for k, out in enumerate((out0, out1, out2, out3)):
            for x in range(per):
                for l in range(f // 128):
                    at = j * per * f + x * f + 128 * l
                    out[:, at : at + 128] = wide[
                        l, pl.ds((ep ^ k) * per + x, n, stride=e), :
                    ].astype(bf16)


def pack_experts(sc, wg, wu, wd):
    n, e, f = wg.shape
    return kernel_call(
        pack_experts_body,
        (sds((n, 3 * e * f // GROUP), bf16),) * GROUP,
        [smem()] + [vmem()] * 3,
        "pack_experts",
        [VM((f // 128, n * e, 128), f32)],
    )(sc, wg, wu, wd)


def rotate_pairs(u, cosine, sine):
    lane = lax.broadcasted_iota(jnp.int32, u.shape, 1)
    low = lane % HEAD_SIZE < HEAD_SIZE // 2
    turned = jnp.where(low, pltpu.roll(u, 96, 1), pltpu.roll(u, 32, 1))
    return u * cosine + turned * sine


def both_lanes(pair, odd):
    lane = lax.broadcasted_iota(jnp.int32, pair.shape, 1)
    other = pltpu.roll(pair, 64, 1)
    first = lane < HEAD_SIZE
    return jnp.where(first, other, pair) if odd else jnp.where(first, pair, other)


def two_heads(pair):
    lane = lax.broadcasted_iota(jnp.int32, pair.shape, 1)
    zero = jnp.zeros_like(pair)
    return jnp.concatenate(
        [jnp.where(lane < HEAD_SIZE, pair, zero), jnp.where(lane < HEAD_SIZE, zero, pair)], 0
    )


def one_pair(rows):
    n = rows.shape[0] // 2
    lane = lax.broadcasted_iota(jnp.int32, (n, rows.shape[1]), 1)
    return jnp.where(lane < HEAD_SIZE, rows[:n], rows[n:])


def allowed_mask(seg, valid):
    n = seg.shape[1]
    r = lax.broadcasted_iota(jnp.int32, (n, n), 0)
    col = lax.broadcasted_iota(jnp.int32, (n, n), 1)
    seg_row = jnp.broadcast_to(seg.astype(f32), (n, n))
    seg_col = jnp.sum(jnp.where(r == col, seg_row, 0.0), axis=1, keepdims=True)
    live = jnp.broadcast_to(valid.astype(f32), (n, n)) > 0
    return ((seg_col == seg_row) & (col <= r) & live) | (r == col)


def softmax_rows(q2, k2, allowed2):
    s = dot_t(q2, k2) * (1.0 / HEAD_SIZE)
    s = jnp.where(allowed2, s, negative)
    e = jnp.exp(s - jnp.max(s, axis=1, keepdims=True))
    return e / jnp.sum(e, axis=1, keepdims=True)


def attn_fwd_body(sc, x_own, x_oth, seg, valid, cosine, sine, *refs):
    pieces = refs[:8]
    hn_out, qkv_out, o_out, misc_out, gains_out, w_out, w, x, sem = refs[8:]
    ep, rep, core = sc[0], sc[1], sc[2]
    copies = piece_copies(pieces, w, sem, ep, rep)
    for cp in copies:
        cp.start()
    half = x_own.shape[0]
    x[pl.ds(core * half, half), :] = x_own[...].astype(f32)
    x[pl.ds((1 - core) * half, half), :] = x_oth[...].astype(f32)
    allowed = allowed_mask(seg[...], valid[...])
    allowed2 = jnp.concatenate([allowed, allowed], 0)
    inputs = x[...]
    normed = inputs * lax.rsqrt(jnp.mean(inputs * inputs, axis=1, keepdims=True) + epsilon)
    for cp in copies:
        cp.wait()
    pw = w.shape[2] - MISC
    misc = w[:, :, pw:].reshape(MODEL_WIDTH, MISC)
    pick = lax.broadcasted_iota(jnp.int32, (8, MISC), 0) + EXPERTS
    pick = (pick == lax.broadcasted_iota(jnp.int32, (8, MISC), 1)).astype(f32).astype(bf16)
    gains = dot_t(pick, misc)
    gains_out[...] = gains
    misc_out[...] = misc
    hn = (normed * gains[0:1, :]).astype(bf16)
    hn_out[...] = hn
    proj = w[:, :, :pw].reshape(MODEL_WIDTH, pw)
    w_out[...] = proj
    qkv = dot(hn, proj)
    n = hn.shape[0]
    groups = pw // 128
    kv0 = groups // 2
    for g in range(groups):
        u = qkv[:, 128 * g : 128 * (g + 1)]
        if g < kv0 + kv0 // 2:
            u = rotate_pairs(u, cosine[...], sine[...])
        qkv_out[:, 128 * g : 128 * (g + 1)] = u.astype(bf16)
    for m in range(kv0):
        g = kv0 + m // 2
        k2 = both_lanes(qkv_out[:, 128 * g : 128 * (g + 1)].astype(f32), m % 2).astype(bf16)
        g = g + kv0 // 2
        v2 = both_lanes(qkv_out[:, 128 * g : 128 * (g + 1)].astype(f32), m % 2).astype(bf16)
        q2 = two_heads(qkv_out[:, 128 * m : 128 * (m + 1)].astype(f32)).astype(bf16)
        p = softmax_rows(q2, k2, allowed2).astype(bf16)
        o_out[:, 128 * m : 128 * (m + 1)] = one_pair(dot(p, v2)).astype(bf16)


def attn_fwd(sc, x_own, x_oth, seg, valid, cosine, sine, pieces):
    n = 2 * x_own.shape[0]
    cols = pieces[0].shape[1]
    pw = cols - MISC
    return kernel_call(
        attn_fwd_body,
        (
            sds((n, MODEL_WIDTH), bf16),
            sds((n, pw), bf16),
            sds((n, pw // 2), bf16),
            sds((MODEL_WIDTH, MISC), bf16),
            sds((8, MODEL_WIDTH), f32),
            sds((MODEL_WIDTH, pw), bf16),
        ),
        [smem()] + [vmem()] * 6 + [anym()] * 8,
        "attn_fwd",
        [VM((16, 64, cols), bf16), VM((n, MODEL_WIDTH), f32), pltpu.SemaphoreType.DMA((16,))],
        flops=2 * n * MODEL_WIDTH * pw * 2,
        moved=8 << 20,
    )(sc, x_own, x_oth, seg, valid, cosine, sine, *pieces)


def attn_proj_body(sc, o, *refs):
    pieces = refs[:8]
    own_out, away_out, w_out, w, sem = refs[8:]
    ep, rep, core = sc[0], sc[1], sc[2]
    copies = piece_copies(pieces, w, sem, ep, rep)
    for cp in copies:
        cp.start()
    for cp in copies:
        cp.wait()
    half = own_out.shape[0]
    ws = w[...].reshape(MODEL_WIDTH, w.shape[2])
    w_out[...] = ws
    away_out[...] = dot_t(o[pl.ds((1 - core) * half, half), :], ws)
    own_out[...] = dot_t(o[pl.ds(core * half, half), :], ws)


def attn_proj(sc, o, pieces):
    half = o.shape[0] // 2
    cols = o.shape[1]
    return kernel_call(
        attn_proj_body,
        (
            sds((half, MODEL_WIDTH), f32),
            sds((half, MODEL_WIDTH), f32),
            sds((MODEL_WIDTH, cols), bf16),
        ),
        [smem(), vmem()] + [anym()] * 8,
        "attn_proj",
        [VM((16, 64, cols), bf16), pltpu.SemaphoreType.DMA((16,))],
        flops=4 * half * MODEL_WIDTH * cols,
        moved=4 << 20,
    )(sc, o, *pieces)


def second_norm_body(x, y_own, y_oth, gains, resid_out, hm_out):
    resid = x[...].astype(f32) + (y_own[...] + y_oth[...])
    resid_out[...] = resid
    inv = lax.rsqrt(jnp.mean(resid * resid, axis=1, keepdims=True) + epsilon)
    hm_out[...] = (resid * inv * gains[1:2, :]).astype(bf16)


def second_norm(x, y_own, y_oth, gains):
    return kernel_call(
        second_norm_body,
        (sds(y_own.shape, f32), sds(y_own.shape, bf16)),
        [vmem()] * 4,
        "second_norm",
    )(x, y_own, y_oth, gains)


def gates_of(hm, misc, ids):
    rows = hm.shape[0]
    logits = dot(hm, misc)
    lane = lax.broadcasted_iota(jnp.int32, (rows, MISC), 1)
    named = lane < 0
    eye = lax.broadcasted_iota(jnp.int32, (rows, rows), 0) == lax.broadcasted_iota(
        jnp.int32, (rows, rows), 1
    )
    for j in range(TOPK):
        row = jnp.broadcast_to(ids[j : j + 1, :].astype(f32), (rows, rows))
        col = jnp.sum(jnp.where(eye, row, 0.0), axis=1, keepdims=True).astype(jnp.int32)
        named = named | (lane == col)
    top = jnp.max(jnp.where(named, logits, negative), axis=1, keepdims=True)
    e = jnp.where(named, jnp.exp(logits - top), 0.0)
    return e / jnp.sum(e, axis=1, keepdims=True)


def expert_copies(own, other, w, sem, ep, rep, ew):
    wide = piece_copies(own, w.at[0], sem, ep, rep, (0, 2 * ew), 0)
    wide += piece_copies(other, w.at[1], sem, ep, rep, (0, 2 * ew), 16)
    down = piece_copies(own, w.at[0], sem, ep, rep, (2 * ew, ew), 32)
    down += piece_copies(other, w.at[1], sem, ep, rep, (2 * ew, ew), 48)
    return wide, down


def expert_fwd_body(sc, h0, h1, h2, h3, i0, i1, i2, i3, misc, *refs):
    own, other = refs[:8], refs[8:16]
    mix0, mix1, mix2, mix3, a_out, b_out, gates_out, w, hm, acc, sem = refs[16:]
    ep, rep = sc[0], sc[1]
    half = h0.shape[0]
    experts = EXPERTS // GROUP
    ew = w.shape[3] // 3
    ff = ew // experts
    wide, down = expert_copies(own, other, w, sem, ep, rep, ew)
    for cp in wide:
        cp.start()
    for cp in down:
        cp.start()
    for j, (h, i) in enumerate(((h0, i0), (h1, i1), (h2, i2), (h3, i3))):
        hm[pl.ds(j * half, half), :] = h[...]
        gates_out[pl.ds(j * half, half), :] = gates_of(h[...], misc[...], i[...])
    acc[...] = jnp.zeros_like(acc)
    lane = lax.broadcasted_iota(jnp.int32, (GROUP * half, MISC), 1)
    for cp in wide:
        cp.wait()
    for cp in down:
        cp.wait()

    def tile(t, carry):
        c = t // experts
        e = t % experts
        rows = hm[...]
        at = pl.multiple_of(e * ff, ff)
        wg = w[c, :, :, pl.ds(at, ff)].reshape(MODEL_WIDTH, ff)
        wu = w[c, :, :, pl.ds(ew + at, ff)].reshape(MODEL_WIDTH, ff)
        wd = w[c, :, :, pl.ds(2 * ew + at, ff)].reshape(MODEL_WIDTH, ff)
        a = dot(rows, wg)
        b = dot(rows, wu)
        g = jnp.sum(
            jnp.where(lane == ep * experts + e, gates_out[...], 0.0), axis=1, keepdims=True
        )
        h = (a * jax.nn.sigmoid(a) * b).astype(bf16)
        hs = (h.astype(f32) * g).astype(bf16)
        to = pl.multiple_of(t * ff, ff)
        a_out[:, pl.ds(to, ff)] = a
        b_out[:, pl.ds(to, ff)] = b
        acc[...] += dot_t(hs, wd)
        return carry

    lax.fori_loop(0, 2 * experts, tile, 0)
    mix0[...] = acc[0:half, :]
    for j, m in enumerate((mix1, mix2, mix3)):
        m[...] = acc[(j + 1) * half : (j + 2) * half, :].astype(bf16)


def expert_fwd(sc, hs, ids, misc, own, other):
    half = hs[0].shape[0]
    cols = own[0].shape[1]
    wide = 2 * cols // 3
    rows = GROUP * half
    return kernel_call(
        expert_fwd_body,
        (
            sds((half, MODEL_WIDTH), f32),
            sds((half, MODEL_WIDTH), bf16),
            sds((half, MODEL_WIDTH), bf16),
            sds((half, MODEL_WIDTH), bf16),
            sds((rows, wide), f32),
            sds((rows, wide), f32),
            sds((rows, MISC), f32),
        ),
        [smem()] + [vmem()] * 9 + [anym()] * 16,
        "expert_fwd",
        [
            VM((2, 16, 64, cols), bf16),
            VM((rows, MODEL_WIDTH), bf16),
            VM((rows, MODEL_WIDTH), f32),
            pltpu.SemaphoreType.DMA((64,)),
        ],
        flops=6 * rows * MODEL_WIDTH * wide,
        moved=24 << 20,
    )(sc, *hs, *ids, misc, *own, *other)


def expert_bwd_body(sc, g0, g1, g2, g3, gates, a_in, b_in, *refs):
    own, other = refs[:8], refs[8:16]
    back0, back1, back2, back3, ga_out, gb_out, hs_out, w, go, acc, gsum, sem = refs[16:]
    ep, rep = sc[0], sc[1]
    half = g0.shape[0]
    experts = EXPERTS // GROUP
    ew = w.shape[3] // 3
    ff = ew // experts
    wide, down = expert_copies(own, other, w, sem, ep, rep, ew)
    for cp in down:
        cp.start()
    for cp in wide:
        cp.start()
    for j, g in enumerate((g0, g1, g2, g3)):
        go[pl.ds(j * half, half), :] = g[...]
    acc[...] = jnp.zeros_like(acc)
    gsum[...] = jnp.zeros_like(gsum)
    lane = lax.broadcasted_iota(jnp.int32, (GROUP * half, MISC), 1)
    for cp in down:
        cp.wait()
    for cp in wide:
        cp.wait()

    def tile(t, carry):
        c = t // experts
        e = t % experts
        at = pl.multiple_of(e * ff, ff)
        wg = w[c, :, :, pl.ds(at, ff)].reshape(MODEL_WIDTH, ff)
        wu = w[c, :, :, pl.ds(ew + at, ff)].reshape(MODEL_WIDTH, ff)
        wd = w[c, :, :, pl.ds(2 * ew + at, ff)].reshape(MODEL_WIDTH, ff)
        to = pl.multiple_of(t * ff, ff)
        a = a_in[:, pl.ds(to, ff)]
        b = b_in[:, pl.ds(to, ff)]
        u = dot(go[...], wd)
        mine = lane == ep * experts + e
        g = jnp.sum(jnp.where(mine, gates[...], 0.0), axis=1, keepdims=True)
        s = jax.nn.sigmoid(a)
        silu = a * s
        h = (silu * b).astype(bf16).astype(f32)
        gsum[...] += jnp.where(mine, jnp.sum(h * u, axis=1, keepdims=True), 0.0)
        gh = u * g
        ga = (gh * b * s * (1.0 + a * (1.0 - s))).astype(bf16)
        gb = (gh * silu).astype(bf16)
        ga_out[:, pl.ds(to, ff)] = ga
        gb_out[:, pl.ds(to, ff)] = gb
        hs_out[:, pl.ds(to, ff)] = (h * g).astype(bf16)
        acc[...] += dot_t(ga, wg) + dot_t(gb, wu)
        return carry

    lax.fori_loop(0, 2 * experts, tile, 0)
    back0[:, :MODEL_WIDTH] = acc[0:half, :]
    back0[:, MODEL_WIDTH:] = gsum[0:half, :]
    for j, m in enumerate((back1, back2, back3)):
        m[:, :MODEL_WIDTH] = acc[(j + 1) * half : (j + 2) * half, :].astype(bf16)
        m[:, MODEL_WIDTH:] = gsum[(j + 1) * half : (j + 2) * half, :].astype(bf16)


def expert_bwd(sc, gs, gates, a, b, own, other):
    half = gs[0].shape[0]
    cols = own[0].shape[1]
    wide = a.shape[1]
    rows = GROUP * half
    full = MODEL_WIDTH + MISC
    return kernel_call(
        expert_bwd_body,
        (
            sds((half, full), f32),
            sds((half, full), bf16),
            sds((half, full), bf16),
            sds((half, full), bf16),
            sds((rows, wide), bf16),
            sds((rows, wide), bf16),
            sds((rows, wide), bf16),
        ),
        [smem()] + [vmem()] * 7 + [anym()] * 16,
        "expert_bwd",
        [
            VM((2, 16, 64, cols), bf16),
            VM((rows, MODEL_WIDTH), bf16),
            VM((rows, MODEL_WIDTH), f32),
            VM((rows, MISC), f32),
            pltpu.SemaphoreType.DMA((64,)),
        ],
        flops=6 * rows * MODEL_WIDTH * wide,
        moved=32 << 20,
    )(sc, *gs, gates, a, b, *own, *other)


def loss_body(resid, m0, m1, m2, m3, teacher, live, gains, scale, result_out, g_out, glow_out, err_out):
    mix = m0[...] + (m1[...].astype(f32) + m2[...].astype(f32) + m3[...].astype(f32))
    result = resid[...] + mix
    result_out[...] = result.astype(bf16)
    differ = result - teacher[...].astype(f32)
    rows = gains.shape[1] // scale.shape[1]
    total = jnp.sum(gains[2:3, :], axis=1, keepdims=True) / rows
    weighted = live[...] * differ
    g = (scale.shape[0] * scale.shape[1]) / total * weighted
    g_out[...] = g
    glow_out[...] = g.astype(bf16)
    err_out[...] = jnp.broadcast_to(jnp.sum(weighted * differ, axis=0, keepdims=True), err_out.shape)


def loss_grad(resid, mixes, teacher, live, gains, seq_len, n):
    shape = resid.shape
    return kernel_call(
        loss_body,
        (sds(shape, bf16), sds(shape, f32), sds(shape, bf16), sds((8, shape[1]), f32)),
        [vmem()] * 9,
        "loss_grad",
    )(resid, *mixes, teacher, live, gains, jnp.zeros((seq_len, n), f32))


def second_back_body(b0, b1, b2, b3, gates, misc, hm, resid, gains, g_out, gy_out, gres_out, rows_out):
    half = resid.shape[0]
    total = b0[...] + (b1[...].astype(f32) + b2[...].astype(f32) + b3[...].astype(f32))
    gp = total[:, MODEL_WIDTH:]
    gate = gates[0:half, :]
    gl = (gate * (gp - jnp.sum(gate * gp, axis=1, keepdims=True))).astype(bf16)
    ghm = total[:, :MODEL_WIDTH] + dot_t(gl, misc[...])
    x = resid[...]
    inv = lax.rsqrt(jnp.mean(x * x, axis=1, keepdims=True) + epsilon)
    normed = x * inv
    rows = dot_o(gl, hm[...])
    gain_row = jnp.sum(ghm * normed, axis=0, keepdims=True)
    at = lax.broadcasted_iota(jnp.int32, rows.shape, 0)
    rows_out[...] = jnp.where(at == EXPERTS + 1, gain_row, rows)
    scaled = ghm * gains[1:2, :]
    gres = g_out[...] + inv * (
        scaled - normed * jnp.mean(scaled * normed, axis=1, keepdims=True)
    )
    gres_out[...] = gres
    gy_out[...] = gres.astype(bf16)


def second_back(backs, gates, misc, hm, resid, gains, g_out):
    shape = resid.shape
    return kernel_call(
        second_back_body,
        (sds(shape, bf16), sds(shape, f32), sds((MISC, shape[1]), f32)),
        [vmem()] * 10,
        "second_back",
    )(*backs, gates, misc, hm, resid, gains, g_out)


def attn_bwd_body(
    sc, gy_own, gy_oth, o, qkv, seg, valid, cosine, sine, proj_w, out_w, gqkv_out, gy_out, own_out, away_out, low
):
    core = sc[2]
    half = gy_own.shape[0]
    n = 2 * half
    gy_out[pl.ds(core * half, half), :] = gy_own[...]
    gy_out[pl.ds((1 - core) * half, half), :] = gy_oth[...]
    low[...] = dot(gy_out[...], out_w[...]).astype(bf16)
    allowed = allowed_mask(seg[...], valid[...])
    allowed2 = jnp.concatenate([allowed, allowed], 0)
    pw = qkv.shape[1]
    kv0 = pw // 256
    lane = lax.broadcasted_iota(jnp.int32, (n, 128), 1)
    scale = 1.0 / HEAD_SIZE
    held = {}
    for m in range(kv0):
        gk_at = kv0 + m // 2
        gv_at = gk_at + kv0 // 2
        k2 = both_lanes(qkv[:, 128 * gk_at : 128 * (gk_at + 1)].astype(f32), m % 2).astype(bf16)
        v2 = both_lanes(qkv[:, 128 * gv_at : 128 * (gv_at + 1)].astype(f32), m % 2).astype(bf16)
        q2 = two_heads(qkv[:, 128 * m : 128 * (m + 1)].astype(f32)).astype(bf16)
        go2 = two_heads(low[:, 128 * m : 128 * (m + 1)].astype(f32)).astype(bf16)
        p = softmax_rows(q2, k2, allowed2)
        gp = dot_t(go2, v2)
        gs = (p * (gp - jnp.sum(p * gp, axis=1, keepdims=True))).astype(bf16)
        gq = one_pair(dot(gs, k2)) * scale
        gqkv_out[:, 128 * m : 128 * (m + 1)] = rotate_pairs(gq, cosine[...], -sine[...]).astype(bf16)
        gk = dot_o(gs, q2) * scale
        gv = dot_o(p.astype(bf16), go2)
        gk = gk + pltpu.roll(gk, 64, 1)
        gv = gv + pltpu.roll(gv, 64, 1)
        if m % 2 == 0:
            held = {"k": gk, "v": gv}
        else:
            gk = jnp.where(lane < HEAD_SIZE, held["k"], gk)
            gv = jnp.where(lane < HEAD_SIZE, held["v"], gv)
            gqkv_out[:, 128 * gk_at : 128 * (gk_at + 1)] = rotate_pairs(
                gk, cosine[...], -sine[...]
            ).astype(bf16)
            gqkv_out[:, 128 * gv_at : 128 * (gv_at + 1)] = gv.astype(bf16)
    away_out[...] = dot_t(gqkv_out[pl.ds((1 - core) * half, half), :], proj_w[...]).astype(bf16)
    own_out[...] = dot_t(gqkv_out[pl.ds(core * half, half), :], proj_w[...])


def attn_bwd(sc, gy_own, gy_oth, o, qkv, seg, valid, cosine, sine, proj_w, out_w):
    half = gy_own.shape[0]
    n = 2 * half
    pw = qkv.shape[1]
    return kernel_call(
        attn_bwd_body,
        (
            sds((n, pw), bf16),
            sds((n, MODEL_WIDTH), bf16),
            sds((half, MODEL_WIDTH), f32),
            sds((half, MODEL_WIDTH), bf16),
        ),
        [smem()] + [vmem()] * 10,
        "attn_bwd",
        [VM((n, o.shape[1]), bf16)],
        flops=6 * n * MODEL_WIDTH * pw,
        moved=8 << 20,
    )(sc, gy_own, gy_oth, o, qkv, seg, valid, cosine, sine, proj_w, out_w)


def first_back_body(g_own, g_oth, x, gains, gres, rows, err, ginput_out, rows_out):
    ghn = g_own[...] + g_oth[...].astype(f32)
    inputs = x[...].astype(f32)
    inv = lax.rsqrt(jnp.mean(inputs * inputs, axis=1, keepdims=True) + epsilon)
    normed = inputs * inv
    gain_row = jnp.sum(ghn * normed, axis=0, keepdims=True)
    scaled = ghn * gains[0:1, :]
    ginput_out[...] = (
        gres[...] + inv * (scaled - normed * jnp.mean(scaled * normed, axis=1, keepdims=True))
    ).astype(bf16)
    e = err[...]
    for shift in (64, 128, 256, 512):
        e = e + pltpu.roll(e, shift, 1)
    at = lax.broadcasted_iota(jnp.int32, rows.shape, 0)
    r = jnp.where(at == EXPERTS, gain_row, rows[...])
    rows_out[...] = jnp.where(at == EXPERTS + 2, e[0:1, :], r)


def first_back(g_own, g_oth, x, gains, gres, rows, err):
    return kernel_call(
        first_back_body,
        (sds(gres.shape, bf16), sds(rows.shape, f32)),
        [vmem()] * 7,
        "first_back",
    )(g_own, g_oth, x, gains, gres, rows, err)


def store_relative(outs, at, ep, rep, value, cols, keep=None):
    for j in range(16):
        to = 4 * ((j % 4) ^ rep) + ((j // 4) ^ ep)
        outs[to, :, cols] = value[64 * j : 64 * (j + 1), :].astype(outs.dtype)


def attn_dw_body(sc, gy, o, hn, gqkv, rows, out):
    ep, rep = sc[0], sc[1]
    pw = gqkv.shape[1]
    qw = o.shape[1]
    store_relative(out, None, ep, rep, dot_o(hn[...], gqkv[...]), slice(0, pw))
    store_relative(out, None, ep, rep, dot_o(gy[...], o[...]), slice(pw, pw + qw))
    store_relative(out, None, ep, rep, jnp.transpose(rows[...]), slice(pw + qw, pw + qw + MISC))


def attn_dw(sc, gy, o, hn, gqkv, rows):
    width = gqkv.shape[1] + o.shape[1] + MISC
    return kernel_call(
        attn_dw_body,
        sds((16, 64, width), f32),
        [smem()] + [vmem()] * 5,
        "attn_dw",
        flops=2 * MODEL_WIDTH * gqkv.shape[0] * width,
        moved=8 << 20,
    )(sc, gy, o, hn, gqkv, rows)


def expert_dw_body(sc, x0, x1, x2, x3, y, own_out, away_out, xt):
    i = pl.program_id(0)
    ep, rep = sc[0], sc[1]
    half = x0.shape[0]

    @pl.when(i == 0)
    def _():
        for j, x in enumerate((x0, x1, x2, x3)):
            xt[:, j * half : (j + 1) * half] = jnp.transpose(x[...])

    g = dot(xt[...], y[...])

    @pl.when(i < 4)
    def _():
        store_relative(away_out, None, ep, rep, g, slice(None))

    @pl.when(i >= 4)
    def _():
        store_relative(own_out, None, ep, rep, g, slice(None))


def expert_dw(sc, xs, y):
    half = xs[0].shape[0]
    tile = y.shape[1] // 8
    whole = pl.BlockSpec((half, MODEL_WIDTH), lambda i: (0, 0))
    return pl.pallas_call(
        expert_dw_body,
        grid=(8,),
        out_shape=(sds((16, 64, 4 * tile), f32), sds((16, 64, 4 * tile), bf16)),
        in_specs=[smem()]
        + [whole] * 4
        + [pl.BlockSpec((4 * half, tile), lambda i: (0, (i + 4) % 8))],
        out_specs=(
            pl.BlockSpec((16, 64, tile), lambda i: (0, 0, jnp.maximum(i - 4, 0))),
            pl.BlockSpec((16, 64, tile), lambda i: (0, 0, jnp.minimum(i, 3))),
        ),
        scratch_shapes=[VM((MODEL_WIDTH, 4 * half), bf16)],
        compiler_params=pltpu.CompilerParams(vmem_limit_bytes=VMEM_BYTES),
        cost_estimate=pl.CostEstimate(
            flops=8 * half * MODEL_WIDTH * 8 * tile, bytes_accessed=12 << 20, transcendentals=0
        ),
        name="expert_dw",
    )(sc, *xs, y)


def unpack_grad_body(sc, g0, g1, g2, g3, out, wide):
    ep = sc[0]
    n = g0.shape[0]
    experts = EXPERTS // GROUP
    ff = g0.shape[1] // experts
    for k, g in enumerate((g0, g1, g2, g3)):
        for e in range(experts):
            for l in range(ff // 128):
                at = e * ff + 128 * l
                wide[l, pl.ds((ep ^ k) * experts + e, n, stride=EXPERTS), :] = g[
                    :, at : at + 128
                ].astype(f32)
    for l in range(ff // 128):
        out[:, 128 * l : 128 * (l + 1)] = wide[l]


def unpack_grad(sc, parts):
    n, wide = parts[0].shape
    ff = wide * GROUP // EXPERTS
    out = kernel_call(
        unpack_grad_body,
        sds((n * EXPERTS, ff), f32),
        [smem()] + [vmem()] * 4,
        "unpack_grad",
        [VM((ff // 128, n * EXPERTS, 128), f32)],
    )(sc, *parts)
    return out.reshape(n, EXPERTS, ff)


def fast(
    c,
    tokens,
    segment_ids,
    valid,
    expert_ids,
    teacher,
    attn_gain,
    w_query,
    key_projection,
    value_projection,
    w_out,
    moe_gain,
    w_router,
    w_gate,
    w_up,
    w_down,
):
    half = tokens.shape[0]
    seq_len = expert_ids.shape[0]
    rows = w_query.shape[0]
    qw, kw = w_query.shape[1], key_projection.shape[1]
    pw = qw + 2 * kw
    sc = jnp.stack([c.ep, c.rep, c.core]).astype(jnp.int32)

    def my_half(v, axis=0):
        return lax.dynamic_slice_in_dim(v, c.core * half, half, axis)

    def group_pair(parts):
        return [jnp.concatenate(parts[:2], 0), jnp.concatenate(parts[2:], 0)]

    def spread(pair, after=()):
        a, b = (tie(p, *after) for p in pair)
        xa, ya = c.swap(a, 1), c.swap(a, 2)
        xb, yb = c.swap(b, 1), c.swap(b, 2)
        return [*pair, xa, xb, ya, yb, c.swap(xa, 2), c.swap(yb, 1)]

    tokens_oth = c.other(tokens)
    front = pack_front(
        w_query, key_projection, value_projection, w_router, attn_gain, moe_gain, valid
    )
    front_z = c.gather_group(front)
    front_p = spread(group_pair(front_z))
    out_z = c.gather_group(tie(w_out, *front_z[1:]))
    out_p = spread(group_pair(out_z), front_p[2:6])
    ids = my_half(tie(expert_ids, *front_z[1:]).T, 1)
    ids_g = c.gather_group(ids)
    packed = pack_experts(sc, *tie((w_gate, w_up, w_down), front))
    exp_z = [packed[0]] + [
        c.swap(tie(packed[k], *out_z[1:]), c.reps * k) for k in range(1, GROUP)
    ]
    exp_own = spread(group_pair(exp_z), front_p[6:])
    exp_oth = [c.other(p) for p in exp_own]

    cosine, sine = rope_tables(seq_len, 128)
    hn, qkv, o, misc, gains, proj_w = attn_fwd(
        sc, tokens, tokens_oth, segment_ids, valid, cosine, sine, front_p
    )
    y_own, y_away, out_w = attn_proj(sc, o, out_p)
    resid, hm = second_norm(tokens, y_own, c.other(y_away), gains)

    hms = c.gather_group(hm)
    mix0, mix1, mix2, mix3, a, b, gates = expert_fwd(sc, hms, ids_g, misc, exp_own, exp_oth)
    mixes = [mix0] + [c.swap(m, c.reps * (j + 1)) for j, m in enumerate((mix1, mix2, mix3))]
    live = my_half(valid[0]).astype(f32)[:, None]
    result, g_out, g_low, err = loss_grad(
        resid, mixes, my_half(teacher), live, gains, seq_len, c.n
    )

    gos = c.gather_group(g_low)
    back0, back1, back2, back3, ga, gb, hs = expert_bwd(sc, gos, gates, a, b, exp_own, exp_oth)
    backs = [back0] + [c.swap(m, c.reps * (j + 1)) for j, m in enumerate((back1, back2, back3))]
    sums = []
    for xs, y in ((hms, ga), (hms, gb), (gos, hs)):
        own, away = expert_dw(sc, xs, y)
        sums.append((own, c.other(away)))

    def replica_sum(s):
        rx = c.swap(jnp.concatenate([s[12:14], s[4:6]], 0).astype(bf16), 1)
        ry = c.swap(jnp.concatenate([s[14:16], s[10:12]], 0).astype(bf16), 2)
        sx = c.swap((s[6:8] + ry[0:2].astype(f32)).astype(bf16), 1)
        sy = c.swap((s[8:10] + rx[0:2].astype(f32)).astype(bf16), 2)
        return (
            s[0:2] + (rx[2:4].astype(f32) + sy.astype(f32)),
            s[2:4] + (ry[2:4].astype(f32) + sx.astype(f32)),
        )

    def from_group(pair):
        low, high = pair
        sent = [low[1], high[0], high[1]]
        return [low[0]] + [
            c.swap(v.astype(bf16), c.reps * (k + 1)) for k, v in enumerate(sent)
        ]

    expert_grads = []
    for own, got in sums:
        parts = from_group(replica_sum(own + got.astype(f32)))
        expert_grads.append(unpack_grad(sc, parts))

    gy, gres, rows_g = second_back(backs, gates, misc, hm, resid, gains, g_out)
    gqkv, gy_all, ghn_own, ghn_away = attn_bwd(
        sc, gy, c.other(gy), o, qkv, segment_ids, valid, cosine, sine, proj_w, out_w
    )
    grad_input, rows_g = first_back(
        ghn_own, c.other(ghn_away), tokens, gains, gres, rows_g, err
    )
    attn_s = attn_dw(sc, gy_all, o, hn, gqkv, rows_g)
    parts = from_group(replica_sum(attn_s))
    own_w = parts[0] + (
        parts[1].astype(f32) + parts[2].astype(f32) + parts[3].astype(f32)
    )
    misc_own = own_w[:, pw + qw :]
    misc_own = misc_own + c.other(misc_own)
    live_total = jnp.sum(gains[2]) / rows
    loss = jnp.sum(misc_own[:, EXPERTS + 2]) / (2.0 * MODEL_WIDTH * live_total)
    return (
        loss,
        result,
        grad_input,
        misc_own[:, EXPERTS],
        own_w[:, :qw],
        own_w[:, qw : qw + kw],
        own_w[:, qw + kw : pw],
        own_w[:, pw : pw + qw],
        misc_own[:, EXPERTS + 1],
        misc_own[:, :EXPERTS],
        *expert_grads,
    )


def shards(
    tokens,
    segment_ids,
    valid,
    expert_ids,
    teacher,
    attn_gain,
    w_query,
    key_projection,
    value_projection,
    w_out,
    moe_gain,
    w_router,
    w_gate,
    w_up,
    w_down,
):
    c = Comm()
    if c.reps == 4 and w_query.shape[0] == 64:
        return fast(
            c,
            tokens,
            segment_ids,
            valid,
            expert_ids,
            teacher,
            attn_gain,
            w_query,
            key_projection,
            value_projection,
            w_out,
            moe_gain,
            w_router,
            w_gate,
            w_up,
            w_down,
        )
    half = tokens.shape[0]
    seq_len = expert_ids.shape[0]
    rows = w_query.shape[0]
    qw, kw = w_query.shape[1], key_projection.shape[1]
    ff = w_gate.shape[2]
    local_experts = EXPERTS // GROUP
    ew = local_experts * ff
    heads = qw // HEAD_SIZE
    kv_heads = kw // HEAD_SIZE
    per = heads // kv_heads
    scale = 1.0 / HEAD_SIZE
    first_core = c.core == 0

    def join_rows(own, other):
        return jnp.where(
            first_core, jnp.concatenate([own, other], 0), jnp.concatenate([other, own], 0)
        )

    def my_half(v):
        return lax.dynamic_slice_in_dim(v, c.core * half, half, 0)

    live_row = valid[0]
    live_count = jnp.sum(live_row).astype(f32)
    misc = jnp.concatenate(
        [
            w_router,
            attn_gain[:, None],
            moe_gain[:, None],
            jnp.broadcast_to(live_count.astype(bf16), (rows, 1)),
            jnp.zeros((rows, MISC - EXPERTS - 3), bf16),
        ],
        1,
    )
    front = jnp.concatenate([w_query, key_projection, value_projection, misc], 1)
    inputs_low = join_rows(tokens, c.other(tokens))

    def gather_attention(v):
        z = c.stack_group(c.gather_group(v))
        mid = z.shape[2] // 2
        return jnp.concatenate(
            [c.gather_reps(z[:, :, :mid], False), c.gather_reps(z[:, :, mid:], True)], 1
        )

    front_w = gather_attention(front)
    out_w = gather_attention(w_out)
    ids_half = my_half(expert_ids)
    ids_group = jnp.concatenate(c.gather_group(ids_half), 0)

    gate_up = jnp.concatenate(
        [w_gate.reshape(rows, GROUP, ew), w_up.reshape(rows, GROUP, ew)], 2
    ).transpose(1, 0, 2)
    gate_up_z = c.stack_group(c.all_to_group(gate_up))
    down_z = c.stack_group(c.all_to_group(w_down.reshape(rows, GROUP, ew).transpose(1, 0, 2)))
    gate_w = c.gather_reps(gate_up_z[:, :, :ew], False)
    up_w = c.gather_reps(gate_up_z[:, :, ew:], True)
    down_w = jnp.concatenate(
        [
            c.gather_reps(down_z[:, :, : ew // 2], False),
            c.gather_reps(down_z[:, :, ew // 2 :], True),
        ],
        1,
    )
    gate_ws = (gate_w, c.other(gate_w))
    up_ws = (up_w, c.other(up_w))
    down_ws = (down_w, c.other(down_w))

    pw = qw + 2 * kw
    proj_w = front_w[:, :pw]
    router_w = front_w[:, pw : pw + EXPERTS]
    gain_one = front_w[:, pw + EXPERTS].astype(f32)[None, :]
    gain_two = front_w[:, pw + EXPERTS + 1].astype(f32)[None, :]
    counts = front_w[:, pw + EXPERTS + 2].astype(f32).reshape(c.n, rows)[:, 0]
    live_total = jnp.sum(counts)

    inputs = inputs_low.astype(f32)
    inv_one = lax.rsqrt(jnp.mean(inputs * inputs, -1, keepdims=True) + epsilon)
    normed_one = inputs * inv_one
    attention_hidden = (normed_one * gain_one).astype(bf16)
    cosine, sine = rope_tables(seq_len, qw + kw)
    qkv = dot(attention_hidden, proj_w)
    qk_raw = qkv[:, : qw + kw]
    qk = (qk_raw * cosine + swap_halves(qk_raw) * sine).astype(bf16)
    q = qk[:, :qw].reshape(seq_len, kv_heads, per, HEAD_SIZE)
    k = qk[:, qw:].reshape(seq_len, kv_heads, HEAD_SIZE)
    v = qkv[:, qw + kw :].astype(bf16).reshape(seq_len, kv_heads, HEAD_SIZE)
    seg_row = segment_ids[0]
    places = jnp.arange(seq_len)
    allowed = (seg_row[:, None] == seg_row[None, :]) & (places[None, :] <= places[:, None]) & (
        live_row[None, :] > 0
    ) | (places[None, :] == places[:, None])
    scores = jnp.einsum("qkgd,skd->kgqs", q, k, preferred_element_type=f32) * scale
    scores = jnp.where(allowed[None, None], scores, negative)
    top_score = jnp.max(scores, -1, keepdims=True)
    exp_scores = jnp.exp(scores - top_score)
    probs = exp_scores / jnp.sum(exp_scores, -1, keepdims=True)
    probs_low = probs.astype(bf16)
    attn_out = (
        jnp.einsum("kgqs,skd->qkgd", probs_low, v, preferred_element_type=f32)
        .astype(bf16)
        .reshape(seq_len, qw)
    )
    proj_part = dot_t(attn_out, out_w)
    theirs = lax.dynamic_slice_in_dim(proj_part, (1 - c.core) * half, half, 0)
    inputs_half = tokens.astype(f32)
    resid = inputs_half + (my_half(proj_part) + c.other(theirs))
    inv_two = lax.rsqrt(jnp.mean(resid * resid, -1, keepdims=True) + epsilon)
    normed_two = resid * inv_two
    hidden_moe = (normed_two * gain_two).astype(bf16)

    hm = jnp.concatenate(c.gather_group(hidden_moe), 0)
    logits = dot(hm, router_w)
    named = jnp.any(ids_group[:, :, None] == jnp.arange(EXPERTS)[None, None, :], 1)
    masked = jnp.where(named, logits, negative)
    shifted = jnp.where(named, jnp.exp(logits - jnp.max(masked, -1, keepdims=True)), 0.0)
    gates = shifted / jnp.sum(shifted, -1, keepdims=True)
    my_gates = lax.dynamic_slice_in_dim(gates, c.ep * local_experts, local_experts, 1)
    wide = jnp.repeat(my_gates, ff, axis=1)

    kept = []
    mixed = 0.0
    for gw, uw, dw in zip(gate_ws, up_ws, down_ws):
        a = dot(hm, gw)
        b = dot(hm, uw)
        sigma = jax.nn.sigmoid(a)
        h = (a * sigma * b).astype(bf16)
        hs = (h.astype(f32) * wide).astype(bf16)
        mixed = mixed + dot_t(hs, dw)
        kept.append((a, b, h, hs))
    mixed = mixed.reshape(GROUP, half, MODEL_WIDTH)
    mix = mixed[0]
    for j in range(1, GROUP):
        mix = mix + c.swap(mixed[j].astype(bf16), c.reps * j).astype(f32)
    result = resid + mix

    live = my_half(live_row).astype(f32)[:, None]
    differ = result - my_half(teacher).astype(f32)
    err_cols = jnp.sum(live * differ * differ, 0)
    grad_out = seq_len * c.n / live_total * live * differ
    go = jnp.concatenate(c.gather_group(grad_out.astype(bf16)), 0)

    grad_hm = 0.0
    grad_gates = 0.0
    low = []
    for (a, b, h, hs), gw, uw, dw in zip(kept, gate_ws, up_ws, down_ws):
        u = dot(go, dw)
        grad_gates = grad_gates + jnp.sum(
            (h.astype(f32) * u).reshape(GROUP * half, local_experts, ff), -1
        )
        gh = u * wide
        sigma = jax.nn.sigmoid(a)
        ga = (gh * b * sigma * (1.0 + a * (1.0 - sigma))).astype(bf16)
        gb = (gh * a * sigma).astype(bf16)
        grad_hm = grad_hm + dot_t(ga, gw) + dot_t(gb, uw)
        low.append((ga, gb))
    gg = jnp.zeros((GROUP * half, MISC), f32)
    gg = lax.dynamic_update_slice_in_dim(gg, grad_gates, c.ep * local_experts, 1)
    back = jnp.concatenate([grad_hm, gg], 1).reshape(GROUP, half, MODEL_WIDTH + MISC)
    back_sum = back[0]
    for j in range(1, GROUP):
        back_sum = back_sum + c.swap(back[j].astype(bf16), c.reps * j).astype(f32)

    weight_sums = []
    for own, other in (
        ((hm, low[0][0]), (hm, low[1][0])),
        ((hm, low[0][1]), (hm, low[1][1])),
        ((go, kept[0][3]), (go, kept[1][3])),
    ):
        away = dot_o(*other).astype(bf16)
        weight_sums.append(dot_o(*own) + c.other(away).astype(f32))
    gate_s = c.scatter_reps(weight_sums[0], False)
    up_s = c.scatter_reps(weight_sums[1], True)
    down_s = jnp.concatenate(
        [
            c.scatter_reps(weight_sums[2][:, : ew // 2], False),
            c.scatter_reps(weight_sums[2][:, ew // 2 :], True),
        ],
        2,
    )
    sums = jnp.concatenate([gate_s, up_s, down_s], 2)
    sums_low = sums.astype(bf16)
    parts = [c.block(sums, 0)] + [
        c.swap(c.block(sums_low, k), c.reps * k).astype(f32) for k in range(1, GROUP)
    ]
    finished = c.stack_group(parts)

    def expert_grad(j):
        g = finished[:, :, j * ew : (j + 1) * ew].transpose(1, 0, 2)
        return g.reshape(rows, EXPERTS, ff)

    grad_probs = back_sum[:, MODEL_WIDTH : MODEL_WIDTH + EXPERTS]
    gate_probs = gates[:half]
    grad_logits = (
        gate_probs * (grad_probs - jnp.sum(gate_probs * grad_probs, -1, keepdims=True))
    ).astype(bf16)
    grad_hidden = back_sum[:, :MODEL_WIDTH] + dot_t(grad_logits, router_w)
    router_part = dot_o(hidden_moe, grad_logits)
    gain_two_part = jnp.sum(grad_hidden * normed_two, 0)
    scaled_two = grad_hidden * gain_two
    grad_resid = grad_out + inv_two * (
        scaled_two - normed_two * jnp.mean(scaled_two * normed_two, -1, keepdims=True)
    )
    gy_half = grad_resid.astype(bf16)
    gy = join_rows(gy_half, c.other(gy_half))

    out_part = dot_o(gy, attn_out)
    grad_attn = dot(gy, out_w).astype(bf16).reshape(seq_len, kv_heads, per, HEAD_SIZE)
    gp = jnp.einsum("qkgd,skd->kgqs", grad_attn, v, preferred_element_type=f32)
    gs = (probs * (gp - jnp.sum(probs * gp, -1, keepdims=True))).astype(bf16)
    gq = jnp.einsum("kgqs,skd->qkgd", gs, k, preferred_element_type=f32) * scale
    gk = jnp.einsum("kgqs,qkgd->skd", gs, q, preferred_element_type=f32) * scale
    gv = jnp.einsum("kgqs,qkgd->skd", probs_low, grad_attn, preferred_element_type=f32)
    gqk = jnp.concatenate([gq.reshape(seq_len, qw), gk.reshape(seq_len, kw)], 1)
    gqk = gqk * cosine - swap_halves(gqk) * sine
    gqkv = jnp.concatenate([gqk.astype(bf16), gv.astype(bf16).reshape(seq_len, kw)], 1)
    ghn_part = dot_t(gqkv, proj_w)
    ghn_low = ghn_part.astype(bf16)
    ghn = my_half(ghn_part) + c.other(
        lax.dynamic_slice_in_dim(ghn_low, (1 - c.core) * half, half, 0)
    ).astype(f32)
    proj_part_grad = dot_o(attention_hidden, gqkv)
    normed_half = my_half(normed_one)
    gain_one_part = jnp.sum(ghn * normed_half, 0)
    scaled_one = ghn * gain_one
    grad_input = grad_resid + my_half(inv_one) * (
        scaled_one - normed_half * jnp.mean(scaled_one * normed_half, -1, keepdims=True)
    )

    err_rows = jnp.sum(err_cols.reshape(MODEL_WIDTH // rows, rows), 0)
    misc_part = jnp.concatenate(
        [
            router_part,
            gain_one_part[:, None],
            gain_two_part[:, None],
            jnp.tile(err_rows, c.n)[:, None],
            jnp.zeros((MODEL_WIDTH, MISC - EXPERTS - 3), f32),
        ],
        1,
    )
    back_w = jnp.concatenate([proj_part_grad, out_part, misc_part], 1)
    mid = (back_w.shape[1] // 256) * 128
    attn_s = jnp.concatenate(
        [c.scatter_reps(back_w[:, :mid], False), c.scatter_reps(back_w[:, mid:], True)], 2
    )
    attn_low = attn_s.astype(bf16)
    own_w = c.block(attn_s, 0)
    for k_ in range(1, GROUP):
        own_w = own_w + c.swap(c.block(attn_low, k_), c.reps * k_).astype(f32)
    misc_own = own_w[:, pw + qw :]
    misc_own = misc_own + c.other(misc_own)
    loss = jnp.sum(misc_own[:, EXPERTS + 2]) / (2.0 * MODEL_WIDTH * live_total)

    return (
        loss,
        result.astype(bf16),
        grad_input.astype(bf16),
        misc_own[:, EXPERTS],
        own_w[:, :qw],
        own_w[:, qw : qw + kw],
        own_w[:, qw + kw : pw],
        own_w[:, pw : pw + qw],
        misc_own[:, EXPERTS + 1],
        misc_own[:, :EXPERTS],
        expert_grad(0),
        expert_grad(1),
        expert_grad(2),
    )


def solution(mesh):
    placed = (
        P(("dp", "tensor"), None),
        P("dp", None),
        P("dp", None),
        P("dp", None),
        P("dp", None),
        P("dp"),
        P("dp", "tensor"),
        P("dp", "tensor"),
        P("dp", "tensor"),
        P("dp", "tensor"),
        P("dp"),
        P("dp", None),
        P("dp", None, "tensor"),
        P("dp", None, "tensor"),
        P("dp", None, "tensor"),
    )
    return jax.shard_map(
        shards,
        mesh=mesh,
        in_specs=placed,
        out_specs=(
            P(),
            P(("dp", "tensor"), None),
            P(("dp", "tensor"), None),
            P("dp"),
            P("dp", "tensor"),
            P("dp", "tensor"),
            P("dp", "tensor"),
            P("dp", "tensor"),
            P("dp"),
            P("dp", None),
            P("dp", None, "tensor"),
            P("dp", None, "tensor"),
            P("dp", None, "tensor"),
        ),
        check_vma=False,
    )
```

```python
import jax
import jax.numpy as jnp
from jax import lax
from jax.experimental import pallas as pl
from jax.experimental.pallas import tpu as pltpu
from jax.sharding import PartitionSpec as P

MODEL_WIDTH = 1024
HEAD_SIZE = 64
TOPK = 8
EXPERTS = 16
GROUP = 4
MISC = 128
VMEM_BYTES = 60 << 20

epsilon = 1e-06
negative = -1e30
rope_base = 10000.0
f32 = jnp.float32
bf16 = jnp.bfloat16

INNER = (((1,), (1,)), ((), ()))
OUTER = (((0,), (0,)), ((), ()))


def dot(a, b):
    return jnp.dot(a, b, preferred_element_type=f32)


def dot_t(a, b):
    return lax.dot_general(a, b, INNER, preferred_element_type=f32)


def dot_o(a, b):
    return lax.dot_general(a, b, OUTER, preferred_element_type=f32)


def tie(v, *after):
    return lax.optimization_barrier((v, after))[0]


def rope_tables(length, width):
    half = HEAD_SIZE // 2
    places = jnp.arange(length).astype(f32)
    freqs = rope_base ** (-2.0 * jnp.arange(half).astype(f32) / HEAD_SIZE)
    angles = places[:, None] * freqs[None, :]
    cosine, sine = jnp.cos(angles), jnp.sin(angles)
    reps = width // HEAD_SIZE
    return (
        jnp.tile(jnp.concatenate([cosine, cosine], 1), (1, reps)),
        jnp.tile(jnp.concatenate([-sine, sine], 1), (1, reps)),
    )


def swap_halves(u):
    half = HEAD_SIZE // 2
    low = (jnp.arange(u.shape[1]) % HEAD_SIZE) < half
    return jnp.where(low[None, :], jnp.roll(u, -half, 1), jnp.roll(u, half, 1))


class Comm:
    def __init__(self):
        self.n = lax.axis_size("dp")
        self.me = lax.axis_index("dp")
        self.core = lax.axis_index("tensor")
        self.reps = self.n // GROUP
        self.ep = self.me // self.reps
        self.rep = self.me % self.reps
        self.bits = [1 << k for k in range(self.reps.bit_length() - 1)]

    def swap(self, v, mask):
        return lax.ppermute(v, "dp", [(i, i ^ mask) for i in range(self.n)])

    def other(self, v):
        return lax.ppermute(v, "tensor", [(0, 1), (1, 0)])

    def bit(self, b):
        return (self.rep // b) % 2

    def gather_reps(self, z, last_first):
        rows, cols = z.shape[1:]
        k = len(self.bits)
        out = jnp.zeros((GROUP,) + (2,) * k + (rows, cols), z.dtype)
        zero = jnp.int32(0)
        order = list(self.bits)
        if last_first:
            order = order[::-1]
        done = set()

        def place(block, flipped):
            start = [zero]
            for b in reversed(self.bits):
                if b in done:
                    start.append(zero)
                elif b == flipped:
                    start.append(1 - self.bit(b))
                else:
                    start.append(self.bit(b))
            return start + [zero, zero]

        cur = z.reshape((GROUP,) + (1,) * k + (rows, cols))
        out = lax.dynamic_update_slice(out, cur, place(cur, None))
        for b in order:
            got = self.swap(cur, b)
            out = lax.dynamic_update_slice(out, got, place(got, b))
            done.add(b)
            if len(done) < k:
                start = place(out, None)
                shape = [GROUP] + [2 if c in done else 1 for c in reversed(self.bits)]
                cur = lax.dynamic_slice(out, start, shape + [rows, cols])
        return out.reshape(GROUP * self.reps * rows, cols)

    def stack_group(self, parts, axis=0):
        parts = jnp.stack(parts, 0)
        idx = self.ep ^ jnp.arange(GROUP)
        return jnp.concatenate(
            [lax.dynamic_index_in_dim(parts, idx[j], 0, keepdims=True) for j in range(GROUP)], 0
        )

    def gather_group(self, v):
        return [v] + [self.swap(v, self.reps * k) for k in range(1, GROUP)]

    def block(self, v, k):
        return lax.dynamic_index_in_dim(v, self.ep ^ k, 0, keepdims=False)

    def all_to_group(self, v):
        return [self.block(v, 0)] + [
            self.swap(self.block(v, k), self.reps * k) for k in range(1, GROUP)
        ]

    def scatter_reps(self, s, last_first):
        cols = s.shape[1]
        k = len(self.bits)
        rows = s.shape[0] // (GROUP * self.reps)
        s = s.reshape((GROUP,) + (2,) * k + (rows, cols))
        order = list(self.bits)
        if last_first:
            order = order[::-1]
        for b in order:
            axis = 1 + list(reversed(self.bits)).index(b)
            mine = self.bit(b)
            send = lax.dynamic_slice_in_dim(s, 1 - mine, 1, axis).astype(bf16)
            keep = lax.dynamic_slice_in_dim(s, mine, 1, axis)
            s = keep + self.swap(send, b).astype(f32)
        return s.reshape(GROUP, rows, cols)


VM = pltpu.VMEM


def vmem():
    return pl.BlockSpec(memory_space=pltpu.VMEM)


def anym():
    return pl.BlockSpec(memory_space=pltpu.HBM)


def smem():
    return pl.BlockSpec(memory_space=pltpu.SMEM)


def sds(shape, dtype):
    return jax.ShapeDtypeStruct(shape, dtype)


def kernel_call(body, out_shape, in_specs, name, scratch=()):
    return pl.pallas_call(
        body,
        out_shape=out_shape,
        in_specs=in_specs,
        out_specs=jax.tree.map(lambda _: vmem(), out_shape),
        scratch_shapes=list(scratch),
        compiler_params=pltpu.CompilerParams(vmem_limit_bytes=VMEM_BYTES),
        name=name,
    )


def piece_copies(pieces, dst, sem, ep, rep, cols=None, first=0):
    copies = []
    for j, piece in enumerate(pieces):
        m, h = j // 2, j % 2
        for i in range(2):
            at = (ep ^ (2 * h + i)) * 4 + (rep ^ m)
            src, to = piece.at[pl.ds(64 * i, 64)], dst.at[at]
            if cols is not None:
                src, to = src.at[:, pl.ds(*cols)], to.at[:, pl.ds(*cols)]
            copies.append(pltpu.make_async_copy(src, to, sem.at[first + 2 * j + i]))
    return copies


NAMED = 32


def pack_front_body(wq, wk, wv, wo, wr, g1, g2, valid, ids, out):
    qw, kw = wq.shape[1], wk.shape[1]
    pw = qw + 2 * kw
    n = wq.shape[0]
    out[:, 0:qw] = wq[...]
    out[:, qw : qw + kw] = wk[...]
    out[:, qw + kw : pw] = wv[...]
    out[:, pw + MISC :] = wo[...]
    count = jnp.sum(valid[...].astype(f32), axis=1, keepdims=True)
    expert = lax.broadcasted_iota(jnp.int32, (EXPERTS, ids.shape[1]), 0)
    named = jnp.zeros(expert.shape, f32)
    for k in range(TOPK):
        named = jnp.where(ids[k : k + 1, :] == expert, 1.0, named)
    quarters = [named[:, n * j : n * (j + 1)] for j in range(ids.shape[1] // n)]
    top = jnp.concatenate([wr[...].astype(f32), jnp.zeros((NAMED - EXPERTS, n), f32)], 0)
    row = lax.broadcasted_iota(jnp.int32, top.shape, 0)
    top = jnp.where(row == EXPERTS, g1[...].astype(f32), top)
    top = jnp.where(row == EXPERTS + 1, g2[...].astype(f32), top)
    top = jnp.where(row == EXPERTS + 2, count, top)
    rest = jnp.zeros((MISC - NAMED - EXPERTS * len(quarters), n), f32)
    base = jnp.concatenate([top, *quarters, rest], 0)
    eye = lax.broadcasted_iota(jnp.int32, (n, n), 0) == lax.broadcasted_iota(jnp.int32, (n, n), 1)
    misc = dot_t(eye.astype(f32).astype(bf16), base.astype(bf16))
    out[:, pw : pw + MISC] = misc.astype(bf16)


def pack_front(wq, wk, wv, wo, wr, g1, g2, valid, ids):
    n = wq.shape[0]
    width = wq.shape[1] + 2 * wk.shape[1] + MISC + wo.shape[1]
    return kernel_call(pack_front_body, sds((n, width), bf16), [vmem()] * 9, "pack_front")(
        wq, wk, wv, wo, wr.T, g1[None, :], g2[None, :], valid, ids.T
    )


def pack_experts_body(sc, wg, wu, wd, out0, out1, out2, out3, wide):
    ep = sc[0]
    n, e, f = wg.shape
    per = e // GROUP
    for j, w in enumerate((wg, wu, wd)):
        for l in range(f // 128):
            wide[l] = w[:, :, 128 * l : 128 * (l + 1)].astype(f32).reshape(n * e, 128)
        for k, out in enumerate((out0, out1, out2, out3)):
            for x in range(per):
                for l in range(f // 128):
                    at = j * per * f + x * f + 128 * l
                    out[:, at : at + 128] = wide[
                        l, pl.ds((ep ^ k) * per + x, n, stride=e), :
                    ].astype(bf16)


def pack_experts(sc, wg, wu, wd):
    n, e, f = wg.shape
    return kernel_call(
        pack_experts_body,
        (sds((n, 3 * e * f // GROUP), bf16),) * GROUP,
        [smem()] + [vmem()] * 3,
        "pack_experts",
        [VM((f // 128, n * e, 128), f32)],
    )(sc, wg, wu, wd)


def rotate_pairs(u, cosine, sine):
    lane = lax.broadcasted_iota(jnp.int32, u.shape, 1)
    low = lane % HEAD_SIZE < HEAD_SIZE // 2
    turned = jnp.where(low, pltpu.roll(u, 96, 1), pltpu.roll(u, 32, 1))
    return u * cosine + turned * sine


def both_lanes(pair, odd):
    lane = lax.broadcasted_iota(jnp.int32, pair.shape, 1)
    other = pltpu.roll(pair, 64, 1)
    first = lane < HEAD_SIZE
    return jnp.where(first, other, pair) if odd else jnp.where(first, pair, other)


def two_heads(pair):
    lane = lax.broadcasted_iota(jnp.int32, pair.shape, 1)
    zero = jnp.zeros_like(pair)
    return jnp.concatenate(
        [jnp.where(lane < HEAD_SIZE, pair, zero), jnp.where(lane < HEAD_SIZE, zero, pair)], 0
    )


def one_pair(rows):
    n = rows.shape[0] // 2
    lane = lax.broadcasted_iota(jnp.int32, (n, rows.shape[1]), 1)
    return jnp.where(lane < HEAD_SIZE, rows[:n], rows[n:])


def allowed_mask(seg, valid):
    n = seg.shape[1]
    r = lax.broadcasted_iota(jnp.int32, (n, n), 0)
    col = lax.broadcasted_iota(jnp.int32, (n, n), 1)
    seg_row = jnp.broadcast_to(seg.astype(f32), (n, n))
    seg_col = jnp.sum(jnp.where(r == col, seg_row, 0.0), axis=1, keepdims=True)
    live = jnp.broadcast_to(valid.astype(f32), (n, n)) > 0
    return ((seg_col == seg_row) & (col <= r) & live) | (r == col)


def softmax_rows(q2, k2, allowed2):
    s = dot_t(q2, k2) * (1.0 / HEAD_SIZE)
    s = jnp.where(allowed2, s, negative)
    e = jnp.exp(s - jnp.max(s, axis=1, keepdims=True))
    return e / jnp.sum(e, axis=1, keepdims=True)


def attn_fwd_body(sc, x_own, x_oth, seg, valid, cosine, sine, *refs):
    pieces = refs[:8]
    own_out, away_out, hn_out, qkv_out, o_out, misc_out, gains_out, w_out, w, x, sem = refs[8:]
    ep, rep, core = sc[0], sc[1], sc[2]
    copies = piece_copies(pieces, w, sem, ep, rep)
    for cp in copies:
        cp.start()
    half = x_own.shape[0]
    n = 2 * half
    x[pl.ds(core * half, half), :] = x_own[...].astype(f32)
    x[pl.ds((1 - core) * half, half), :] = x_oth[...].astype(f32)
    allowed = allowed_mask(seg[...], valid[...])
    allowed2 = jnp.concatenate([allowed, allowed], 0)
    inputs = x[...]
    normed = inputs * lax.rsqrt(jnp.mean(inputs * inputs, axis=1, keepdims=True) + epsilon)
    for cp in copies:
        cp.wait()
    pw = qkv_out.shape[1]
    misc = w[:, :, pw : pw + MISC].reshape(MODEL_WIDTH, MISC)
    pick = lax.broadcasted_iota(jnp.int32, (8, MISC), 0) + EXPERTS
    pick = (pick == lax.broadcasted_iota(jnp.int32, (8, MISC), 1)).astype(f32).astype(bf16)
    gains = dot_t(pick, misc)
    gains_out[...] = gains
    misc_out[...] = misc
    hn = (normed * gains[0:1, :]).astype(bf16)
    hn_out[...] = hn
    w_out[...] = w[...].reshape(w_out.shape)
    qkv = dot(hn, w[:, :, :pw].reshape(MODEL_WIDTH, pw))
    groups = pw // 128
    kv0 = groups // 2
    for g in range(groups):
        u = qkv[:, 128 * g : 128 * (g + 1)]
        if g < kv0 + kv0 // 2:
            u = rotate_pairs(u, cosine[...], sine[...])
        qkv_out[:, 128 * g : 128 * (g + 1)] = u.astype(bf16)
    for m in range(kv0):
        g = kv0 + m // 2
        k2 = both_lanes(qkv_out[:, 128 * g : 128 * (g + 1)].astype(f32), m % 2).astype(bf16)
        g = g + kv0 // 2
        v2 = both_lanes(qkv_out[:, 128 * g : 128 * (g + 1)].astype(f32), m % 2).astype(bf16)
        q2 = two_heads(qkv_out[:, 128 * m : 128 * (m + 1)].astype(f32)).astype(bf16)
        p = softmax_rows(q2, k2, allowed2).astype(bf16)
        o_out[:, 128 * m : 128 * (m + 1)] = one_pair(dot(p, v2)).astype(bf16)
    wo = w[:, :, pw + MISC :].reshape(MODEL_WIDTH, o_out.shape[1])
    away_out[...] = dot_t(o_out[pl.ds((1 - core) * half, half), :], wo)
    own_out[...] = dot_t(o_out[pl.ds(core * half, half), :], wo)


def attn_fwd(sc, x_own, x_oth, seg, valid, cosine, sine, pieces, qw):
    half = x_own.shape[0]
    n = 2 * half
    cols = pieces[0].shape[1]
    pw = cols - MISC - qw
    return kernel_call(
        attn_fwd_body,
        (
            sds((half, MODEL_WIDTH), f32),
            sds((half, MODEL_WIDTH), f32),
            sds((n, MODEL_WIDTH), bf16),
            sds((n, pw), bf16),
            sds((n, qw), bf16),
            sds((MODEL_WIDTH, MISC), bf16),
            sds((8, MODEL_WIDTH), f32),
            sds((MODEL_WIDTH, cols), bf16),
        ),
        [smem()] + [vmem()] * 6 + [anym()] * 8,
        "attn_fwd",
        [VM((16, 64, cols), bf16), VM((n, MODEL_WIDTH), f32), pltpu.SemaphoreType.DMA((16,))],
    )(sc, x_own, x_oth, seg, valid, cosine, sine, *pieces)


def second_norm_body(x, y_own, y_oth, gains, resid_out, hm_out):
    resid = x[...].astype(f32) + (y_own[...] + y_oth[...])
    resid_out[...] = resid
    inv = lax.rsqrt(jnp.mean(resid * resid, axis=1, keepdims=True) + epsilon)
    hm_out[...] = (resid * inv * gains[1:2, :]).astype(bf16)


def second_norm(x, y_own, y_oth, gains):
    return kernel_call(
        second_norm_body,
        (sds(y_own.shape, f32), sds(y_own.shape, bf16)),
        [vmem()] * 4,
        "second_norm",
    )(x, y_own, y_oth, gains)


def named_rows(block, j):
    moved = pltpu.roll(block.astype(f32), MISC - NAMED - EXPERTS * j, 1)
    lane = lax.broadcasted_iota(jnp.int32, moved.shape, 1)
    return (moved > 0.5) & (lane < EXPERTS)


def gates_of(hm, misc, named):
    logits = dot(hm, misc)
    top = jnp.max(jnp.where(named, logits, negative), axis=1, keepdims=True)
    e = jnp.where(named, jnp.exp(logits - top), 0.0)
    return e / jnp.sum(e, axis=1, keepdims=True)


def expert_fwd_body(sc, misc, *refs):
    chunks, pieces = refs[:8], refs[8:16]
    own_out, away_out, a_out, b_out, gates_out, w, hm, acc, sem = refs[16:]
    ep, rep, core = sc[0], sc[1], sc[2]
    half = chunks[0].shape[0]
    experts = EXPERTS // GROUP
    ew = w.shape[2] // 3
    ff = ew // experts
    wide = piece_copies(pieces, w, sem, ep, rep, (0, 2 * ew), 0)
    down = piece_copies(pieces, w, sem, ep, rep, (2 * ew, ew), 16)
    for cp in wide:
        cp.start()
    for cp in down:
        cp.start()
    for j, chunk in enumerate(chunks):
        hm[pl.ds(j * half, half), :] = chunk[...]
        k = j % GROUP
        at = pl.multiple_of(((ep ^ k) * 4 + rep) * 64, 64)
        block = misc[pl.ds(at, 64), :]
        mine = core == (0 if j < GROUP else 1)
        quarters = [named_rows(block, q) for q in range(4)]
        first = jnp.concatenate([q.astype(f32) for q in quarters[:2]], 0)
        second = jnp.concatenate([q.astype(f32) for q in quarters[2:]], 0)
        named = jnp.where(mine, first, second) > 0.5
        gates_out[pl.ds(j * half, half), :] = gates_of(chunk[...], misc[...], named)
    acc[...] = jnp.zeros_like(acc)
    lane = lax.broadcasted_iota(jnp.int32, gates_out.shape, 1)
    for cp in wide:
        cp.wait()
    for cp in down:
        cp.wait()

    def tile(e, carry):
        rows = hm[...]
        at = pl.multiple_of(e * ff, ff)
        a = dot(rows, w[:, :, pl.ds(at, ff)].reshape(MODEL_WIDTH, ff))
        b = dot(rows, w[:, :, pl.ds(ew + at, ff)].reshape(MODEL_WIDTH, ff))
        g = jnp.sum(
            jnp.where(lane == ep * experts + e, gates_out[...], 0.0), axis=1, keepdims=True
        )
        h = (a * jax.nn.sigmoid(a) * b).astype(bf16)
        hs = (h.astype(f32) * g).astype(bf16)
        a_out[:, pl.ds(at, ff)] = a
        b_out[:, pl.ds(at, ff)] = b
        acc[...] += dot_t(hs, w[:, :, pl.ds(2 * ew + at, ff)].reshape(MODEL_WIDTH, ff))
        return carry

    lax.fori_loop(0, experts, tile, 0)
    own_out[...] = acc[: GROUP * half, :]
    away_out[...] = acc[GROUP * half :, :].astype(bf16)


def expert_fwd(sc, misc, chunks, pieces):
    half = chunks[0].shape[0]
    cols = pieces[0].shape[1]
    ew = cols // 3
    rows = GROUP * half
    return kernel_call(
        expert_fwd_body,
        (
            sds((rows, MODEL_WIDTH), f32),
            sds((rows, MODEL_WIDTH), bf16),
            sds((2 * rows, ew), f32),
            sds((2 * rows, ew), f32),
            sds((2 * rows, MISC), f32),
        ),
        [smem()] + [vmem()] * 9 + [anym()] * 8,
        "expert_fwd",
        [
            VM((16, 64, cols), bf16),
            VM((2 * rows, MODEL_WIDTH), bf16),
            VM((2 * rows, MODEL_WIDTH), f32),
            pltpu.SemaphoreType.DMA((32,)),
        ],
    )(sc, misc, *chunks, *pieces)


def core_sum_body(own, got, out0, out1, out2, out3):
    half = out0.shape[0]
    for j, out in enumerate((out0, out1, out2, out3)):
        at = pl.ds(j * half, half)
        out[...] = (own[at, :] + got[at, :].astype(f32)).astype(out.dtype)


def core_sum(own, got):
    shape = (own.shape[0] // GROUP, own.shape[1])
    return kernel_call(
        core_sum_body,
        (sds(shape, f32), sds(shape, bf16), sds(shape, bf16), sds(shape, bf16)),
        [vmem()] * 2,
        "core_sum",
    )(own, got)


def expert_bwd_body(sc, gates, a_in, b_in, *refs):
    chunks, pieces = refs[:8], refs[8:16]
    own_out, away_out, ga_out, gb_out, hs_out, w, go, acc, gsum, sem = refs[16:]
    ep, rep = sc[0], sc[1]
    half = chunks[0].shape[0]
    rows = GROUP * half
    experts = EXPERTS // GROUP
    ew = w.shape[2] // 3
    ff = ew // experts
    wide = piece_copies(pieces, w, sem, ep, rep, (0, 2 * ew), 0)
    down = piece_copies(pieces, w, sem, ep, rep, (2 * ew, ew), 16)
    for cp in down:
        cp.start()
    for cp in wide:
        cp.start()
    for j, chunk in enumerate(chunks):
        go[pl.ds(j * half, half), :] = chunk[...]
    acc[...] = jnp.zeros_like(acc)
    gsum[...] = jnp.zeros_like(gsum)
    lane = lax.broadcasted_iota(jnp.int32, gsum.shape, 1)
    for cp in down:
        cp.wait()
    for cp in wide:
        cp.wait()

    def tile(e, carry):
        at = pl.multiple_of(e * ff, ff)
        a = a_in[:, pl.ds(at, ff)]
        b = b_in[:, pl.ds(at, ff)]
        u = dot(go[...], w[:, :, pl.ds(2 * ew + at, ff)].reshape(MODEL_WIDTH, ff))
        mine = lane == ep * experts + e
        g = jnp.sum(jnp.where(mine, gates[...], 0.0), axis=1, keepdims=True)
        s = jax.nn.sigmoid(a)
        silu = a * s
        h = (silu * b).astype(bf16).astype(f32)
        gsum[...] += jnp.where(mine, jnp.sum(h * u, axis=1, keepdims=True), 0.0)
        gh = u * g
        ga = (gh * b * s * (1.0 + a * (1.0 - s))).astype(bf16)
        gb = (gh * silu).astype(bf16)
        ga_out[:, pl.ds(at, ff)] = ga
        gb_out[:, pl.ds(at, ff)] = gb
        hs_out[:, pl.ds(at, ff)] = (h * g).astype(bf16)
        wg = w[:, :, pl.ds(at, ff)].reshape(MODEL_WIDTH, ff)
        wu = w[:, :, pl.ds(ew + at, ff)].reshape(MODEL_WIDTH, ff)
        acc[...] += dot_t(ga, wg) + dot_t(gb, wu)
        return carry

    lax.fori_loop(0, experts, tile, 0)
    own_out[:, :MODEL_WIDTH] = acc[:rows, :]
    own_out[:, MODEL_WIDTH:] = gsum[:rows, :]
    away_out[:, :MODEL_WIDTH] = acc[rows:, :].astype(bf16)
    away_out[:, MODEL_WIDTH:] = gsum[rows:, :].astype(bf16)


def expert_bwd(sc, gates, a, b, chunks, pieces):
    half = chunks[0].shape[0]
    cols = pieces[0].shape[1]
    ew = cols // 3
    rows = GROUP * half
    full = MODEL_WIDTH + MISC
    return kernel_call(
        expert_bwd_body,
        (
            sds((rows, full), f32),
            sds((rows, full), bf16),
            sds((2 * rows, ew), bf16),
            sds((2 * rows, ew), bf16),
            sds((2 * rows, ew), bf16),
        ),
        [smem()] + [vmem()] * 11 + [anym()] * 8,
        "expert_bwd",
        [
            VM((16, 64, cols), bf16),
            VM((2 * rows, MODEL_WIDTH), bf16),
            VM((2 * rows, MODEL_WIDTH), f32),
            VM((2 * rows, MISC), f32),
            pltpu.SemaphoreType.DMA((32,)),
        ],
    )(sc, gates, a, b, *chunks, *pieces)


def loss_body(resid, m0, m1, m2, m3, teacher, live, gains, scale, result_out, g_out, glow_out, err_out):
    mix = m0[...] + (m1[...].astype(f32) + m2[...].astype(f32) + m3[...].astype(f32))
    result = resid[...] + mix
    result_out[...] = result.astype(bf16)
    differ = result - teacher[...].astype(f32)
    rows = gains.shape[1] // scale.shape[1]
    total = jnp.sum(gains[2:3, :], axis=1, keepdims=True) / rows
    weighted = live[...] * differ
    g = (scale.shape[0] * scale.shape[1]) / total * weighted
    g_out[...] = g
    glow_out[...] = g.astype(bf16)
    err_out[...] = jnp.broadcast_to(jnp.sum(weighted * differ, axis=0, keepdims=True), err_out.shape)


def loss_grad(resid, mixes, teacher, live, gains, seq_len, n):
    shape = resid.shape
    return kernel_call(
        loss_body,
        (sds(shape, bf16), sds(shape, f32), sds(shape, bf16), sds((8, shape[1]), f32)),
        [vmem()] * 9,
        "loss_grad",
    )(resid, *mixes, teacher, live, gains, jnp.zeros((seq_len, n), f32))


def second_back_body(b0, b1, b2, b3, gates, misc, hm, resid, gains, g_out, gy_out, gres_out, rows_out):
    half = resid.shape[0]
    total = b0[...] + (b1[...].astype(f32) + b2[...].astype(f32) + b3[...].astype(f32))
    gp = total[:, MODEL_WIDTH:]
    gate = gates[0:half, :]
    gl = (gate * (gp - jnp.sum(gate * gp, axis=1, keepdims=True))).astype(bf16)
    ghm = total[:, :MODEL_WIDTH] + dot_t(gl, misc[...])
    x = resid[...]
    inv = lax.rsqrt(jnp.mean(x * x, axis=1, keepdims=True) + epsilon)
    normed = x * inv
    rows = dot_o(gl, hm[...])
    gain_row = jnp.sum(ghm * normed, axis=0, keepdims=True)
    at = lax.broadcasted_iota(jnp.int32, rows.shape, 0)
    rows_out[...] = jnp.where(at == EXPERTS + 1, gain_row, rows)
    scaled = ghm * gains[1:2, :]
    gres = g_out[...] + inv * (
        scaled - normed * jnp.mean(scaled * normed, axis=1, keepdims=True)
    )
    gres_out[...] = gres
    gy_out[...] = gres.astype(bf16)


def second_back(backs, gates, misc, hm, resid, gains, g_out):
    shape = resid.shape
    return kernel_call(
        second_back_body,
        (sds(shape, bf16), sds(shape, f32), sds((MISC, shape[1]), f32)),
        [vmem()] * 10,
        "second_back",
    )(*backs, gates, misc, hm, resid, gains, g_out)


def attn_bwd_body(
    sc, gy_own, gy_oth, o, qkv, seg, valid, cosine, sine, w, gqkv_out, gy_out, own_out, away_out, low
):
    core = sc[2]
    half = gy_own.shape[0]
    n = 2 * half
    gy_out[pl.ds(core * half, half), :] = gy_own[...]
    gy_out[pl.ds((1 - core) * half, half), :] = gy_oth[...]
    pw = qkv.shape[1]
    low[...] = dot(gy_out[...], w[:, pw + MISC :]).astype(bf16)
    allowed = allowed_mask(seg[...], valid[...])
    allowed2 = jnp.concatenate([allowed, allowed], 0)
    kv0 = pw // 256
    lane = lax.broadcasted_iota(jnp.int32, (n, 128), 1)
    scale = 1.0 / HEAD_SIZE
    held = {}
    for m in range(kv0):
        gk_at = kv0 + m // 2
        gv_at = gk_at + kv0 // 2
        k2 = both_lanes(qkv[:, 128 * gk_at : 128 * (gk_at + 1)].astype(f32), m % 2).astype(bf16)
        v2 = both_lanes(qkv[:, 128 * gv_at : 128 * (gv_at + 1)].astype(f32), m % 2).astype(bf16)
        q2 = two_heads(qkv[:, 128 * m : 128 * (m + 1)].astype(f32)).astype(bf16)
        go2 = two_heads(low[:, 128 * m : 128 * (m + 1)].astype(f32)).astype(bf16)
        p = softmax_rows(q2, k2, allowed2)
        gp = dot_t(go2, v2)
        gs = (p * (gp - jnp.sum(p * gp, axis=1, keepdims=True))).astype(bf16)
        gq = one_pair(dot(gs, k2)) * scale
        gqkv_out[:, 128 * m : 128 * (m + 1)] = rotate_pairs(gq, cosine[...], -sine[...]).astype(bf16)
        gk = dot_o(gs, q2) * scale
        gv = dot_o(p.astype(bf16), go2)
        gk = gk + pltpu.roll(gk, 64, 1)
        gv = gv + pltpu.roll(gv, 64, 1)
        if m % 2 == 0:
            held = {"k": gk, "v": gv}
        else:
            gk = jnp.where(lane < HEAD_SIZE, held["k"], gk)
            gv = jnp.where(lane < HEAD_SIZE, held["v"], gv)
            gqkv_out[:, 128 * gk_at : 128 * (gk_at + 1)] = rotate_pairs(
                gk, cosine[...], -sine[...]
            ).astype(bf16)
            gqkv_out[:, 128 * gv_at : 128 * (gv_at + 1)] = gv.astype(bf16)
    away_out[...] = dot_t(gqkv_out[pl.ds((1 - core) * half, half), :], w[:, :pw]).astype(bf16)
    own_out[...] = dot_t(gqkv_out[pl.ds(core * half, half), :], w[:, :pw])


def attn_bwd(sc, gy_own, gy_oth, o, qkv, seg, valid, cosine, sine, w):
    half = gy_own.shape[0]
    n = 2 * half
    pw = qkv.shape[1]
    return kernel_call(
        attn_bwd_body,
        (
            sds((n, pw), bf16),
            sds((n, MODEL_WIDTH), bf16),
            sds((half, MODEL_WIDTH), f32),
            sds((half, MODEL_WIDTH), bf16),
        ),
        [smem()] + [vmem()] * 9,
        "attn_bwd",
        [VM((n, o.shape[1]), bf16)],
    )(sc, gy_own, gy_oth, o, qkv, seg, valid, cosine, sine, w)


def first_back_body(g_own, g_oth, x, gains, gres, rows, err, ginput_out, rows_out):
    ghn = g_own[...] + g_oth[...].astype(f32)
    inputs = x[...].astype(f32)
    inv = lax.rsqrt(jnp.mean(inputs * inputs, axis=1, keepdims=True) + epsilon)
    normed = inputs * inv
    gain_row = jnp.sum(ghn * normed, axis=0, keepdims=True)
    scaled = ghn * gains[0:1, :]
    ginput_out[...] = (
        gres[...] + inv * (scaled - normed * jnp.mean(scaled * normed, axis=1, keepdims=True))
    ).astype(bf16)
    e = err[...]
    for shift in (64, 128, 256, 512):
        e = e + pltpu.roll(e, shift, 1)
    at = lax.broadcasted_iota(jnp.int32, rows.shape, 0)
    r = jnp.where(at == EXPERTS, gain_row, rows[...])
    rows_out[...] = jnp.where(at == EXPERTS + 2, e[0:1, :], r)


def first_back(g_own, g_oth, x, gains, gres, rows, err):
    return kernel_call(
        first_back_body,
        (sds(gres.shape, bf16), sds(rows.shape, f32)),
        [vmem()] * 7,
        "first_back",
    )(g_own, g_oth, x, gains, gres, rows, err)


SEND_X = (12, 13, 4, 5)
SEND_Y = (14, 15, 10, 11)
KEPT = (0, 1, 2, 3, 6, 7, 8, 9)


def store_relative(out, ep, rep, value, cols):
    for j in range(16):
        to = 4 * ((j % 4) ^ rep) + ((j // 4) ^ ep)
        out[to, :, cols] = value[64 * j : 64 * (j + 1), :]


def split_relative(full, x_out, y_out, kept_out):
    for j, at in enumerate(SEND_X):
        x_out[j] = full[at].astype(bf16)
    for j, at in enumerate(SEND_Y):
        y_out[j] = full[at].astype(bf16)
    for j, at in enumerate(KEPT):
        kept_out[j] = full[at]


def attn_dw_body(sc, gy, o, hn, gqkv, rows, x_out, y_out, kept_out, full):
    ep, rep = sc[0], sc[1]
    pw = gqkv.shape[1]
    qw = o.shape[1]
    store_relative(full, ep, rep, dot_o(hn[...], gqkv[...]), slice(0, pw))
    store_relative(full, ep, rep, dot_o(gy[...], o[...]), slice(pw, pw + qw))
    store_relative(full, ep, rep, jnp.transpose(rows[...]), slice(pw + qw, pw + qw + MISC))
    split_relative(full, x_out, y_out, kept_out)


def attn_dw(sc, gy, o, hn, gqkv, rows):
    width = gqkv.shape[1] + o.shape[1] + MISC
    return kernel_call(
        attn_dw_body,
        (sds((4, 64, width), bf16), sds((4, 64, width), bf16), sds((8, 64, width), f32)),
        [smem()] + [vmem()] * 5,
        "attn_dw",
        [VM((16, 64, width), f32)],
    )(sc, gy, o, hn, gqkv, rows)


def expert_dw_body(sc, *refs):
    n = len(refs) - 13
    chunks, ys = refs[:8], refs[8 : 8 + n]
    x_out, y_out, kept_out, xt, full = refs[8 + n :]
    ep, rep = sc[0], sc[1]
    half = chunks[0].shape[0]

    @pl.when(pl.program_id(0) == 0)
    def _():
        for j, x in enumerate(chunks):
            xt[:, j * half : (j + 1) * half] = jnp.transpose(x[...])

    for j, y in enumerate(ys):

        @pl.when(pl.program_id(0) // 4 == j)
        def _():
            store_relative(full, ep, rep, dot(xt[...], y[...]), slice(None))

    split_relative(full, x_out, y_out, kept_out)


def expert_dw(sc, chunks, ys):
    half = chunks[0].shape[0]
    tile = ys[0].shape[1] // 4
    steps = 4 * len(ys)
    wide = tile * steps
    whole = pl.BlockSpec((half, MODEL_WIDTH), lambda i: (0, 0))
    return pl.pallas_call(
        expert_dw_body,
        grid=(steps,),
        out_shape=(sds((4, 64, wide), bf16), sds((4, 64, wide), bf16), sds((8, 64, wide), f32)),
        in_specs=[smem()]
        + [whole] * 8
        + [
            pl.BlockSpec((8 * half, tile), lambda i, j=j: (0, jnp.clip(i - 4 * j, 0, 3)))
            for j in range(len(ys))
        ],
        out_specs=(
            pl.BlockSpec((4, 64, tile), lambda i: (0, 0, i)),
            pl.BlockSpec((4, 64, tile), lambda i: (0, 0, i)),
            pl.BlockSpec((8, 64, tile), lambda i: (0, 0, i)),
        ),
        scratch_shapes=[VM((MODEL_WIDTH, 8 * half), bf16), VM((16, 64, tile), f32)],
        compiler_params=pltpu.CompilerParams(vmem_limit_bytes=VMEM_BYTES),
        name="expert_dw",
    )(sc, *chunks, *ys)


def relay_body(kept, rx, ry, sx_out, sy_out, own_out):
    sx_out[...] = (kept[4:6] + ry[0:2].astype(f32)).astype(bf16)
    sy_out[...] = (kept[6:8] + rx[0:2].astype(f32)).astype(bf16)
    own_out[0:2] = kept[0:2] + rx[2:4].astype(f32)
    own_out[2:4] = kept[2:4] + ry[2:4].astype(f32)


def relay(kept, rx, ry):
    rows, wide = kept.shape[1:]
    return kernel_call(
        relay_body,
        (sds((2, rows, wide), bf16), sds((2, rows, wide), bf16), sds((4, rows, wide), f32)),
        [vmem()] * 3,
        "relay",
    )(kept, rx, ry)


def owned_body(own, rx, ry, out0, out1, out2, out3):
    out0[...] = own[0] + ry[0].astype(f32)
    out1[...] = (own[1] + ry[1].astype(f32)).astype(bf16)
    out2[...] = (own[2] + rx[0].astype(f32)).astype(bf16)
    out3[...] = (own[3] + rx[1].astype(f32)).astype(bf16)


def owned(own, rx, ry):
    shape = own.shape[1:]
    return kernel_call(
        owned_body,
        (sds(shape, f32), sds(shape, bf16), sds(shape, bf16), sds(shape, bf16)),
        [vmem()] * 3,
        "owned",
    )(own, rx, ry)


def unpack_grad_body(sc, g0, g1, g2, g3, out, wide):
    ep = sc[0]
    n = g0.shape[0]
    experts = EXPERTS // GROUP
    ff = g0.shape[1] // experts
    for k, g in enumerate((g0, g1, g2, g3)):
        for e in range(experts):
            for l in range(ff // 128):
                at = e * ff + 128 * l
                wide[l, pl.ds((ep ^ k) * experts + e, n, stride=EXPERTS), :] = g[
                    :, at : at + 128
                ].astype(f32)
    for l in range(ff // 128):
        out[:, 128 * l : 128 * (l + 1)] = wide[l]


def unpack_grad(sc, parts):
    n, wide = parts[0].shape
    ff = wide * GROUP // EXPERTS
    out = kernel_call(
        unpack_grad_body,
        sds((n * EXPERTS, ff), f32),
        [smem()] + [vmem()] * 4,
        "unpack_grad",
        [VM((ff // 128, n * EXPERTS, 128), f32)],
    )(sc, *parts)
    return out.reshape(n, EXPERTS, ff)


def fast(
    c,
    tokens,
    segment_ids,
    valid,
    expert_ids,
    teacher,
    attn_gain,
    w_query,
    key_projection,
    value_projection,
    w_out,
    moe_gain,
    w_router,
    w_gate,
    w_up,
    w_down,
):
    half = tokens.shape[0]
    seq_len = expert_ids.shape[0]
    rows = w_query.shape[0]
    qw, kw = w_query.shape[1], key_projection.shape[1]
    pw = qw + 2 * kw
    sc = jnp.stack([c.ep, c.rep, c.core]).astype(jnp.int32)

    def my_half(v, axis=0):
        return lax.dynamic_slice_in_dim(v, c.core * half, half, axis)

    def group_pair(parts):
        return [jnp.concatenate(parts[:2], 0), jnp.concatenate(parts[2:], 0)]

    def spread(pair, after=()):
        a = tie(pair[0], *after)
        xa, ya = c.swap(a, 1), c.swap(a, 2)
        b = pair[1]
        xb, yb = c.swap(b, 1), c.swap(b, 2)
        return [*pair, xa, xb, ya, yb, c.swap(tie(xa, xb, yb), 2), c.swap(tie(yb, xb), 1)]

    tokens_oth = c.other(tokens)
    front = pack_front(
        w_query,
        key_projection,
        value_projection,
        w_out,
        w_router,
        attn_gain,
        moe_gain,
        valid,
        expert_ids,
    )
    front_z = c.gather_group(front)
    front_p = spread(group_pair(front_z))
    packed = pack_experts(sc, *tie((w_gate, w_up, w_down), front))
    exp_z = [packed[0]] + [
        c.swap(tie(packed[k], front_p[2], front_p[4]), c.reps * k) for k in range(1, GROUP)
    ]
    exp_p = spread(group_pair(exp_z), front_p[6:])

    cosine, sine = rope_tables(seq_len, 128)
    y_own, y_away, hn, qkv, o, misc, gains, attn_w = attn_fwd(
        sc, tokens, tokens_oth, segment_ids, valid, cosine, sine, front_p, qw
    )
    resid, hm = second_norm(tokens, y_own, c.other(y_away), gains)

    def all_rows(v):
        own = c.gather_group(v)
        return own + [c.other(tie(v, own[1]))] + [c.other(x) for x in own[1:]]

    def group_sum(own, away):
        parts = core_sum(own, c.other(away))
        return [parts[0]] + [c.swap(parts[k], c.reps * k) for k in range(1, GROUP)]

    hms = all_rows(hm)
    mix_own, mix_away, a, b, gates = expert_fwd(sc, misc, hms, exp_p)
    mixes = group_sum(mix_own, mix_away)
    live = my_half(valid[0]).astype(f32)[:, None]
    result, g_out, g_low, err = loss_grad(
        resid, mixes, my_half(teacher), live, gains, seq_len, c.n
    )

    gos = all_rows(g_low)
    back_own, back_away, ga, gb, hs = expert_bwd(sc, gates, a, b, gos, exp_p)
    backs = group_sum(back_own, back_away)

    def replica_sum(x_send, y_send, kept):
        sx, sy, own = relay(kept, c.swap(x_send, 1), c.swap(y_send, 2))
        return owned(own, c.swap(sx, 1), c.swap(sy, 2))

    def from_group(parts):
        return [parts[0]] + [c.swap(parts[k], c.reps * k) for k in range(1, GROUP)]

    dw_gate_up = expert_dw(sc, hms, (ga, gb))
    dw_down = expert_dw(sc, gos, (hs,))
    backs = tie(backs, dw_gate_up, dw_down)
    dw_down = tie(dw_down, backs)
    gate_up_parts = from_group(replica_sum(*dw_gate_up))
    down_parts = from_group(replica_sum(*dw_down))
    ew = ga.shape[1]
    expert_grads = [
        unpack_grad(sc, [p[:, :ew] for p in gate_up_parts]),
        unpack_grad(sc, [p[:, ew:] for p in gate_up_parts]),
        unpack_grad(sc, down_parts),
    ]

    gy, gres, rows_g = second_back(backs, gates, misc, hm, resid, gains, g_out)
    gqkv, gy_all, ghn_own, ghn_away = attn_bwd(
        sc, gy, c.other(gy), o, qkv, segment_ids, valid, cosine, sine, attn_w
    )
    grad_input, rows_g = first_back(
        ghn_own, c.other(ghn_away), tokens, gains, gres, rows_g, err
    )
    parts = from_group(replica_sum(*attn_dw(sc, gy_all, o, hn, gqkv, rows_g)))
    own_w = parts[0] + (
        parts[1].astype(f32) + parts[2].astype(f32) + parts[3].astype(f32)
    )
    misc_own = own_w[:, pw + qw :]
    misc_own = misc_own + c.other(misc_own)
    live_total = jnp.sum(gains[2]) / rows
    loss = jnp.sum(misc_own[:, EXPERTS + 2]) / (2.0 * MODEL_WIDTH * live_total)
    return (
        loss,
        result,
        grad_input,
        misc_own[:, EXPERTS],
        own_w[:, :qw],
        own_w[:, qw : qw + kw],
        own_w[:, qw + kw : pw],
        own_w[:, pw : pw + qw],
        misc_own[:, EXPERTS + 1],
        misc_own[:, :EXPERTS],
        *expert_grads,
    )


def shards(
    tokens,
    segment_ids,
    valid,
    expert_ids,
    teacher,
    attn_gain,
    w_query,
    key_projection,
    value_projection,
    w_out,
    moe_gain,
    w_router,
    w_gate,
    w_up,
    w_down,
):
    c = Comm()
    if c.reps == 4 and w_query.shape[0] == 64:
        return fast(
            c,
            tokens,
            segment_ids,
            valid,
            expert_ids,
            teacher,
            attn_gain,
            w_query,
            key_projection,
            value_projection,
            w_out,
            moe_gain,
            w_router,
            w_gate,
            w_up,
            w_down,
        )
    half = tokens.shape[0]
    seq_len = expert_ids.shape[0]
    rows = w_query.shape[0]
    qw, kw = w_query.shape[1], key_projection.shape[1]
    ff = w_gate.shape[2]
    local_experts = EXPERTS // GROUP
    ew = local_experts * ff
    heads = qw // HEAD_SIZE
    kv_heads = kw // HEAD_SIZE
    per = heads // kv_heads
    scale = 1.0 / HEAD_SIZE
    first_core = c.core == 0

    def join_rows(own, other):
        return jnp.where(
            first_core, jnp.concatenate([own, other], 0), jnp.concatenate([other, own], 0)
        )

    def my_half(v):
        return lax.dynamic_slice_in_dim(v, c.core * half, half, 0)

    live_row = valid[0]
    live_count = jnp.sum(live_row).astype(f32)
    misc = jnp.concatenate(
        [
            w_router,
            attn_gain[:, None],
            moe_gain[:, None],
            jnp.broadcast_to(live_count.astype(bf16), (rows, 1)),
            jnp.zeros((rows, MISC - EXPERTS - 3), bf16),
        ],
        1,
    )
    front = jnp.concatenate([w_query, key_projection, value_projection, misc], 1)
    inputs_low = join_rows(tokens, c.other(tokens))

    def gather_attention(v):
        z = c.stack_group(c.gather_group(v))
        mid = z.shape[2] // 2
        return jnp.concatenate(
            [c.gather_reps(z[:, :, :mid], False), c.gather_reps(z[:, :, mid:], True)], 1
        )

    front_w = gather_attention(front)
    out_w = gather_attention(w_out)
    ids_half = my_half(expert_ids)
    ids_group = jnp.concatenate(c.gather_group(ids_half), 0)

    gate_up = jnp.concatenate(
        [w_gate.reshape(rows, GROUP, ew), w_up.reshape(rows, GROUP, ew)], 2
    ).transpose(1, 0, 2)
    gate_up_z = c.stack_group(c.all_to_group(gate_up))
    down_z = c.stack_group(c.all_to_group(w_down.reshape(rows, GROUP, ew).transpose(1, 0, 2)))
    gate_w = c.gather_reps(gate_up_z[:, :, :ew], False)
    up_w = c.gather_reps(gate_up_z[:, :, ew:], True)
    down_w = jnp.concatenate(
        [
            c.gather_reps(down_z[:, :, : ew // 2], False),
            c.gather_reps(down_z[:, :, ew // 2 :], True),
        ],
        1,
    )
    gate_ws = (gate_w, c.other(gate_w))
    up_ws = (up_w, c.other(up_w))
    down_ws = (down_w, c.other(down_w))

    pw = qw + 2 * kw
    proj_w = front_w[:, :pw]
    router_w = front_w[:, pw : pw + EXPERTS]
    gain_one = front_w[:, pw + EXPERTS].astype(f32)[None, :]
    gain_two = front_w[:, pw + EXPERTS + 1].astype(f32)[None, :]
    counts = front_w[:, pw + EXPERTS + 2].astype(f32).reshape(c.n, rows)[:, 0]
    live_total = jnp.sum(counts)

    inputs = inputs_low.astype(f32)
    inv_one = lax.rsqrt(jnp.mean(inputs * inputs, -1, keepdims=True) + epsilon)
    normed_one = inputs * inv_one
    attention_hidden = (normed_one * gain_one).astype(bf16)
    cosine, sine = rope_tables(seq_len, qw + kw)
    qkv = dot(attention_hidden, proj_w)
    qk_raw = qkv[:, : qw + kw]
    qk = (qk_raw * cosine + swap_halves(qk_raw) * sine).astype(bf16)
    q = qk[:, :qw].reshape(seq_len, kv_heads, per, HEAD_SIZE)
    k = qk[:, qw:].reshape(seq_len, kv_heads, HEAD_SIZE)
    v = qkv[:, qw + kw :].astype(bf16).reshape(seq_len, kv_heads, HEAD_SIZE)
    seg_row = segment_ids[0]
    places = jnp.arange(seq_len)
    allowed = (seg_row[:, None] == seg_row[None, :]) & (places[None, :] <= places[:, None]) & (
        live_row[None, :] > 0
    ) | (places[None, :] == places[:, None])
    scores = jnp.einsum("qkgd,skd->kgqs", q, k, preferred_element_type=f32) * scale
    scores = jnp.where(allowed[None, None], scores, negative)
    top_score = jnp.max(scores, -1, keepdims=True)
    exp_scores = jnp.exp(scores - top_score)
    probs = exp_scores / jnp.sum(exp_scores, -1, keepdims=True)
    probs_low = probs.astype(bf16)
    attn_out = (
        jnp.einsum("kgqs,skd->qkgd", probs_low, v, preferred_element_type=f32)
        .astype(bf16)
        .reshape(seq_len, qw)
    )
    proj_part = dot_t(attn_out, out_w)
    theirs = lax.dynamic_slice_in_dim(proj_part, (1 - c.core) * half, half, 0)
    inputs_half = tokens.astype(f32)
    resid = inputs_half + (my_half(proj_part) + c.other(theirs))
    inv_two = lax.rsqrt(jnp.mean(resid * resid, -1, keepdims=True) + epsilon)
    normed_two = resid * inv_two
    hidden_moe = (normed_two * gain_two).astype(bf16)

    hm = jnp.concatenate(c.gather_group(hidden_moe), 0)
    logits = dot(hm, router_w)
    named = jnp.any(ids_group[:, :, None] == jnp.arange(EXPERTS)[None, None, :], 1)
    masked = jnp.where(named, logits, negative)
    shifted = jnp.where(named, jnp.exp(logits - jnp.max(masked, -1, keepdims=True)), 0.0)
    gates = shifted / jnp.sum(shifted, -1, keepdims=True)
    my_gates = lax.dynamic_slice_in_dim(gates, c.ep * local_experts, local_experts, 1)
    wide = jnp.repeat(my_gates, ff, axis=1)

    kept = []
    mixed = 0.0
    for gw, uw, dw in zip(gate_ws, up_ws, down_ws):
        a = dot(hm, gw)
        b = dot(hm, uw)
        sigma = jax.nn.sigmoid(a)
        h = (a * sigma * b).astype(bf16)
        hs = (h.astype(f32) * wide).astype(bf16)
        mixed = mixed + dot_t(hs, dw)
        kept.append((a, b, h, hs))
    mixed = mixed.reshape(GROUP, half, MODEL_WIDTH)
    mix = mixed[0]
    for j in range(1, GROUP):
        mix = mix + c.swap(mixed[j].astype(bf16), c.reps * j).astype(f32)
    result = resid + mix

    live = my_half(live_row).astype(f32)[:, None]
    differ = result - my_half(teacher).astype(f32)
    err_cols = jnp.sum(live * differ * differ, 0)
    grad_out = seq_len * c.n / live_total * live * differ
    go = jnp.concatenate(c.gather_group(grad_out.astype(bf16)), 0)

    grad_hm = 0.0
    grad_gates = 0.0
    low = []
    for (a, b, h, hs), gw, uw, dw in zip(kept, gate_ws, up_ws, down_ws):
        u = dot(go, dw)
        grad_gates = grad_gates + jnp.sum(
            (h.astype(f32) * u).reshape(GROUP * half, local_experts, ff), -1
        )
        gh = u * wide
        sigma = jax.nn.sigmoid(a)
        ga = (gh * b * sigma * (1.0 + a * (1.0 - sigma))).astype(bf16)
        gb = (gh * a * sigma).astype(bf16)
        grad_hm = grad_hm + dot_t(ga, gw) + dot_t(gb, uw)
        low.append((ga, gb))
    gg = jnp.zeros((GROUP * half, MISC), f32)
    gg = lax.dynamic_update_slice_in_dim(gg, grad_gates, c.ep * local_experts, 1)
    back = jnp.concatenate([grad_hm, gg], 1).reshape(GROUP, half, MODEL_WIDTH + MISC)
    back_sum = back[0]
    for j in range(1, GROUP):
        back_sum = back_sum + c.swap(back[j].astype(bf16), c.reps * j).astype(f32)

    weight_sums = []
    for own, other in (
        ((hm, low[0][0]), (hm, low[1][0])),
        ((hm, low[0][1]), (hm, low[1][1])),
        ((go, kept[0][3]), (go, kept[1][3])),
    ):
        away = dot_o(*other).astype(bf16)
        weight_sums.append(dot_o(*own) + c.other(away).astype(f32))
    gate_s = c.scatter_reps(weight_sums[0], False)
    up_s = c.scatter_reps(weight_sums[1], True)
    down_s = jnp.concatenate(
        [
            c.scatter_reps(weight_sums[2][:, : ew // 2], False),
            c.scatter_reps(weight_sums[2][:, ew // 2 :], True),
        ],
        2,
    )
    sums = jnp.concatenate([gate_s, up_s, down_s], 2)
    sums_low = sums.astype(bf16)
    parts = [c.block(sums, 0)] + [
        c.swap(c.block(sums_low, k), c.reps * k).astype(f32) for k in range(1, GROUP)
    ]
    finished = c.stack_group(parts)

    def expert_grad(j):
        g = finished[:, :, j * ew : (j + 1) * ew].transpose(1, 0, 2)
        return g.reshape(rows, EXPERTS, ff)

    grad_probs = back_sum[:, MODEL_WIDTH : MODEL_WIDTH + EXPERTS]
    gate_probs = gates[:half]
    grad_logits = (
        gate_probs * (grad_probs - jnp.sum(gate_probs * grad_probs, -1, keepdims=True))
    ).astype(bf16)
    grad_hidden = back_sum[:, :MODEL_WIDTH] + dot_t(grad_logits, router_w)
    router_part = dot_o(hidden_moe, grad_logits)
    gain_two_part = jnp.sum(grad_hidden * normed_two, 0)
    scaled_two = grad_hidden * gain_two
    grad_resid = grad_out + inv_two * (
        scaled_two - normed_two * jnp.mean(scaled_two * normed_two, -1, keepdims=True)
    )
    gy_half = grad_resid.astype(bf16)
    gy = join_rows(gy_half, c.other(gy_half))

    out_part = dot_o(gy, attn_out)
    grad_attn = dot(gy, out_w).astype(bf16).reshape(seq_len, kv_heads, per, HEAD_SIZE)
    gp = jnp.einsum("qkgd,skd->kgqs", grad_attn, v, preferred_element_type=f32)
    gs = (probs * (gp - jnp.sum(probs * gp, -1, keepdims=True))).astype(bf16)
    gq = jnp.einsum("kgqs,skd->qkgd", gs, k, preferred_element_type=f32) * scale
    gk = jnp.einsum("kgqs,qkgd->skd", gs, q, preferred_element_type=f32) * scale
    gv = jnp.einsum("kgqs,qkgd->skd", probs_low, grad_attn, preferred_element_type=f32)
    gqk = jnp.concatenate([gq.reshape(seq_len, qw), gk.reshape(seq_len, kw)], 1)
    gqk = gqk * cosine - swap_halves(gqk) * sine
    gqkv = jnp.concatenate([gqk.astype(bf16), gv.astype(bf16).reshape(seq_len, kw)], 1)
    ghn_part = dot_t(gqkv, proj_w)
    ghn_low = ghn_part.astype(bf16)
    ghn = my_half(ghn_part) + c.other(
        lax.dynamic_slice_in_dim(ghn_low, (1 - c.core) * half, half, 0)
    ).astype(f32)
    proj_part_grad = dot_o(attention_hidden, gqkv)
    normed_half = my_half(normed_one)
    gain_one_part = jnp.sum(ghn * normed_half, 0)
    scaled_one = ghn * gain_one
    grad_input = grad_resid + my_half(inv_one) * (
        scaled_one - normed_half * jnp.mean(scaled_one * normed_half, -1, keepdims=True)
    )

    err_rows = jnp.sum(err_cols.reshape(MODEL_WIDTH // rows, rows), 0)
    misc_part = jnp.concatenate(
        [
            router_part,
            gain_one_part[:, None],
            gain_two_part[:, None],
            jnp.tile(err_rows, c.n)[:, None],
            jnp.zeros((MODEL_WIDTH, MISC - EXPERTS - 3), f32),
        ],
        1,
    )
    back_w = jnp.concatenate([proj_part_grad, out_part, misc_part], 1)
    mid = (back_w.shape[1] // 256) * 128
    attn_s = jnp.concatenate(
        [c.scatter_reps(back_w[:, :mid], False), c.scatter_reps(back_w[:, mid:], True)], 2
    )
    attn_low = attn_s.astype(bf16)
    own_w = c.block(attn_s, 0)
    for k_ in range(1, GROUP):
        own_w = own_w + c.swap(c.block(attn_low, k_), c.reps * k_).astype(f32)
    misc_own = own_w[:, pw + qw :]
    misc_own = misc_own + c.other(misc_own)
    loss = jnp.sum(misc_own[:, EXPERTS + 2]) / (2.0 * MODEL_WIDTH * live_total)

    return (
        loss,
        result.astype(bf16),
        grad_input.astype(bf16),
        misc_own[:, EXPERTS],
        own_w[:, :qw],
        own_w[:, qw : qw + kw],
        own_w[:, qw + kw : pw],
        own_w[:, pw : pw + qw],
        misc_own[:, EXPERTS + 1],
        misc_own[:, :EXPERTS],
        expert_grad(0),
        expert_grad(1),
        expert_grad(2),
    )


def solution(mesh):
    placed = (
        P(("dp", "tensor"), None),
        P("dp", None),
        P("dp", None),
        P("dp", None),
        P("dp", None),
        P("dp"),
        P("dp", "tensor"),
        P("dp", "tensor"),
        P("dp", "tensor"),
        P("dp", "tensor"),
        P("dp"),
        P("dp", None),
        P("dp", None, "tensor"),
        P("dp", None, "tensor"),
        P("dp", None, "tensor"),
    )
    return jax.shard_map(
        shards,
        mesh=mesh,
        in_specs=placed,
        out_specs=(
            P(),
            P(("dp", "tensor"), None),
            P(("dp", "tensor"), None),
            P("dp"),
            P("dp", "tensor"),
            P("dp", "tensor"),
            P("dp", "tensor"),
            P("dp", "tensor"),
            P("dp"),
            P("dp", None),
            P("dp", None, "tensor"),
            P("dp", None, "tensor"),
            P("dp", None, "tensor"),
        ),
        check_vma=False,
    )
```

```python
import jax
import jax.numpy as jnp
from jax import lax
from jax.experimental import pallas as pl
from jax.experimental.pallas import tpu as pltpu
from jax.sharding import PartitionSpec as P

MODEL_WIDTH = 1024
HEAD_SIZE = 64
TOPK = 8
EXPERTS = 16
GROUP = 4
MISC = 128
DIRECT = False
EARLY = False
ORDER = {'packed': ('front',), 'e1': ('fax', 'fay'), 'e2': ('fax', 'fay'), 'e3': ('fax', 'fay'), 'fad': ('fbx', 'fby'), 'fbd': ('fbx',), 'xax': ('fad', 'fbd'), 'xay': ('fad', 'fbd'), 'xad': ('xbx', 'xby'), 'xbd': ('xbx',), 'ht0': ('h1',), 'gt0': ('g1',), 'second': ('dwgu', 'dwdn'), 'dnx': ('b1', 'b2', 'b3'), 'dny': ('b1', 'b2', 'b3'), 'adw': ('gux2', 'guy2', 'dnx', 'dny')}
VMEM_BYTES = 60 << 20

epsilon = 1e-06
negative = -1e30
rope_base = 10000.0
f32 = jnp.float32
bf16 = jnp.bfloat16

INNER = (((1,), (1,)), ((), ()))
OUTER = (((0,), (0,)), ((), ()))


def dot(a, b):
    return jnp.dot(a, b, preferred_element_type=f32)


def dot_t(a, b):
    return lax.dot_general(a, b, INNER, preferred_element_type=f32)


def dot_o(a, b):
    return lax.dot_general(a, b, OUTER, preferred_element_type=f32)


def tie(v, *after):
    return lax.optimization_barrier((v, after))[0]


def rope_tables(length, width):
    half = HEAD_SIZE // 2
    places = jnp.arange(length).astype(f32)
    freqs = rope_base ** (-2.0 * jnp.arange(half).astype(f32) / HEAD_SIZE)
    angles = places[:, None] * freqs[None, :]
    cosine, sine = jnp.cos(angles), jnp.sin(angles)
    reps = width // HEAD_SIZE
    return (
        jnp.tile(jnp.concatenate([cosine, cosine], 1), (1, reps)),
        jnp.tile(jnp.concatenate([-sine, sine], 1), (1, reps)),
    )


def swap_halves(u):
    half = HEAD_SIZE // 2
    low = (jnp.arange(u.shape[1]) % HEAD_SIZE) < half
    return jnp.where(low[None, :], jnp.roll(u, -half, 1), jnp.roll(u, half, 1))


class Comm:
    def __init__(self):
        self.n = lax.axis_size("dp")
        self.me = lax.axis_index("dp")
        self.core = lax.axis_index("tensor")
        self.reps = self.n // GROUP
        self.ep = self.me // self.reps
        self.rep = self.me % self.reps
        self.bits = [1 << k for k in range(self.reps.bit_length() - 1)]

    def swap(self, v, mask):
        return lax.ppermute(v, "dp", [(i, i ^ mask) for i in range(self.n)])

    def other(self, v):
        return lax.ppermute(v, "tensor", [(0, 1), (1, 0)])

    def bit(self, b):
        return (self.rep // b) % 2

    def gather_reps(self, z, last_first):
        rows, cols = z.shape[1:]
        k = len(self.bits)
        out = jnp.zeros((GROUP,) + (2,) * k + (rows, cols), z.dtype)
        zero = jnp.int32(0)
        order = list(self.bits)
        if last_first:
            order = order[::-1]
        done = set()

        def place(block, flipped):
            start = [zero]
            for b in reversed(self.bits):
                if b in done:
                    start.append(zero)
                elif b == flipped:
                    start.append(1 - self.bit(b))
                else:
                    start.append(self.bit(b))
            return start + [zero, zero]

        cur = z.reshape((GROUP,) + (1,) * k + (rows, cols))
        out = lax.dynamic_update_slice(out, cur, place(cur, None))
        for b in order:
            got = self.swap(cur, b)
            out = lax.dynamic_update_slice(out, got, place(got, b))
            done.add(b)
            if len(done) < k:
                start = place(out, None)
                shape = [GROUP] + [2 if c in done else 1 for c in reversed(self.bits)]
                cur = lax.dynamic_slice(out, start, shape + [rows, cols])
        return out.reshape(GROUP * self.reps * rows, cols)

    def stack_group(self, parts, axis=0):
        parts = jnp.stack(parts, 0)
        idx = self.ep ^ jnp.arange(GROUP)
        return jnp.concatenate(
            [lax.dynamic_index_in_dim(parts, idx[j], 0, keepdims=True) for j in range(GROUP)], 0
        )

    def gather_group(self, v):
        return [v] + [self.swap(v, self.reps * k) for k in range(1, GROUP)]

    def block(self, v, k):
        return lax.dynamic_index_in_dim(v, self.ep ^ k, 0, keepdims=False)

    def all_to_group(self, v):
        return [self.block(v, 0)] + [
            self.swap(self.block(v, k), self.reps * k) for k in range(1, GROUP)
        ]

    def scatter_reps(self, s, last_first):
        cols = s.shape[1]
        k = len(self.bits)
        rows = s.shape[0] // (GROUP * self.reps)
        s = s.reshape((GROUP,) + (2,) * k + (rows, cols))
        order = list(self.bits)
        if last_first:
            order = order[::-1]
        for b in order:
            axis = 1 + list(reversed(self.bits)).index(b)
            mine = self.bit(b)
            send = lax.dynamic_slice_in_dim(s, 1 - mine, 1, axis).astype(bf16)
            keep = lax.dynamic_slice_in_dim(s, mine, 1, axis)
            s = keep + self.swap(send, b).astype(f32)
        return s.reshape(GROUP, rows, cols)


VM = pltpu.VMEM


def vmem():
    return pl.BlockSpec(memory_space=pltpu.VMEM)


def anym():
    return pl.BlockSpec(memory_space=pltpu.HBM)


def smem():
    return pl.BlockSpec(memory_space=pltpu.SMEM)


def sds(shape, dtype):
    return jax.ShapeDtypeStruct(shape, dtype)


def kernel_call(body, out_shape, in_specs, name, scratch=()):
    return pl.pallas_call(
        body,
        out_shape=out_shape,
        in_specs=in_specs,
        out_specs=jax.tree.map(lambda _: vmem(), out_shape),
        scratch_shapes=list(scratch),
        compiler_params=pltpu.CompilerParams(vmem_limit_bytes=VMEM_BYTES),
        name=name,
    )


def piece_copies(pieces, dst, sem, ep, rep, cols=None, first=0):
    copies = []
    for j, piece in enumerate(pieces):
        m, h = j // 2, j % 2
        for i in range(2):
            at = (ep ^ (2 * h + i)) * 4 + (rep ^ m)
            src, to = piece.at[pl.ds(64 * i, 64)], dst.at[at]
            if cols is not None:
                src, to = src.at[:, pl.ds(*cols)], to.at[:, pl.ds(*cols)]
            copies.append(pltpu.make_async_copy(src, to, sem.at[first + 2 * j + i]))
    return copies


NAMED = 32


def pack_front_body(wq, wk, wv, wo, wr, g1, g2, valid, ids, out):
    qw, kw = wq.shape[1], wk.shape[1]
    pw = qw + 2 * kw
    n = wq.shape[0]
    out[:, 0:qw] = wq[...]
    out[:, qw : qw + kw] = wk[...]
    out[:, qw + kw : pw] = wv[...]
    out[:, pw + MISC :] = wo[...]
    count = jnp.sum(valid[...].astype(f32), axis=1, keepdims=True)
    expert = lax.broadcasted_iota(jnp.int32, (EXPERTS, ids.shape[1]), 0)
    named = jnp.zeros(expert.shape, f32)
    for k in range(TOPK):
        named = jnp.where(ids[k : k + 1, :] == expert, 1.0, named)
    quarters = [named[:, n * j : n * (j + 1)] for j in range(ids.shape[1] // n)]
    top = jnp.concatenate([wr[...].astype(f32), jnp.zeros((NAMED - EXPERTS, n), f32)], 0)
    row = lax.broadcasted_iota(jnp.int32, top.shape, 0)
    top = jnp.where(row == EXPERTS, g1[...].astype(f32), top)
    top = jnp.where(row == EXPERTS + 1, g2[...].astype(f32), top)
    top = jnp.where(row == EXPERTS + 2, count, top)
    rest = jnp.zeros((MISC - NAMED - EXPERTS * len(quarters), n), f32)
    base = jnp.concatenate([top, *quarters, rest], 0)
    eye = lax.broadcasted_iota(jnp.int32, (n, n), 0) == lax.broadcasted_iota(jnp.int32, (n, n), 1)
    misc = dot_t(eye.astype(f32).astype(bf16), base.astype(bf16))
    out[:, pw : pw + MISC] = misc.astype(bf16)


def pack_front(wq, wk, wv, wo, wr, g1, g2, valid, ids):
    n = wq.shape[0]
    width = wq.shape[1] + 2 * wk.shape[1] + MISC + wo.shape[1]
    return kernel_call(pack_front_body, sds((n, width), bf16), [vmem()] * 9, "pack_front")(
        wq, wk, wv, wo, wr.T, g1[None, :], g2[None, :], valid, ids.T
    )


def pack_experts_body(sc, wg, wu, wd, out0, out1, out2, out3, wide):
    ep = sc[0]
    n, e, f = wg.shape
    per = e // GROUP
    for j, w in enumerate((wg, wu, wd)):
        for l in range(f // 128):
            wide[l] = w[:, :, 128 * l : 128 * (l + 1)].astype(f32).reshape(n * e, 128)
        for k, out in enumerate((out0, out1, out2, out3)):
            for x in range(per):
                for l in range(f // 128):
                    at = j * per * f + x * f + 128 * l
                    out[:, at : at + 128] = wide[
                        l, pl.ds((ep ^ k) * per + x, n, stride=e), :
                    ].astype(bf16)


def pack_experts(sc, wg, wu, wd):
    n, e, f = wg.shape
    return kernel_call(
        pack_experts_body,
        (sds((n, 3 * e * f // GROUP), bf16),) * GROUP,
        [smem()] + [vmem()] * 3,
        "pack_experts",
        [VM((f // 128, n * e, 128), f32)],
    )(sc, wg, wu, wd)


def rotate_pairs(u, cosine, sine):
    lane = lax.broadcasted_iota(jnp.int32, u.shape, 1)
    low = lane % HEAD_SIZE < HEAD_SIZE // 2
    turned = jnp.where(low, pltpu.roll(u, 96, 1), pltpu.roll(u, 32, 1))
    return u * cosine + turned * sine


def both_lanes(pair, odd):
    lane = lax.broadcasted_iota(jnp.int32, pair.shape, 1)
    other = pltpu.roll(pair, 64, 1)
    first = lane < HEAD_SIZE
    return jnp.where(first, other, pair) if odd else jnp.where(first, pair, other)


def two_heads(pair):
    lane = lax.broadcasted_iota(jnp.int32, pair.shape, 1)
    zero = jnp.zeros_like(pair)
    return jnp.concatenate(
        [jnp.where(lane < HEAD_SIZE, pair, zero), jnp.where(lane < HEAD_SIZE, zero, pair)], 0
    )


def one_pair(rows):
    n = rows.shape[0] // 2
    lane = lax.broadcasted_iota(jnp.int32, (n, rows.shape[1]), 1)
    return jnp.where(lane < HEAD_SIZE, rows[:n], rows[n:])


def allowed_mask(seg, valid):
    n = seg.shape[1]
    r = lax.broadcasted_iota(jnp.int32, (n, n), 0)
    col = lax.broadcasted_iota(jnp.int32, (n, n), 1)
    seg_row = jnp.broadcast_to(seg.astype(f32), (n, n))
    seg_col = jnp.sum(jnp.where(r == col, seg_row, 0.0), axis=1, keepdims=True)
    live = jnp.broadcast_to(valid.astype(f32), (n, n)) > 0
    return ((seg_col == seg_row) & (col <= r) & live) | (r == col)


def softmax_rows(q2, k2, allowed2):
    s = dot_t(q2, k2) * (1.0 / HEAD_SIZE)
    s = jnp.where(allowed2, s, negative)
    e = jnp.exp(s - jnp.max(s, axis=1, keepdims=True))
    return e / jnp.sum(e, axis=1, keepdims=True)


def attn_fwd_body(sc, x_own, x_oth, seg, valid, cosine, sine, *refs):
    pieces = refs[:8]
    own_out, away_out, hn_out, qkv_out, o_out, misc_out, gains_out, w_out, w, x, sem = refs[8:]
    ep, rep, core = sc[0], sc[1], sc[2]
    copies = piece_copies(pieces, w, sem, ep, rep)
    for cp in copies:
        cp.start()
    half = x_own.shape[0]
    n = 2 * half
    x[pl.ds(core * half, half), :] = x_own[...].astype(f32)
    x[pl.ds((1 - core) * half, half), :] = x_oth[...].astype(f32)
    allowed = allowed_mask(seg[...], valid[...])
    allowed2 = jnp.concatenate([allowed, allowed], 0)
    inputs = x[...]
    normed = inputs * lax.rsqrt(jnp.mean(inputs * inputs, axis=1, keepdims=True) + epsilon)
    for cp in copies:
        cp.wait()
    pw = qkv_out.shape[1]
    misc = w[:, :, pw : pw + MISC].reshape(MODEL_WIDTH, MISC)
    pick = lax.broadcasted_iota(jnp.int32, (8, MISC), 0) + EXPERTS
    pick = (pick == lax.broadcasted_iota(jnp.int32, (8, MISC), 1)).astype(f32).astype(bf16)
    gains = dot_t(pick, misc)
    gains_out[...] = gains
    misc_out[...] = misc
    hn = (normed * gains[0:1, :]).astype(bf16)
    hn_out[...] = hn
    w_out[...] = w[...].reshape(w_out.shape)
    qkv = dot(hn, w[:, :, :pw].reshape(MODEL_WIDTH, pw))
    groups = pw // 128
    kv0 = groups // 2
    for g in range(groups):
        u = qkv[:, 128 * g : 128 * (g + 1)]
        if g < kv0 + kv0 // 2:
            u = rotate_pairs(u, cosine[...], sine[...])
        qkv_out[:, 128 * g : 128 * (g + 1)] = u.astype(bf16)
    for m in range(kv0):
        g = kv0 + m // 2
        k2 = both_lanes(qkv_out[:, 128 * g : 128 * (g + 1)].astype(f32), m % 2).astype(bf16)
        g = g + kv0 // 2
        v2 = both_lanes(qkv_out[:, 128 * g : 128 * (g + 1)].astype(f32), m % 2).astype(bf16)
        q2 = two_heads(qkv_out[:, 128 * m : 128 * (m + 1)].astype(f32)).astype(bf16)
        p = softmax_rows(q2, k2, allowed2).astype(bf16)
        o_out[:, 128 * m : 128 * (m + 1)] = one_pair(dot(p, v2)).astype(bf16)
    wo = w[:, :, pw + MISC :].reshape(MODEL_WIDTH, o_out.shape[1])
    away_out[...] = dot_t(o_out[pl.ds((1 - core) * half, half), :], wo)
    own_out[...] = dot_t(o_out[pl.ds(core * half, half), :], wo)


def attn_fwd(sc, x_own, x_oth, seg, valid, cosine, sine, pieces, qw):
    half = x_own.shape[0]
    n = 2 * half
    cols = pieces[0].shape[1]
    pw = cols - MISC - qw
    return kernel_call(
        attn_fwd_body,
        (
            sds((half, MODEL_WIDTH), f32),
            sds((half, MODEL_WIDTH), f32),
            sds((n, MODEL_WIDTH), bf16),
            sds((n, pw), bf16),
            sds((n, qw), bf16),
            sds((MODEL_WIDTH, MISC), bf16),
            sds((8, MODEL_WIDTH), f32),
            sds((MODEL_WIDTH, cols), bf16),
        ),
        [smem()] + [vmem()] * 6 + [anym()] * 8,
        "attn_fwd",
        [VM((16, 64, cols), bf16), VM((n, MODEL_WIDTH), f32), pltpu.SemaphoreType.DMA((16,))],
    )(sc, x_own, x_oth, seg, valid, cosine, sine, *pieces)


def second_norm_body(x, y_own, y_oth, gains, resid_out, hm_out):
    resid = x[...].astype(f32) + (y_own[...] + y_oth[...])
    resid_out[...] = resid
    inv = lax.rsqrt(jnp.mean(resid * resid, axis=1, keepdims=True) + epsilon)
    hm_out[...] = (resid * inv * gains[1:2, :]).astype(bf16)


def second_norm(x, y_own, y_oth, gains):
    return kernel_call(
        second_norm_body,
        (sds(y_own.shape, f32), sds(y_own.shape, bf16)),
        [vmem()] * 4,
        "second_norm",
    )(x, y_own, y_oth, gains)


def named_rows(block, j):
    moved = pltpu.roll(block.astype(f32), MISC - NAMED - EXPERTS * j, 1)
    lane = lax.broadcasted_iota(jnp.int32, moved.shape, 1)
    return (moved > 0.5) & (lane < EXPERTS)


def gates_of(hm, misc, named):
    logits = dot(hm, misc)
    top = jnp.max(jnp.where(named, logits, negative), axis=1, keepdims=True)
    e = jnp.where(named, jnp.exp(logits - top), 0.0)
    return e / jnp.sum(e, axis=1, keepdims=True)


def expert_fwd_body(sc, misc, *refs):
    chunks, pieces = refs[:8], refs[8:16]
    own_out, away_out, a_out, b_out, gates_out, w, hm, acc, sem = refs[16:]
    ep, rep, core = sc[0], sc[1], sc[2]
    half = chunks[0].shape[0]
    experts = EXPERTS // GROUP
    ew = w.shape[2] // 3
    ff = ew // experts
    wide = piece_copies(pieces, w, sem, ep, rep, (0, 2 * ew), 0)
    down = piece_copies(pieces, w, sem, ep, rep, (2 * ew, ew), 16)
    for cp in wide:
        cp.start()
    for cp in down:
        cp.start()
    for j, chunk in enumerate(chunks):
        hm[pl.ds(j * half, half), :] = chunk[...]
        k = j % GROUP
        at = pl.multiple_of(((ep ^ k) * 4 + rep) * 64, 64)
        block = misc[pl.ds(at, 64), :]
        mine = core == (0 if j < GROUP else 1)
        quarters = [named_rows(block, q) for q in range(4)]
        first = jnp.concatenate([q.astype(f32) for q in quarters[:2]], 0)
        second = jnp.concatenate([q.astype(f32) for q in quarters[2:]], 0)
        named = jnp.where(mine, first, second) > 0.5
        gates_out[pl.ds(j * half, half), :] = gates_of(chunk[...], misc[...], named)
    acc[...] = jnp.zeros_like(acc)
    lane = lax.broadcasted_iota(jnp.int32, gates_out.shape, 1)
    for cp in wide:
        cp.wait()
    for cp in down:
        cp.wait()

    def tile(e, carry):
        rows = hm[...]
        at = pl.multiple_of(e * ff, ff)
        a = dot(rows, w[:, :, pl.ds(at, ff)].reshape(MODEL_WIDTH, ff))
        b = dot(rows, w[:, :, pl.ds(ew + at, ff)].reshape(MODEL_WIDTH, ff))
        g = jnp.sum(
            jnp.where(lane == ep * experts + e, gates_out[...], 0.0), axis=1, keepdims=True
        )
        h = (a * jax.nn.sigmoid(a) * b).astype(bf16)
        hs = (h.astype(f32) * g).astype(bf16)
        a_out[:, pl.ds(at, ff)] = a
        b_out[:, pl.ds(at, ff)] = b
        acc[...] += dot_t(hs, w[:, :, pl.ds(2 * ew + at, ff)].reshape(MODEL_WIDTH, ff))
        return carry

    lax.fori_loop(0, experts, tile, 0)
    own_out[...] = acc[: GROUP * half, :]
    away_out[...] = acc[GROUP * half :, :].astype(bf16)


def expert_fwd(sc, misc, chunks, pieces):
    half = chunks[0].shape[0]
    cols = pieces[0].shape[1]
    ew = cols // 3
    rows = GROUP * half
    return kernel_call(
        expert_fwd_body,
        (
            sds((rows, MODEL_WIDTH), f32),
            sds((rows, MODEL_WIDTH), bf16),
            sds((2 * rows, ew), f32),
            sds((2 * rows, ew), f32),
            sds((2 * rows, MISC), f32),
        ),
        [smem()] + [vmem()] * 9 + [anym()] * 8,
        "expert_fwd",
        [
            VM((16, 64, cols), bf16),
            VM((2 * rows, MODEL_WIDTH), bf16),
            VM((2 * rows, MODEL_WIDTH), f32),
            pltpu.SemaphoreType.DMA((32,)),
        ],
    )(sc, misc, *chunks, *pieces)


def core_sum_body(own, got, out0, out1, out2, out3):
    half = out0.shape[0]
    for j, out in enumerate((out0, out1, out2, out3)):
        at = pl.ds(j * half, half)
        out[...] = (own[at, :] + got[at, :].astype(f32)).astype(out.dtype)


def core_sum(own, got):
    shape = (own.shape[0] // GROUP, own.shape[1])
    return kernel_call(
        core_sum_body,
        (sds(shape, f32), sds(shape, bf16), sds(shape, bf16), sds(shape, bf16)),
        [vmem()] * 2,
        "core_sum",
    )(own, got)


def expert_bwd_body(sc, gates, a_in, b_in, *refs):
    chunks, pieces = refs[:8], refs[8:16]
    own_out, away_out, ga_out, gb_out, hs_out, w, go, acc, gsum, sem = refs[16:]
    ep, rep = sc[0], sc[1]
    half = chunks[0].shape[0]
    rows = GROUP * half
    experts = EXPERTS // GROUP
    ew = w.shape[2] // 3
    ff = ew // experts
    wide = piece_copies(pieces, w, sem, ep, rep, (0, 2 * ew), 0)
    down = piece_copies(pieces, w, sem, ep, rep, (2 * ew, ew), 16)
    for cp in down:
        cp.start()
    for cp in wide:
        cp.start()
    for j, chunk in enumerate(chunks):
        go[pl.ds(j * half, half), :] = chunk[...]
    acc[...] = jnp.zeros_like(acc)
    gsum[...] = jnp.zeros_like(gsum)
    lane = lax.broadcasted_iota(jnp.int32, gsum.shape, 1)
    for cp in down:
        cp.wait()
    for cp in wide:
        cp.wait()

    def tile(e, carry):
        at = pl.multiple_of(e * ff, ff)
        a = a_in[:, pl.ds(at, ff)]
        b = b_in[:, pl.ds(at, ff)]
        u = dot(go[...], w[:, :, pl.ds(2 * ew + at, ff)].reshape(MODEL_WIDTH, ff))
        mine = lane == ep * experts + e
        g = jnp.sum(jnp.where(mine, gates[...], 0.0), axis=1, keepdims=True)
        s = jax.nn.sigmoid(a)
        silu = a * s
        h = (silu * b).astype(bf16).astype(f32)
        gsum[...] += jnp.where(mine, jnp.sum(h * u, axis=1, keepdims=True), 0.0)
        gh = u * g
        ga = (gh * b * s * (1.0 + a * (1.0 - s))).astype(bf16)
        gb = (gh * silu).astype(bf16)
        ga_out[:, pl.ds(at, ff)] = ga
        gb_out[:, pl.ds(at, ff)] = gb
        hs_out[:, pl.ds(at, ff)] = (h * g).astype(bf16)
        wg = w[:, :, pl.ds(at, ff)].reshape(MODEL_WIDTH, ff)
        wu = w[:, :, pl.ds(ew + at, ff)].reshape(MODEL_WIDTH, ff)
        acc[...] += dot_t(ga, wg) + dot_t(gb, wu)
        return carry

    lax.fori_loop(0, experts, tile, 0)
    own_out[:, :MODEL_WIDTH] = acc[:rows, :]
    own_out[:, MODEL_WIDTH:] = gsum[:rows, :]
    away_out[:, :MODEL_WIDTH] = acc[rows:, :].astype(bf16)
    away_out[:, MODEL_WIDTH:] = gsum[rows:, :].astype(bf16)


def expert_bwd(sc, gates, a, b, chunks, pieces):
    half = chunks[0].shape[0]
    cols = pieces[0].shape[1]
    ew = cols // 3
    rows = GROUP * half
    full = MODEL_WIDTH + MISC
    return kernel_call(
        expert_bwd_body,
        (
            sds((rows, full), f32),
            sds((rows, full), bf16),
            sds((2 * rows, ew), bf16),
            sds((2 * rows, ew), bf16),
            sds((2 * rows, ew), bf16),
        ),
        [smem()] + [vmem()] * 11 + [anym()] * 8,
        "expert_bwd",
        [
            VM((16, 64, cols), bf16),
            VM((2 * rows, MODEL_WIDTH), bf16),
            VM((2 * rows, MODEL_WIDTH), f32),
            VM((2 * rows, MISC), f32),
            pltpu.SemaphoreType.DMA((32,)),
        ],
    )(sc, gates, a, b, *chunks, *pieces)


def loss_body(resid, m0, m1, m2, m3, teacher, live, gains, scale, result_out, g_out, glow_out, err_out):
    mix = m0[...] + (m1[...].astype(f32) + m2[...].astype(f32) + m3[...].astype(f32))
    result = resid[...] + mix
    result_out[...] = result.astype(bf16)
    differ = result - teacher[...].astype(f32)
    rows = gains.shape[1] // scale.shape[1]
    total = jnp.sum(gains[2:3, :], axis=1, keepdims=True) / rows
    weighted = live[...] * differ
    g = (scale.shape[0] * scale.shape[1]) / total * weighted
    g_out[...] = g
    glow_out[...] = g.astype(bf16)
    err_out[...] = jnp.broadcast_to(jnp.sum(weighted * differ, axis=0, keepdims=True), err_out.shape)


def loss_grad(resid, mixes, teacher, live, gains, seq_len, n):
    shape = resid.shape
    return kernel_call(
        loss_body,
        (sds(shape, bf16), sds(shape, f32), sds(shape, bf16), sds((8, shape[1]), f32)),
        [vmem()] * 9,
        "loss_grad",
    )(resid, *mixes, teacher, live, gains, jnp.zeros((seq_len, n), f32))


def second_back_body(b0, b1, b2, b3, gates, misc, hm, resid, gains, g_out, gy_out, gres_out, rows_out):
    half = resid.shape[0]
    total = b0[...] + (b1[...].astype(f32) + b2[...].astype(f32) + b3[...].astype(f32))
    gp = total[:, MODEL_WIDTH:]
    gate = gates[0:half, :]
    gl = (gate * (gp - jnp.sum(gate * gp, axis=1, keepdims=True))).astype(bf16)
    ghm = total[:, :MODEL_WIDTH] + dot_t(gl, misc[...])
    x = resid[...]
    inv = lax.rsqrt(jnp.mean(x * x, axis=1, keepdims=True) + epsilon)
    normed = x * inv
    rows = dot_o(gl, hm[...])
    gain_row = jnp.sum(ghm * normed, axis=0, keepdims=True)
    at = lax.broadcasted_iota(jnp.int32, rows.shape, 0)
    rows_out[...] = jnp.where(at == EXPERTS + 1, gain_row, rows)
    scaled = ghm * gains[1:2, :]
    gres = g_out[...] + inv * (
        scaled - normed * jnp.mean(scaled * normed, axis=1, keepdims=True)
    )
    gres_out[...] = gres
    gy_out[...] = gres.astype(bf16)


def second_back(backs, gates, misc, hm, resid, gains, g_out):
    shape = resid.shape
    return kernel_call(
        second_back_body,
        (sds(shape, bf16), sds(shape, f32), sds((MISC, shape[1]), f32)),
        [vmem()] * 10,
        "second_back",
    )(*backs, gates, misc, hm, resid, gains, g_out)


def attn_bwd_body(
    sc, gy_own, gy_oth, o, qkv, seg, valid, cosine, sine, w, gqkv_out, gy_out, own_out, away_out, low
):
    core = sc[2]
    half = gy_own.shape[0]
    n = 2 * half
    gy_out[pl.ds(core * half, half), :] = gy_own[...]
    gy_out[pl.ds((1 - core) * half, half), :] = gy_oth[...]
    pw = qkv.shape[1]
    low[...] = dot(gy_out[...], w[:, pw + MISC :]).astype(bf16)
    allowed = allowed_mask(seg[...], valid[...])
    allowed2 = jnp.concatenate([allowed, allowed], 0)
    kv0 = pw // 256
    lane = lax.broadcasted_iota(jnp.int32, (n, 128), 1)
    scale = 1.0 / HEAD_SIZE
    held = {}
    for m in range(kv0):
        gk_at = kv0 + m // 2
        gv_at = gk_at + kv0 // 2
        k2 = both_lanes(qkv[:, 128 * gk_at : 128 * (gk_at + 1)].astype(f32), m % 2).astype(bf16)
        v2 = both_lanes(qkv[:, 128 * gv_at : 128 * (gv_at + 1)].astype(f32), m % 2).astype(bf16)
        q2 = two_heads(qkv[:, 128 * m : 128 * (m + 1)].astype(f32)).astype(bf16)
        go2 = two_heads(low[:, 128 * m : 128 * (m + 1)].astype(f32)).astype(bf16)
        p = softmax_rows(q2, k2, allowed2)
        gp = dot_t(go2, v2)
        gs = (p * (gp - jnp.sum(p * gp, axis=1, keepdims=True))).astype(bf16)
        gq = one_pair(dot(gs, k2)) * scale
        gqkv_out[:, 128 * m : 128 * (m + 1)] = rotate_pairs(gq, cosine[...], -sine[...]).astype(bf16)
        gk = dot_o(gs, q2) * scale
        gv = dot_o(p.astype(bf16), go2)
        gk = gk + pltpu.roll(gk, 64, 1)
        gv = gv + pltpu.roll(gv, 64, 1)
        if m % 2 == 0:
            held = {"k": gk, "v": gv}
        else:
            gk = jnp.where(lane < HEAD_SIZE, held["k"], gk)
            gv = jnp.where(lane < HEAD_SIZE, held["v"], gv)
            gqkv_out[:, 128 * gk_at : 128 * (gk_at + 1)] = rotate_pairs(
                gk, cosine[...], -sine[...]
            ).astype(bf16)
            gqkv_out[:, 128 * gv_at : 128 * (gv_at + 1)] = gv.astype(bf16)
    away_out[...] = dot_t(gqkv_out[pl.ds((1 - core) * half, half), :], w[:, :pw]).astype(bf16)
    own_out[...] = dot_t(gqkv_out[pl.ds(core * half, half), :], w[:, :pw])


def attn_bwd(sc, gy_own, gy_oth, o, qkv, seg, valid, cosine, sine, w):
    half = gy_own.shape[0]
    n = 2 * half
    pw = qkv.shape[1]
    return kernel_call(
        attn_bwd_body,
        (
            sds((n, pw), bf16),
            sds((n, MODEL_WIDTH), bf16),
            sds((half, MODEL_WIDTH), f32),
            sds((half, MODEL_WIDTH), bf16),
        ),
        [smem()] + [vmem()] * 9,
        "attn_bwd",
        [VM((n, o.shape[1]), bf16)],
    )(sc, gy_own, gy_oth, o, qkv, seg, valid, cosine, sine, w)


def first_back_body(g_own, g_oth, x, gains, gres, rows, err, ginput_out, rows_out):
    ghn = g_own[...] + g_oth[...].astype(f32)
    inputs = x[...].astype(f32)
    inv = lax.rsqrt(jnp.mean(inputs * inputs, axis=1, keepdims=True) + epsilon)
    normed = inputs * inv
    gain_row = jnp.sum(ghn * normed, axis=0, keepdims=True)
    scaled = ghn * gains[0:1, :]
    ginput_out[...] = (
        gres[...] + inv * (scaled - normed * jnp.mean(scaled * normed, axis=1, keepdims=True))
    ).astype(bf16)
    e = err[...]
    for shift in (64, 128, 256, 512):
        e = e + pltpu.roll(e, shift, 1)
    at = lax.broadcasted_iota(jnp.int32, rows.shape, 0)
    r = jnp.where(at == EXPERTS, gain_row, rows[...])
    rows_out[...] = jnp.where(at == EXPERTS + 2, e[0:1, :], r)


def first_back(g_own, g_oth, x, gains, gres, rows, err):
    return kernel_call(
        first_back_body,
        (sds(gres.shape, bf16), sds(rows.shape, f32)),
        [vmem()] * 7,
        "first_back",
    )(g_own, g_oth, x, gains, gres, rows, err)


SEND_X = (12, 13, 4, 5)
SEND_Y = (14, 15, 10, 11)
KEPT = (0, 1, 2, 3, 6, 7, 8, 9)


def store_relative(out, ep, rep, value, cols):
    for j in range(16):
        to = 4 * ((j % 4) ^ rep) + ((j // 4) ^ ep)
        out[to, :, cols] = value[64 * j : 64 * (j + 1), :]


def split_relative(full, x_out, y_out, kept_out):
    for j, at in enumerate(SEND_X):
        x_out[j] = full[at].astype(bf16)
    for j, at in enumerate(SEND_Y):
        y_out[j] = full[at].astype(bf16)
    for j, at in enumerate(KEPT):
        kept_out[j] = full[at]


def attn_dw_body(sc, gy, o, hn, gqkv, rows, x_out, y_out, kept_out, full):
    ep, rep = sc[0], sc[1]
    pw = gqkv.shape[1]
    qw = o.shape[1]
    store_relative(full, ep, rep, dot_o(hn[...], gqkv[...]), slice(0, pw))
    store_relative(full, ep, rep, dot_o(gy[...], o[...]), slice(pw, pw + qw))
    store_relative(full, ep, rep, jnp.transpose(rows[...]), slice(pw + qw, pw + qw + MISC))
    split_relative(full, x_out, y_out, kept_out)


def attn_dw(sc, gy, o, hn, gqkv, rows):
    width = gqkv.shape[1] + o.shape[1] + MISC
    return kernel_call(
        attn_dw_body,
        (sds((4, 64, width), bf16), sds((4, 64, width), bf16), sds((8, 64, width), f32)),
        [smem()] + [vmem()] * 5,
        "attn_dw",
        [VM((16, 64, width), f32)],
    )(sc, gy, o, hn, gqkv, rows)


def attn_dw3_body(sc, gy, o, hn, gqkv, rows, own_out, x_out, y_out, d_out, full):
    ep, rep = sc[0], sc[1]
    pw = gqkv.shape[1]
    qw = o.shape[1]
    store_relative(full, ep, rep, dot_o(hn[...], gqkv[...]), slice(0, pw))
    store_relative(full, ep, rep, dot_o(gy[...], o[...]), slice(pw, pw + qw))
    store_relative(full, ep, rep, jnp.transpose(rows[...]), slice(pw + qw, pw + qw + MISC))
    own_out[...] = full[0:4]
    for m, out in enumerate((x_out, y_out, d_out)):
        out[...] = full[4 * m + 4 : 4 * m + 8].astype(bf16)


def attn_dw3(sc, gy, o, hn, gqkv, rows):
    width = gqkv.shape[1] + o.shape[1] + MISC
    low = sds((4, 64, width), bf16)
    return kernel_call(
        attn_dw3_body,
        (sds((4, 64, width), f32), low, low, low),
        [smem()] + [vmem()] * 5,
        "attn_dw3",
        [VM((16, 64, width), f32)],
    )(sc, gy, o, hn, gqkv, rows)


def attn_sum3_body(own, x, y, d, *outs):
    for k, out in enumerate(outs):
        total = own[k] + (x[k].astype(f32) + y[k].astype(f32) + d[k].astype(f32))
        out[...] = total.astype(out.dtype)


def attn_sum3(own, x, y, d):
    shape = own.shape[1:]
    low = sds(shape, bf16)
    return kernel_call(
        attn_sum3_body, (sds(shape, f32), low, low, low), [vmem()] * 4, "attn_sum3"
    )(own, x, y, d)


def expert_dw_body(sc, *refs):
    n = len(refs) - 13
    chunks, ys = refs[:8], refs[8 : 8 + n]
    x_out, y_out, kept_out, xt, full = refs[8 + n :]
    ep, rep = sc[0], sc[1]
    half = chunks[0].shape[0]

    @pl.when(pl.program_id(0) == 0)
    def _():
        for j, x in enumerate(chunks):
            xt[:, j * half : (j + 1) * half] = jnp.transpose(x[...])

    for j, y in enumerate(ys):

        @pl.when(pl.program_id(0) // 4 == j)
        def _():
            store_relative(full, ep, rep, dot(xt[...], y[...]), slice(None))

    split_relative(full, x_out, y_out, kept_out)


def expert_dw(sc, chunks, ys):
    half = chunks[0].shape[0]
    tile = ys[0].shape[1] // 4
    steps = 4 * len(ys)
    wide = tile * steps
    whole = pl.BlockSpec((half, MODEL_WIDTH), lambda i: (0, 0))
    return pl.pallas_call(
        expert_dw_body,
        grid=(steps,),
        out_shape=(sds((4, 64, wide), bf16), sds((4, 64, wide), bf16), sds((8, 64, wide), f32)),
        in_specs=[smem()]
        + [whole] * 8
        + [
            pl.BlockSpec((8 * half, tile), lambda i, j=j: (0, jnp.clip(i - 4 * j, 0, 3)))
            for j in range(len(ys))
        ],
        out_specs=(
            pl.BlockSpec((4, 64, tile), lambda i: (0, 0, i)),
            pl.BlockSpec((4, 64, tile), lambda i: (0, 0, i)),
            pl.BlockSpec((8, 64, tile), lambda i: (0, 0, i)),
        ),
        scratch_shapes=[VM((MODEL_WIDTH, 8 * half), bf16), VM((16, 64, tile), f32)],
        compiler_params=pltpu.CompilerParams(vmem_limit_bytes=VMEM_BYTES),
        name="expert_dw",
    )(sc, *chunks, *ys)


def relay_body(kept, rx, ry, sx_out, sy_out, own_out):
    sx_out[...] = (kept[4:6] + ry[0:2].astype(f32)).astype(bf16)
    sy_out[...] = (kept[6:8] + rx[0:2].astype(f32)).astype(bf16)
    own_out[0:2] = kept[0:2] + rx[2:4].astype(f32)
    own_out[2:4] = kept[2:4] + ry[2:4].astype(f32)


def relay(kept, rx, ry):
    rows, wide = kept.shape[1:]
    return kernel_call(
        relay_body,
        (sds((2, rows, wide), bf16), sds((2, rows, wide), bf16), sds((4, rows, wide), f32)),
        [vmem()] * 3,
        "relay",
    )(kept, rx, ry)


def owned_body(own, rx, ry, out0, out1, out2, out3):
    out0[...] = own[0] + ry[0].astype(f32)
    out1[...] = (own[1] + ry[1].astype(f32)).astype(bf16)
    out2[...] = (own[2] + rx[0].astype(f32)).astype(bf16)
    out3[...] = (own[3] + rx[1].astype(f32)).astype(bf16)


def owned(own, rx, ry):
    shape = own.shape[1:]
    return kernel_call(
        owned_body,
        (sds(shape, f32), sds(shape, bf16), sds(shape, bf16), sds(shape, bf16)),
        [vmem()] * 3,
        "owned",
    )(own, rx, ry)


def unpack_grad_body(sc, g0, g1, g2, g3, out, wide):
    ep = sc[0]
    n = g0.shape[0]
    experts = EXPERTS // GROUP
    ff = g0.shape[1] // experts
    for k, g in enumerate((g0, g1, g2, g3)):
        for e in range(experts):
            for l in range(ff // 128):
                at = e * ff + 128 * l
                wide[l, pl.ds((ep ^ k) * experts + e, n, stride=EXPERTS), :] = g[
                    :, at : at + 128
                ].astype(f32)
    for l in range(ff // 128):
        out[:, 128 * l : 128 * (l + 1)] = wide[l]


def unpack_grad(sc, parts):
    n, wide = parts[0].shape
    ff = wide * GROUP // EXPERTS
    out = kernel_call(
        unpack_grad_body,
        sds((n * EXPERTS, ff), f32),
        [smem()] + [vmem()] * 4,
        "unpack_grad",
        [VM((ff // 128, n * EXPERTS, 128), f32)],
    )(sc, *parts)
    return out.reshape(n, EXPERTS, ff)


def fast(
    c,
    tokens,
    segment_ids,
    valid,
    expert_ids,
    teacher,
    attn_gain,
    w_query,
    key_projection,
    value_projection,
    w_out,
    moe_gain,
    w_router,
    w_gate,
    w_up,
    w_down,
):
    half = tokens.shape[0]
    seq_len = expert_ids.shape[0]
    rows = w_query.shape[0]
    qw, kw = w_query.shape[1], key_projection.shape[1]
    pw = qw + 2 * kw
    sc = jnp.stack([c.ep, c.rep, c.core]).astype(jnp.int32)

    def my_half(v, axis=0):
        return lax.dynamic_slice_in_dim(v, c.core * half, half, axis)

    made = {}

    def held(name, v):
        wanted = ORDER.get(name, ())
        return tie(v, *[made[w] for w in wanted]) if wanted else v

    def run(name, f, *args):
        got = f(*held(name, args))
        made[name] = min(jax.tree.leaves(got), key=lambda x: x.size * x.dtype.itemsize)
        return got

    def send(name, v, mask):
        made[name] = c.swap(held(name, v), mask)
        return made[name]

    def cross(name, v):
        made[name] = c.other(held(name, v))
        return made[name]

    def to_group(name, parts):
        return [send(f"{name}{k}", v, c.reps * k) for k, v in enumerate(parts, 1)]

    def pair(a, b):
        return jnp.concatenate([a, b], 0)

    def spread(name, a, b):
        ax, ay = send(name + "ax", a, 1), send(name + "ay", a, 2)
        bx, by = send(name + "bx", b, 1), send(name + "by", b, 2)
        ad, bd = send(name + "ad", ax, 2), send(name + "bd", by, 1)
        return [a, b, ax, bx, ay, by, ad, bd]

    tokens_oth = cross("tokens", tokens)
    front = run(
        "front",
        pack_front,
        w_query,
        key_projection,
        value_projection,
        w_out,
        w_router,
        attn_gain,
        moe_gain,
        valid,
        expert_ids,
    )
    z1, z2, z3 = to_group("z", [front] * 3)
    packed = run("packed", pack_experts, sc, w_gate, w_up, w_down)
    front_p = spread("f", pair(front, z1), pair(z2, z3))
    e1, e2, e3 = to_group("e", packed[1:])
    exp_a = pair(packed[0], e1)

    cosine, sine = rope_tables(seq_len, 128)
    y_own, y_away, hn, qkv, o, misc, gains, attn_w = run(
        "attn",
        lambda *v: attn_fwd(*v, qw),
        sc,
        tokens,
        tokens_oth,
        segment_ids,
        valid,
        cosine,
        sine,
        front_p,
    )
    y_oth = cross("y", y_away)
    exp_p = spread("x", exp_a, pair(e2, e3))
    resid, hm = run("norm", second_norm, tokens, y_own, y_oth, gains)

    def all_rows(name, v):
        own = [v] + to_group(name, [v] * 3)
        return own + [cross(f"{name}t{k}", x) for k, x in enumerate(own)]

    hms = all_rows("h", hm)
    mix_own, mix_away, a, b, gates = run("efwd", expert_fwd, sc, misc, hms, exp_p)
    mixes = run("msum", core_sum, mix_own, cross("mt", mix_away))
    mixes = [mixes[0]] + to_group("m", mixes[1:])
    live = my_half(valid[0]).astype(f32)[:, None]
    result, g_out, g_low, err = loss_grad(
        resid, mixes, my_half(teacher), live, gains, seq_len, c.n
    )

    gos = all_rows("g", g_low)
    back_own, back_away, ga, gb, hs = run("ebwd", expert_bwd, sc, gates, a, b, gos, exp_p)
    backs = run("bsum", core_sum, back_own, cross("bt", back_away))
    backs = [backs[0]] + to_group("b", backs[1:])

    def first_step(name, x_send, y_send, kept):
        return kept, send(name + "x", x_send, 1), send(name + "y", y_send, 2)

    def second_step(name, sx, sy, own):
        return own, send(name + "x2", sx, 1), send(name + "y2", sy, 2)

    dw_gu = run("dwgu", lambda *v: expert_dw(v[0], v[1], v[2:]), sc, hms, ga, gb)
    dw_dn = run("dwdn", lambda *v: expert_dw(v[0], v[1], v[2:]), sc, gos, hs)
    gu = run("gurelay", relay, *first_step("gu", *dw_gu))
    gu = second_step("gu", *gu)
    dn_1 = first_step("dn", *dw_dn)

    gy, gres, rows_g = run(
        "second", second_back, backs, gates, misc, hm, resid, gains, g_out
    )
    gqkv, gy_all, ghn_own, ghn_away = run(
        "abwd",
        attn_bwd,
        sc,
        gy,
        cross("gy", gy),
        o,
        qkv,
        segment_ids,
        valid,
        cosine,
        sine,
        attn_w,
    )
    grad_input, rows_g = run(
        "first", first_back, ghn_own, cross("ghn", ghn_away), tokens, gains, gres, rows_g, err
    )
    if EARLY:
        dn = second_step("dn", *run("dnrelay", relay, *dn_1))
        gu0, *gu_low = run("guown", owned, *gu)
        gu_got = to_group("guz", gu_low)
    if DIRECT:
        attn_own, ax, ay, ad = run("adw", attn_dw3, sc, gy_all, o, hn, gqkv, rows_g)
        ax, ay, ad = send("ax", ax, 1), send("ay", ay, 2), send("ad", ad, 3)
    else:
        at = first_step("a", *run("adw", attn_dw, sc, gy_all, o, hn, gqkv, rows_g))
    if not EARLY:
        gu0, *gu_low = run("guown", owned, *gu)
        dn = second_step("dn", *run("dnrelay", relay, *dn_1))
        gu_got = to_group("guz", gu_low)
    if DIRECT:
        w0, *w_low = run("asum", attn_sum3, attn_own, ax, ay, ad)
    else:
        w0, *w_low = run("aown", owned, *second_step("a", *run("arelay", relay, *at)))
    w_got = to_group("az", w_low)
    dn0, *dn_low = run("dnown", owned, *dn)
    dn_got = to_group("dnz", dn_low)
    ew = ga.shape[1]
    parts = [gu0, *gu_got]
    expert_grads = [
        run("ug", unpack_grad, sc, [p[:, :ew] for p in parts]),
        run("uu", unpack_grad, sc, [p[:, ew:] for p in parts]),
        run("ud", unpack_grad, sc, [dn0, *dn_got]),
    ]
    own_w = w0 + (w_got[0].astype(f32) + w_got[1].astype(f32) + w_got[2].astype(f32))
    misc_own = own_w[:, pw + qw :]
    misc_own = misc_own + c.other(misc_own)
    live_total = jnp.sum(gains[2]) / rows
    loss = jnp.sum(misc_own[:, EXPERTS + 2]) / (2.0 * MODEL_WIDTH * live_total)
    return (
        loss,
        result,
        grad_input,
        misc_own[:, EXPERTS],
        own_w[:, :qw],
        own_w[:, qw : qw + kw],
        own_w[:, qw + kw : pw],
        own_w[:, pw : pw + qw],
        misc_own[:, EXPERTS + 1],
        misc_own[:, :EXPERTS],
        *expert_grads,
    )


def shards(
    tokens,
    segment_ids,
    valid,
    expert_ids,
    teacher,
    attn_gain,
    w_query,
    key_projection,
    value_projection,
    w_out,
    moe_gain,
    w_router,
    w_gate,
    w_up,
    w_down,
):
    c = Comm()
    if c.reps == 4 and w_query.shape[0] == 64:
        return fast(
            c,
            tokens,
            segment_ids,
            valid,
            expert_ids,
            teacher,
            attn_gain,
            w_query,
            key_projection,
            value_projection,
            w_out,
            moe_gain,
            w_router,
            w_gate,
            w_up,
            w_down,
        )
    half = tokens.shape[0]
    seq_len = expert_ids.shape[0]
    rows = w_query.shape[0]
    qw, kw = w_query.shape[1], key_projection.shape[1]
    ff = w_gate.shape[2]
    local_experts = EXPERTS // GROUP
    ew = local_experts * ff
    heads = qw // HEAD_SIZE
    kv_heads = kw // HEAD_SIZE
    per = heads // kv_heads
    scale = 1.0 / HEAD_SIZE
    first_core = c.core == 0

    def join_rows(own, other):
        return jnp.where(
            first_core, jnp.concatenate([own, other], 0), jnp.concatenate([other, own], 0)
        )

    def my_half(v):
        return lax.dynamic_slice_in_dim(v, c.core * half, half, 0)

    live_row = valid[0]
    live_count = jnp.sum(live_row).astype(f32)
    misc = jnp.concatenate(
        [
            w_router,
            attn_gain[:, None],
            moe_gain[:, None],
            jnp.broadcast_to(live_count.astype(bf16), (rows, 1)),
            jnp.zeros((rows, MISC - EXPERTS - 3), bf16),
        ],
        1,
    )
    front = jnp.concatenate([w_query, key_projection, value_projection, misc], 1)
    inputs_low = join_rows(tokens, c.other(tokens))

    def gather_attention(v):
        z = c.stack_group(c.gather_group(v))
        mid = z.shape[2] // 2
        return jnp.concatenate(
            [c.gather_reps(z[:, :, :mid], False), c.gather_reps(z[:, :, mid:], True)], 1
        )

    front_w = gather_attention(front)
    out_w = gather_attention(w_out)
    ids_half = my_half(expert_ids)
    ids_group = jnp.concatenate(c.gather_group(ids_half), 0)

    gate_up = jnp.concatenate(
        [w_gate.reshape(rows, GROUP, ew), w_up.reshape(rows, GROUP, ew)], 2
    ).transpose(1, 0, 2)
    gate_up_z = c.stack_group(c.all_to_group(gate_up))
    down_z = c.stack_group(c.all_to_group(w_down.reshape(rows, GROUP, ew).transpose(1, 0, 2)))
    gate_w = c.gather_reps(gate_up_z[:, :, :ew], False)
    up_w = c.gather_reps(gate_up_z[:, :, ew:], True)
    down_w = jnp.concatenate(
        [
            c.gather_reps(down_z[:, :, : ew // 2], False),
            c.gather_reps(down_z[:, :, ew // 2 :], True),
        ],
        1,
    )
    gate_ws = (gate_w, c.other(gate_w))
    up_ws = (up_w, c.other(up_w))
    down_ws = (down_w, c.other(down_w))

    pw = qw + 2 * kw
    proj_w = front_w[:, :pw]
    router_w = front_w[:, pw : pw + EXPERTS]
    gain_one = front_w[:, pw + EXPERTS].astype(f32)[None, :]
    gain_two = front_w[:, pw + EXPERTS + 1].astype(f32)[None, :]
    counts = front_w[:, pw + EXPERTS + 2].astype(f32).reshape(c.n, rows)[:, 0]
    live_total = jnp.sum(counts)

    inputs = inputs_low.astype(f32)
    inv_one = lax.rsqrt(jnp.mean(inputs * inputs, -1, keepdims=True) + epsilon)
    normed_one = inputs * inv_one
    attention_hidden = (normed_one * gain_one).astype(bf16)
    cosine, sine = rope_tables(seq_len, qw + kw)
    qkv = dot(attention_hidden, proj_w)
    qk_raw = qkv[:, : qw + kw]
    qk = (qk_raw * cosine + swap_halves(qk_raw) * sine).astype(bf16)
    q = qk[:, :qw].reshape(seq_len, kv_heads, per, HEAD_SIZE)
    k = qk[:, qw:].reshape(seq_len, kv_heads, HEAD_SIZE)
    v = qkv[:, qw + kw :].astype(bf16).reshape(seq_len, kv_heads, HEAD_SIZE)
    seg_row = segment_ids[0]
    places = jnp.arange(seq_len)
    allowed = (seg_row[:, None] == seg_row[None, :]) & (places[None, :] <= places[:, None]) & (
        live_row[None, :] > 0
    ) | (places[None, :] == places[:, None])
    scores = jnp.einsum("qkgd,skd->kgqs", q, k, preferred_element_type=f32) * scale
    scores = jnp.where(allowed[None, None], scores, negative)
    top_score = jnp.max(scores, -1, keepdims=True)
    exp_scores = jnp.exp(scores - top_score)
    probs = exp_scores / jnp.sum(exp_scores, -1, keepdims=True)
    probs_low = probs.astype(bf16)
    attn_out = (
        jnp.einsum("kgqs,skd->qkgd", probs_low, v, preferred_element_type=f32)
        .astype(bf16)
        .reshape(seq_len, qw)
    )
    proj_part = dot_t(attn_out, out_w)
    theirs = lax.dynamic_slice_in_dim(proj_part, (1 - c.core) * half, half, 0)
    inputs_half = tokens.astype(f32)
    resid = inputs_half + (my_half(proj_part) + c.other(theirs))
    inv_two = lax.rsqrt(jnp.mean(resid * resid, -1, keepdims=True) + epsilon)
    normed_two = resid * inv_two
    hidden_moe = (normed_two * gain_two).astype(bf16)

    hm = jnp.concatenate(c.gather_group(hidden_moe), 0)
    logits = dot(hm, router_w)
    named = jnp.any(ids_group[:, :, None] == jnp.arange(EXPERTS)[None, None, :], 1)
    masked = jnp.where(named, logits, negative)
    shifted = jnp.where(named, jnp.exp(logits - jnp.max(masked, -1, keepdims=True)), 0.0)
    gates = shifted / jnp.sum(shifted, -1, keepdims=True)
    my_gates = lax.dynamic_slice_in_dim(gates, c.ep * local_experts, local_experts, 1)
    wide = jnp.repeat(my_gates, ff, axis=1)

    kept = []
    mixed = 0.0
    for gw, uw, dw in zip(gate_ws, up_ws, down_ws):
        a = dot(hm, gw)
        b = dot(hm, uw)
        sigma = jax.nn.sigmoid(a)
        h = (a * sigma * b).astype(bf16)
        hs = (h.astype(f32) * wide).astype(bf16)
        mixed = mixed + dot_t(hs, dw)
        kept.append((a, b, h, hs))
    mixed = mixed.reshape(GROUP, half, MODEL_WIDTH)
    mix = mixed[0]
    for j in range(1, GROUP):
        mix = mix + c.swap(mixed[j].astype(bf16), c.reps * j).astype(f32)
    result = resid + mix

    live = my_half(live_row).astype(f32)[:, None]
    differ = result - my_half(teacher).astype(f32)
    err_cols = jnp.sum(live * differ * differ, 0)
    grad_out = seq_len * c.n / live_total * live * differ
    go = jnp.concatenate(c.gather_group(grad_out.astype(bf16)), 0)

    grad_hm = 0.0
    grad_gates = 0.0
    low = []
    for (a, b, h, hs), gw, uw, dw in zip(kept, gate_ws, up_ws, down_ws):
        u = dot(go, dw)
        grad_gates = grad_gates + jnp.sum(
            (h.astype(f32) * u).reshape(GROUP * half, local_experts, ff), -1
        )
        gh = u * wide
        sigma = jax.nn.sigmoid(a)
        ga = (gh * b * sigma * (1.0 + a * (1.0 - sigma))).astype(bf16)
        gb = (gh * a * sigma).astype(bf16)
        grad_hm = grad_hm + dot_t(ga, gw) + dot_t(gb, uw)
        low.append((ga, gb))
    gg = jnp.zeros((GROUP * half, MISC), f32)
    gg = lax.dynamic_update_slice_in_dim(gg, grad_gates, c.ep * local_experts, 1)
    back = jnp.concatenate([grad_hm, gg], 1).reshape(GROUP, half, MODEL_WIDTH + MISC)
    back_sum = back[0]
    for j in range(1, GROUP):
        back_sum = back_sum + c.swap(back[j].astype(bf16), c.reps * j).astype(f32)

    weight_sums = []
    for own, other in (
        ((hm, low[0][0]), (hm, low[1][0])),
        ((hm, low[0][1]), (hm, low[1][1])),
        ((go, kept[0][3]), (go, kept[1][3])),
    ):
        away = dot_o(*other).astype(bf16)
        weight_sums.append(dot_o(*own) + c.other(away).astype(f32))
    gate_s = c.scatter_reps(weight_sums[0], False)
    up_s = c.scatter_reps(weight_sums[1], True)
    down_s = jnp.concatenate(
        [
            c.scatter_reps(weight_sums[2][:, : ew // 2], False),
            c.scatter_reps(weight_sums[2][:, ew // 2 :], True),
        ],
        2,
    )
    sums = jnp.concatenate([gate_s, up_s, down_s], 2)
    sums_low = sums.astype(bf16)
    parts = [c.block(sums, 0)] + [
        c.swap(c.block(sums_low, k), c.reps * k).astype(f32) for k in range(1, GROUP)
    ]
    finished = c.stack_group(parts)

    def expert_grad(j):
        g = finished[:, :, j * ew : (j + 1) * ew].transpose(1, 0, 2)
        return g.reshape(rows, EXPERTS, ff)

    grad_probs = back_sum[:, MODEL_WIDTH : MODEL_WIDTH + EXPERTS]
    gate_probs = gates[:half]
    grad_logits = (
        gate_probs * (grad_probs - jnp.sum(gate_probs * grad_probs, -1, keepdims=True))
    ).astype(bf16)
    grad_hidden = back_sum[:, :MODEL_WIDTH] + dot_t(grad_logits, router_w)
    router_part = dot_o(hidden_moe, grad_logits)
    gain_two_part = jnp.sum(grad_hidden * normed_two, 0)
    scaled_two = grad_hidden * gain_two
    grad_resid = grad_out + inv_two * (
        scaled_two - normed_two * jnp.mean(scaled_two * normed_two, -1, keepdims=True)
    )
    gy_half = grad_resid.astype(bf16)
    gy = join_rows(gy_half, c.other(gy_half))

    out_part = dot_o(gy, attn_out)
    grad_attn = dot(gy, out_w).astype(bf16).reshape(seq_len, kv_heads, per, HEAD_SIZE)
    gp = jnp.einsum("qkgd,skd->kgqs", grad_attn, v, preferred_element_type=f32)
    gs = (probs * (gp - jnp.sum(probs * gp, -1, keepdims=True))).astype(bf16)
    gq = jnp.einsum("kgqs,skd->qkgd", gs, k, preferred_element_type=f32) * scale
    gk = jnp.einsum("kgqs,qkgd->skd", gs, q, preferred_element_type=f32) * scale
    gv = jnp.einsum("kgqs,qkgd->skd", probs_low, grad_attn, preferred_element_type=f32)
    gqk = jnp.concatenate([gq.reshape(seq_len, qw), gk.reshape(seq_len, kw)], 1)
    gqk = gqk * cosine - swap_halves(gqk) * sine
    gqkv = jnp.concatenate([gqk.astype(bf16), gv.astype(bf16).reshape(seq_len, kw)], 1)
    ghn_part = dot_t(gqkv, proj_w)
    ghn_low = ghn_part.astype(bf16)
    ghn = my_half(ghn_part) + c.other(
        lax.dynamic_slice_in_dim(ghn_low, (1 - c.core) * half, half, 0)
    ).astype(f32)
    proj_part_grad = dot_o(attention_hidden, gqkv)
    normed_half = my_half(normed_one)
    gain_one_part = jnp.sum(ghn * normed_half, 0)
    scaled_one = ghn * gain_one
    grad_input = grad_resid + my_half(inv_one) * (
        scaled_one - normed_half * jnp.mean(scaled_one * normed_half, -1, keepdims=True)
    )

    err_rows = jnp.sum(err_cols.reshape(MODEL_WIDTH // rows, rows), 0)
    misc_part = jnp.concatenate(
        [
            router_part,
            gain_one_part[:, None],
            gain_two_part[:, None],
            jnp.tile(err_rows, c.n)[:, None],
            jnp.zeros((MODEL_WIDTH, MISC - EXPERTS - 3), f32),
        ],
        1,
    )
    back_w = jnp.concatenate([proj_part_grad, out_part, misc_part], 1)
    mid = (back_w.shape[1] // 256) * 128
    attn_s = jnp.concatenate(
        [c.scatter_reps(back_w[:, :mid], False), c.scatter_reps(back_w[:, mid:], True)], 2
    )
    attn_low = attn_s.astype(bf16)
    own_w = c.block(attn_s, 0)
    for k_ in range(1, GROUP):
        own_w = own_w + c.swap(c.block(attn_low, k_), c.reps * k_).astype(f32)
    misc_own = own_w[:, pw + qw :]
    misc_own = misc_own + c.other(misc_own)
    loss = jnp.sum(misc_own[:, EXPERTS + 2]) / (2.0 * MODEL_WIDTH * live_total)

    return (
        loss,
        result.astype(bf16),
        grad_input.astype(bf16),
        misc_own[:, EXPERTS],
        own_w[:, :qw],
        own_w[:, qw : qw + kw],
        own_w[:, qw + kw : pw],
        own_w[:, pw : pw + qw],
        misc_own[:, EXPERTS + 1],
        misc_own[:, :EXPERTS],
        expert_grad(0),
        expert_grad(1),
        expert_grad(2),
    )


def solution(mesh):
    placed = (
        P(("dp", "tensor"), None),
        P("dp", None),
        P("dp", None),
        P("dp", None),
        P("dp", None),
        P("dp"),
        P("dp", "tensor"),
        P("dp", "tensor"),
        P("dp", "tensor"),
        P("dp", "tensor"),
        P("dp"),
        P("dp", None),
        P("dp", None, "tensor"),
        P("dp", None, "tensor"),
        P("dp", None, "tensor"),
    )
    return jax.shard_map(
        shards,
        mesh=mesh,
        in_specs=placed,
        out_specs=(
            P(),
            P(("dp", "tensor"), None),
            P(("dp", "tensor"), None),
            P("dp"),
            P("dp", "tensor"),
            P("dp", "tensor"),
            P("dp", "tensor"),
            P("dp", "tensor"),
            P("dp"),
            P("dp", None),
            P("dp", None, "tensor"),
            P("dp", None, "tensor"),
            P("dp", None, "tensor"),
        ),
        check_vma=False,
    )
```

```python
import jax
import jax.numpy as jnp
from jax import lax
from jax.experimental import pallas as pl
from jax.experimental.pallas import tpu as pltpu
from jax.sharding import PartitionSpec as P

MODEL_WIDTH = 1024
HEAD_SIZE = 64
TOPK = 8
EXPERTS = 16
GROUP = 4
MISC = 128
DIRECT = False
EARLY = False
ORDER = {'e2': ('fax', 'fay'), 'fad': ('fbx', 'fby', 'fax', 'fay'), 'xax': ('fad', 'fbd', 'z3'), 'xay': ('fad', 'fbd'), 'xad': ('xbx', 'fby'), 'ht0': ('y', 'norm'), 'second': ('dwgu', 'dwdn', 'gurelay'), 'dny': ('b1', 'gt3', 'gux', 'guy'), 'adw': ('gux2', 'guy2', 'dnx', 'dny', 'abwd'), 'ug': ('ax', 'ay', 'arelay'), 'uu': ('ax', 'ay', 'arelay'), 'abwd': ('b1', 'dnx', 'dny'), 'ht1': ('y', 'norm'), 'b2': ('efwd', 'mt', 'gt2'), 'm1': ('h1', 'h2', 'h3'), 'ad': ('first',), 'm2': ('xbx', 'xby', 'h1'), 'guown': ('gy', 'gux2', 'guy2'), 'dnz1': ('ax', 'guz1', 'guz2', 'guz3', 'ay'), 'dnz2': ('ax',), 'dnz3': ('ax', 'ay'), 'dwdn': ('g1',), 'az1': ('aown',), 'az2': ('aown',), 'gy': ('b1', 'b2', 'b3', 'ebwd'), 'ht2': ('attn', 'xbx'), 'ht3': ('attn', 'xbx', 'xay'), 'g3': ('h2',), 'guz3': ('guz1', 'guz2'), 'first': ('gurelay',), 'gux': ('gt2',), 'guy': ('g1', 'g2'), 'b1': ('mt', 'gt1', 'gt2'), 'b3': ('mt', 'gt2'), 'gurelay': ('g2', 'gt0'), 'norm': ('xbx', 'xby'), 'dnx': ('gux', 'guy'), 'ax': ('second',), 'ay': ('second',), 'ghn': ('gux2', 'guy2')}
VMEM_BYTES = 60 << 20

epsilon = 1e-06
negative = -1e30
rope_base = 10000.0
f32 = jnp.float32
bf16 = jnp.bfloat16

INNER = (((1,), (1,)), ((), ()))
OUTER = (((0,), (0,)), ((), ()))


def dot(a, b):
    return jnp.dot(a, b, preferred_element_type=f32)


def dot_t(a, b):
    return lax.dot_general(a, b, INNER, preferred_element_type=f32)


def dot_o(a, b):
    return lax.dot_general(a, b, OUTER, preferred_element_type=f32)


def tie(v, *after):
    return lax.optimization_barrier((v, after))[0]


def rope_tables(length, width):
    half = HEAD_SIZE // 2
    places = jnp.arange(length).astype(f32)
    freqs = rope_base ** (-2.0 * jnp.arange(half).astype(f32) / HEAD_SIZE)
    angles = places[:, None] * freqs[None, :]
    cosine, sine = jnp.cos(angles), jnp.sin(angles)
    reps = width // HEAD_SIZE
    return (
        jnp.tile(jnp.concatenate([cosine, cosine], 1), (1, reps)),
        jnp.tile(jnp.concatenate([-sine, sine], 1), (1, reps)),
    )


def swap_halves(u):
    half = HEAD_SIZE // 2
    low = (jnp.arange(u.shape[1]) % HEAD_SIZE) < half
    return jnp.where(low[None, :], jnp.roll(u, -half, 1), jnp.roll(u, half, 1))


class Comm:
    def __init__(self):
        self.n = lax.axis_size("dp")
        self.me = lax.axis_index("dp")
        self.core = lax.axis_index("tensor")
        self.reps = self.n // GROUP
        self.ep = self.me // self.reps
        self.rep = self.me % self.reps
        self.bits = [1 << k for k in range(self.reps.bit_length() - 1)]

    def swap(self, v, mask):
        return lax.ppermute(v, "dp", [(i, i ^ mask) for i in range(self.n)])

    def other(self, v):
        return lax.ppermute(v, "tensor", [(0, 1), (1, 0)])

    def bit(self, b):
        return (self.rep // b) % 2

    def gather_reps(self, z, last_first):
        rows, cols = z.shape[1:]
        k = len(self.bits)
        out = jnp.zeros((GROUP,) + (2,) * k + (rows, cols), z.dtype)
        zero = jnp.int32(0)
        order = list(self.bits)
        if last_first:
            order = order[::-1]
        done = set()

        def place(block, flipped):
            start = [zero]
            for b in reversed(self.bits):
                if b in done:
                    start.append(zero)
                elif b == flipped:
                    start.append(1 - self.bit(b))
                else:
                    start.append(self.bit(b))
            return start + [zero, zero]

        cur = z.reshape((GROUP,) + (1,) * k + (rows, cols))
        out = lax.dynamic_update_slice(out, cur, place(cur, None))
        for b in order:
            got = self.swap(cur, b)
            out = lax.dynamic_update_slice(out, got, place(got, b))
            done.add(b)
            if len(done) < k:
                start = place(out, None)
                shape = [GROUP] + [2 if c in done else 1 for c in reversed(self.bits)]
                cur = lax.dynamic_slice(out, start, shape + [rows, cols])
        return out.reshape(GROUP * self.reps * rows, cols)

    def stack_group(self, parts, axis=0):
        parts = jnp.stack(parts, 0)
        idx = self.ep ^ jnp.arange(GROUP)
        return jnp.concatenate(
            [lax.dynamic_index_in_dim(parts, idx[j], 0, keepdims=True) for j in range(GROUP)], 0
        )

    def gather_group(self, v):
        return [v] + [self.swap(v, self.reps * k) for k in range(1, GROUP)]

    def block(self, v, k):
        return lax.dynamic_index_in_dim(v, self.ep ^ k, 0, keepdims=False)

    def all_to_group(self, v):
        return [self.block(v, 0)] + [
            self.swap(self.block(v, k), self.reps * k) for k in range(1, GROUP)
        ]

    def scatter_reps(self, s, last_first):
        cols = s.shape[1]
        k = len(self.bits)
        rows = s.shape[0] // (GROUP * self.reps)
        s = s.reshape((GROUP,) + (2,) * k + (rows, cols))
        order = list(self.bits)
        if last_first:
            order = order[::-1]
        for b in order:
            axis = 1 + list(reversed(self.bits)).index(b)
            mine = self.bit(b)
            send = lax.dynamic_slice_in_dim(s, 1 - mine, 1, axis).astype(bf16)
            keep = lax.dynamic_slice_in_dim(s, mine, 1, axis)
            s = keep + self.swap(send, b).astype(f32)
        return s.reshape(GROUP, rows, cols)


VM = pltpu.VMEM


def vmem():
    return pl.BlockSpec(memory_space=pltpu.VMEM)


def anym():
    return pl.BlockSpec(memory_space=pltpu.HBM)


def smem():
    return pl.BlockSpec(memory_space=pltpu.SMEM)


def sds(shape, dtype):
    return jax.ShapeDtypeStruct(shape, dtype)


def kernel_call(body, out_shape, in_specs, name, scratch=()):
    return pl.pallas_call(
        body,
        out_shape=out_shape,
        in_specs=in_specs,
        out_specs=jax.tree.map(lambda _: vmem(), out_shape),
        scratch_shapes=list(scratch),
        compiler_params=pltpu.CompilerParams(vmem_limit_bytes=VMEM_BYTES),
        name=name,
    )


def piece_copies(pieces, dst, sem, ep, rep, cols=None, first=0):
    copies = []
    for j, piece in enumerate(pieces):
        m, h = j // 2, j % 2
        for i in range(2):
            at = (ep ^ (2 * h + i)) * 4 + (rep ^ m)
            src, to = piece.at[pl.ds(64 * i, 64)], dst.at[at]
            if cols is not None:
                src, to = src.at[:, pl.ds(*cols)], to.at[:, pl.ds(*cols)]
            copies.append(pltpu.make_async_copy(src, to, sem.at[first + 2 * j + i]))
    return copies


NAMED = 32


def pack_front_body(wq, wk, wv, wo, wr, g1, g2, valid, ids, out):
    qw, kw = wq.shape[1], wk.shape[1]
    pw = qw + 2 * kw
    n = wq.shape[0]
    out[:, 0:qw] = wq[...]
    out[:, qw : qw + kw] = wk[...]
    out[:, qw + kw : pw] = wv[...]
    out[:, pw + MISC :] = wo[...]
    count = jnp.sum(valid[...].astype(f32), axis=1, keepdims=True)
    expert = lax.broadcasted_iota(jnp.int32, (EXPERTS, ids.shape[1]), 0)
    named = jnp.zeros(expert.shape, f32)
    for k in range(TOPK):
        named = jnp.where(ids[k : k + 1, :] == expert, 1.0, named)
    quarters = [named[:, n * j : n * (j + 1)] for j in range(ids.shape[1] // n)]
    top = jnp.concatenate([wr[...].astype(f32), jnp.zeros((NAMED - EXPERTS, n), f32)], 0)
    row = lax.broadcasted_iota(jnp.int32, top.shape, 0)
    top = jnp.where(row == EXPERTS, g1[...].astype(f32), top)
    top = jnp.where(row == EXPERTS + 1, g2[...].astype(f32), top)
    top = jnp.where(row == EXPERTS + 2, count, top)
    rest = jnp.zeros((MISC - NAMED - EXPERTS * len(quarters), n), f32)
    base = jnp.concatenate([top, *quarters, rest], 0)
    eye = lax.broadcasted_iota(jnp.int32, (n, n), 0) == lax.broadcasted_iota(jnp.int32, (n, n), 1)
    misc = dot_t(eye.astype(f32).astype(bf16), base.astype(bf16))
    out[:, pw : pw + MISC] = misc.astype(bf16)


def pack_front(wq, wk, wv, wo, wr, g1, g2, valid, ids):
    n = wq.shape[0]
    width = wq.shape[1] + 2 * wk.shape[1] + MISC + wo.shape[1]
    return kernel_call(pack_front_body, sds((n, width), bf16), [vmem()] * 9, "pack_front")(
        wq, wk, wv, wo, wr.T, g1[None, :], g2[None, :], valid, ids.T
    )


def pack_experts_body(sc, wg, wu, wd, out0, out1, out2, out3, wide):
    ep = sc[0]
    n, e, f = wg.shape
    per = e // GROUP
    for j, w in enumerate((wg, wu, wd)):
        for l in range(f // 128):
            wide[l] = w[:, :, 128 * l : 128 * (l + 1)].astype(f32).reshape(n * e, 128)
        for k, out in enumerate((out0, out1, out2, out3)):
            for x in range(per):
                for l in range(f // 128):
                    at = j * per * f + x * f + 128 * l
                    out[:, at : at + 128] = wide[
                        l, pl.ds((ep ^ k) * per + x, n, stride=e), :
                    ].astype(bf16)


def pack_experts(sc, wg, wu, wd):
    n, e, f = wg.shape
    return kernel_call(
        pack_experts_body,
        (sds((n, 3 * e * f // GROUP), bf16),) * GROUP,
        [smem()] + [vmem()] * 3,
        "pack_experts",
        [VM((f // 128, n * e, 128), f32)],
    )(sc, wg, wu, wd)


def rotate_pairs(u, cosine, sine):
    lane = lax.broadcasted_iota(jnp.int32, u.shape, 1)
    low = lane % HEAD_SIZE < HEAD_SIZE // 2
    turned = jnp.where(low, pltpu.roll(u, 96, 1), pltpu.roll(u, 32, 1))
    return u * cosine + turned * sine


def both_lanes(pair, odd):
    lane = lax.broadcasted_iota(jnp.int32, pair.shape, 1)
    other = pltpu.roll(pair, 64, 1)
    first = lane < HEAD_SIZE
    return jnp.where(first, other, pair) if odd else jnp.where(first, pair, other)


def two_heads(pair):
    lane = lax.broadcasted_iota(jnp.int32, pair.shape, 1)
    zero = jnp.zeros_like(pair)
    return jnp.concatenate(
        [jnp.where(lane < HEAD_SIZE, pair, zero), jnp.where(lane < HEAD_SIZE, zero, pair)], 0
    )


def one_pair(rows):
    n = rows.shape[0] // 2
    lane = lax.broadcasted_iota(jnp.int32, (n, rows.shape[1]), 1)
    return jnp.where(lane < HEAD_SIZE, rows[:n], rows[n:])


def allowed_mask(seg, valid):
    n = seg.shape[1]
    r = lax.broadcasted_iota(jnp.int32, (n, n), 0)
    col = lax.broadcasted_iota(jnp.int32, (n, n), 1)
    seg_row = jnp.broadcast_to(seg.astype(f32), (n, n))
    seg_col = jnp.sum(jnp.where(r == col, seg_row, 0.0), axis=1, keepdims=True)
    live = jnp.broadcast_to(valid.astype(f32), (n, n)) > 0
    return ((seg_col == seg_row) & (col <= r) & live) | (r == col)


def softmax_rows(q2, k2, allowed2):
    s = dot_t(q2, k2) * (1.0 / HEAD_SIZE)
    s = jnp.where(allowed2, s, negative)
    e = jnp.exp(s - jnp.max(s, axis=1, keepdims=True))
    return e / jnp.sum(e, axis=1, keepdims=True)


def attn_fwd_body(sc, x_own, x_oth, seg, valid, cosine, sine, *refs):
    pieces = refs[:8]
    own_out, away_out, hn_out, qkv_out, o_out, misc_out, gains_out, w_out, w, x, sem = refs[8:]
    ep, rep, core = sc[0], sc[1], sc[2]
    copies = piece_copies(pieces, w, sem, ep, rep)
    for cp in copies:
        cp.start()
    half = x_own.shape[0]
    n = 2 * half
    x[pl.ds(core * half, half), :] = x_own[...].astype(f32)
    x[pl.ds((1 - core) * half, half), :] = x_oth[...].astype(f32)
    allowed = allowed_mask(seg[...], valid[...])
    allowed2 = jnp.concatenate([allowed, allowed], 0)
    inputs = x[...]
    normed = inputs * lax.rsqrt(jnp.mean(inputs * inputs, axis=1, keepdims=True) + epsilon)
    for cp in copies:
        cp.wait()
    pw = qkv_out.shape[1]
    misc = w[:, :, pw : pw + MISC].reshape(MODEL_WIDTH, MISC)
    pick = lax.broadcasted_iota(jnp.int32, (8, MISC), 0) + EXPERTS
    pick = (pick == lax.broadcasted_iota(jnp.int32, (8, MISC), 1)).astype(f32).astype(bf16)
    gains = dot_t(pick, misc)
    gains_out[...] = gains
    misc_out[...] = misc
    hn = (normed * gains[0:1, :]).astype(bf16)
    hn_out[...] = hn
    w_out[...] = w[...].reshape(w_out.shape)
    qkv = dot(hn, w[:, :, :pw].reshape(MODEL_WIDTH, pw))
    groups = pw // 128
    kv0 = groups // 2
    for g in range(groups):
        u = qkv[:, 128 * g : 128 * (g + 1)]
        if g < kv0 + kv0 // 2:
            u = rotate_pairs(u, cosine[...], sine[...])
        qkv_out[:, 128 * g : 128 * (g + 1)] = u.astype(bf16)
    for m in range(kv0):
        g = kv0 + m // 2
        k2 = both_lanes(qkv_out[:, 128 * g : 128 * (g + 1)].astype(f32), m % 2).astype(bf16)
        g = g + kv0 // 2
        v2 = both_lanes(qkv_out[:, 128 * g : 128 * (g + 1)].astype(f32), m % 2).astype(bf16)
        q2 = two_heads(qkv_out[:, 128 * m : 128 * (m + 1)].astype(f32)).astype(bf16)
        p = softmax_rows(q2, k2, allowed2).astype(bf16)
        o_out[:, 128 * m : 128 * (m + 1)] = one_pair(dot(p, v2)).astype(bf16)
    wo = w[:, :, pw + MISC :].reshape(MODEL_WIDTH, o_out.shape[1])
    away_out[...] = dot_t(o_out[pl.ds((1 - core) * half, half), :], wo)
    own_out[...] = dot_t(o_out[pl.ds(core * half, half), :], wo)


def attn_fwd(sc, x_own, x_oth, seg, valid, cosine, sine, pieces, qw):
    half = x_own.shape[0]
    n = 2 * half
    cols = pieces[0].shape[1]
    pw = cols - MISC - qw
    return kernel_call(
        attn_fwd_body,
        (
            sds((half, MODEL_WIDTH), f32),
            sds((half, MODEL_WIDTH), f32),
            sds((n, MODEL_WIDTH), bf16),
            sds((n, pw), bf16),
            sds((n, qw), bf16),
            sds((MODEL_WIDTH, MISC), bf16),
            sds((8, MODEL_WIDTH), f32),
            sds((MODEL_WIDTH, cols), bf16),
        ),
        [smem()] + [vmem()] * 6 + [anym()] * 8,
        "attn_fwd",
        [VM((16, 64, cols), bf16), VM((n, MODEL_WIDTH), f32), pltpu.SemaphoreType.DMA((16,))],
    )(sc, x_own, x_oth, seg, valid, cosine, sine, *pieces)


def second_norm_body(x, y_own, y_oth, gains, resid_out, hm_out):
    resid = x[...].astype(f32) + (y_own[...] + y_oth[...])
    resid_out[...] = resid
    inv = lax.rsqrt(jnp.mean(resid * resid, axis=1, keepdims=True) + epsilon)
    hm_out[...] = (resid * inv * gains[1:2, :]).astype(bf16)


def second_norm(x, y_own, y_oth, gains):
    return kernel_call(
        second_norm_body,
        (sds(y_own.shape, f32), sds(y_own.shape, bf16)),
        [vmem()] * 4,
        "second_norm",
    )(x, y_own, y_oth, gains)


def named_rows(block, j):
    moved = pltpu.roll(block.astype(f32), MISC - NAMED - EXPERTS * j, 1)
    lane = lax.broadcasted_iota(jnp.int32, moved.shape, 1)
    return (moved > 0.5) & (lane < EXPERTS)


def gates_of(hm, misc, named):
    logits = dot(hm, misc)
    top = jnp.max(jnp.where(named, logits, negative), axis=1, keepdims=True)
    e = jnp.where(named, jnp.exp(logits - top), 0.0)
    return e / jnp.sum(e, axis=1, keepdims=True)


def expert_fwd_body(sc, misc, *refs):
    chunks, pieces = refs[:8], refs[8:16]
    own_out, away_out, a_out, b_out, gates_out, w, hm, acc, sem = refs[16:]
    ep, rep, core = sc[0], sc[1], sc[2]
    half = chunks[0].shape[0]
    experts = EXPERTS // GROUP
    ew = w.shape[2] // 3
    ff = ew // experts
    wide = piece_copies(pieces, w, sem, ep, rep, (0, 2 * ew), 0)
    down = piece_copies(pieces, w, sem, ep, rep, (2 * ew, ew), 16)
    for cp in wide:
        cp.start()
    for cp in down:
        cp.start()
    for j, chunk in enumerate(chunks):
        hm[pl.ds(j * half, half), :] = chunk[...]
        k = j % GROUP
        at = pl.multiple_of(((ep ^ k) * 4 + rep) * 64, 64)
        block = misc[pl.ds(at, 64), :]
        mine = core == (0 if j < GROUP else 1)
        quarters = [named_rows(block, q) for q in range(4)]
        first = jnp.concatenate([q.astype(f32) for q in quarters[:2]], 0)
        second = jnp.concatenate([q.astype(f32) for q in quarters[2:]], 0)
        named = jnp.where(mine, first, second) > 0.5
        gates_out[pl.ds(j * half, half), :] = gates_of(chunk[...], misc[...], named)
    acc[...] = jnp.zeros_like(acc)
    lane = lax.broadcasted_iota(jnp.int32, gates_out.shape, 1)
    for cp in wide:
        cp.wait()
    for cp in down:
        cp.wait()

    def tile(e, carry):
        rows = hm[...]
        at = pl.multiple_of(e * ff, ff)
        a = dot(rows, w[:, :, pl.ds(at, ff)].reshape(MODEL_WIDTH, ff))
        b = dot(rows, w[:, :, pl.ds(ew + at, ff)].reshape(MODEL_WIDTH, ff))
        g = jnp.sum(
            jnp.where(lane == ep * experts + e, gates_out[...], 0.0), axis=1, keepdims=True
        )
        h = (a * jax.nn.sigmoid(a) * b).astype(bf16)
        hs = (h.astype(f32) * g).astype(bf16)
        a_out[:, pl.ds(at, ff)] = a
        b_out[:, pl.ds(at, ff)] = b
        acc[...] += dot_t(hs, w[:, :, pl.ds(2 * ew + at, ff)].reshape(MODEL_WIDTH, ff))
        return carry

    lax.fori_loop(0, experts, tile, 0)
    own_out[...] = acc[: GROUP * half, :]
    away_out[...] = acc[GROUP * half :, :].astype(bf16)


def expert_fwd(sc, misc, chunks, pieces):
    half = chunks[0].shape[0]
    cols = pieces[0].shape[1]
    ew = cols // 3
    rows = GROUP * half
    return kernel_call(
        expert_fwd_body,
        (
            sds((rows, MODEL_WIDTH), f32),
            sds((rows, MODEL_WIDTH), bf16),
            sds((2 * rows, ew), f32),
            sds((2 * rows, ew), f32),
            sds((2 * rows, MISC), f32),
        ),
        [smem()] + [vmem()] * 9 + [anym()] * 8,
        "expert_fwd",
        [
            VM((16, 64, cols), bf16),
            VM((2 * rows, MODEL_WIDTH), bf16),
            VM((2 * rows, MODEL_WIDTH), f32),
            pltpu.SemaphoreType.DMA((32,)),
        ],
    )(sc, misc, *chunks, *pieces)


def core_sum_body(own, got, out0, out1, out2, out3):
    half = out0.shape[0]
    for j, out in enumerate((out0, out1, out2, out3)):
        at = pl.ds(j * half, half)
        out[...] = (own[at, :] + got[at, :].astype(f32)).astype(out.dtype)


def core_sum(own, got):
    shape = (own.shape[0] // GROUP, own.shape[1])
    return kernel_call(
        core_sum_body,
        (sds(shape, f32), sds(shape, bf16), sds(shape, bf16), sds(shape, bf16)),
        [vmem()] * 2,
        "core_sum",
    )(own, got)


def expert_bwd_body(sc, gates, a_in, b_in, *refs):
    chunks, pieces = refs[:8], refs[8:16]
    own_out, away_out, ga_out, gb_out, hs_out, w, go, acc, gsum, sem = refs[16:]
    ep, rep = sc[0], sc[1]
    half = chunks[0].shape[0]
    rows = GROUP * half
    experts = EXPERTS // GROUP
    ew = w.shape[2] // 3
    ff = ew // experts
    wide = piece_copies(pieces, w, sem, ep, rep, (0, 2 * ew), 0)
    down = piece_copies(pieces, w, sem, ep, rep, (2 * ew, ew), 16)
    for cp in down:
        cp.start()
    for cp in wide:
        cp.start()
    for j, chunk in enumerate(chunks):
        go[pl.ds(j * half, half), :] = chunk[...]
    acc[...] = jnp.zeros_like(acc)
    gsum[...] = jnp.zeros_like(gsum)
    lane = lax.broadcasted_iota(jnp.int32, gsum.shape, 1)
    for cp in down:
        cp.wait()
    for cp in wide:
        cp.wait()

    def tile(e, carry):
        at = pl.multiple_of(e * ff, ff)
        a = a_in[:, pl.ds(at, ff)]
        b = b_in[:, pl.ds(at, ff)]
        u = dot(go[...], w[:, :, pl.ds(2 * ew + at, ff)].reshape(MODEL_WIDTH, ff))
        mine = lane == ep * experts + e
        g = jnp.sum(jnp.where(mine, gates[...], 0.0), axis=1, keepdims=True)
        s = jax.nn.sigmoid(a)
        silu = a * s
        h = (silu * b).astype(bf16).astype(f32)
        gsum[...] += jnp.where(mine, jnp.sum(h * u, axis=1, keepdims=True), 0.0)
        gh = u * g
        ga = (gh * b * s * (1.0 + a * (1.0 - s))).astype(bf16)
        gb = (gh * silu).astype(bf16)
        ga_out[:, pl.ds(at, ff)] = ga
        gb_out[:, pl.ds(at, ff)] = gb
        hs_out[:, pl.ds(at, ff)] = (h * g).astype(bf16)
        wg = w[:, :, pl.ds(at, ff)].reshape(MODEL_WIDTH, ff)
        wu = w[:, :, pl.ds(ew + at, ff)].reshape(MODEL_WIDTH, ff)
        acc[...] += dot_t(ga, wg) + dot_t(gb, wu)
        return carry

    lax.fori_loop(0, experts, tile, 0)
    own_out[:, :MODEL_WIDTH] = acc[:rows, :]
    own_out[:, MODEL_WIDTH:] = gsum[:rows, :]
    away_out[:, :MODEL_WIDTH] = acc[rows:, :].astype(bf16)
    away_out[:, MODEL_WIDTH:] = gsum[rows:, :].astype(bf16)


def expert_bwd(sc, gates, a, b, chunks, pieces):
    half = chunks[0].shape[0]
    cols = pieces[0].shape[1]
    ew = cols // 3
    rows = GROUP * half
    full = MODEL_WIDTH + MISC
    return kernel_call(
        expert_bwd_body,
        (
            sds((rows, full), f32),
            sds((rows, full), bf16),
            sds((2 * rows, ew), bf16),
            sds((2 * rows, ew), bf16),
            sds((2 * rows, ew), bf16),
        ),
        [smem()] + [vmem()] * 11 + [anym()] * 8,
        "expert_bwd",
        [
            VM((16, 64, cols), bf16),
            VM((2 * rows, MODEL_WIDTH), bf16),
            VM((2 * rows, MODEL_WIDTH), f32),
            VM((2 * rows, MISC), f32),
            pltpu.SemaphoreType.DMA((32,)),
        ],
    )(sc, gates, a, b, *chunks, *pieces)


def loss_body(resid, m0, m1, m2, m3, teacher, live, gains, scale, result_out, g_out, glow_out, err_out):
    mix = m0[...] + (m1[...].astype(f32) + m2[...].astype(f32) + m3[...].astype(f32))
    result = resid[...] + mix
    result_out[...] = result.astype(bf16)
    differ = result - teacher[...].astype(f32)
    rows = gains.shape[1] // scale.shape[1]
    total = jnp.sum(gains[2:3, :], axis=1, keepdims=True) / rows
    weighted = live[...] * differ
    g = (scale.shape[0] * scale.shape[1]) / total * weighted
    g_out[...] = g
    glow_out[...] = g.astype(bf16)
    err_out[...] = jnp.broadcast_to(jnp.sum(weighted * differ, axis=0, keepdims=True), err_out.shape)


def loss_grad(resid, mixes, teacher, live, gains, seq_len, n):
    shape = resid.shape
    return kernel_call(
        loss_body,
        (sds(shape, bf16), sds(shape, f32), sds(shape, bf16), sds((8, shape[1]), f32)),
        [vmem()] * 9,
        "loss_grad",
    )(resid, *mixes, teacher, live, gains, jnp.zeros((seq_len, n), f32))


def second_back_body(b0, b1, b2, b3, gates, misc, hm, resid, gains, g_out, gy_out, gres_out, rows_out):
    half = resid.shape[0]
    total = b0[...] + (b1[...].astype(f32) + b2[...].astype(f32) + b3[...].astype(f32))
    gp = total[:, MODEL_WIDTH:]
    gate = gates[0:half, :]
    gl = (gate * (gp - jnp.sum(gate * gp, axis=1, keepdims=True))).astype(bf16)
    ghm = total[:, :MODEL_WIDTH] + dot_t(gl, misc[...])
    x = resid[...]
    inv = lax.rsqrt(jnp.mean(x * x, axis=1, keepdims=True) + epsilon)
    normed = x * inv
    rows = dot_o(gl, hm[...])
    gain_row = jnp.sum(ghm * normed, axis=0, keepdims=True)
    at = lax.broadcasted_iota(jnp.int32, rows.shape, 0)
    rows_out[...] = jnp.where(at == EXPERTS + 1, gain_row, rows)
    scaled = ghm * gains[1:2, :]
    gres = g_out[...] + inv * (
        scaled - normed * jnp.mean(scaled * normed, axis=1, keepdims=True)
    )
    gres_out[...] = gres
    gy_out[...] = gres.astype(bf16)


def second_back(backs, gates, misc, hm, resid, gains, g_out):
    shape = resid.shape
    return kernel_call(
        second_back_body,
        (sds(shape, bf16), sds(shape, f32), sds((MISC, shape[1]), f32)),
        [vmem()] * 10,
        "second_back",
    )(*backs, gates, misc, hm, resid, gains, g_out)


def attn_bwd_body(
    sc, gy_own, gy_oth, o, qkv, seg, valid, cosine, sine, w, gqkv_out, gy_out, own_out, away_out, low
):
    core = sc[2]
    half = gy_own.shape[0]
    n = 2 * half
    gy_out[pl.ds(core * half, half), :] = gy_own[...]
    gy_out[pl.ds((1 - core) * half, half), :] = gy_oth[...]
    pw = qkv.shape[1]
    low[...] = dot(gy_out[...], w[:, pw + MISC :]).astype(bf16)
    allowed = allowed_mask(seg[...], valid[...])
    allowed2 = jnp.concatenate([allowed, allowed], 0)
    kv0 = pw // 256
    lane = lax.broadcasted_iota(jnp.int32, (n, 128), 1)
    scale = 1.0 / HEAD_SIZE
    held = {}
    for m in range(kv0):
        gk_at = kv0 + m // 2
        gv_at = gk_at + kv0 // 2
        k2 = both_lanes(qkv[:, 128 * gk_at : 128 * (gk_at + 1)].astype(f32), m % 2).astype(bf16)
        v2 = both_lanes(qkv[:, 128 * gv_at : 128 * (gv_at + 1)].astype(f32), m % 2).astype(bf16)
        q2 = two_heads(qkv[:, 128 * m : 128 * (m + 1)].astype(f32)).astype(bf16)
        go2 = two_heads(low[:, 128 * m : 128 * (m + 1)].astype(f32)).astype(bf16)
        p = softmax_rows(q2, k2, allowed2)
        gp = dot_t(go2, v2)
        gs = (p * (gp - jnp.sum(p * gp, axis=1, keepdims=True))).astype(bf16)
        gq = one_pair(dot(gs, k2)) * scale
        gqkv_out[:, 128 * m : 128 * (m + 1)] = rotate_pairs(gq, cosine[...], -sine[...]).astype(bf16)
        gk = dot_o(gs, q2) * scale
        gv = dot_o(p.astype(bf16), go2)
        gk = gk + pltpu.roll(gk, 64, 1)
        gv = gv + pltpu.roll(gv, 64, 1)
        if m % 2 == 0:
            held = {"k": gk, "v": gv}
        else:
            gk = jnp.where(lane < HEAD_SIZE, held["k"], gk)
            gv = jnp.where(lane < HEAD_SIZE, held["v"], gv)
            gqkv_out[:, 128 * gk_at : 128 * (gk_at + 1)] = rotate_pairs(
                gk, cosine[...], -sine[...]
            ).astype(bf16)
            gqkv_out[:, 128 * gv_at : 128 * (gv_at + 1)] = gv.astype(bf16)
    away_out[...] = dot_t(gqkv_out[pl.ds((1 - core) * half, half), :], w[:, :pw]).astype(bf16)
    own_out[...] = dot_t(gqkv_out[pl.ds(core * half, half), :], w[:, :pw])


def attn_bwd(sc, gy_own, gy_oth, o, qkv, seg, valid, cosine, sine, w):
    half = gy_own.shape[0]
    n = 2 * half
    pw = qkv.shape[1]
    return kernel_call(
        attn_bwd_body,
        (
            sds((n, pw), bf16),
            sds((n, MODEL_WIDTH), bf16),
            sds((half, MODEL_WIDTH), f32),
            sds((half, MODEL_WIDTH), bf16),
        ),
        [smem()] + [vmem()] * 9,
        "attn_bwd",
        [VM((n, o.shape[1]), bf16)],
    )(sc, gy_own, gy_oth, o, qkv, seg, valid, cosine, sine, w)


def first_back_body(g_own, g_oth, x, gains, gres, rows, err, ginput_out, rows_out):
    ghn = g_own[...] + g_oth[...].astype(f32)
    inputs = x[...].astype(f32)
    inv = lax.rsqrt(jnp.mean(inputs * inputs, axis=1, keepdims=True) + epsilon)
    normed = inputs * inv
    gain_row = jnp.sum(ghn * normed, axis=0, keepdims=True)
    scaled = ghn * gains[0:1, :]
    ginput_out[...] = (
        gres[...] + inv * (scaled - normed * jnp.mean(scaled * normed, axis=1, keepdims=True))
    ).astype(bf16)
    e = err[...]
    for shift in (64, 128, 256, 512):
        e = e + pltpu.roll(e, shift, 1)
    at = lax.broadcasted_iota(jnp.int32, rows.shape, 0)
    r = jnp.where(at == EXPERTS, gain_row, rows[...])
    rows_out[...] = jnp.where(at == EXPERTS + 2, e[0:1, :], r)


def first_back(g_own, g_oth, x, gains, gres, rows, err):
    return kernel_call(
        first_back_body,
        (sds(gres.shape, bf16), sds(rows.shape, f32)),
        [vmem()] * 7,
        "first_back",
    )(g_own, g_oth, x, gains, gres, rows, err)


SEND_X = (12, 13, 4, 5)
SEND_Y = (14, 15, 10, 11)
KEPT = (0, 1, 2, 3, 6, 7, 8, 9)


def store_relative(out, ep, rep, value, cols):
    for j in range(16):
        to = 4 * ((j % 4) ^ rep) + ((j // 4) ^ ep)
        out[to, :, cols] = value[64 * j : 64 * (j + 1), :]


def split_relative(full, x_out, y_out, kept_out):
    for j, at in enumerate(SEND_X):
        x_out[j] = full[at].astype(bf16)
    for j, at in enumerate(SEND_Y):
        y_out[j] = full[at].astype(bf16)
    for j, at in enumerate(KEPT):
        kept_out[j] = full[at]


def attn_dw_body(sc, gy, o, hn, gqkv, rows, x_out, y_out, kept_out, full):
    ep, rep = sc[0], sc[1]
    pw = gqkv.shape[1]
    qw = o.shape[1]
    store_relative(full, ep, rep, dot_o(hn[...], gqkv[...]), slice(0, pw))
    store_relative(full, ep, rep, dot_o(gy[...], o[...]), slice(pw, pw + qw))
    store_relative(full, ep, rep, jnp.transpose(rows[...]), slice(pw + qw, pw + qw + MISC))
    split_relative(full, x_out, y_out, kept_out)


def attn_dw(sc, gy, o, hn, gqkv, rows):
    width = gqkv.shape[1] + o.shape[1] + MISC
    return kernel_call(
        attn_dw_body,
        (sds((4, 64, width), bf16), sds((4, 64, width), bf16), sds((8, 64, width), f32)),
        [smem()] + [vmem()] * 5,
        "attn_dw",
        [VM((16, 64, width), f32)],
    )(sc, gy, o, hn, gqkv, rows)


def attn_dw3_body(sc, gy, o, hn, gqkv, rows, own_out, x_out, y_out, d_out, full):
    ep, rep = sc[0], sc[1]
    pw = gqkv.shape[1]
    qw = o.shape[1]
    store_relative(full, ep, rep, dot_o(hn[...], gqkv[...]), slice(0, pw))
    store_relative(full, ep, rep, dot_o(gy[...], o[...]), slice(pw, pw + qw))
    store_relative(full, ep, rep, jnp.transpose(rows[...]), slice(pw + qw, pw + qw + MISC))
    own_out[...] = full[0:4]
    for m, out in enumerate((x_out, y_out, d_out)):
        out[...] = full[4 * m + 4 : 4 * m + 8].astype(bf16)


def attn_dw3(sc, gy, o, hn, gqkv, rows):
    width = gqkv.shape[1] + o.shape[1] + MISC
    low = sds((4, 64, width), bf16)
    return kernel_call(
        attn_dw3_body,
        (sds((4, 64, width), f32), low, low, low),
        [smem()] + [vmem()] * 5,
        "attn_dw3",
        [VM((16, 64, width), f32)],
    )(sc, gy, o, hn, gqkv, rows)


def attn_sum3_body(own, x, y, d, *outs):
    for k, out in enumerate(outs):
        total = own[k] + (x[k].astype(f32) + y[k].astype(f32) + d[k].astype(f32))
        out[...] = total.astype(out.dtype)


def attn_sum3(own, x, y, d):
    shape = own.shape[1:]
    low = sds(shape, bf16)
    return kernel_call(
        attn_sum3_body, (sds(shape, f32), low, low, low), [vmem()] * 4, "attn_sum3"
    )(own, x, y, d)


def expert_dw_body(sc, *refs):
    n = len(refs) - 13
    chunks, ys = refs[:8], refs[8 : 8 + n]
    x_out, y_out, kept_out, xt, full = refs[8 + n :]
    ep, rep = sc[0], sc[1]
    half = chunks[0].shape[0]

    @pl.when(pl.program_id(0) == 0)
    def _():
        for j, x in enumerate(chunks):
            xt[:, j * half : (j + 1) * half] = jnp.transpose(x[...])

    for j, y in enumerate(ys):

        @pl.when(pl.program_id(0) // 4 == j)
        def _():
            store_relative(full, ep, rep, dot(xt[...], y[...]), slice(None))

    split_relative(full, x_out, y_out, kept_out)


def expert_dw(sc, chunks, ys):
    half = chunks[0].shape[0]
    tile = ys[0].shape[1] // 4
    steps = 4 * len(ys)
    wide = tile * steps
    whole = pl.BlockSpec((half, MODEL_WIDTH), lambda i: (0, 0))
    return pl.pallas_call(
        expert_dw_body,
        grid=(steps,),
        out_shape=(sds((4, 64, wide), bf16), sds((4, 64, wide), bf16), sds((8, 64, wide), f32)),
        in_specs=[smem()]
        + [whole] * 8
        + [
            pl.BlockSpec((8 * half, tile), lambda i, j=j: (0, jnp.clip(i - 4 * j, 0, 3)))
            for j in range(len(ys))
        ],
        out_specs=(
            pl.BlockSpec((4, 64, tile), lambda i: (0, 0, i)),
            pl.BlockSpec((4, 64, tile), lambda i: (0, 0, i)),
            pl.BlockSpec((8, 64, tile), lambda i: (0, 0, i)),
        ),
        scratch_shapes=[VM((MODEL_WIDTH, 8 * half), bf16), VM((16, 64, tile), f32)],
        compiler_params=pltpu.CompilerParams(vmem_limit_bytes=VMEM_BYTES),
        name="expert_dw",
    )(sc, *chunks, *ys)


def relay_body(kept, rx, ry, sx_out, sy_out, own_out):
    sx_out[...] = (kept[4:6] + ry[0:2].astype(f32)).astype(bf16)
    sy_out[...] = (kept[6:8] + rx[0:2].astype(f32)).astype(bf16)
    own_out[0:2] = kept[0:2] + rx[2:4].astype(f32)
    own_out[2:4] = kept[2:4] + ry[2:4].astype(f32)


def relay(kept, rx, ry):
    rows, wide = kept.shape[1:]
    return kernel_call(
        relay_body,
        (sds((2, rows, wide), bf16), sds((2, rows, wide), bf16), sds((4, rows, wide), f32)),
        [vmem()] * 3,
        "relay",
    )(kept, rx, ry)


def owned_body(own, rx, ry, out0, out1, out2, out3):
    out0[...] = own[0] + ry[0].astype(f32)
    out1[...] = (own[1] + ry[1].astype(f32)).astype(bf16)
    out2[...] = (own[2] + rx[0].astype(f32)).astype(bf16)
    out3[...] = (own[3] + rx[1].astype(f32)).astype(bf16)


def owned(own, rx, ry):
    shape = own.shape[1:]
    return kernel_call(
        owned_body,
        (sds(shape, f32), sds(shape, bf16), sds(shape, bf16), sds(shape, bf16)),
        [vmem()] * 3,
        "owned",
    )(own, rx, ry)


def unpack_grad_body(sc, g0, g1, g2, g3, out, wide):
    ep = sc[0]
    n = g0.shape[0]
    experts = EXPERTS // GROUP
    ff = g0.shape[1] // experts
    for k, g in enumerate((g0, g1, g2, g3)):
        for e in range(experts):
            for l in range(ff // 128):
                at = e * ff + 128 * l
                wide[l, pl.ds((ep ^ k) * experts + e, n, stride=EXPERTS), :] = g[
                    :, at : at + 128
                ].astype(f32)
    for l in range(ff // 128):
        out[:, 128 * l : 128 * (l + 1)] = wide[l]


def unpack_grad(sc, parts):
    n, wide = parts[0].shape
    ff = wide * GROUP // EXPERTS
    out = kernel_call(
        unpack_grad_body,
        sds((n * EXPERTS, ff), f32),
        [smem()] + [vmem()] * 4,
        "unpack_grad",
        [VM((ff // 128, n * EXPERTS, 128), f32)],
    )(sc, *parts)
    return out.reshape(n, EXPERTS, ff)


def fast(
    c,
    tokens,
    segment_ids,
    valid,
    expert_ids,
    teacher,
    attn_gain,
    w_query,
    key_projection,
    value_projection,
    w_out,
    moe_gain,
    w_router,
    w_gate,
    w_up,
    w_down,
):
    half = tokens.shape[0]
    seq_len = expert_ids.shape[0]
    rows = w_query.shape[0]
    qw, kw = w_query.shape[1], key_projection.shape[1]
    pw = qw + 2 * kw
    sc = jnp.stack([c.ep, c.rep, c.core]).astype(jnp.int32)

    def my_half(v, axis=0):
        return lax.dynamic_slice_in_dim(v, c.core * half, half, axis)

    made = {}

    def held(name, v):
        wanted = ORDER.get(name, ())
        return tie(v, *[made[w] for w in wanted]) if wanted else v

    def run(name, f, *args):
        got = f(*held(name, args))
        made[name] = min(jax.tree.leaves(got), key=lambda x: x.size * x.dtype.itemsize)
        return got

    def send(name, v, mask):
        made[name] = c.swap(held(name, v), mask)
        return made[name]

    def cross(name, v):
        made[name] = c.other(held(name, v))
        return made[name]

    def to_group(name, parts):
        return [send(f"{name}{k}", v, c.reps * k) for k, v in enumerate(parts, 1)]

    def pair(a, b):
        return jnp.concatenate([a, b], 0)

    def spread(name, a, b):
        ax, ay = send(name + "ax", a, 1), send(name + "ay", a, 2)
        bx, by = send(name + "bx", b, 1), send(name + "by", b, 2)
        ad, bd = send(name + "ad", ax, 2), send(name + "bd", by, 1)
        return [a, b, ax, bx, ay, by, ad, bd]

    tokens_oth = cross("tokens", tokens)
    front = run(
        "front",
        pack_front,
        w_query,
        key_projection,
        value_projection,
        w_out,
        w_router,
        attn_gain,
        moe_gain,
        valid,
        expert_ids,
    )
    z1, z2, z3 = to_group("z", [front] * 3)
    packed = run("packed", pack_experts, sc, w_gate, w_up, w_down)
    front_p = spread("f", pair(front, z1), pair(z2, z3))
    e1, e2, e3 = to_group("e", packed[1:])
    exp_a = pair(packed[0], e1)

    cosine, sine = rope_tables(seq_len, 128)
    y_own, y_away, hn, qkv, o, misc, gains, attn_w = run(
        "attn",
        lambda *v: attn_fwd(*v, qw),
        sc,
        tokens,
        tokens_oth,
        segment_ids,
        valid,
        cosine,
        sine,
        front_p,
    )
    y_oth = cross("y", y_away)
    exp_p = spread("x", exp_a, pair(e2, e3))
    resid, hm = run("norm", second_norm, tokens, y_own, y_oth, gains)

    def all_rows(name, v):
        own = [v] + to_group(name, [v] * 3)
        return own + [cross(f"{name}t{k}", x) for k, x in enumerate(own)]

    hms = all_rows("h", hm)
    mix_own, mix_away, a, b, gates = run("efwd", expert_fwd, sc, misc, hms, exp_p)
    mixes = run("msum", core_sum, mix_own, cross("mt", mix_away))
    mixes = [mixes[0]] + to_group("m", mixes[1:])
    live = my_half(valid[0]).astype(f32)[:, None]
    result, g_out, g_low, err = loss_grad(
        resid, mixes, my_half(teacher), live, gains, seq_len, c.n
    )

    gos = all_rows("g", g_low)
    back_own, back_away, ga, gb, hs = run("ebwd", expert_bwd, sc, gates, a, b, gos, exp_p)
    backs = run("bsum", core_sum, back_own, cross("bt", back_away))
    backs = [backs[0]] + to_group("b", backs[1:])

    def first_step(name, x_send, y_send, kept):
        return kept, send(name + "x", x_send, 1), send(name + "y", y_send, 2)

    def second_step(name, sx, sy, own):
        return own, send(name + "x2", sx, 1), send(name + "y2", sy, 2)

    dw_gu = run("dwgu", lambda *v: expert_dw(v[0], v[1], v[2:]), sc, hms, ga, gb)
    dw_dn = run("dwdn", lambda *v: expert_dw(v[0], v[1], v[2:]), sc, gos, hs)
    gu = run("gurelay", relay, *first_step("gu", *dw_gu))
    gu = second_step("gu", *gu)
    dn_1 = first_step("dn", *dw_dn)

    gy, gres, rows_g = run(
        "second", second_back, backs, gates, misc, hm, resid, gains, g_out
    )
    gqkv, gy_all, ghn_own, ghn_away = run(
        "abwd",
        attn_bwd,
        sc,
        gy,
        cross("gy", gy),
        o,
        qkv,
        segment_ids,
        valid,
        cosine,
        sine,
        attn_w,
    )
    grad_input, rows_g = run(
        "first", first_back, ghn_own, cross("ghn", ghn_away), tokens, gains, gres, rows_g, err
    )
    if EARLY:
        dn = second_step("dn", *run("dnrelay", relay, *dn_1))
        gu0, *gu_low = run("guown", owned, *gu)
        gu_got = to_group("guz", gu_low)
    if DIRECT:
        attn_own, ax, ay, ad = run("adw", attn_dw3, sc, gy_all, o, hn, gqkv, rows_g)
        ax, ay, ad = send("ax", ax, 1), send("ay", ay, 2), send("ad", ad, 3)
    else:
        at = first_step("a", *run("adw", attn_dw, sc, gy_all, o, hn, gqkv, rows_g))
    if not EARLY:
        gu0, *gu_low = run("guown", owned, *gu)
        dn = second_step("dn", *run("dnrelay", relay, *dn_1))
        gu_got = to_group("guz", gu_low)
    if DIRECT:
        w0, *w_low = run("asum", attn_sum3, attn_own, ax, ay, ad)
    else:
        w0, *w_low = run("aown", owned, *second_step("a", *run("arelay", relay, *at)))
    w_got = to_group("az", w_low)
    dn0, *dn_low = run("dnown", owned, *dn)
    dn_got = to_group("dnz", dn_low)
    ew = ga.shape[1]
    parts = [gu0, *gu_got]
    expert_grads = [
        run("ug", unpack_grad, sc, [p[:, :ew] for p in parts]),
        run("uu", unpack_grad, sc, [p[:, ew:] for p in parts]),
        run("ud", unpack_grad, sc, [dn0, *dn_got]),
    ]
    own_w = w0 + (w_got[0].astype(f32) + w_got[1].astype(f32) + w_got[2].astype(f32))
    misc_own = own_w[:, pw + qw :]
    misc_own = misc_own + c.other(misc_own)
    live_total = jnp.sum(gains[2]) / rows
    loss = jnp.sum(misc_own[:, EXPERTS + 2]) / (2.0 * MODEL_WIDTH * live_total)
    return (
        loss,
        result,
        grad_input,
        misc_own[:, EXPERTS],
        own_w[:, :qw],
        own_w[:, qw : qw + kw],
        own_w[:, qw + kw : pw],
        own_w[:, pw : pw + qw],
        misc_own[:, EXPERTS + 1],
        misc_own[:, :EXPERTS],
        *expert_grads,
    )


def shards(
    tokens,
    segment_ids,
    valid,
    expert_ids,
    teacher,
    attn_gain,
    w_query,
    key_projection,
    value_projection,
    w_out,
    moe_gain,
    w_router,
    w_gate,
    w_up,
    w_down,
):
    c = Comm()
    if c.reps == 4 and w_query.shape[0] == 64:
        return fast(
            c,
            tokens,
            segment_ids,
            valid,
            expert_ids,
            teacher,
            attn_gain,
            w_query,
            key_projection,
            value_projection,
            w_out,
            moe_gain,
            w_router,
            w_gate,
            w_up,
            w_down,
        )
    half = tokens.shape[0]
    seq_len = expert_ids.shape[0]
    rows = w_query.shape[0]
    qw, kw = w_query.shape[1], key_projection.shape[1]
    ff = w_gate.shape[2]
    local_experts = EXPERTS // GROUP
    ew = local_experts * ff
    heads = qw // HEAD_SIZE
    kv_heads = kw // HEAD_SIZE
    per = heads // kv_heads
    scale = 1.0 / HEAD_SIZE
    first_core = c.core == 0

    def join_rows(own, other):
        return jnp.where(
            first_core, jnp.concatenate([own, other], 0), jnp.concatenate([other, own], 0)
        )

    def my_half(v):
        return lax.dynamic_slice_in_dim(v, c.core * half, half, 0)

    live_row = valid[0]
    live_count = jnp.sum(live_row).astype(f32)
    misc = jnp.concatenate(
        [
            w_router,
            attn_gain[:, None],
            moe_gain[:, None],
            jnp.broadcast_to(live_count.astype(bf16), (rows, 1)),
            jnp.zeros((rows, MISC - EXPERTS - 3), bf16),
        ],
        1,
    )
    front = jnp.concatenate([w_query, key_projection, value_projection, misc], 1)
    inputs_low = join_rows(tokens, c.other(tokens))

    def gather_attention(v):
        z = c.stack_group(c.gather_group(v))
        mid = z.shape[2] // 2
        return jnp.concatenate(
            [c.gather_reps(z[:, :, :mid], False), c.gather_reps(z[:, :, mid:], True)], 1
        )

    front_w = gather_attention(front)
    out_w = gather_attention(w_out)
    ids_half = my_half(expert_ids)
    ids_group = jnp.concatenate(c.gather_group(ids_half), 0)

    gate_up = jnp.concatenate(
        [w_gate.reshape(rows, GROUP, ew), w_up.reshape(rows, GROUP, ew)], 2
    ).transpose(1, 0, 2)
    gate_up_z = c.stack_group(c.all_to_group(gate_up))
    down_z = c.stack_group(c.all_to_group(w_down.reshape(rows, GROUP, ew).transpose(1, 0, 2)))
    gate_w = c.gather_reps(gate_up_z[:, :, :ew], False)
    up_w = c.gather_reps(gate_up_z[:, :, ew:], True)
    down_w = jnp.concatenate(
        [
            c.gather_reps(down_z[:, :, : ew // 2], False),
            c.gather_reps(down_z[:, :, ew // 2 :], True),
        ],
        1,
    )
    gate_ws = (gate_w, c.other(gate_w))
    up_ws = (up_w, c.other(up_w))
    down_ws = (down_w, c.other(down_w))

    pw = qw + 2 * kw
    proj_w = front_w[:, :pw]
    router_w = front_w[:, pw : pw + EXPERTS]
    gain_one = front_w[:, pw + EXPERTS].astype(f32)[None, :]
    gain_two = front_w[:, pw + EXPERTS + 1].astype(f32)[None, :]
    counts = front_w[:, pw + EXPERTS + 2].astype(f32).reshape(c.n, rows)[:, 0]
    live_total = jnp.sum(counts)

    inputs = inputs_low.astype(f32)
    inv_one = lax.rsqrt(jnp.mean(inputs * inputs, -1, keepdims=True) + epsilon)
    normed_one = inputs * inv_one
    attention_hidden = (normed_one * gain_one).astype(bf16)
    cosine, sine = rope_tables(seq_len, qw + kw)
    qkv = dot(attention_hidden, proj_w)
    qk_raw = qkv[:, : qw + kw]
    qk = (qk_raw * cosine + swap_halves(qk_raw) * sine).astype(bf16)
    q = qk[:, :qw].reshape(seq_len, kv_heads, per, HEAD_SIZE)
    k = qk[:, qw:].reshape(seq_len, kv_heads, HEAD_SIZE)
    v = qkv[:, qw + kw :].astype(bf16).reshape(seq_len, kv_heads, HEAD_SIZE)
    seg_row = segment_ids[0]
    places = jnp.arange(seq_len)
    allowed = (seg_row[:, None] == seg_row[None, :]) & (places[None, :] <= places[:, None]) & (
        live_row[None, :] > 0
    ) | (places[None, :] == places[:, None])
    scores = jnp.einsum("qkgd,skd->kgqs", q, k, preferred_element_type=f32) * scale
    scores = jnp.where(allowed[None, None], scores, negative)
    top_score = jnp.max(scores, -1, keepdims=True)
    exp_scores = jnp.exp(scores - top_score)
    probs = exp_scores / jnp.sum(exp_scores, -1, keepdims=True)
    probs_low = probs.astype(bf16)
    attn_out = (
        jnp.einsum("kgqs,skd->qkgd", probs_low, v, preferred_element_type=f32)
        .astype(bf16)
        .reshape(seq_len, qw)
    )
    proj_part = dot_t(attn_out, out_w)
    theirs = lax.dynamic_slice_in_dim(proj_part, (1 - c.core) * half, half, 0)
    inputs_half = tokens.astype(f32)
    resid = inputs_half + (my_half(proj_part) + c.other(theirs))
    inv_two = lax.rsqrt(jnp.mean(resid * resid, -1, keepdims=True) + epsilon)
    normed_two = resid * inv_two
    hidden_moe = (normed_two * gain_two).astype(bf16)

    hm = jnp.concatenate(c.gather_group(hidden_moe), 0)
    logits = dot(hm, router_w)
    named = jnp.any(ids_group[:, :, None] == jnp.arange(EXPERTS)[None, None, :], 1)
    masked = jnp.where(named, logits, negative)
    shifted = jnp.where(named, jnp.exp(logits - jnp.max(masked, -1, keepdims=True)), 0.0)
    gates = shifted / jnp.sum(shifted, -1, keepdims=True)
    my_gates = lax.dynamic_slice_in_dim(gates, c.ep * local_experts, local_experts, 1)
    wide = jnp.repeat(my_gates, ff, axis=1)

    kept = []
    mixed = 0.0
    for gw, uw, dw in zip(gate_ws, up_ws, down_ws):
        a = dot(hm, gw)
        b = dot(hm, uw)
        sigma = jax.nn.sigmoid(a)
        h = (a * sigma * b).astype(bf16)
        hs = (h.astype(f32) * wide).astype(bf16)
        mixed = mixed + dot_t(hs, dw)
        kept.append((a, b, h, hs))
    mixed = mixed.reshape(GROUP, half, MODEL_WIDTH)
    mix = mixed[0]
    for j in range(1, GROUP):
        mix = mix + c.swap(mixed[j].astype(bf16), c.reps * j).astype(f32)
    result = resid + mix

    live = my_half(live_row).astype(f32)[:, None]
    differ = result - my_half(teacher).astype(f32)
    err_cols = jnp.sum(live * differ * differ, 0)
    grad_out = seq_len * c.n / live_total * live * differ
    go = jnp.concatenate(c.gather_group(grad_out.astype(bf16)), 0)

    grad_hm = 0.0
    grad_gates = 0.0
    low = []
    for (a, b, h, hs), gw, uw, dw in zip(kept, gate_ws, up_ws, down_ws):
        u = dot(go, dw)
        grad_gates = grad_gates + jnp.sum(
            (h.astype(f32) * u).reshape(GROUP * half, local_experts, ff), -1
        )
        gh = u * wide
        sigma = jax.nn.sigmoid(a)
        ga = (gh * b * sigma * (1.0 + a * (1.0 - sigma))).astype(bf16)
        gb = (gh * a * sigma).astype(bf16)
        grad_hm = grad_hm + dot_t(ga, gw) + dot_t(gb, uw)
        low.append((ga, gb))
    gg = jnp.zeros((GROUP * half, MISC), f32)
    gg = lax.dynamic_update_slice_in_dim(gg, grad_gates, c.ep * local_experts, 1)
    back = jnp.concatenate([grad_hm, gg], 1).reshape(GROUP, half, MODEL_WIDTH + MISC)
    back_sum = back[0]
    for j in range(1, GROUP):
        back_sum = back_sum + c.swap(back[j].astype(bf16), c.reps * j).astype(f32)

    weight_sums = []
    for own, other in (
        ((hm, low[0][0]), (hm, low[1][0])),
        ((hm, low[0][1]), (hm, low[1][1])),
        ((go, kept[0][3]), (go, kept[1][3])),
    ):
        away = dot_o(*other).astype(bf16)
        weight_sums.append(dot_o(*own) + c.other(away).astype(f32))
    gate_s = c.scatter_reps(weight_sums[0], False)
    up_s = c.scatter_reps(weight_sums[1], True)
    down_s = jnp.concatenate(
        [
            c.scatter_reps(weight_sums[2][:, : ew // 2], False),
            c.scatter_reps(weight_sums[2][:, ew // 2 :], True),
        ],
        2,
    )
    sums = jnp.concatenate([gate_s, up_s, down_s], 2)
    sums_low = sums.astype(bf16)
    parts = [c.block(sums, 0)] + [
        c.swap(c.block(sums_low, k), c.reps * k).astype(f32) for k in range(1, GROUP)
    ]
    finished = c.stack_group(parts)

    def expert_grad(j):
        g = finished[:, :, j * ew : (j + 1) * ew].transpose(1, 0, 2)
        return g.reshape(rows, EXPERTS, ff)

    grad_probs = back_sum[:, MODEL_WIDTH : MODEL_WIDTH + EXPERTS]
    gate_probs = gates[:half]
    grad_logits = (
        gate_probs * (grad_probs - jnp.sum(gate_probs * grad_probs, -1, keepdims=True))
    ).astype(bf16)
    grad_hidden = back_sum[:, :MODEL_WIDTH] + dot_t(grad_logits, router_w)
    router_part = dot_o(hidden_moe, grad_logits)
    gain_two_part = jnp.sum(grad_hidden * normed_two, 0)
    scaled_two = grad_hidden * gain_two
    grad_resid = grad_out + inv_two * (
        scaled_two - normed_two * jnp.mean(scaled_two * normed_two, -1, keepdims=True)
    )
    gy_half = grad_resid.astype(bf16)
    gy = join_rows(gy_half, c.other(gy_half))

    out_part = dot_o(gy, attn_out)
    grad_attn = dot(gy, out_w).astype(bf16).reshape(seq_len, kv_heads, per, HEAD_SIZE)
    gp = jnp.einsum("qkgd,skd->kgqs", grad_attn, v, preferred_element_type=f32)
    gs = (probs * (gp - jnp.sum(probs * gp, -1, keepdims=True))).astype(bf16)
    gq = jnp.einsum("kgqs,skd->qkgd", gs, k, preferred_element_type=f32) * scale
    gk = jnp.einsum("kgqs,qkgd->skd", gs, q, preferred_element_type=f32) * scale
    gv = jnp.einsum("kgqs,qkgd->skd", probs_low, grad_attn, preferred_element_type=f32)
    gqk = jnp.concatenate([gq.reshape(seq_len, qw), gk.reshape(seq_len, kw)], 1)
    gqk = gqk * cosine - swap_halves(gqk) * sine
    gqkv = jnp.concatenate([gqk.astype(bf16), gv.astype(bf16).reshape(seq_len, kw)], 1)
    ghn_part = dot_t(gqkv, proj_w)
    ghn_low = ghn_part.astype(bf16)
    ghn = my_half(ghn_part) + c.other(
        lax.dynamic_slice_in_dim(ghn_low, (1 - c.core) * half, half, 0)
    ).astype(f32)
    proj_part_grad = dot_o(attention_hidden, gqkv)
    normed_half = my_half(normed_one)
    gain_one_part = jnp.sum(ghn * normed_half, 0)
    scaled_one = ghn * gain_one
    grad_input = grad_resid + my_half(inv_one) * (
        scaled_one - normed_half * jnp.mean(scaled_one * normed_half, -1, keepdims=True)
    )

    err_rows = jnp.sum(err_cols.reshape(MODEL_WIDTH // rows, rows), 0)
    misc_part = jnp.concatenate(
        [
            router_part,
            gain_one_part[:, None],
            gain_two_part[:, None],
            jnp.tile(err_rows, c.n)[:, None],
            jnp.zeros((MODEL_WIDTH, MISC - EXPERTS - 3), f32),
        ],
        1,
    )
    back_w = jnp.concatenate([proj_part_grad, out_part, misc_part], 1)
    mid = (back_w.shape[1] // 256) * 128
    attn_s = jnp.concatenate(
        [c.scatter_reps(back_w[:, :mid], False), c.scatter_reps(back_w[:, mid:], True)], 2
    )
    attn_low = attn_s.astype(bf16)
    own_w = c.block(attn_s, 0)
    for k_ in range(1, GROUP):
        own_w = own_w + c.swap(c.block(attn_low, k_), c.reps * k_).astype(f32)
    misc_own = own_w[:, pw + qw :]
    misc_own = misc_own + c.other(misc_own)
    loss = jnp.sum(misc_own[:, EXPERTS + 2]) / (2.0 * MODEL_WIDTH * live_total)

    return (
        loss,
        result.astype(bf16),
        grad_input.astype(bf16),
        misc_own[:, EXPERTS],
        own_w[:, :qw],
        own_w[:, qw : qw + kw],
        own_w[:, qw + kw : pw],
        own_w[:, pw : pw + qw],
        misc_own[:, EXPERTS + 1],
        misc_own[:, :EXPERTS],
        expert_grad(0),
        expert_grad(1),
        expert_grad(2),
    )


def solution(mesh):
    placed = (
        P(("dp", "tensor"), None),
        P("dp", None),
        P("dp", None),
        P("dp", None),
        P("dp", None),
        P("dp"),
        P("dp", "tensor"),
        P("dp", "tensor"),
        P("dp", "tensor"),
        P("dp", "tensor"),
        P("dp"),
        P("dp", None),
        P("dp", None, "tensor"),
        P("dp", None, "tensor"),
        P("dp", None, "tensor"),
    )
    return jax.shard_map(
        shards,
        mesh=mesh,
        in_specs=placed,
        out_specs=(
            P(),
            P(("dp", "tensor"), None),
            P(("dp", "tensor"), None),
            P("dp"),
            P("dp", "tensor"),
            P("dp", "tensor"),
            P("dp", "tensor"),
            P("dp", "tensor"),
            P("dp"),
            P("dp", None),
            P("dp", None, "tensor"),
            P("dp", None, "tensor"),
            P("dp", None, "tensor"),
        ),
        check_vma=False,
    )
```

```python
import functools

import jax
import jax.numpy as jnp
import numpy as np
from jax import lax
from jax.experimental import pallas as pl
from jax.experimental.pallas import tpu as pltpu
from jax.sharding import PartitionSpec as P

MODEL_WIDTH = 1024
HEAD_SIZE = 64
TOPK = 8
EXPERTS = 16
GROUP = 4
MISC = 128
DIRECT = False
FWHOLE = False
XWHOLE = False
CHUNK = False
MERGE = False
EARLY = False
ORDER = {'e2': ('fax', 'fay'), 'fad': ('fbx', 'fby', 'fax', 'fay'), 'xax': ('fad', 'fbd', 'z3'), 'xay': ('fad', 'fbd'), 'xad': ('xbx', 'fby'), 'ht0': ('y', 'norm'), 'second': ('dwgu', 'dwdn', 'gurelay'), 'dny': ('b1', 'gt3', 'gux', 'guy'), 'adw': ('gux2', 'guy2', 'dnx', 'dny', 'abwd'), 'ug': ('ax', 'ay', 'arelay'), 'uu': ('ax', 'ay', 'arelay'), 'abwd': ('b1', 'dnx', 'dny'), 'ht1': ('y', 'norm'), 'b2': ('efwda', 'mta', 'gt2'), 'm1': ('h1', 'h2', 'h3'), 'ad': ('first',), 'm2': ('xbx', 'xby', 'h1'), 'guown': ('gy', 'gux2', 'guy2'), 'dnz1': ('ax', 'guz1', 'guz2', 'guz3', 'ay'), 'dnz2': ('ax',), 'dnz3': ('ax', 'ay'), 'dwdn': ('g1',), 'az1': ('aown',), 'az2': ('aown',), 'gy': ('b1', 'b2', 'b3', 'ebwda'), 'ht2': ('attn', 'xbx'), 'ht3': ('attn', 'xbx', 'xay'), 'g3': ('h2',), 'guz3': ('guz1', 'guz2'), 'first': ('gurelay',), 'gux': ('gt2',), 'guy': ('g1', 'g2'), 'b1': ('mta', 'gt1', 'gt2'), 'b3': ('mta', 'gt2'), 'gurelay': ('g2', 'gt0'), 'norm': ('xbx', 'xby'), 'dnx': ('gux', 'guy'), 'ax': ('second',), 'ay': ('second',), 'ghn': ('gux2', 'guy2')}
VMEM_BYTES = 60 << 20
SMALL_BYTES = 16 << 20
SMALL = ("core_sum", "loss_grad")

epsilon = 1e-06
negative = -1e30
rope_base = 10000.0
f32 = jnp.float32
bf16 = jnp.bfloat16

INNER = (((1,), (1,)), ((), ()))
OUTER = (((0,), (0,)), ((), ()))


def dot(a, b):
    return jnp.dot(a, b, preferred_element_type=f32)


def dot_t(a, b):
    return lax.dot_general(a, b, INNER, preferred_element_type=f32)


def dot_o(a, b):
    return lax.dot_general(a, b, OUTER, preferred_element_type=f32)


def tie(v, *after):
    return lax.optimization_barrier((v, after))[0]


def rope_tables(length, width):
    half = HEAD_SIZE // 2
    places = jnp.arange(length).astype(f32)
    freqs = rope_base ** (-2.0 * jnp.arange(half).astype(f32) / HEAD_SIZE)
    angles = places[:, None] * freqs[None, :]
    cosine, sine = jnp.cos(angles), jnp.sin(angles)
    reps = width // HEAD_SIZE
    return (
        jnp.tile(jnp.concatenate([cosine, cosine], 1), (1, reps)),
        jnp.tile(jnp.concatenate([-sine, sine], 1), (1, reps)),
    )


def swap_halves(u):
    half = HEAD_SIZE // 2
    low = (jnp.arange(u.shape[1]) % HEAD_SIZE) < half
    return jnp.where(low[None, :], jnp.roll(u, -half, 1), jnp.roll(u, half, 1))


class Comm:
    def __init__(self):
        self.n = lax.axis_size("dp")
        self.me = lax.axis_index("dp")
        self.core = lax.axis_index("tensor")
        self.reps = self.n // GROUP
        self.ep = self.me // self.reps
        self.rep = self.me % self.reps
        self.bits = [1 << k for k in range(self.reps.bit_length() - 1)]

    def swap(self, v, mask):
        return lax.ppermute(v, "dp", [(i, i ^ mask) for i in range(self.n)])

    def other(self, v):
        return lax.ppermute(v, "tensor", [(0, 1), (1, 0)])

    def bit(self, b):
        return (self.rep // b) % 2

    def gather_reps(self, z, last_first):
        rows, cols = z.shape[1:]
        k = len(self.bits)
        out = jnp.zeros((GROUP,) + (2,) * k + (rows, cols), z.dtype)
        zero = jnp.int32(0)
        order = list(self.bits)
        if last_first:
            order = order[::-1]
        done = set()

        def place(block, flipped):
            start = [zero]
            for b in reversed(self.bits):
                if b in done:
                    start.append(zero)
                elif b == flipped:
                    start.append(1 - self.bit(b))
                else:
                    start.append(self.bit(b))
            return start + [zero, zero]

        cur = z.reshape((GROUP,) + (1,) * k + (rows, cols))
        out = lax.dynamic_update_slice(out, cur, place(cur, None))
        for b in order:
            got = self.swap(cur, b)
            out = lax.dynamic_update_slice(out, got, place(got, b))
            done.add(b)
            if len(done) < k:
                start = place(out, None)
                shape = [GROUP] + [2 if c in done else 1 for c in reversed(self.bits)]
                cur = lax.dynamic_slice(out, start, shape + [rows, cols])
        return out.reshape(GROUP * self.reps * rows, cols)

    def stack_group(self, parts, axis=0):
        parts = jnp.stack(parts, 0)
        idx = self.ep ^ jnp.arange(GROUP)
        return jnp.concatenate(
            [lax.dynamic_index_in_dim(parts, idx[j], 0, keepdims=True) for j in range(GROUP)], 0
        )

    def gather_group(self, v):
        return [v] + [self.swap(v, self.reps * k) for k in range(1, GROUP)]

    def block(self, v, k):
        return lax.dynamic_index_in_dim(v, self.ep ^ k, 0, keepdims=False)

    def all_to_group(self, v):
        return [self.block(v, 0)] + [
            self.swap(self.block(v, k), self.reps * k) for k in range(1, GROUP)
        ]

    def scatter_reps(self, s, last_first):
        cols = s.shape[1]
        k = len(self.bits)
        rows = s.shape[0] // (GROUP * self.reps)
        s = s.reshape((GROUP,) + (2,) * k + (rows, cols))
        order = list(self.bits)
        if last_first:
            order = order[::-1]
        for b in order:
            axis = 1 + list(reversed(self.bits)).index(b)
            mine = self.bit(b)
            send = lax.dynamic_slice_in_dim(s, 1 - mine, 1, axis).astype(bf16)
            keep = lax.dynamic_slice_in_dim(s, mine, 1, axis)
            s = keep + self.swap(send, b).astype(f32)
        return s.reshape(GROUP, rows, cols)


VM = pltpu.VMEM


def vmem():
    return pl.BlockSpec(memory_space=pltpu.VMEM)


def anym():
    return pl.BlockSpec(memory_space=pltpu.HBM)


def smem():
    return pl.BlockSpec(memory_space=pltpu.SMEM)


def sds(shape, dtype):
    return jax.ShapeDtypeStruct(shape, dtype)


def kernel_call(body, out_shape, in_specs, name, scratch=()):
    return pl.pallas_call(
        body,
        out_shape=out_shape,
        in_specs=in_specs,
        out_specs=jax.tree.map(lambda _: vmem(), out_shape),
        scratch_shapes=list(scratch),
        compiler_params=pltpu.CompilerParams(
            vmem_limit_bytes=SMALL_BYTES if name in SMALL else VMEM_BYTES
        ),
        name=name,
    )


def piece_copies(pieces, dst, sem, ep, rep, cols=None, first=0):
    copies = []
    for j, piece in enumerate(pieces):
        m, h = j // 2, j % 2
        base = 128 * h if piece.shape[0] == 256 else 0
        for i in range(2):
            at = (ep ^ (2 * h + i)) * 4 + (rep ^ m)
            src, to = piece.at[pl.ds(base + 64 * i, 64)], dst.at[at]
            if cols is not None:
                src, to = src.at[:, pl.ds(*cols)], to.at[:, pl.ds(*cols)]
            copies.append(pltpu.make_async_copy(src, to, sem.at[first + 2 * j + i]))
    return copies


NAMED = 32


def pack_front_body(wq, wk, wv, wo, wr, g1, g2, valid, ids, out):
    qw, kw = wq.shape[1], wk.shape[1]
    pw = qw + 2 * kw
    n = wq.shape[0]
    out[:, 0:qw] = wq[...]
    out[:, qw : qw + kw] = wk[...]
    out[:, qw + kw : pw] = wv[...]
    out[:, pw + MISC :] = wo[...]
    count = jnp.sum(valid[...].astype(f32), axis=1, keepdims=True)
    expert = lax.broadcasted_iota(jnp.int32, (EXPERTS, ids.shape[1]), 0)
    named = jnp.zeros(expert.shape, f32)
    for k in range(TOPK):
        named = jnp.where(ids[k : k + 1, :] == expert, 1.0, named)
    quarters = [named[:, n * j : n * (j + 1)] for j in range(ids.shape[1] // n)]
    top = jnp.concatenate([wr[...].astype(f32), jnp.zeros((NAMED - EXPERTS, n), f32)], 0)
    row = lax.broadcasted_iota(jnp.int32, top.shape, 0)
    top = jnp.where(row == EXPERTS, g1[...].astype(f32), top)
    top = jnp.where(row == EXPERTS + 1, g2[...].astype(f32), top)
    top = jnp.where(row == EXPERTS + 2, count, top)
    rest = jnp.zeros((MISC - NAMED - EXPERTS * len(quarters), n), f32)
    base = jnp.concatenate([top, *quarters, rest], 0)
    eye = lax.broadcasted_iota(jnp.int32, (n, n), 0) == lax.broadcasted_iota(jnp.int32, (n, n), 1)
    misc = dot_t(eye.astype(f32).astype(bf16), base.astype(bf16))
    out[:, pw : pw + MISC] = misc.astype(bf16)


def pack_front(wq, wk, wv, wo, wr, g1, g2, valid, ids):
    n = wq.shape[0]
    width = wq.shape[1] + 2 * wk.shape[1] + MISC + wo.shape[1]
    return kernel_call(pack_front_body, sds((n, width), bf16), [vmem()] * 9, "pack_front")(
        wq, wk, wv, wo, wr.T, g1[None, :], g2[None, :], valid, ids.T
    )


def pack_experts_body(sc, wg, wu, wd, out0, out1, out2, out3, wide):
    ep = sc[0]
    n, e, f = wg.shape
    per = e // GROUP
    for j, w in enumerate((wg, wu, wd)):
        for l in range(f // 128):
            wide[l] = w[:, :, 128 * l : 128 * (l + 1)].astype(f32).reshape(n * e, 128)
        for k, out in enumerate((out0, out1, out2, out3)):
            for x in range(per):
                for l in range(f // 128):
                    at = j * per * f + x * f + 128 * l
                    out[:, at : at + 128] = wide[
                        l, pl.ds((ep ^ k) * per + x, n, stride=e), :
                    ].astype(bf16)


def pack_experts(sc, wg, wu, wd):
    n, e, f = wg.shape
    return kernel_call(
        pack_experts_body,
        (sds((n, 3 * e * f // GROUP), bf16),) * GROUP,
        [smem()] + [vmem()] * 3,
        "pack_experts",
        [VM((f // 128, n * e, 128), f32)],
    )(sc, wg, wu, wd)


def rope_constants(length):
    half = HEAD_SIZE // 2
    freqs = np.float32(rope_base) ** (np.float32(-2.0 / HEAD_SIZE) * np.arange(half, dtype=np.float32))
    angles = np.arange(length, dtype=np.float32)[:, None] * freqs[None, :]
    cosine, sine = np.cos(angles), np.sin(angles)
    return (
        jnp.asarray(np.concatenate([cosine] * 4, 1), f32),
        jnp.asarray(np.concatenate([-sine, sine] * 2, 1), f32),
    )


def rotate_pairs(u, cosine, sine):
    lane = lax.broadcasted_iota(jnp.int32, u.shape, 1)
    low = lane % HEAD_SIZE < HEAD_SIZE // 2
    turned = jnp.where(low, pltpu.roll(u, 96, 1), pltpu.roll(u, 32, 1))
    return u * cosine + turned * sine


def both_lanes(pair, odd):
    lane = lax.broadcasted_iota(jnp.int32, pair.shape, 1)
    other = pltpu.roll(pair, 64, 1)
    first = lane < HEAD_SIZE
    return jnp.where(first, other, pair) if odd else jnp.where(first, pair, other)


def two_heads(pair):
    lane = lax.broadcasted_iota(jnp.int32, pair.shape, 1)
    zero = jnp.zeros_like(pair)
    return jnp.concatenate(
        [jnp.where(lane < HEAD_SIZE, pair, zero), jnp.where(lane < HEAD_SIZE, zero, pair)], 0
    )


def one_pair(rows):
    n = rows.shape[0] // 2
    lane = lax.broadcasted_iota(jnp.int32, (n, rows.shape[1]), 1)
    return jnp.where(lane < HEAD_SIZE, rows[:n], rows[n:])


def allowed_mask(seg, valid):
    n = seg.shape[1]
    r = lax.broadcasted_iota(jnp.int32, (n, n), 0)
    col = lax.broadcasted_iota(jnp.int32, (n, n), 1)
    seg_row = jnp.broadcast_to(seg.astype(f32), (n, n))
    seg_col = jnp.sum(jnp.where(r == col, seg_row, 0.0), axis=1, keepdims=True)
    live = jnp.broadcast_to(valid.astype(f32), (n, n)) > 0
    return ((seg_col == seg_row) & (col <= r) & live) | (r == col)


def softmax_rows(q2, k2, allowed2):
    s = dot_t(q2, k2) * (1.0 / HEAD_SIZE)
    s = jnp.where(allowed2, s, negative)
    e = jnp.exp(s - jnp.max(s, axis=1, keepdims=True))
    return e / jnp.sum(e, axis=1, keepdims=True)


def attn_fwd_body(sc, x_own, x_oth, seg, valid, cosine, sine, *refs):
    pieces = refs[:8]
    own_out, away_out, hn_out, qkv_out, o_out, misc_out, gains_out, w_out, turn_out = refs[8:17]
    w, x, sem = refs[17:]
    turn_out[0] = cosine[...]
    turn_out[1] = sine[...]
    ep, rep, core = sc[0], sc[1], sc[2]
    copies = piece_copies(pieces, w, sem, ep, rep)
    for cp in copies:
        cp.start()
    half = x_own.shape[0]
    n = 2 * half
    x[pl.ds(core * half, half), :] = x_own[...].astype(f32)
    x[pl.ds((1 - core) * half, half), :] = x_oth[...].astype(f32)
    allowed = allowed_mask(seg[...], valid[...])
    allowed2 = jnp.concatenate([allowed, allowed], 0)
    inputs = x[...]
    normed = inputs * lax.rsqrt(jnp.mean(inputs * inputs, axis=1, keepdims=True) + epsilon)
    for cp in copies:
        cp.wait()
    pw = qkv_out.shape[1]
    misc = w[:, :, pw : pw + MISC].reshape(MODEL_WIDTH, MISC)
    pick = lax.broadcasted_iota(jnp.int32, (8, MISC), 0) + EXPERTS
    pick = (pick == lax.broadcasted_iota(jnp.int32, (8, MISC), 1)).astype(f32).astype(bf16)
    gains = dot_t(pick, misc)
    gains_out[...] = gains
    misc_out[...] = misc
    hn = (normed * gains[0:1, :]).astype(bf16)
    hn_out[...] = hn
    w_out[...] = w[...].reshape(w_out.shape)
    qkv = dot(hn, w[:, :, :pw].reshape(MODEL_WIDTH, pw))
    groups = pw // 128
    kv0 = groups // 2
    for g in range(groups):
        u = qkv[:, 128 * g : 128 * (g + 1)]
        if g < kv0 + kv0 // 2:
            u = rotate_pairs(u, cosine[...], sine[...])
        qkv_out[:, 128 * g : 128 * (g + 1)] = u.astype(bf16)
    for m in range(kv0):
        g = kv0 + m // 2
        k2 = both_lanes(qkv_out[:, 128 * g : 128 * (g + 1)].astype(f32), m % 2).astype(bf16)
        g = g + kv0 // 2
        v2 = both_lanes(qkv_out[:, 128 * g : 128 * (g + 1)].astype(f32), m % 2).astype(bf16)
        q2 = two_heads(qkv_out[:, 128 * m : 128 * (m + 1)].astype(f32)).astype(bf16)
        p = softmax_rows(q2, k2, allowed2).astype(bf16)
        o_out[:, 128 * m : 128 * (m + 1)] = one_pair(dot(p, v2)).astype(bf16)
    wo = w[:, :, pw + MISC :].reshape(MODEL_WIDTH, o_out.shape[1])
    away_out[...] = dot_t(o_out[pl.ds((1 - core) * half, half), :], wo)
    own_out[...] = dot_t(o_out[pl.ds(core * half, half), :], wo)


def attn_fwd(sc, x_own, x_oth, seg, valid, cosine, sine, pieces, qw):
    half = x_own.shape[0]
    n = 2 * half
    cols = pieces[0].shape[1]
    pw = cols - MISC - qw
    return kernel_call(
        attn_fwd_body,
        (
            sds((half, MODEL_WIDTH), f32),
            sds((half, MODEL_WIDTH), f32),
            sds((n, MODEL_WIDTH), bf16),
            sds((n, pw), bf16),
            sds((n, qw), bf16),
            sds((MODEL_WIDTH, MISC), bf16),
            sds((8, MODEL_WIDTH), f32),
            sds((MODEL_WIDTH, cols), bf16),
            sds((2,) + cosine.shape, f32),
        ),
        [smem()] + [vmem()] * 6 + [anym()] * 8,
        "attn_fwd",
        [VM((16, 64, cols), bf16), VM((n, MODEL_WIDTH), f32), pltpu.SemaphoreType.DMA((16,))],
    )(sc, x_own, x_oth, seg, valid, cosine, sine, *pieces)


def second_norm_body(x, y_own, y_oth, gains, resid_out, hm_out):
    resid = x[...].astype(f32) + (y_own[...] + y_oth[...])
    resid_out[...] = resid
    inv = lax.rsqrt(jnp.mean(resid * resid, axis=1, keepdims=True) + epsilon)
    hm_out[...] = (resid * inv * gains[1:2, :]).astype(bf16)


def second_norm(x, y_own, y_oth, gains):
    return kernel_call(
        second_norm_body,
        (sds(y_own.shape, f32), sds(y_own.shape, bf16)),
        [vmem()] * 4,
        "second_norm",
    )(x, y_own, y_oth, gains)


def named_rows(block, j):
    moved = pltpu.roll(block.astype(f32), MISC - NAMED - EXPERTS * j, 1)
    lane = lax.broadcasted_iota(jnp.int32, moved.shape, 1)
    return (moved > 0.5) & (lane < EXPERTS)


def gates_of(hm, misc, named):
    logits = dot(hm, misc)
    top = jnp.max(jnp.where(named, logits, negative), axis=1, keepdims=True)
    e = jnp.where(named, jnp.exp(logits - top), 0.0)
    return e / jnp.sum(e, axis=1, keepdims=True)


def expert_fwd_body(sets, sc, misc, *refs):
    chunks, pieces = refs[:8], refs[8:16]
    own_out, away_out = refs[16:18]
    saved = refs[18 : 18 + 3 * len(sets)]
    w, hm, acc, gates, sem = refs[18 + 3 * len(sets) :]
    ep, rep, core = sc[0], sc[1], sc[2]
    half = chunks[0].shape[0]
    experts = EXPERTS // GROUP
    ew = w.shape[2] // 3
    ff = ew // experts
    part = 2 * half * len(sets[0])
    wide = piece_copies(pieces, w, sem, ep, rep, (0, 2 * ew), 0)
    down = piece_copies(pieces, w, sem, ep, rep, (2 * ew, ew), 16)
    for cp in wide + down:
        cp.start()
    order = [(k, other) for ks in sets for other in (False, True) for k in ks]
    for j, (k, other) in enumerate(order):
        here = pl.ds(j * half, half)
        chunk = chunks[k + GROUP * other][...]
        hm[here, :] = chunk
        at = pl.multiple_of(((ep ^ k) * 4 + rep) * 64, 64)
        block = misc[pl.ds(at, 64), :]
        mine = core == (1 if other else 0)
        quarters = [named_rows(block, q).astype(f32) for q in range(4)]
        first = jnp.concatenate(quarters[:2], 0)
        second = jnp.concatenate(quarters[2:], 0)
        gates[here, :] = jnp.where(mine, first, second)
    gates[...] = gates_of(hm[...], misc[...], gates[...] > 0.5)
    for n in range(len(sets)):
        saved[3 * n][...] = gates[n * part : (n + 1) * part, :]
    acc[...] = jnp.zeros_like(acc)
    lane = lax.broadcasted_iota(jnp.int32, gates.shape, 1)
    for cp in wide + down:
        cp.wait()

    def tile(e, carry):
        x = hm[...]
        at = pl.multiple_of(e * ff, ff)
        a = dot(x, w[:, :, pl.ds(at, ff)].reshape(MODEL_WIDTH, ff))
        b = dot(x, w[:, :, pl.ds(ew + at, ff)].reshape(MODEL_WIDTH, ff))
        g = jnp.sum(jnp.where(lane == ep * experts + e, gates[...], 0.0), axis=1, keepdims=True)
        h = (a * jax.nn.sigmoid(a) * b).astype(bf16)
        hs = (h.astype(f32) * g).astype(bf16)
        for n in range(len(sets)):
            saved[3 * n + 1][:, pl.ds(at, ff)] = a[n * part : (n + 1) * part, :]
            saved[3 * n + 2][:, pl.ds(at, ff)] = b[n * part : (n + 1) * part, :]
        acc[...] += dot_t(hs, w[:, :, pl.ds(2 * ew + at, ff)].reshape(MODEL_WIDTH, ff))
        return carry

    lax.fori_loop(0, experts, tile, 0)
    for j, (k, other) in enumerate(order):
        to = pl.ds(k * half, half)
        value = acc[j * half : (j + 1) * half, :]
        if other:
            away_out[to, :] = value.astype(bf16)
        else:
            own_out[to, :] = value


def expert_fwd(sets, sc, misc, chunks, pieces):
    half = chunks[0].shape[0]
    cols = pieces[0].shape[1]
    ew = cols // 3
    rows = GROUP * half
    part = 2 * half * len(sets[0])
    saved = (sds((part, MISC), f32), sds((part, ew), f32), sds((part, ew), f32)) * len(sets)
    return kernel_call(
        functools.partial(expert_fwd_body, sets),
        (sds((rows, MODEL_WIDTH), f32), sds((rows, MODEL_WIDTH), bf16)) + saved,
        [smem()] + [vmem()] * 9 + [anym()] * 8,
        "expert_fwd",
        [
            VM((16, 64, cols), bf16),
            VM((2 * rows, MODEL_WIDTH), bf16),
            VM((2 * rows, MODEL_WIDTH), f32),
            VM((2 * rows, MISC), f32),
            pltpu.SemaphoreType.DMA((32,)),
        ],
    )(sc, misc, *chunks, *pieces)


def core_sum_body(own, got, *outs):
    half = outs[0].shape[0]
    for j, out in enumerate(outs):
        at = pl.ds(j * half, half)
        out[...] = (own[at, :] + got[at, :].astype(f32)).astype(out.dtype)


def core_sum(ks, own, got):
    shape = (own.shape[0] // len(ks), own.shape[1])
    return kernel_call(
        core_sum_body,
        tuple(sds(shape, bf16 if k else f32) for k in ks),
        [vmem()] * 2,
        "core_sum",
    )(own, got)


def expert_bwd_body(ks, sc, gates, a_in, b_in, *refs):
    n = 2 * len(ks)
    chunks, pieces = refs[:n], refs[n : n + 8]
    own_out, away_out, ga_out, gb_out, hs_out, w, go, gsum, sem = refs[n + 8 :]
    ep, rep = sc[0], sc[1]
    half = chunks[0].shape[0]
    rows = len(ks) * half
    experts = EXPERTS // GROUP
    ew = w.shape[2] // 3
    ff = ew // experts
    wide = piece_copies(pieces, w, sem, ep, rep, (0, 2 * ew), 0)
    down = piece_copies(pieces, w, sem, ep, rep, (2 * ew, ew), 16)
    for cp in down + wide:
        cp.start()
    for j, chunk in enumerate(chunks):
        go[pl.ds(j * half, half), :] = chunk[...]
    gsum[...] = jnp.zeros_like(gsum)
    lane = lax.broadcasted_iota(jnp.int32, gsum.shape, 1)
    for cp in down + wide:
        cp.wait()

    def tile(e, carry):
        at = pl.multiple_of(e * ff, ff)
        a = a_in[:, pl.ds(at, ff)]
        b = b_in[:, pl.ds(at, ff)]
        u = dot(go[...], w[:, :, pl.ds(2 * ew + at, ff)].reshape(MODEL_WIDTH, ff))
        mine = lane == ep * experts + e
        g = jnp.sum(jnp.where(mine, gates[...], 0.0), axis=1, keepdims=True)
        s = jax.nn.sigmoid(a)
        silu = a * s
        h = (silu * b).astype(bf16).astype(f32)
        gsum[...] += jnp.where(mine, jnp.sum(h * u, axis=1, keepdims=True), 0.0)
        gh = u * g
        ga = (gh * b * s * (1.0 + a * (1.0 - s))).astype(bf16)
        gb = (gh * silu).astype(bf16)
        ga_out[:, pl.ds(at, ff)] = ga
        gb_out[:, pl.ds(at, ff)] = gb
        hs_out[:, pl.ds(at, ff)] = (h * g).astype(bf16)
        return carry

    lax.fori_loop(0, experts, tile, 0)

    def columns(n, carry):
        wg = w[pl.ds(4 * n, 4), :, :ew].reshape(256, ew)
        wu = w[pl.ds(4 * n, 4), :, ew : 2 * ew].reshape(256, ew)
        got = dot_t(ga_out[...], wg) + dot_t(gb_out[...], wu)
        cols = pl.ds(pl.multiple_of(256 * n, 256), 256)
        own_out[:, cols] = got[:rows, :]
        away_out[:, cols] = got[rows:, :].astype(bf16)
        return carry

    lax.fori_loop(0, MODEL_WIDTH // 256, columns, 0)
    own_out[:, MODEL_WIDTH:] = gsum[:rows, :]
    away_out[:, MODEL_WIDTH:] = gsum[rows:, :].astype(bf16)


def expert_bwd(ks, sc, gates, a, b, chunks, pieces):
    half = chunks[0].shape[0]
    cols = pieces[0].shape[1]
    ew = cols // 3
    rows = len(ks) * half
    full = MODEL_WIDTH + MISC
    low = sds((2 * rows, ew), bf16)
    return kernel_call(
        functools.partial(expert_bwd_body, ks),
        (sds((rows, full), f32), sds((rows, full), bf16), low, low, low),
        [smem()] + [vmem()] * (3 + len(chunks)) + [anym()] * 8,
        "expert_bwd",
        [
            VM((16, 64, cols), bf16),
            VM((2 * rows, MODEL_WIDTH), bf16),
            VM((2 * rows, MISC), f32),
            pltpu.SemaphoreType.DMA((32,)),
        ],
    )(sc, gates, a, b, *chunks, *pieces)


def loss_body(resid, m0, m1, m2, m3, teacher, live, gains, scale, result_out, g_out, glow_out, err_out):
    mix = m0[...] + (m1[...].astype(f32) + m2[...].astype(f32) + m3[...].astype(f32))
    result = resid[...] + mix
    result_out[...] = result.astype(bf16)
    differ = result - teacher[...].astype(f32)
    rows = gains.shape[1] // scale.shape[1]
    total = jnp.sum(gains[2:3, :], axis=1, keepdims=True) / rows
    weighted = live[...] * differ
    g = (scale.shape[0] * scale.shape[1]) / total * weighted
    g_out[...] = g
    glow_out[...] = g.astype(bf16)
    err_out[...] = jnp.broadcast_to(jnp.sum(weighted * differ, axis=0, keepdims=True), err_out.shape)


def loss_grad(resid, mixes, teacher, live, gains, seq_len, n):
    shape = resid.shape
    return kernel_call(
        loss_body,
        (sds(shape, bf16), sds(shape, f32), sds(shape, bf16), sds((8, shape[1]), f32)),
        [vmem()] * 9,
        "loss_grad",
    )(resid, *mixes, teacher, live, gains, jnp.zeros((seq_len, n), f32))


def second_back_body(b0, b1, b2, b3, gates, misc, hm, resid, gains, g_out, gy_out, gres_out, rows_out):
    half = resid.shape[0]
    total = b0[...] + (b1[...].astype(f32) + b2[...].astype(f32) + b3[...].astype(f32))
    gp = total[:, MODEL_WIDTH:]
    gate = gates[0:half, :]
    gl = (gate * (gp - jnp.sum(gate * gp, axis=1, keepdims=True))).astype(bf16)
    ghm = total[:, :MODEL_WIDTH] + dot_t(gl, misc[...])
    x = resid[...]
    inv = lax.rsqrt(jnp.mean(x * x, axis=1, keepdims=True) + epsilon)
    normed = x * inv
    rows = dot_o(gl, hm[...])
    gain_row = jnp.sum(ghm * normed, axis=0, keepdims=True)
    at = lax.broadcasted_iota(jnp.int32, rows.shape, 0)
    rows_out[...] = jnp.where(at == EXPERTS + 1, gain_row, rows)
    scaled = ghm * gains[1:2, :]
    gres = g_out[...] + inv * (
        scaled - normed * jnp.mean(scaled * normed, axis=1, keepdims=True)
    )
    gres_out[...] = gres
    gy_out[...] = gres.astype(bf16)


def second_back(backs, gates, misc, hm, resid, gains, g_out):
    shape = resid.shape
    return kernel_call(
        second_back_body,
        (sds(shape, bf16), sds(shape, f32), sds((MISC, shape[1]), f32)),
        [vmem()] * 10,
        "second_back",
    )(*backs, gates, misc, hm, resid, gains, g_out)


def attn_bwd_body(
    sc, gy_own, gy_oth, o, qkv, seg, valid, turn, w, gqkv_out, gy_out, own_out, away_out, low
):
    core = sc[2]
    half = gy_own.shape[0]
    n = 2 * half
    gy_out[pl.ds(core * half, half), :] = gy_own[...]
    gy_out[pl.ds((1 - core) * half, half), :] = gy_oth[...]
    pw = qkv.shape[1]
    low[...] = dot(gy_out[...], w[:, pw + MISC :]).astype(bf16)
    allowed = allowed_mask(seg[...], valid[...])
    allowed2 = jnp.concatenate([allowed, allowed], 0)
    kv0 = pw // 256
    lane = lax.broadcasted_iota(jnp.int32, (n, 128), 1)
    scale = 1.0 / HEAD_SIZE
    held = {}
    for m in range(kv0):
        gk_at = kv0 + m // 2
        gv_at = gk_at + kv0 // 2
        k2 = both_lanes(qkv[:, 128 * gk_at : 128 * (gk_at + 1)].astype(f32), m % 2).astype(bf16)
        v2 = both_lanes(qkv[:, 128 * gv_at : 128 * (gv_at + 1)].astype(f32), m % 2).astype(bf16)
        q2 = two_heads(qkv[:, 128 * m : 128 * (m + 1)].astype(f32)).astype(bf16)
        go2 = two_heads(low[:, 128 * m : 128 * (m + 1)].astype(f32)).astype(bf16)
        p = softmax_rows(q2, k2, allowed2)
        gp = dot_t(go2, v2)
        gs = (p * (gp - jnp.sum(p * gp, axis=1, keepdims=True))).astype(bf16)
        gq = one_pair(dot(gs, k2)) * scale
        gqkv_out[:, 128 * m : 128 * (m + 1)] = rotate_pairs(gq, turn[0], -turn[1]).astype(bf16)
        gk = dot_o(gs, q2) * scale
        gv = dot_o(p.astype(bf16), go2)
        gk = gk + pltpu.roll(gk, 64, 1)
        gv = gv + pltpu.roll(gv, 64, 1)
        if m % 2 == 0:
            held = {"k": gk, "v": gv}
        else:
            gk = jnp.where(lane < HEAD_SIZE, held["k"], gk)
            gv = jnp.where(lane < HEAD_SIZE, held["v"], gv)
            gqkv_out[:, 128 * gk_at : 128 * (gk_at + 1)] = rotate_pairs(
                gk, turn[0], -turn[1]
            ).astype(bf16)
            gqkv_out[:, 128 * gv_at : 128 * (gv_at + 1)] = gv.astype(bf16)
    away_out[...] = dot_t(gqkv_out[pl.ds((1 - core) * half, half), :], w[:, :pw]).astype(bf16)
    own_out[...] = dot_t(gqkv_out[pl.ds(core * half, half), :], w[:, :pw])


def attn_bwd(sc, gy_own, gy_oth, o, qkv, seg, valid, turn, w):
    half = gy_own.shape[0]
    n = 2 * half
    pw = qkv.shape[1]
    return kernel_call(
        attn_bwd_body,
        (
            sds((n, pw), bf16),
            sds((n, MODEL_WIDTH), bf16),
            sds((half, MODEL_WIDTH), f32),
            sds((half, MODEL_WIDTH), bf16),
        ),
        [smem()] + [vmem()] * 8,
        "attn_bwd",
        [VM((n, o.shape[1]), bf16)],
    )(sc, gy_own, gy_oth, o, qkv, seg, valid, turn, w)


def first_back_body(g_own, g_oth, x, gains, gres, rows, err, ginput_out, rows_out):
    ghn = g_own[...] + g_oth[...].astype(f32)
    inputs = x[...].astype(f32)
    inv = lax.rsqrt(jnp.mean(inputs * inputs, axis=1, keepdims=True) + epsilon)
    normed = inputs * inv
    gain_row = jnp.sum(ghn * normed, axis=0, keepdims=True)
    scaled = ghn * gains[0:1, :]
    ginput_out[...] = (
        gres[...] + inv * (scaled - normed * jnp.mean(scaled * normed, axis=1, keepdims=True))
    ).astype(bf16)
    e = err[...]
    for shift in (64, 128, 256, 512):
        e = e + pltpu.roll(e, shift, 1)
    at = lax.broadcasted_iota(jnp.int32, rows.shape, 0)
    r = jnp.where(at == EXPERTS, gain_row, rows[...])
    rows_out[...] = jnp.where(at == EXPERTS + 2, e[0:1, :], r)


def first_back(g_own, g_oth, x, gains, gres, rows, err):
    return kernel_call(
        first_back_body,
        (sds(gres.shape, bf16), sds(rows.shape, f32)),
        [vmem()] * 7,
        "first_back",
    )(g_own, g_oth, x, gains, gres, rows, err)


SEND_X = (12, 13, 4, 5)
SEND_Y = (14, 15, 10, 11)
KEPT = (0, 1, 2, 3, 6, 7, 8, 9)


def store_relative(out, ep, rep, value, cols):
    for j in range(16):
        to = 4 * ((j % 4) ^ rep) + ((j // 4) ^ ep)
        out[to, :, cols] = value[64 * j : 64 * (j + 1), :]


def split_relative(full, x_out, y_out, kept_out):
    for j, at in enumerate(SEND_X):
        x_out[j] = full[at].astype(bf16)
    for j, at in enumerate(SEND_Y):
        y_out[j] = full[at].astype(bf16)
    for j, at in enumerate(KEPT):
        kept_out[j] = full[at]


def attn_dw_body(sc, gy, o, hn, gqkv, rows, x_out, y_out, kept_out, full):
    ep, rep = sc[0], sc[1]
    pw = gqkv.shape[1]
    qw = o.shape[1]
    store_relative(full, ep, rep, dot_o(hn[...], gqkv[...]), slice(0, pw))
    store_relative(full, ep, rep, dot_o(gy[...], o[...]), slice(pw, pw + qw))
    store_relative(full, ep, rep, jnp.transpose(rows[...]), slice(pw + qw, pw + qw + MISC))
    split_relative(full, x_out, y_out, kept_out)


def attn_dw(sc, gy, o, hn, gqkv, rows):
    width = gqkv.shape[1] + o.shape[1] + MISC
    return kernel_call(
        attn_dw_body,
        (sds((4, 64, width), bf16), sds((4, 64, width), bf16), sds((8, 64, width), f32)),
        [smem()] + [vmem()] * 5,
        "attn_dw",
        [VM((16, 64, width), f32)],
    )(sc, gy, o, hn, gqkv, rows)


def attn_dw3_body(sc, gy, o, hn, gqkv, rows, own_out, x_out, y_out, d_out, full):
    ep, rep = sc[0], sc[1]
    pw = gqkv.shape[1]
    qw = o.shape[1]
    store_relative(full, ep, rep, dot_o(hn[...], gqkv[...]), slice(0, pw))
    store_relative(full, ep, rep, dot_o(gy[...], o[...]), slice(pw, pw + qw))
    store_relative(full, ep, rep, jnp.transpose(rows[...]), slice(pw + qw, pw + qw + MISC))
    own_out[...] = full[0:4]
    for m, out in enumerate((x_out, y_out, d_out)):
        out[...] = full[4 * m + 4 : 4 * m + 8].astype(bf16)


def attn_dw3(sc, gy, o, hn, gqkv, rows):
    width = gqkv.shape[1] + o.shape[1] + MISC
    low = sds((4, 64, width), bf16)
    return kernel_call(
        attn_dw3_body,
        (sds((4, 64, width), f32), low, low, low),
        [smem()] + [vmem()] * 5,
        "attn_dw3",
        [VM((16, 64, width), f32)],
    )(sc, gy, o, hn, gqkv, rows)


def attn_sum3_body(own, x, y, d, *outs):
    for k, out in enumerate(outs):
        total = own[k] + (x[k].astype(f32) + y[k].astype(f32) + d[k].astype(f32))
        out[...] = total.astype(out.dtype)


def attn_sum3(own, x, y, d):
    shape = own.shape[1:]
    low = sds(shape, bf16)
    return kernel_call(
        attn_sum3_body, (sds(shape, f32), low, low, low), [vmem()] * 4, "attn_sum3"
    )(own, x, y, d)


def expert_dw_body(plan, parts, sc, *refs):
    n = 8 * (1 + max(plan))
    chunks = refs[:n]
    ys = refs[n : n + parts * len(plan)]
    x_out, y_out, kept_out, xt, full = refs[n + parts * len(plan) :]
    ep, rep = sc[0], sc[1]
    half = chunks[0].shape[0]
    step = pl.program_id(0)
    for which in sorted(set(plan)):

        @pl.when(step == 4 * plan.index(which))
        def _():
            for j, x in enumerate(chunks[8 * which : 8 * which + 8]):
                xt[:, j * half : (j + 1) * half] = jnp.transpose(x[...])

    for j in range(len(plan)):

        @pl.when(step // 4 == j)
        def _():
            got = ys[parts * j : parts * (j + 1)]
            rows = got[0].shape[0]
            g = dot(xt[:, :rows], got[0][...])
            for p in range(1, parts):
                g = g + dot(xt[:, p * rows : (p + 1) * rows], got[p][...])
            store_relative(full, ep, rep, g, slice(None))

    split_relative(full, x_out, y_out, kept_out)


def expert_dw(sc, chunk_sets, plan, ys):
    half = chunk_sets[0][0].shape[0]
    parts = len(ys[0])
    rows, wide = ys[0][0].shape
    tile = wide // 4
    steps = 4 * len(plan)
    whole = pl.BlockSpec((half, MODEL_WIDTH), lambda i: (0, 0))
    shape = (4, 64, steps * tile)
    return pl.pallas_call(
        functools.partial(expert_dw_body, plan, parts),
        grid=(steps,),
        out_shape=(sds(shape, bf16), sds(shape, bf16), sds((8,) + shape[1:], f32)),
        in_specs=[smem()]
        + [whole] * (8 * len(chunk_sets))
        + [
            pl.BlockSpec((rows, tile), lambda i, j=j: (0, jnp.clip(i - 4 * j, 0, 3)))
            for j in range(len(plan))
            for _ in range(parts)
        ],
        out_specs=(
            pl.BlockSpec((4, 64, tile), lambda i: (0, 0, i)),
            pl.BlockSpec((4, 64, tile), lambda i: (0, 0, i)),
            pl.BlockSpec((8, 64, tile), lambda i: (0, 0, i)),
        ),
        scratch_shapes=[VM((MODEL_WIDTH, 8 * half), bf16), VM((16, 64, tile), f32)],
        compiler_params=pltpu.CompilerParams(vmem_limit_bytes=VMEM_BYTES),
        name="expert_dw",
    )(sc, *[x for xs in chunk_sets for x in xs], *[y for part in ys for y in part])


def relay_body(kept, rx, ry, sx_out, sy_out, own_out):
    sx_out[...] = (kept[4:6] + ry[0:2].astype(f32)).astype(bf16)
    sy_out[...] = (kept[6:8] + rx[0:2].astype(f32)).astype(bf16)
    own_out[0:2] = kept[0:2] + rx[2:4].astype(f32)
    own_out[2:4] = kept[2:4] + ry[2:4].astype(f32)


def relay(kept, rx, ry):
    rows, wide = kept.shape[1:]
    return kernel_call(
        relay_body,
        (sds((2, rows, wide), bf16), sds((2, rows, wide), bf16), sds((4, rows, wide), f32)),
        [vmem()] * 3,
        "relay",
    )(kept, rx, ry)


def owned_body(own, rx, ry, out0, out1, out2, out3):
    out0[...] = own[0] + ry[0].astype(f32)
    out1[...] = (own[1] + ry[1].astype(f32)).astype(bf16)
    out2[...] = (own[2] + rx[0].astype(f32)).astype(bf16)
    out3[...] = (own[3] + rx[1].astype(f32)).astype(bf16)


def owned(own, rx, ry):
    shape = own.shape[1:]
    return kernel_call(
        owned_body,
        (sds(shape, f32), sds(shape, bf16), sds(shape, bf16), sds(shape, bf16)),
        [vmem()] * 3,
        "owned",
    )(own, rx, ry)


def unpack_grad_body(sc, g0, g1, g2, g3, out, wide):
    ep = sc[0]
    n = g0.shape[0]
    experts = EXPERTS // GROUP
    ff = g0.shape[1] // experts
    for k, g in enumerate((g0, g1, g2, g3)):
        for e in range(experts):
            for l in range(ff // 128):
                at = e * ff + 128 * l
                wide[l, pl.ds((ep ^ k) * experts + e, n, stride=EXPERTS), :] = g[
                    :, at : at + 128
                ].astype(f32)
    for l in range(ff // 128):
        out[:, 128 * l : 128 * (l + 1)] = wide[l]


def unpack_grad(sc, parts):
    n, wide = parts[0].shape
    ff = wide * GROUP // EXPERTS
    out = kernel_call(
        unpack_grad_body,
        sds((n * EXPERTS, ff), f32),
        [smem()] + [vmem()] * 4,
        "unpack_grad",
        [VM((ff // 128, n * EXPERTS, 128), f32)],
    )(sc, *parts)
    return out.reshape(n, EXPERTS, ff)


def fast(
    c,
    tokens,
    segment_ids,
    valid,
    expert_ids,
    teacher,
    attn_gain,
    w_query,
    key_projection,
    value_projection,
    w_out,
    moe_gain,
    w_router,
    w_gate,
    w_up,
    w_down,
):
    half = tokens.shape[0]
    seq_len = expert_ids.shape[0]
    rows = w_query.shape[0]
    qw, kw = w_query.shape[1], key_projection.shape[1]
    pw = qw + 2 * kw
    sc = jnp.stack([c.ep, c.rep, c.core]).astype(jnp.int32)

    def my_half(v, axis=0):
        return lax.dynamic_slice_in_dim(v, c.core * half, half, axis)

    made = {}

    def held(name, v):
        wanted = [w for w in ORDER.get(name, ()) if w in made]
        return tie(v, *[made[w] for w in wanted]) if wanted else v

    def run(name, f, *args):
        got = f(*held(name, args))
        made[name] = min(jax.tree.leaves(got), key=lambda x: x.size * x.dtype.itemsize)
        return got

    def send(name, v, mask):
        made[name] = c.swap(held(name, v), mask)
        return made[name]

    def cross(name, v):
        made[name] = c.other(held(name, v))
        return made[name]

    def to_group(name, parts):
        return [send(f"{name}{k}", v, c.reps * k) for k, v in enumerate(parts, 1)]

    def pair(a, b):
        return jnp.concatenate([a, b], 0)

    def spread(name, a, b, whole):
        if whole:
            z = pair(a, b)
            x, y = send(name + "ax", z, 1), send(name + "ay", z, 2)
            d, e = send(name + "ad", x[:128], 2), send(name + "bd", y[128:], 1)
            return [z, z, x, x, y, y, d, e]
        ax, ay = send(name + "ax", a, 1), send(name + "ay", a, 2)
        bx, by = send(name + "bx", b, 1), send(name + "by", b, 2)
        ad, bd = send(name + "ad", ax, 2), send(name + "bd", by, 1)
        return [a, b, ax, bx, ay, by, ad, bd]

    tokens_oth = cross("tokens", tokens)
    front = run(
        "front",
        pack_front,
        w_query,
        key_projection,
        value_projection,
        w_out,
        w_router,
        attn_gain,
        moe_gain,
        valid,
        expert_ids,
    )
    z1, z2, z3 = to_group("z", [front] * 3)
    packed = run("packed", pack_experts, sc, w_gate, w_up, w_down)
    front_p = spread("f", pair(front, z1), pair(z2, z3), FWHOLE)
    e1, e2, e3 = to_group("e", packed[1:])
    exp_a = pair(packed[0], e1)

    cosine, sine = rope_tables(seq_len, 128)
    y_own, y_away, hn, qkv, o, misc, gains, attn_w, turn = run(
        "attn",
        lambda *v: attn_fwd(*v, qw),
        sc,
        tokens,
        tokens_oth,
        segment_ids,
        valid,
        cosine,
        sine,
        front_p,
    )
    y_oth = cross("y", y_away)
    exp_p = spread("x", exp_a, pair(e2, e3), XWHOLE)
    resid, hm = run("norm", second_norm, tokens, y_own, y_oth, gains)

    def all_rows(name, v):
        own = [v] + to_group(name, [v] * 3)
        return own + [cross(f"{name}t{k}", x) for k, x in enumerate(own)]

    hms = all_rows("h", hm)
    sets = {"n": (0, 1), "f": (2, 3)} if CHUNK else {"a": (0, 1, 2, 3)}

    def rows_of(v, ks):
        return [v[k] for k in ks] + [v[GROUP + k] for k in ks]

    mix_own, mix_away, *saved = run(
        "efwda", functools.partial(expert_fwd, tuple(sets.values())), sc, misc, hms, exp_p
    )
    kept = {name: saved[3 * n : 3 * n + 3] for n, name in enumerate(sets)}
    mixes = run(
        "msuma", functools.partial(core_sum, (0, 1, 2, 3)), mix_own, cross("mta", mix_away)
    )
    mixes = [mixes[0]] + to_group("m", mixes[1:])
    live = my_half(valid[0]).astype(f32)[:, None]
    result, g_out, g_low, err = loss_grad(
        resid, mixes, my_half(teacher), live, gains, seq_len, c.n
    )

    gos = [g_low] + to_group("g", [g_low] * 3) + [None] * GROUP
    done = {}
    for name, ks in sets.items():
        for k in ks:
            gos[GROUP + k] = cross(f"gt{k}", gos[k])
        done[name] = run(
            "ebwd" + name,
            functools.partial(expert_bwd, ks),
            sc,
            *kept[name],
            rows_of(gos, ks),
            exp_p,
        )
    backs = {}
    for name in reversed(sets):
        ks = sets[name]
        own, away = done[name][:2]
        got = run(
            "bsum" + name, functools.partial(core_sum, ks), own, cross("bt" + name, away)
        )
        for k, v in zip(ks, got):
            backs[k] = send(f"b{k}", v, c.reps * k) if k else v
    backs = [backs[k] for k in range(GROUP)]
    lows = [done[name][2:] for name in sets]
    gates = kept[next(iter(sets))][0]
    ga, gb, hs = ([low[j] for low in lows] for j in range(3))
    hm_rows = [x for ks in sets.values() for x in rows_of(hms, ks)]
    go_rows = [x for ks in sets.values() for x in rows_of(gos, ks)]

    def first_step(name, x_send, y_send, kept):
        return kept, send(name + "x", x_send, 1), send(name + "y", y_send, 2)

    def second_step(name, sx, sy, own):
        return own, send(name + "x2", sx, 1), send(name + "y2", sy, 2)

    def dw(name, chunk_sets, plan, ys):
        return run(name, lambda v, x, y: expert_dw(v, x, plan, y), sc, chunk_sets, ys)

    if MERGE:
        dw_gu = dw("dwgu", [hm_rows, go_rows], (0, 0, 1), [ga, gb, hs])
        made["dwdn"] = made["dwgu"]
    else:
        dw_gu = dw("dwgu", [hm_rows], (0, 0), [ga, gb])
        dw_dn = dw("dwdn", [go_rows], (0,), [hs])
    gu = run("gurelay", relay, *first_step("gu", *dw_gu))
    gu = second_step("gu", *gu)
    if MERGE:
        for name in ("dnx", "dny"):
            made[name] = made[name.replace("dn", "gu")]
    else:
        dn_1 = first_step("dn", *dw_dn)

    gy, gres, rows_g = run(
        "second", second_back, backs, gates, misc, hm, resid, gains, g_out
    )
    gqkv, gy_all, ghn_own, ghn_away = run(
        "abwd",
        attn_bwd,
        sc,
        gy,
        cross("gy", gy),
        o,
        qkv,
        segment_ids,
        valid,
        turn,
        attn_w,
    )
    grad_input, rows_g = run(
        "first", first_back, ghn_own, cross("ghn", ghn_away), tokens, gains, gres, rows_g, err
    )
    if EARLY:
        if not MERGE:
            dn = second_step("dn", *run("dnrelay", relay, *dn_1))
        gu0, *gu_low = run("guown", owned, *gu)
        gu_got = to_group("guz", gu_low)
    if DIRECT:
        attn_own, ax, ay, ad = run("adw", attn_dw3, sc, gy_all, o, hn, gqkv, rows_g)
        ax, ay, ad = send("ax", ax, 1), send("ay", ay, 2), send("ad", ad, 3)
    else:
        at = first_step("a", *run("adw", attn_dw, sc, gy_all, o, hn, gqkv, rows_g))
    if not EARLY:
        gu0, *gu_low = run("guown", owned, *gu)
        if not MERGE:
            dn = second_step("dn", *run("dnrelay", relay, *dn_1))
        gu_got = to_group("guz", gu_low)
    if DIRECT:
        w0, *w_low = run("asum", attn_sum3, attn_own, ax, ay, ad)
    else:
        w0, *w_low = run("aown", owned, *second_step("a", *run("arelay", relay, *at)))
    w_got = to_group("az", w_low)
    parts = [gu0, *gu_got]
    ew = hs[0].shape[1]
    if MERGE:
        last = [p[:, 2 * ew :] for p in parts]
    else:
        dn0, *dn_low = run("dnown", owned, *dn)
        last = [dn0, *to_group("dnz", dn_low)]
    expert_grads = [
        run("ug", unpack_grad, sc, [p[:, :ew] for p in parts]),
        run("uu", unpack_grad, sc, [p[:, ew : 2 * ew] for p in parts]),
        run("ud", unpack_grad, sc, last),
    ]
    own_w = w0 + (w_got[0].astype(f32) + w_got[1].astype(f32) + w_got[2].astype(f32))
    misc_own = own_w[:, pw + qw :]
    misc_own = misc_own + c.other(misc_own)
    live_total = jnp.sum(gains[2]) / rows
    loss = jnp.sum(misc_own[:, EXPERTS + 2]) / (2.0 * MODEL_WIDTH * live_total)
    return (
        loss,
        result,
        grad_input,
        misc_own[:, EXPERTS],
        own_w[:, :qw],
        own_w[:, qw : qw + kw],
        own_w[:, qw + kw : pw],
        own_w[:, pw : pw + qw],
        misc_own[:, EXPERTS + 1],
        misc_own[:, :EXPERTS],
        *expert_grads,
    )


def shards(
    tokens,
    segment_ids,
    valid,
    expert_ids,
    teacher,
    attn_gain,
    w_query,
    key_projection,
    value_projection,
    w_out,
    moe_gain,
    w_router,
    w_gate,
    w_up,
    w_down,
):
    c = Comm()
    if c.reps == 4 and w_query.shape[0] == 64:
        return fast(
            c,
            tokens,
            segment_ids,
            valid,
            expert_ids,
            teacher,
            attn_gain,
            w_query,
            key_projection,
            value_projection,
            w_out,
            moe_gain,
            w_router,
            w_gate,
            w_up,
            w_down,
        )
    half = tokens.shape[0]
    seq_len = expert_ids.shape[0]
    rows = w_query.shape[0]
    qw, kw = w_query.shape[1], key_projection.shape[1]
    ff = w_gate.shape[2]
    local_experts = EXPERTS // GROUP
    ew = local_experts * ff
    heads = qw // HEAD_SIZE
    kv_heads = kw // HEAD_SIZE
    per = heads // kv_heads
    scale = 1.0 / HEAD_SIZE
    first_core = c.core == 0

    def join_rows(own, other):
        return jnp.where(
            first_core, jnp.concatenate([own, other], 0), jnp.concatenate([other, own], 0)
        )

    def my_half(v):
        return lax.dynamic_slice_in_dim(v, c.core * half, half, 0)

    live_row = valid[0]
    live_count = jnp.sum(live_row).astype(f32)
    misc = jnp.concatenate(
        [
            w_router,
            attn_gain[:, None],
            moe_gain[:, None],
            jnp.broadcast_to(live_count.astype(bf16), (rows, 1)),
            jnp.zeros((rows, MISC - EXPERTS - 3), bf16),
        ],
        1,
    )
    front = jnp.concatenate([w_query, key_projection, value_projection, misc], 1)
    inputs_low = join_rows(tokens, c.other(tokens))

    def gather_attention(v):
        z = c.stack_group(c.gather_group(v))
        mid = z.shape[2] // 2
        return jnp.concatenate(
            [c.gather_reps(z[:, :, :mid], False), c.gather_reps(z[:, :, mid:], True)], 1
        )

    front_w = gather_attention(front)
    out_w = gather_attention(w_out)
    ids_half = my_half(expert_ids)
    ids_group = jnp.concatenate(c.gather_group(ids_half), 0)

    gate_up = jnp.concatenate(
        [w_gate.reshape(rows, GROUP, ew), w_up.reshape(rows, GROUP, ew)], 2
    ).transpose(1, 0, 2)
    gate_up_z = c.stack_group(c.all_to_group(gate_up))
    down_z = c.stack_group(c.all_to_group(w_down.reshape(rows, GROUP, ew).transpose(1, 0, 2)))
    gate_w = c.gather_reps(gate_up_z[:, :, :ew], False)
    up_w = c.gather_reps(gate_up_z[:, :, ew:], True)
    down_w = jnp.concatenate(
        [
            c.gather_reps(down_z[:, :, : ew // 2], False),
            c.gather_reps(down_z[:, :, ew // 2 :], True),
        ],
        1,
    )
    gate_ws = (gate_w, c.other(gate_w))
    up_ws = (up_w, c.other(up_w))
    down_ws = (down_w, c.other(down_w))

    pw = qw + 2 * kw
    proj_w = front_w[:, :pw]
    router_w = front_w[:, pw : pw + EXPERTS]
    gain_one = front_w[:, pw + EXPERTS].astype(f32)[None, :]
    gain_two = front_w[:, pw + EXPERTS + 1].astype(f32)[None, :]
    counts = front_w[:, pw + EXPERTS + 2].astype(f32).reshape(c.n, rows)[:, 0]
    live_total = jnp.sum(counts)

    inputs = inputs_low.astype(f32)
    inv_one = lax.rsqrt(jnp.mean(inputs * inputs, -1, keepdims=True) + epsilon)
    normed_one = inputs * inv_one
    attention_hidden = (normed_one * gain_one).astype(bf16)
    cosine, sine = rope_tables(seq_len, qw + kw)
    qkv = dot(attention_hidden, proj_w)
    qk_raw = qkv[:, : qw + kw]
    qk = (qk_raw * cosine + swap_halves(qk_raw) * sine).astype(bf16)
    q = qk[:, :qw].reshape(seq_len, kv_heads, per, HEAD_SIZE)
    k = qk[:, qw:].reshape(seq_len, kv_heads, HEAD_SIZE)
    v = qkv[:, qw + kw :].astype(bf16).reshape(seq_len, kv_heads, HEAD_SIZE)
    seg_row = segment_ids[0]
    places = jnp.arange(seq_len)
    allowed = (seg_row[:, None] == seg_row[None, :]) & (places[None, :] <= places[:, None]) & (
        live_row[None, :] > 0
    ) | (places[None, :] == places[:, None])
    scores = jnp.einsum("qkgd,skd->kgqs", q, k, preferred_element_type=f32) * scale
    scores = jnp.where(allowed[None, None], scores, negative)
    top_score = jnp.max(scores, -1, keepdims=True)
    exp_scores = jnp.exp(scores - top_score)
    probs = exp_scores / jnp.sum(exp_scores, -1, keepdims=True)
    probs_low = probs.astype(bf16)
    attn_out = (
        jnp.einsum("kgqs,skd->qkgd", probs_low, v, preferred_element_type=f32)
        .astype(bf16)
        .reshape(seq_len, qw)
    )
    proj_part = dot_t(attn_out, out_w)
    theirs = lax.dynamic_slice_in_dim(proj_part, (1 - c.core) * half, half, 0)
    inputs_half = tokens.astype(f32)
    resid = inputs_half + (my_half(proj_part) + c.other(theirs))
    inv_two = lax.rsqrt(jnp.mean(resid * resid, -1, keepdims=True) + epsilon)
    normed_two = resid * inv_two
    hidden_moe = (normed_two * gain_two).astype(bf16)

    hm = jnp.concatenate(c.gather_group(hidden_moe), 0)
    logits = dot(hm, router_w)
    named = jnp.any(ids_group[:, :, None] == jnp.arange(EXPERTS)[None, None, :], 1)
    masked = jnp.where(named, logits, negative)
    shifted = jnp.where(named, jnp.exp(logits - jnp.max(masked, -1, keepdims=True)), 0.0)
    gates = shifted / jnp.sum(shifted, -1, keepdims=True)
    my_gates = lax.dynamic_slice_in_dim(gates, c.ep * local_experts, local_experts, 1)
    wide = jnp.repeat(my_gates, ff, axis=1)

    kept = []
    mixed = 0.0
    for gw, uw, dw in zip(gate_ws, up_ws, down_ws):
        a = dot(hm, gw)
        b = dot(hm, uw)
        sigma = jax.nn.sigmoid(a)
        h = (a * sigma * b).astype(bf16)
        hs = (h.astype(f32) * wide).astype(bf16)
        mixed = mixed + dot_t(hs, dw)
        kept.append((a, b, h, hs))
    mixed = mixed.reshape(GROUP, half, MODEL_WIDTH)
    mix = mixed[0]
    for j in range(1, GROUP):
        mix = mix + c.swap(mixed[j].astype(bf16), c.reps * j).astype(f32)
    result = resid + mix

    live = my_half(live_row).astype(f32)[:, None]
    differ = result - my_half(teacher).astype(f32)
    err_cols = jnp.sum(live * differ * differ, 0)
    grad_out = seq_len * c.n / live_total * live * differ
    go = jnp.concatenate(c.gather_group(grad_out.astype(bf16)), 0)

    grad_hm = 0.0
    grad_gates = 0.0
    low = []
    for (a, b, h, hs), gw, uw, dw in zip(kept, gate_ws, up_ws, down_ws):
        u = dot(go, dw)
        grad_gates = grad_gates + jnp.sum(
            (h.astype(f32) * u).reshape(GROUP * half, local_experts, ff), -1
        )
        gh = u * wide
        sigma = jax.nn.sigmoid(a)
        ga = (gh * b * sigma * (1.0 + a * (1.0 - sigma))).astype(bf16)
        gb = (gh * a * sigma).astype(bf16)
        grad_hm = grad_hm + dot_t(ga, gw) + dot_t(gb, uw)
        low.append((ga, gb))
    gg = jnp.zeros((GROUP * half, MISC), f32)
    gg = lax.dynamic_update_slice_in_dim(gg, grad_gates, c.ep * local_experts, 1)
    back = jnp.concatenate([grad_hm, gg], 1).reshape(GROUP, half, MODEL_WIDTH + MISC)
    back_sum = back[0]
    for j in range(1, GROUP):
        back_sum = back_sum + c.swap(back[j].astype(bf16), c.reps * j).astype(f32)

    weight_sums = []
    for own, other in (
        ((hm, low[0][0]), (hm, low[1][0])),
        ((hm, low[0][1]), (hm, low[1][1])),
        ((go, kept[0][3]), (go, kept[1][3])),
    ):
        away = dot_o(*other).astype(bf16)
        weight_sums.append(dot_o(*own) + c.other(away).astype(f32))
    gate_s = c.scatter_reps(weight_sums[0], False)
    up_s = c.scatter_reps(weight_sums[1], True)
    down_s = jnp.concatenate(
        [
            c.scatter_reps(weight_sums[2][:, : ew // 2], False),
            c.scatter_reps(weight_sums[2][:, ew // 2 :], True),
        ],
        2,
    )
    sums = jnp.concatenate([gate_s, up_s, down_s], 2)
    sums_low = sums.astype(bf16)
    parts = [c.block(sums, 0)] + [
        c.swap(c.block(sums_low, k), c.reps * k).astype(f32) for k in range(1, GROUP)
    ]
    finished = c.stack_group(parts)

    def expert_grad(j):
        g = finished[:, :, j * ew : (j + 1) * ew].transpose(1, 0, 2)
        return g.reshape(rows, EXPERTS, ff)

    grad_probs = back_sum[:, MODEL_WIDTH : MODEL_WIDTH + EXPERTS]
    gate_probs = gates[:half]
    grad_logits = (
        gate_probs * (grad_probs - jnp.sum(gate_probs * grad_probs, -1, keepdims=True))
    ).astype(bf16)
    grad_hidden = back_sum[:, :MODEL_WIDTH] + dot_t(grad_logits, router_w)
    router_part = dot_o(hidden_moe, grad_logits)
    gain_two_part = jnp.sum(grad_hidden * normed_two, 0)
    scaled_two = grad_hidden * gain_two
    grad_resid = grad_out + inv_two * (
        scaled_two - normed_two * jnp.mean(scaled_two * normed_two, -1, keepdims=True)
    )
    gy_half = grad_resid.astype(bf16)
    gy = join_rows(gy_half, c.other(gy_half))

    out_part = dot_o(gy, attn_out)
    grad_attn = dot(gy, out_w).astype(bf16).reshape(seq_len, kv_heads, per, HEAD_SIZE)
    gp = jnp.einsum("qkgd,skd->kgqs", grad_attn, v, preferred_element_type=f32)
    gs = (probs * (gp - jnp.sum(probs * gp, -1, keepdims=True))).astype(bf16)
    gq = jnp.einsum("kgqs,skd->qkgd", gs, k, preferred_element_type=f32) * scale
    gk = jnp.einsum("kgqs,qkgd->skd", gs, q, preferred_element_type=f32) * scale
    gv = jnp.einsum("kgqs,qkgd->skd", probs_low, grad_attn, preferred_element_type=f32)
    gqk = jnp.concatenate([gq.reshape(seq_len, qw), gk.reshape(seq_len, kw)], 1)
    gqk = gqk * cosine - swap_halves(gqk) * sine
    gqkv = jnp.concatenate([gqk.astype(bf16), gv.astype(bf16).reshape(seq_len, kw)], 1)
    ghn_part = dot_t(gqkv, proj_w)
    ghn_low = ghn_part.astype(bf16)
    ghn = my_half(ghn_part) + c.other(
        lax.dynamic_slice_in_dim(ghn_low, (1 - c.core) * half, half, 0)
    ).astype(f32)
    proj_part_grad = dot_o(attention_hidden, gqkv)
    normed_half = my_half(normed_one)
    gain_one_part = jnp.sum(ghn * normed_half, 0)
    scaled_one = ghn * gain_one
    grad_input = grad_resid + my_half(inv_one) * (
        scaled_one - normed_half * jnp.mean(scaled_one * normed_half, -1, keepdims=True)
    )

    err_rows = jnp.sum(err_cols.reshape(MODEL_WIDTH // rows, rows), 0)
    misc_part = jnp.concatenate(
        [
            router_part,
            gain_one_part[:, None],
            gain_two_part[:, None],
            jnp.tile(err_rows, c.n)[:, None],
            jnp.zeros((MODEL_WIDTH, MISC - EXPERTS - 3), f32),
        ],
        1,
    )
    back_w = jnp.concatenate([proj_part_grad, out_part, misc_part], 1)
    mid = (back_w.shape[1] // 256) * 128
    attn_s = jnp.concatenate(
        [c.scatter_reps(back_w[:, :mid], False), c.scatter_reps(back_w[:, mid:], True)], 2
    )
    attn_low = attn_s.astype(bf16)
    own_w = c.block(attn_s, 0)
    for k_ in range(1, GROUP):
        own_w = own_w + c.swap(c.block(attn_low, k_), c.reps * k_).astype(f32)
    misc_own = own_w[:, pw + qw :]
    misc_own = misc_own + c.other(misc_own)
    loss = jnp.sum(misc_own[:, EXPERTS + 2]) / (2.0 * MODEL_WIDTH * live_total)

    return (
        loss,
        result.astype(bf16),
        grad_input.astype(bf16),
        misc_own[:, EXPERTS],
        own_w[:, :qw],
        own_w[:, qw : qw + kw],
        own_w[:, qw + kw : pw],
        own_w[:, pw : pw + qw],
        misc_own[:, EXPERTS + 1],
        misc_own[:, :EXPERTS],
        expert_grad(0),
        expert_grad(1),
        expert_grad(2),
    )


def solution(mesh):
    placed = (
        P(("dp", "tensor"), None),
        P("dp", None),
        P("dp", None),
        P("dp", None),
        P("dp", None),
        P("dp"),
        P("dp", "tensor"),
        P("dp", "tensor"),
        P("dp", "tensor"),
        P("dp", "tensor"),
        P("dp"),
        P("dp", None),
        P("dp", None, "tensor"),
        P("dp", None, "tensor"),
        P("dp", None, "tensor"),
    )
    return jax.shard_map(
        shards,
        mesh=mesh,
        in_specs=placed,
        out_specs=(
            P(),
            P(("dp", "tensor"), None),
            P(("dp", "tensor"), None),
            P("dp"),
            P("dp", "tensor"),
            P("dp", "tensor"),
            P("dp", "tensor"),
            P("dp", "tensor"),
            P("dp"),
            P("dp", None),
            P("dp", None, "tensor"),
            P("dp", None, "tensor"),
            P("dp", None, "tensor"),
        ),
        check_vma=False,
    )
```

```python
import functools

import jax
import jax.numpy as jnp
import numpy as np
from jax import lax
from jax.experimental import pallas as pl
from jax.experimental.pallas import tpu as pltpu
from jax.sharding import PartitionSpec as P

MODEL_WIDTH = 1024
HEAD_SIZE = 64
TOPK = 8
EXPERTS = 16
GROUP = 4
MISC = 128
DIRECT = False
FWHOLE = False
XWHOLE = False
CHUNK = False
MERGE = False
EARLY = False
ORDER = {'e2': ('fax', 'fay'), 'fad': ('fbx', 'fby', 'fax', 'fay'), 'xax': ('fad', 'fbd', 'z3'), 'xay': ('fad', 'fbd'), 'xad': ('xbx',), 'ht0': ('y', 'norm'), 'second': ('dwgu', 'dwdn', 'gurelay'), 'dny': ('b1', 'gt3', 'gux', 'guy'), 'adw': ('gux2', 'guy2', 'dnx', 'dny', 'abwd'), 'ug': ('ax', 'ay', 'arelay'), 'uu': ('ax', 'ay', 'arelay'), 'abwd': ('b1', 'dnx', 'dny'), 'ht1': ('y', 'norm'), 'b2': ('efwda', 'mta', 'gt2'), 'm1': ('h1', 'h2', 'h3'), 'ad': ('first',), 'm2': ('xbx', 'xby', 'h1'), 'guown': ('gy', 'gux2', 'guy2'), 'dnz1': ('ax', 'guz1', 'guz2', 'guz3', 'ay'), 'dnz2': ('ax',), 'dnz3': ('ax', 'ay'), 'dwdn': ('g1',), 'az1': ('aown',), 'az2': ('aown',), 'gy': ('b1', 'b2', 'b3', 'ebwda'), 'ht2': ('attn', 'xbx'), 'ht3': ('attn', 'xbx', 'xay'), 'g3': ('h2',), 'guz3': ('guz1', 'guz2'), 'first': ('gurelay',), 'gux': ('gt2',), 'guy': ('g1', 'g2'), 'b1': ('mta', 'gt1', 'gt2'), 'b3': ('mta', 'gt2'), 'gurelay': ('g2', 'gt0'), 'norm': ('xbx', 'xby'), 'dnx': ('guy',), 'ax': ('second',), 'ay': ('second',), 'ghn': ('gux2', 'guy2')}
VMEM_BYTES = 60 << 20
SMALL_BYTES = 16 << 20
SMALL = ("core_sum", "loss_grad", "second_norm")

epsilon = 1e-06
negative = -1e30
rope_base = 10000.0
f32 = jnp.float32
bf16 = jnp.bfloat16

INNER = (((1,), (1,)), ((), ()))
OUTER = (((0,), (0,)), ((), ()))


def dot(a, b):
    return jnp.dot(a, b, preferred_element_type=f32)


def dot_t(a, b):
    return lax.dot_general(a, b, INNER, preferred_element_type=f32)


def dot_o(a, b):
    return lax.dot_general(a, b, OUTER, preferred_element_type=f32)


def tie(v, *after):
    return lax.optimization_barrier((v, after))[0]


def rope_tables(length, width):
    half = HEAD_SIZE // 2
    places = jnp.arange(length).astype(f32)
    freqs = rope_base ** (-2.0 * jnp.arange(half).astype(f32) / HEAD_SIZE)
    angles = places[:, None] * freqs[None, :]
    cosine, sine = jnp.cos(angles), jnp.sin(angles)
    reps = width // HEAD_SIZE
    return (
        jnp.tile(jnp.concatenate([cosine, cosine], 1), (1, reps)),
        jnp.tile(jnp.concatenate([-sine, sine], 1), (1, reps)),
    )


def swap_halves(u):
    half = HEAD_SIZE // 2
    low = (jnp.arange(u.shape[1]) % HEAD_SIZE) < half
    return jnp.where(low[None, :], jnp.roll(u, -half, 1), jnp.roll(u, half, 1))


class Comm:
    def __init__(self):
        self.n = lax.axis_size("dp")
        self.me = lax.axis_index("dp")
        self.core = lax.axis_index("tensor")
        self.reps = self.n // GROUP
        self.ep = self.me // self.reps
        self.rep = self.me % self.reps
        self.bits = [1 << k for k in range(self.reps.bit_length() - 1)]

    def swap(self, v, mask):
        return lax.ppermute(v, "dp", [(i, i ^ mask) for i in range(self.n)])

    def other(self, v):
        return lax.ppermute(v, "tensor", [(0, 1), (1, 0)])

    def bit(self, b):
        return (self.rep // b) % 2

    def gather_reps(self, z, last_first):
        rows, cols = z.shape[1:]
        k = len(self.bits)
        out = jnp.zeros((GROUP,) + (2,) * k + (rows, cols), z.dtype)
        zero = jnp.int32(0)
        order = list(self.bits)
        if last_first:
            order = order[::-1]
        done = set()

        def place(block, flipped):
            start = [zero]
            for b in reversed(self.bits):
                if b in done:
                    start.append(zero)
                elif b == flipped:
                    start.append(1 - self.bit(b))
                else:
                    start.append(self.bit(b))
            return start + [zero, zero]

        cur = z.reshape((GROUP,) + (1,) * k + (rows, cols))
        out = lax.dynamic_update_slice(out, cur, place(cur, None))
        for b in order:
            got = self.swap(cur, b)
            out = lax.dynamic_update_slice(out, got, place(got, b))
            done.add(b)
            if len(done) < k:
                start = place(out, None)
                shape = [GROUP] + [2 if c in done else 1 for c in reversed(self.bits)]
                cur = lax.dynamic_slice(out, start, shape + [rows, cols])
        return out.reshape(GROUP * self.reps * rows, cols)

    def stack_group(self, parts, axis=0):
        parts = jnp.stack(parts, 0)
        idx = self.ep ^ jnp.arange(GROUP)
        return jnp.concatenate(
            [lax.dynamic_index_in_dim(parts, idx[j], 0, keepdims=True) for j in range(GROUP)], 0
        )

    def gather_group(self, v):
        return [v] + [self.swap(v, self.reps * k) for k in range(1, GROUP)]

    def block(self, v, k):
        return lax.dynamic_index_in_dim(v, self.ep ^ k, 0, keepdims=False)

    def all_to_group(self, v):
        return [self.block(v, 0)] + [
            self.swap(self.block(v, k), self.reps * k) for k in range(1, GROUP)
        ]

    def scatter_reps(self, s, last_first):
        cols = s.shape[1]
        k = len(self.bits)
        rows = s.shape[0] // (GROUP * self.reps)
        s = s.reshape((GROUP,) + (2,) * k + (rows, cols))
        order = list(self.bits)
        if last_first:
            order = order[::-1]
        for b in order:
            axis = 1 + list(reversed(self.bits)).index(b)
            mine = self.bit(b)
            send = lax.dynamic_slice_in_dim(s, 1 - mine, 1, axis).astype(bf16)
            keep = lax.dynamic_slice_in_dim(s, mine, 1, axis)
            s = keep + self.swap(send, b).astype(f32)
        return s.reshape(GROUP, rows, cols)


VM = pltpu.VMEM


def vmem():
    return pl.BlockSpec(memory_space=pltpu.VMEM)


def anym():
    return pl.BlockSpec(memory_space=pltpu.HBM)


def smem():
    return pl.BlockSpec(memory_space=pltpu.SMEM)


def sds(shape, dtype):
    return jax.ShapeDtypeStruct(shape, dtype)


def kernel_call(body, out_shape, in_specs, name, scratch=()):
    return pl.pallas_call(
        body,
        out_shape=out_shape,
        in_specs=in_specs,
        out_specs=jax.tree.map(lambda _: vmem(), out_shape),
        scratch_shapes=list(scratch),
        compiler_params=pltpu.CompilerParams(
            vmem_limit_bytes=SMALL_BYTES if name in SMALL else VMEM_BYTES
        ),
        name=name,
    )


def piece_copies(pieces, dst, sem, ep, rep, cols=None, first=0):
    copies = []
    for j, piece in enumerate(pieces):
        m, h = j // 2, j % 2
        base = 128 * h if piece.shape[0] == 256 else 0
        for i in range(2):
            at = (ep ^ (2 * h + i)) * 4 + (rep ^ m)
            src, to = piece.at[pl.ds(base + 64 * i, 64)], dst.at[at]
            if cols is not None:
                src, to = src.at[:, pl.ds(*cols)], to.at[:, pl.ds(*cols)]
            copies.append(pltpu.make_async_copy(src, to, sem.at[first + 2 * j + i]))
    return copies


NAMED = 32


def pack_front_body(wq, wk, wv, wo, wr, g1, g2, valid, ids, out):
    qw, kw = wq.shape[1], wk.shape[1]
    pw = qw + 2 * kw
    n = wq.shape[0]
    out[:, 0:qw] = wq[...]
    out[:, qw : qw + kw] = wk[...]
    out[:, qw + kw : pw] = wv[...]
    out[:, pw + MISC :] = wo[...]
    count = jnp.sum(valid[...].astype(f32), axis=1, keepdims=True)
    expert = lax.broadcasted_iota(jnp.int32, (EXPERTS, ids.shape[1]), 0)
    named = jnp.zeros(expert.shape, f32)
    for k in range(TOPK):
        named = jnp.where(ids[k : k + 1, :] == expert, 1.0, named)
    quarters = [named[:, n * j : n * (j + 1)] for j in range(ids.shape[1] // n)]
    top = jnp.concatenate([wr[...].astype(f32), jnp.zeros((NAMED - EXPERTS, n), f32)], 0)
    row = lax.broadcasted_iota(jnp.int32, top.shape, 0)
    top = jnp.where(row == EXPERTS, g1[...].astype(f32), top)
    top = jnp.where(row == EXPERTS + 1, g2[...].astype(f32), top)
    top = jnp.where(row == EXPERTS + 2, count, top)
    rest = jnp.zeros((MISC - NAMED - EXPERTS * len(quarters), n), f32)
    base = jnp.concatenate([top, *quarters, rest], 0)
    eye = lax.broadcasted_iota(jnp.int32, (n, n), 0) == lax.broadcasted_iota(jnp.int32, (n, n), 1)
    misc = dot_t(eye.astype(f32).astype(bf16), base.astype(bf16))
    out[:, pw : pw + MISC] = misc.astype(bf16)


def pack_front(wq, wk, wv, wo, wr, g1, g2, valid, ids):
    n = wq.shape[0]
    width = wq.shape[1] + 2 * wk.shape[1] + MISC + wo.shape[1]
    return kernel_call(pack_front_body, sds((n, width), bf16), [vmem()] * 9, "pack_front")(
        wq, wk, wv, wo, wr.T, g1[None, :], g2[None, :], valid, ids.T
    )


def pack_experts_body(sc, wg, wu, wd, out0, out1, out2, out3, wide):
    ep = sc[0]
    n, e, f = wg.shape
    per = e // GROUP
    for j, w in enumerate((wg, wu, wd)):
        for l in range(f // 128):
            wide[l] = w[:, :, 128 * l : 128 * (l + 1)].astype(f32).reshape(n * e, 128)
        for k, out in enumerate((out0, out1, out2, out3)):
            for x in range(per):
                for l in range(f // 128):
                    at = j * per * f + x * f + 128 * l
                    out[:, at : at + 128] = wide[
                        l, pl.ds((ep ^ k) * per + x, n, stride=e), :
                    ].astype(bf16)


def pack_experts(sc, wg, wu, wd):
    n, e, f = wg.shape
    return kernel_call(
        pack_experts_body,
        (sds((n, 3 * e * f // GROUP), bf16),) * GROUP,
        [smem()] + [vmem()] * 3,
        "pack_experts",
        [VM((f // 128, n * e, 128), f32)],
    )(sc, wg, wu, wd)


def rope_constants(length):
    half = HEAD_SIZE // 2
    freqs = np.float32(rope_base) ** (np.float32(-2.0 / HEAD_SIZE) * np.arange(half, dtype=np.float32))
    angles = np.arange(length, dtype=np.float32)[:, None] * freqs[None, :]
    cosine, sine = np.cos(angles), np.sin(angles)
    return (
        jnp.asarray(np.concatenate([cosine] * 4, 1), f32),
        jnp.asarray(np.concatenate([-sine, sine] * 2, 1), f32),
    )


def rotate_pairs(u, cosine, sine):
    lane = lax.broadcasted_iota(jnp.int32, u.shape, 1)
    low = lane % HEAD_SIZE < HEAD_SIZE // 2
    turned = jnp.where(low, pltpu.roll(u, 96, 1), pltpu.roll(u, 32, 1))
    return u * cosine + turned * sine


def both_lanes(pair, odd):
    lane = lax.broadcasted_iota(jnp.int32, pair.shape, 1)
    other = pltpu.roll(pair, 64, 1)
    first = lane < HEAD_SIZE
    return jnp.where(first, other, pair) if odd else jnp.where(first, pair, other)


def two_heads(pair):
    lane = lax.broadcasted_iota(jnp.int32, pair.shape, 1)
    zero = jnp.zeros_like(pair)
    return jnp.concatenate(
        [jnp.where(lane < HEAD_SIZE, pair, zero), jnp.where(lane < HEAD_SIZE, zero, pair)], 0
    )


def one_pair(rows):
    n = rows.shape[0] // 2
    lane = lax.broadcasted_iota(jnp.int32, (n, rows.shape[1]), 1)
    return jnp.where(lane < HEAD_SIZE, rows[:n], rows[n:])


def allowed_mask(seg, valid):
    n = seg.shape[1]
    r = lax.broadcasted_iota(jnp.int32, (n, n), 0)
    col = lax.broadcasted_iota(jnp.int32, (n, n), 1)
    seg_row = jnp.broadcast_to(seg.astype(f32), (n, n))
    seg_col = jnp.sum(jnp.where(r == col, seg_row, 0.0), axis=1, keepdims=True)
    live = jnp.broadcast_to(valid.astype(f32), (n, n)) > 0
    return ((seg_col == seg_row) & (col <= r) & live) | (r == col)


def softmax_rows(q2, k2, allowed2):
    s = dot_t(q2, k2) * (1.0 / HEAD_SIZE)
    s = jnp.where(allowed2, s, negative)
    e = jnp.exp(s - jnp.max(s, axis=1, keepdims=True))
    return e / jnp.sum(e, axis=1, keepdims=True)


def attn_fwd_body(sc, x_own, x_oth, seg, valid, cosine, sine, *refs):
    pieces = refs[:8]
    own_out, away_out, hn_out, qkv_out, o_out, misc_out, gains_out, w_out, turn_out = refs[8:17]
    w, x, sem = refs[17:]
    turn_out[0] = cosine[...]
    turn_out[1] = sine[...]
    ep, rep, core = sc[0], sc[1], sc[2]
    copies = piece_copies(pieces, w, sem, ep, rep)
    for cp in copies:
        cp.start()
    half = x_own.shape[0]
    n = 2 * half
    x[pl.ds(core * half, half), :] = x_own[...].astype(f32)
    x[pl.ds((1 - core) * half, half), :] = x_oth[...].astype(f32)
    allowed = allowed_mask(seg[...], valid[...])
    allowed2 = jnp.concatenate([allowed, allowed], 0)
    inputs = x[...]
    normed = inputs * lax.rsqrt(jnp.mean(inputs * inputs, axis=1, keepdims=True) + epsilon)
    for cp in copies:
        cp.wait()
    pw = qkv_out.shape[1]
    misc = w[:, :, pw : pw + MISC].reshape(MODEL_WIDTH, MISC)
    pick = lax.broadcasted_iota(jnp.int32, (8, MISC), 0) + EXPERTS
    pick = (pick == lax.broadcasted_iota(jnp.int32, (8, MISC), 1)).astype(f32).astype(bf16)
    gains = dot_t(pick, misc)
    gains_out[...] = gains
    misc_out[...] = misc
    hn = (normed * gains[0:1, :]).astype(bf16)
    hn_out[...] = hn
    w_out[...] = w[...].reshape(w_out.shape)
    qkv = dot(hn, w[:, :, :pw].reshape(MODEL_WIDTH, pw))
    groups = pw // 128
    kv0 = groups // 2
    for g in range(groups):
        u = qkv[:, 128 * g : 128 * (g + 1)]
        if g < kv0 + kv0 // 2:
            u = rotate_pairs(u, cosine[...], sine[...])
        qkv_out[:, 128 * g : 128 * (g + 1)] = u.astype(bf16)
    for m in range(kv0):
        g = kv0 + m // 2
        k2 = both_lanes(qkv_out[:, 128 * g : 128 * (g + 1)].astype(f32), m % 2).astype(bf16)
        g = g + kv0 // 2
        v2 = both_lanes(qkv_out[:, 128 * g : 128 * (g + 1)].astype(f32), m % 2).astype(bf16)
        q2 = two_heads(qkv_out[:, 128 * m : 128 * (m + 1)].astype(f32)).astype(bf16)
        p = softmax_rows(q2, k2, allowed2).astype(bf16)
        o_out[:, 128 * m : 128 * (m + 1)] = one_pair(dot(p, v2)).astype(bf16)
    wo = w[:, :, pw + MISC :].reshape(MODEL_WIDTH, o_out.shape[1])
    away_out[...] = dot_t(o_out[pl.ds((1 - core) * half, half), :], wo)
    own_out[...] = dot_t(o_out[pl.ds(core * half, half), :], wo)


def attn_fwd(sc, x_own, x_oth, seg, valid, cosine, sine, pieces, qw):
    half = x_own.shape[0]
    n = 2 * half
    cols = pieces[0].shape[1]
    pw = cols - MISC - qw
    return kernel_call(
        attn_fwd_body,
        (
            sds((half, MODEL_WIDTH), f32),
            sds((half, MODEL_WIDTH), f32),
            sds((n, MODEL_WIDTH), bf16),
            sds((n, pw), bf16),
            sds((n, qw), bf16),
            sds((MODEL_WIDTH, MISC), bf16),
            sds((8, MODEL_WIDTH), f32),
            sds((MODEL_WIDTH, cols), bf16),
            sds((2,) + cosine.shape, f32),
        ),
        [smem()] + [vmem()] * 6 + [anym()] * 8,
        "attn_fwd",
        [VM((16, 64, cols), bf16), VM((n, MODEL_WIDTH), f32), pltpu.SemaphoreType.DMA((16,))],
    )(sc, x_own, x_oth, seg, valid, cosine, sine, *pieces)


def second_norm_body(x, y_own, y_oth, gains, resid_out, hm_out):
    resid = x[...].astype(f32) + (y_own[...] + y_oth[...])
    resid_out[...] = resid
    inv = lax.rsqrt(jnp.mean(resid * resid, axis=1, keepdims=True) + epsilon)
    hm_out[...] = (resid * inv * gains[1:2, :]).astype(bf16)


def second_norm(x, y_own, y_oth, gains):
    return kernel_call(
        second_norm_body,
        (sds(y_own.shape, f32), sds(y_own.shape, bf16)),
        [vmem()] * 4,
        "second_norm",
    )(x, y_own, y_oth, gains)


def named_rows(block, j):
    moved = pltpu.roll(block.astype(f32), MISC - NAMED - EXPERTS * j, 1)
    lane = lax.broadcasted_iota(jnp.int32, moved.shape, 1)
    return (moved > 0.5) & (lane < EXPERTS)


def gates_of(hm, misc, named):
    logits = dot(hm, misc)
    top = jnp.max(jnp.where(named, logits, negative), axis=1, keepdims=True)
    e = jnp.where(named, jnp.exp(logits - top), 0.0)
    return e / jnp.sum(e, axis=1, keepdims=True)


def expert_fwd_body(sets, sc, misc, *refs):
    chunks, pieces = refs[:8], refs[8:16]
    own_out, away_out = refs[16:18]
    saved = refs[18 : 18 + 3 * len(sets)]
    w, hm, acc, gates, sem = refs[18 + 3 * len(sets) :]
    ep, rep, core = sc[0], sc[1], sc[2]
    half = chunks[0].shape[0]
    experts = EXPERTS // GROUP
    ew = w.shape[2] // 3
    ff = ew // experts
    part = 2 * half * len(sets[0])
    wide = piece_copies(pieces, w, sem, ep, rep, (0, 2 * ew), 0)
    down = piece_copies(pieces, w, sem, ep, rep, (2 * ew, ew), 16)
    for cp in wide + down:
        cp.start()
    order = [(k, other) for ks in sets for other in (False, True) for k in ks]
    for j, (k, other) in enumerate(order):
        here = pl.ds(j * half, half)
        chunk = chunks[k + GROUP * other][...]
        hm[here, :] = chunk
        at = pl.multiple_of(((ep ^ k) * 4 + rep) * 64, 64)
        block = misc[pl.ds(at, 64), :]
        mine = core == (1 if other else 0)
        quarters = [named_rows(block, q).astype(f32) for q in range(4)]
        first = jnp.concatenate(quarters[:2], 0)
        second = jnp.concatenate(quarters[2:], 0)
        gates[here, :] = jnp.where(mine, first, second)
    gates[...] = gates_of(hm[...], misc[...], gates[...] > 0.5)
    for n in range(len(sets)):
        saved[3 * n][...] = gates[n * part : (n + 1) * part, :]
    acc[...] = jnp.zeros_like(acc)
    lane = lax.broadcasted_iota(jnp.int32, gates.shape, 1)
    for cp in wide + down:
        cp.wait()

    def tile(e, carry):
        x = hm[...]
        at = pl.multiple_of(e * ff, ff)
        a = dot(x, w[:, :, pl.ds(at, ff)].reshape(MODEL_WIDTH, ff))
        b = dot(x, w[:, :, pl.ds(ew + at, ff)].reshape(MODEL_WIDTH, ff))
        g = jnp.sum(jnp.where(lane == ep * experts + e, gates[...], 0.0), axis=1, keepdims=True)
        h = (a * jax.nn.sigmoid(a) * b).astype(bf16)
        hs = (h.astype(f32) * g).astype(bf16)
        for n in range(len(sets)):
            saved[3 * n + 1][:, pl.ds(at, ff)] = a[n * part : (n + 1) * part, :]
            saved[3 * n + 2][:, pl.ds(at, ff)] = b[n * part : (n + 1) * part, :]
        acc[...] += dot_t(hs, w[:, :, pl.ds(2 * ew + at, ff)].reshape(MODEL_WIDTH, ff))
        return carry

    lax.fori_loop(0, experts, tile, 0)
    for j, (k, other) in enumerate(order):
        to = pl.ds(k * half, half)
        value = acc[j * half : (j + 1) * half, :]
        if other:
            away_out[to, :] = value.astype(bf16)
        else:
            own_out[to, :] = value


def expert_fwd(sets, sc, misc, chunks, pieces):
    half = chunks[0].shape[0]
    cols = pieces[0].shape[1]
    ew = cols // 3
    rows = GROUP * half
    part = 2 * half * len(sets[0])
    saved = (sds((part, MISC), f32), sds((part, ew), f32), sds((part, ew), f32)) * len(sets)
    return kernel_call(
        functools.partial(expert_fwd_body, sets),
        (sds((rows, MODEL_WIDTH), f32), sds((rows, MODEL_WIDTH), bf16)) + saved,
        [smem()] + [vmem()] * 9 + [anym()] * 8,
        "expert_fwd",
        [
            VM((16, 64, cols), bf16),
            VM((2 * rows, MODEL_WIDTH), bf16),
            VM((2 * rows, MODEL_WIDTH), f32),
            VM((2 * rows, MISC), f32),
            pltpu.SemaphoreType.DMA((32,)),
        ],
    )(sc, misc, *chunks, *pieces)


def core_sum_body(own, got, *outs):
    half = outs[0].shape[0]
    for j, out in enumerate(outs):
        at = pl.ds(j * half, half)
        out[...] = (own[at, :] + got[at, :].astype(f32)).astype(out.dtype)


def core_sum(ks, own, got):
    shape = (own.shape[0] // len(ks), own.shape[1])
    return kernel_call(
        core_sum_body,
        tuple(sds(shape, bf16 if k else f32) for k in ks),
        [vmem()] * 2,
        "core_sum",
    )(own, got)


def expert_bwd_body(ks, sc, gates, a_in, b_in, *refs):
    n = 2 * len(ks)
    chunks, pieces = refs[:n], refs[n : n + 8]
    own_out, away_out, ga_out, gb_out, hs_out, w, go, gsum, sem = refs[n + 8 :]
    ep, rep = sc[0], sc[1]
    half = chunks[0].shape[0]
    rows = len(ks) * half
    experts = EXPERTS // GROUP
    ew = w.shape[2] // 3
    ff = ew // experts
    wide = piece_copies(pieces, w, sem, ep, rep, (0, 2 * ew), 0)
    down = piece_copies(pieces, w, sem, ep, rep, (2 * ew, ew), 16)
    for cp in down + wide:
        cp.start()
    for j, chunk in enumerate(chunks):
        go[pl.ds(j * half, half), :] = chunk[...]
    gsum[...] = jnp.zeros_like(gsum)
    lane = lax.broadcasted_iota(jnp.int32, gsum.shape, 1)
    for cp in down + wide:
        cp.wait()

    def tile(e, carry):
        at = pl.multiple_of(e * ff, ff)
        a = a_in[:, pl.ds(at, ff)]
        b = b_in[:, pl.ds(at, ff)]
        u = dot(go[...], w[:, :, pl.ds(2 * ew + at, ff)].reshape(MODEL_WIDTH, ff))
        mine = lane == ep * experts + e
        g = jnp.sum(jnp.where(mine, gates[...], 0.0), axis=1, keepdims=True)
        s = jax.nn.sigmoid(a)
        silu = a * s
        h = (silu * b).astype(bf16).astype(f32)
        gsum[...] += jnp.where(mine, jnp.sum(h * u, axis=1, keepdims=True), 0.0)
        gh = u * g
        ga = (gh * b * s * (1.0 + a * (1.0 - s))).astype(bf16)
        gb = (gh * silu).astype(bf16)
        ga_out[:, pl.ds(at, ff)] = ga
        gb_out[:, pl.ds(at, ff)] = gb
        hs_out[:, pl.ds(at, ff)] = (h * g).astype(bf16)
        return carry

    lax.fori_loop(0, experts, tile, 0)

    def columns(n, carry):
        wg = w[pl.ds(4 * n, 4), :, :ew].reshape(256, ew)
        wu = w[pl.ds(4 * n, 4), :, ew : 2 * ew].reshape(256, ew)
        got = dot_t(ga_out[...], wg) + dot_t(gb_out[...], wu)
        cols = pl.ds(pl.multiple_of(256 * n, 256), 256)
        own_out[:, cols] = got[:rows, :]
        away_out[:, cols] = got[rows:, :].astype(bf16)
        return carry

    lax.fori_loop(0, MODEL_WIDTH // 256, columns, 0)
    own_out[:, MODEL_WIDTH:] = gsum[:rows, :]
    away_out[:, MODEL_WIDTH:] = gsum[rows:, :].astype(bf16)


def expert_bwd(ks, sc, gates, a, b, chunks, pieces):
    half = chunks[0].shape[0]
    cols = pieces[0].shape[1]
    ew = cols // 3
    rows = len(ks) * half
    full = MODEL_WIDTH + MISC
    low = sds((2 * rows, ew), bf16)
    return kernel_call(
        functools.partial(expert_bwd_body, ks),
        (sds((rows, full), f32), sds((rows, full), bf16), low, low, low),
        [smem()] + [vmem()] * (3 + len(chunks)) + [anym()] * 8,
        "expert_bwd",
        [
            VM((16, 64, cols), bf16),
            VM((2 * rows, MODEL_WIDTH), bf16),
            VM((2 * rows, MISC), f32),
            pltpu.SemaphoreType.DMA((32,)),
        ],
    )(sc, gates, a, b, *chunks, *pieces)


def loss_body(resid, m0, m1, m2, m3, teacher, live, gains, scale, result_out, g_out, glow_out, err_out):
    mix = m0[...] + (m1[...].astype(f32) + m2[...].astype(f32) + m3[...].astype(f32))
    result = resid[...] + mix
    result_out[...] = result.astype(bf16)
    differ = result - teacher[...].astype(f32)
    rows = gains.shape[1] // scale.shape[1]
    total = jnp.sum(gains[2:3, :], axis=1, keepdims=True) / rows
    weighted = live[...] * differ
    g = (scale.shape[0] * scale.shape[1]) / total * weighted
    g_out[...] = g
    glow_out[...] = g.astype(bf16)
    err_out[...] = jnp.broadcast_to(jnp.sum(weighted * differ, axis=0, keepdims=True), err_out.shape)


def loss_grad(resid, mixes, teacher, live, gains, seq_len, n):
    shape = resid.shape
    return kernel_call(
        loss_body,
        (sds(shape, bf16), sds(shape, f32), sds(shape, bf16), sds((8, shape[1]), f32)),
        [vmem()] * 9,
        "loss_grad",
    )(resid, *mixes, teacher, live, gains, jnp.zeros((seq_len, n), f32))


def second_back_body(b0, b1, b2, b3, gates, misc, hm, resid, gains, g_out, gy_out, gres_out, rows_out):
    half = resid.shape[0]
    total = b0[...] + (b1[...].astype(f32) + b2[...].astype(f32) + b3[...].astype(f32))
    gp = total[:, MODEL_WIDTH:]
    gate = gates[0:half, :]
    gl = (gate * (gp - jnp.sum(gate * gp, axis=1, keepdims=True))).astype(bf16)
    ghm = total[:, :MODEL_WIDTH] + dot_t(gl, misc[...])
    x = resid[...]
    inv = lax.rsqrt(jnp.mean(x * x, axis=1, keepdims=True) + epsilon)
    normed = x * inv
    rows = dot_o(gl, hm[...])
    gain_row = jnp.sum(ghm * normed, axis=0, keepdims=True)
    at = lax.broadcasted_iota(jnp.int32, rows.shape, 0)
    rows_out[...] = jnp.where(at == EXPERTS + 1, gain_row, rows)
    scaled = ghm * gains[1:2, :]
    gres = g_out[...] + inv * (
        scaled - normed * jnp.mean(scaled * normed, axis=1, keepdims=True)
    )
    gres_out[...] = gres
    gy_out[...] = gres.astype(bf16)


def second_back(backs, gates, misc, hm, resid, gains, g_out):
    shape = resid.shape
    return kernel_call(
        second_back_body,
        (sds(shape, bf16), sds(shape, f32), sds((MISC, shape[1]), f32)),
        [vmem()] * 10,
        "second_back",
    )(*backs, gates, misc, hm, resid, gains, g_out)


def attn_bwd_body(
    sc, gy_own, gy_oth, o, qkv, seg, valid, turn, w, gqkv_out, gy_out, own_out, away_out, low
):
    core = sc[2]
    half = gy_own.shape[0]
    n = 2 * half
    gy_out[pl.ds(core * half, half), :] = gy_own[...]
    gy_out[pl.ds((1 - core) * half, half), :] = gy_oth[...]
    pw = qkv.shape[1]
    low[...] = dot(gy_out[...], w[:, pw + MISC :]).astype(bf16)
    allowed = allowed_mask(seg[...], valid[...])
    allowed2 = jnp.concatenate([allowed, allowed], 0)
    kv0 = pw // 256
    lane = lax.broadcasted_iota(jnp.int32, (n, 128), 1)
    scale = 1.0 / HEAD_SIZE
    held = {}
    for m in range(kv0):
        gk_at = kv0 + m // 2
        gv_at = gk_at + kv0 // 2
        k2 = both_lanes(qkv[:, 128 * gk_at : 128 * (gk_at + 1)].astype(f32), m % 2).astype(bf16)
        v2 = both_lanes(qkv[:, 128 * gv_at : 128 * (gv_at + 1)].astype(f32), m % 2).astype(bf16)
        q2 = two_heads(qkv[:, 128 * m : 128 * (m + 1)].astype(f32)).astype(bf16)
        go2 = two_heads(low[:, 128 * m : 128 * (m + 1)].astype(f32)).astype(bf16)
        p = softmax_rows(q2, k2, allowed2)
        gp = dot_t(go2, v2)
        gs = (p * (gp - jnp.sum(p * gp, axis=1, keepdims=True))).astype(bf16)
        gq = one_pair(dot(gs, k2)) * scale
        gqkv_out[:, 128 * m : 128 * (m + 1)] = rotate_pairs(gq, turn[0], -turn[1]).astype(bf16)
        gk = dot_o(gs, q2) * scale
        gv = dot_o(p.astype(bf16), go2)
        gk = gk + pltpu.roll(gk, 64, 1)
        gv = gv + pltpu.roll(gv, 64, 1)
        if m % 2 == 0:
            held = {"k": gk, "v": gv}
        else:
            gk = jnp.where(lane < HEAD_SIZE, held["k"], gk)
            gv = jnp.where(lane < HEAD_SIZE, held["v"], gv)
            gqkv_out[:, 128 * gk_at : 128 * (gk_at + 1)] = rotate_pairs(
                gk, turn[0], -turn[1]
            ).astype(bf16)
            gqkv_out[:, 128 * gv_at : 128 * (gv_at + 1)] = gv.astype(bf16)
    away_out[...] = dot_t(gqkv_out[pl.ds((1 - core) * half, half), :], w[:, :pw]).astype(bf16)
    own_out[...] = dot_t(gqkv_out[pl.ds(core * half, half), :], w[:, :pw])


def attn_bwd(sc, gy_own, gy_oth, o, qkv, seg, valid, turn, w):
    half = gy_own.shape[0]
    n = 2 * half
    pw = qkv.shape[1]
    return kernel_call(
        attn_bwd_body,
        (
            sds((n, pw), bf16),
            sds((n, MODEL_WIDTH), bf16),
            sds((half, MODEL_WIDTH), f32),
            sds((half, MODEL_WIDTH), bf16),
        ),
        [smem()] + [vmem()] * 8,
        "attn_bwd",
        [VM((n, o.shape[1]), bf16)],
    )(sc, gy_own, gy_oth, o, qkv, seg, valid, turn, w)


def first_back_body(g_own, g_oth, x, gains, gres, rows, err, ginput_out, rows_out):
    ghn = g_own[...] + g_oth[...].astype(f32)
    inputs = x[...].astype(f32)
    inv = lax.rsqrt(jnp.mean(inputs * inputs, axis=1, keepdims=True) + epsilon)
    normed = inputs * inv
    gain_row = jnp.sum(ghn * normed, axis=0, keepdims=True)
    scaled = ghn * gains[0:1, :]
    ginput_out[...] = (
        gres[...] + inv * (scaled - normed * jnp.mean(scaled * normed, axis=1, keepdims=True))
    ).astype(bf16)
    e = err[...]
    for shift in (64, 128, 256, 512):
        e = e + pltpu.roll(e, shift, 1)
    at = lax.broadcasted_iota(jnp.int32, rows.shape, 0)
    r = jnp.where(at == EXPERTS, gain_row, rows[...])
    rows_out[...] = jnp.where(at == EXPERTS + 2, e[0:1, :], r)


def first_back(g_own, g_oth, x, gains, gres, rows, err):
    return kernel_call(
        first_back_body,
        (sds(gres.shape, bf16), sds(rows.shape, f32)),
        [vmem()] * 7,
        "first_back",
    )(g_own, g_oth, x, gains, gres, rows, err)


SEND_X = (12, 13, 4, 5)
SEND_Y = (14, 15, 10, 11)
KEPT = (0, 1, 2, 3, 6, 7, 8, 9)


def store_relative(out, ep, rep, value, cols):
    for j in range(16):
        to = 4 * ((j % 4) ^ rep) + ((j // 4) ^ ep)
        out[to, :, cols] = value[64 * j : 64 * (j + 1), :]


def split_relative(full, x_out, y_out, kept_out):
    for j, at in enumerate(SEND_X):
        x_out[j] = full[at].astype(bf16)
    for j, at in enumerate(SEND_Y):
        y_out[j] = full[at].astype(bf16)
    for j, at in enumerate(KEPT):
        kept_out[j] = full[at]


def attn_dw_body(sc, gy, o, hn, gqkv, rows, x_out, y_out, kept_out, full):
    ep, rep = sc[0], sc[1]
    pw = gqkv.shape[1]
    qw = o.shape[1]
    store_relative(full, ep, rep, dot_o(hn[...], gqkv[...]), slice(0, pw))
    store_relative(full, ep, rep, dot_o(gy[...], o[...]), slice(pw, pw + qw))
    store_relative(full, ep, rep, jnp.transpose(rows[...]), slice(pw + qw, pw + qw + MISC))
    split_relative(full, x_out, y_out, kept_out)


def attn_dw(sc, gy, o, hn, gqkv, rows):
    width = gqkv.shape[1] + o.shape[1] + MISC
    return kernel_call(
        attn_dw_body,
        (sds((4, 64, width), bf16), sds((4, 64, width), bf16), sds((8, 64, width), f32)),
        [smem()] + [vmem()] * 5,
        "attn_dw",
        [VM((16, 64, width), f32)],
    )(sc, gy, o, hn, gqkv, rows)


def attn_dw3_body(sc, gy, o, hn, gqkv, rows, own_out, x_out, y_out, d_out, full):
    ep, rep = sc[0], sc[1]
    pw = gqkv.shape[1]
    qw = o.shape[1]
    store_relative(full, ep, rep, dot_o(hn[...], gqkv[...]), slice(0, pw))
    store_relative(full, ep, rep, dot_o(gy[...], o[...]), slice(pw, pw + qw))
    store_relative(full, ep, rep, jnp.transpose(rows[...]), slice(pw + qw, pw + qw + MISC))
    own_out[...] = full[0:4]
    for m, out in enumerate((x_out, y_out, d_out)):
        out[...] = full[4 * m + 4 : 4 * m + 8].astype(bf16)


def attn_dw3(sc, gy, o, hn, gqkv, rows):
    width = gqkv.shape[1] + o.shape[1] + MISC
    low = sds((4, 64, width), bf16)
    return kernel_call(
        attn_dw3_body,
        (sds((4, 64, width), f32), low, low, low),
        [smem()] + [vmem()] * 5,
        "attn_dw3",
        [VM((16, 64, width), f32)],
    )(sc, gy, o, hn, gqkv, rows)


def attn_sum3_body(own, x, y, d, *outs):
    for k, out in enumerate(outs):
        total = own[k] + (x[k].astype(f32) + y[k].astype(f32) + d[k].astype(f32))
        out[...] = total.astype(out.dtype)


def attn_sum3(own, x, y, d):
    shape = own.shape[1:]
    low = sds(shape, bf16)
    return kernel_call(
        attn_sum3_body, (sds(shape, f32), low, low, low), [vmem()] * 4, "attn_sum3"
    )(own, x, y, d)


def expert_dw_body(plan, parts, sc, *refs):
    n = 8 * (1 + max(plan))
    chunks = refs[:n]
    ys = refs[n : n + parts * len(plan)]
    x_out, y_out, kept_out, xt, full = refs[n + parts * len(plan) :]
    ep, rep = sc[0], sc[1]
    half = chunks[0].shape[0]
    step = pl.program_id(0)
    for which in sorted(set(plan)):

        @pl.when(step == 4 * plan.index(which))
        def _():
            for j, x in enumerate(chunks[8 * which : 8 * which + 8]):
                xt[:, j * half : (j + 1) * half] = jnp.transpose(x[...])

    for j in range(len(plan)):

        @pl.when(step // 4 == j)
        def _():
            got = ys[parts * j : parts * (j + 1)]
            rows = got[0].shape[0]
            g = dot(xt[:, :rows], got[0][...])
            for p in range(1, parts):
                g = g + dot(xt[:, p * rows : (p + 1) * rows], got[p][...])
            store_relative(full, ep, rep, g, slice(None))

    split_relative(full, x_out, y_out, kept_out)


def expert_dw(sc, chunk_sets, plan, ys):
    half = chunk_sets[0][0].shape[0]
    parts = len(ys[0])
    rows, wide = ys[0][0].shape
    tile = wide // 4
    steps = 4 * len(plan)
    whole = pl.BlockSpec((half, MODEL_WIDTH), lambda i: (0, 0))
    shape = (4, 64, steps * tile)
    return pl.pallas_call(
        functools.partial(expert_dw_body, plan, parts),
        grid=(steps,),
        out_shape=(sds(shape, bf16), sds(shape, bf16), sds((8,) + shape[1:], f32)),
        in_specs=[smem()]
        + [whole] * (8 * len(chunk_sets))
        + [
            pl.BlockSpec((rows, tile), lambda i, j=j: (0, jnp.clip(i - 4 * j, 0, 3)))
            for j in range(len(plan))
            for _ in range(parts)
        ],
        out_specs=(
            pl.BlockSpec((4, 64, tile), lambda i: (0, 0, i)),
            pl.BlockSpec((4, 64, tile), lambda i: (0, 0, i)),
            pl.BlockSpec((8, 64, tile), lambda i: (0, 0, i)),
        ),
        scratch_shapes=[VM((MODEL_WIDTH, 8 * half), bf16), VM((16, 64, tile), f32)],
        compiler_params=pltpu.CompilerParams(vmem_limit_bytes=VMEM_BYTES),
        name="expert_dw",
    )(sc, *[x for xs in chunk_sets for x in xs], *[y for part in ys for y in part])


def relay_body(kept, rx, ry, sx_out, sy_out, own_out):
    sx_out[...] = (kept[4:6] + ry[0:2].astype(f32)).astype(bf16)
    sy_out[...] = (kept[6:8] + rx[0:2].astype(f32)).astype(bf16)
    own_out[0:2] = kept[0:2] + rx[2:4].astype(f32)
    own_out[2:4] = kept[2:4] + ry[2:4].astype(f32)


def relay(kept, rx, ry):
    rows, wide = kept.shape[1:]
    return kernel_call(
        relay_body,
        (sds((2, rows, wide), bf16), sds((2, rows, wide), bf16), sds((4, rows, wide), f32)),
        [vmem()] * 3,
        "relay",
    )(kept, rx, ry)


def owned_body(own, rx, ry, out0, out1, out2, out3):
    out0[...] = own[0] + ry[0].astype(f32)
    out1[...] = (own[1] + ry[1].astype(f32)).astype(bf16)
    out2[...] = (own[2] + rx[0].astype(f32)).astype(bf16)
    out3[...] = (own[3] + rx[1].astype(f32)).astype(bf16)


def owned(own, rx, ry):
    shape = own.shape[1:]
    return kernel_call(
        owned_body,
        (sds(shape, f32), sds(shape, bf16), sds(shape, bf16), sds(shape, bf16)),
        [vmem()] * 3,
        "owned",
    )(own, rx, ry)


def unpack_grad_body(sc, g0, g1, g2, g3, out, wide):
    ep = sc[0]
    n = g0.shape[0]
    experts = EXPERTS // GROUP
    ff = g0.shape[1] // experts
    for k, g in enumerate((g0, g1, g2, g3)):
        for e in range(experts):
            for l in range(ff // 128):
                at = e * ff + 128 * l
                wide[l, pl.ds((ep ^ k) * experts + e, n, stride=EXPERTS), :] = g[
                    :, at : at + 128
                ].astype(f32)
    for l in range(ff // 128):
        out[:, 128 * l : 128 * (l + 1)] = wide[l]


def unpack_grad(sc, parts):
    n, wide = parts[0].shape
    ff = wide * GROUP // EXPERTS
    out = kernel_call(
        unpack_grad_body,
        sds((n * EXPERTS, ff), f32),
        [smem()] + [vmem()] * 4,
        "unpack_grad",
        [VM((ff // 128, n * EXPERTS, 128), f32)],
    )(sc, *parts)
    return out.reshape(n, EXPERTS, ff)


def fast(
    c,
    tokens,
    segment_ids,
    valid,
    expert_ids,
    teacher,
    attn_gain,
    w_query,
    key_projection,
    value_projection,
    w_out,
    moe_gain,
    w_router,
    w_gate,
    w_up,
    w_down,
):
    half = tokens.shape[0]
    seq_len = expert_ids.shape[0]
    rows = w_query.shape[0]
    qw, kw = w_query.shape[1], key_projection.shape[1]
    pw = qw + 2 * kw
    sc = jnp.stack([c.ep, c.rep, c.core]).astype(jnp.int32)

    def my_half(v, axis=0):
        return lax.dynamic_slice_in_dim(v, c.core * half, half, axis)

    made = {}

    def held(name, v):
        wanted = [w for w in ORDER.get(name, ()) if w in made]
        return tie(v, *[made[w] for w in wanted]) if wanted else v

    def run(name, f, *args):
        got = f(*held(name, args))
        made[name] = min(jax.tree.leaves(got), key=lambda x: x.size * x.dtype.itemsize)
        return got

    def send(name, v, mask):
        made[name] = c.swap(held(name, v), mask)
        return made[name]

    def cross(name, v):
        made[name] = c.other(held(name, v))
        return made[name]

    def to_group(name, parts):
        return [send(f"{name}{k}", v, c.reps * k) for k, v in enumerate(parts, 1)]

    def pair(a, b):
        return jnp.concatenate([a, b], 0)

    def spread(name, a, b, whole):
        if whole:
            z = pair(a, b)
            x, y = send(name + "ax", z, 1), send(name + "ay", z, 2)
            d, e = send(name + "ad", x[:128], 2), send(name + "bd", y[128:], 1)
            return [z, z, x, x, y, y, d, e]
        ax, ay = send(name + "ax", a, 1), send(name + "ay", a, 2)
        bx, by = send(name + "bx", b, 1), send(name + "by", b, 2)
        ad, bd = send(name + "ad", ax, 2), send(name + "bd", by, 1)
        return [a, b, ax, bx, ay, by, ad, bd]

    tokens_oth = cross("tokens", tokens)
    front = run(
        "front",
        pack_front,
        w_query,
        key_projection,
        value_projection,
        w_out,
        w_router,
        attn_gain,
        moe_gain,
        valid,
        expert_ids,
    )
    z1, z2, z3 = to_group("z", [front] * 3)
    packed = run("packed", pack_experts, sc, w_gate, w_up, w_down)
    front_p = spread("f", pair(front, z1), pair(z2, z3), FWHOLE)
    e1, e2, e3 = to_group("e", packed[1:])
    exp_a = pair(packed[0], e1)

    cosine, sine = rope_tables(seq_len, 128)
    y_own, y_away, hn, qkv, o, misc, gains, attn_w, turn = run(
        "attn",
        lambda *v: attn_fwd(*v, qw),
        sc,
        tokens,
        tokens_oth,
        segment_ids,
        valid,
        cosine,
        sine,
        front_p,
    )
    y_oth = cross("y", y_away)
    exp_p = spread("x", exp_a, pair(e2, e3), XWHOLE)
    resid, hm = run("norm", second_norm, tokens, y_own, y_oth, gains)

    def all_rows(name, v):
        own = [v] + to_group(name, [v] * 3)
        return own + [cross(f"{name}t{k}", x) for k, x in enumerate(own)]

    hms = all_rows("h", hm)
    sets = {"n": (0, 1), "f": (2, 3)} if CHUNK else {"a": (0, 1, 2, 3)}

    def rows_of(v, ks):
        return [v[k] for k in ks] + [v[GROUP + k] for k in ks]

    mix_own, mix_away, *saved = run(
        "efwda", functools.partial(expert_fwd, tuple(sets.values())), sc, misc, hms, exp_p
    )
    kept = {name: saved[3 * n : 3 * n + 3] for n, name in enumerate(sets)}
    mixes = run(
        "msuma", functools.partial(core_sum, (0, 1, 2, 3)), mix_own, cross("mta", mix_away)
    )
    mixes = [mixes[0]] + to_group("m", mixes[1:])
    live = my_half(valid[0]).astype(f32)[:, None]
    result, g_out, g_low, err = loss_grad(
        resid, mixes, my_half(teacher), live, gains, seq_len, c.n
    )

    gos = [g_low] + to_group("g", [g_low] * 3) + [None] * GROUP
    done = {}
    for name, ks in sets.items():
        for k in ks:
            gos[GROUP + k] = cross(f"gt{k}", gos[k])
        done[name] = run(
            "ebwd" + name,
            functools.partial(expert_bwd, ks),
            sc,
            *kept[name],
            rows_of(gos, ks),
            exp_p,
        )
    backs = {}
    for name in reversed(sets):
        ks = sets[name]
        own, away = done[name][:2]
        got = run(
            "bsum" + name, functools.partial(core_sum, ks), own, cross("bt" + name, away)
        )
        for k, v in zip(ks, got):
            backs[k] = send(f"b{k}", v, c.reps * k) if k else v
    backs = [backs[k] for k in range(GROUP)]
    lows = [done[name][2:] for name in sets]
    gates = kept[next(iter(sets))][0]
    ga, gb, hs = ([low[j] for low in lows] for j in range(3))
    hm_rows = [x for ks in sets.values() for x in rows_of(hms, ks)]
    go_rows = [x for ks in sets.values() for x in rows_of(gos, ks)]

    def first_step(name, x_send, y_send, kept):
        return kept, send(name + "x", x_send, 1), send(name + "y", y_send, 2)

    def second_step(name, sx, sy, own):
        return own, send(name + "x2", sx, 1), send(name + "y2", sy, 2)

    def dw(name, chunk_sets, plan, ys):
        return run(name, lambda v, x, y: expert_dw(v, x, plan, y), sc, chunk_sets, ys)

    if MERGE:
        dw_gu = dw("dwgu", [hm_rows, go_rows], (0, 0, 1), [ga, gb, hs])
        made["dwdn"] = made["dwgu"]
    else:
        dw_gu = dw("dwgu", [hm_rows], (0, 0), [ga, gb])
        dw_dn = dw("dwdn", [go_rows], (0,), [hs])
    gu = run("gurelay", relay, *first_step("gu", *dw_gu))
    gu = second_step("gu", *gu)
    if MERGE:
        for name in ("dnx", "dny"):
            made[name] = made[name.replace("dn", "gu")]
    else:
        dn_1 = first_step("dn", *dw_dn)

    gy, gres, rows_g = run(
        "second", second_back, backs, gates, misc, hm, resid, gains, g_out
    )
    gqkv, gy_all, ghn_own, ghn_away = run(
        "abwd",
        attn_bwd,
        sc,
        gy,
        cross("gy", gy),
        o,
        qkv,
        segment_ids,
        valid,
        turn,
        attn_w,
    )
    grad_input, rows_g = run(
        "first", first_back, ghn_own, cross("ghn", ghn_away), tokens, gains, gres, rows_g, err
    )
    if EARLY:
        if not MERGE:
            dn = second_step("dn", *run("dnrelay", relay, *dn_1))
        gu0, *gu_low = run("guown", owned, *gu)
        gu_got = to_group("guz", gu_low)
    if DIRECT:
        attn_own, ax, ay, ad = run("adw", attn_dw3, sc, gy_all, o, hn, gqkv, rows_g)
        ax, ay, ad = send("ax", ax, 1), send("ay", ay, 2), send("ad", ad, 3)
    else:
        at = first_step("a", *run("adw", attn_dw, sc, gy_all, o, hn, gqkv, rows_g))
    if not EARLY:
        gu0, *gu_low = run("guown", owned, *gu)
        if not MERGE:
            dn = second_step("dn", *run("dnrelay", relay, *dn_1))
        gu_got = to_group("guz", gu_low)
    if DIRECT:
        w0, *w_low = run("asum", attn_sum3, attn_own, ax, ay, ad)
    else:
        w0, *w_low = run("aown", owned, *second_step("a", *run("arelay", relay, *at)))
    w_got = to_group("az", w_low)
    parts = [gu0, *gu_got]
    ew = hs[0].shape[1]
    if MERGE:
        last = [p[:, 2 * ew :] for p in parts]
    else:
        dn0, *dn_low = run("dnown", owned, *dn)
        last = [dn0, *to_group("dnz", dn_low)]
    expert_grads = [
        run("ug", unpack_grad, sc, [p[:, :ew] for p in parts]),
        run("uu", unpack_grad, sc, [p[:, ew : 2 * ew] for p in parts]),
        run("ud", unpack_grad, sc, last),
    ]
    own_w = w0 + (w_got[0].astype(f32) + w_got[1].astype(f32) + w_got[2].astype(f32))
    misc_own = own_w[:, pw + qw :]
    misc_own = misc_own + c.other(misc_own)
    live_total = jnp.sum(gains[2]) / rows
    loss = jnp.sum(misc_own[:, EXPERTS + 2]) / (2.0 * MODEL_WIDTH * live_total)
    return (
        loss,
        result,
        grad_input,
        misc_own[:, EXPERTS],
        own_w[:, :qw],
        own_w[:, qw : qw + kw],
        own_w[:, qw + kw : pw],
        own_w[:, pw : pw + qw],
        misc_own[:, EXPERTS + 1],
        misc_own[:, :EXPERTS],
        *expert_grads,
    )


def shards(
    tokens,
    segment_ids,
    valid,
    expert_ids,
    teacher,
    attn_gain,
    w_query,
    key_projection,
    value_projection,
    w_out,
    moe_gain,
    w_router,
    w_gate,
    w_up,
    w_down,
):
    c = Comm()
    if c.reps == 4 and w_query.shape[0] == 64:
        return fast(
            c,
            tokens,
            segment_ids,
            valid,
            expert_ids,
            teacher,
            attn_gain,
            w_query,
            key_projection,
            value_projection,
            w_out,
            moe_gain,
            w_router,
            w_gate,
            w_up,
            w_down,
        )
    half = tokens.shape[0]
    seq_len = expert_ids.shape[0]
    rows = w_query.shape[0]
    qw, kw = w_query.shape[1], key_projection.shape[1]
    ff = w_gate.shape[2]
    local_experts = EXPERTS // GROUP
    ew = local_experts * ff
    heads = qw // HEAD_SIZE
    kv_heads = kw // HEAD_SIZE
    per = heads // kv_heads
    scale = 1.0 / HEAD_SIZE
    first_core = c.core == 0

    def join_rows(own, other):
        return jnp.where(
            first_core, jnp.concatenate([own, other], 0), jnp.concatenate([other, own], 0)
        )

    def my_half(v):
        return lax.dynamic_slice_in_dim(v, c.core * half, half, 0)

    live_row = valid[0]
    live_count = jnp.sum(live_row).astype(f32)
    misc = jnp.concatenate(
        [
            w_router,
            attn_gain[:, None],
            moe_gain[:, None],
            jnp.broadcast_to(live_count.astype(bf16), (rows, 1)),
            jnp.zeros((rows, MISC - EXPERTS - 3), bf16),
        ],
        1,
    )
    front = jnp.concatenate([w_query, key_projection, value_projection, misc], 1)
    inputs_low = join_rows(tokens, c.other(tokens))

    def gather_attention(v):
        z = c.stack_group(c.gather_group(v))
        mid = z.shape[2] // 2
        return jnp.concatenate(
            [c.gather_reps(z[:, :, :mid], False), c.gather_reps(z[:, :, mid:], True)], 1
        )

    front_w = gather_attention(front)
    out_w = gather_attention(w_out)
    ids_half = my_half(expert_ids)
    ids_group = jnp.concatenate(c.gather_group(ids_half), 0)

    gate_up = jnp.concatenate(
        [w_gate.reshape(rows, GROUP, ew), w_up.reshape(rows, GROUP, ew)], 2
    ).transpose(1, 0, 2)
    gate_up_z = c.stack_group(c.all_to_group(gate_up))
    down_z = c.stack_group(c.all_to_group(w_down.reshape(rows, GROUP, ew).transpose(1, 0, 2)))
    gate_w = c.gather_reps(gate_up_z[:, :, :ew], False)
    up_w = c.gather_reps(gate_up_z[:, :, ew:], True)
    down_w = jnp.concatenate(
        [
            c.gather_reps(down_z[:, :, : ew // 2], False),
            c.gather_reps(down_z[:, :, ew // 2 :], True),
        ],
        1,
    )
    gate_ws = (gate_w, c.other(gate_w))
    up_ws = (up_w, c.other(up_w))
    down_ws = (down_w, c.other(down_w))

    pw = qw + 2 * kw
    proj_w = front_w[:, :pw]
    router_w = front_w[:, pw : pw + EXPERTS]
    gain_one = front_w[:, pw + EXPERTS].astype(f32)[None, :]
    gain_two = front_w[:, pw + EXPERTS + 1].astype(f32)[None, :]
    counts = front_w[:, pw + EXPERTS + 2].astype(f32).reshape(c.n, rows)[:, 0]
    live_total = jnp.sum(counts)

    inputs = inputs_low.astype(f32)
    inv_one = lax.rsqrt(jnp.mean(inputs * inputs, -1, keepdims=True) + epsilon)
    normed_one = inputs * inv_one
    attention_hidden = (normed_one * gain_one).astype(bf16)
    cosine, sine = rope_tables(seq_len, qw + kw)
    qkv = dot(attention_hidden, proj_w)
    qk_raw = qkv[:, : qw + kw]
    qk = (qk_raw * cosine + swap_halves(qk_raw) * sine).astype(bf16)
    q = qk[:, :qw].reshape(seq_len, kv_heads, per, HEAD_SIZE)
    k = qk[:, qw:].reshape(seq_len, kv_heads, HEAD_SIZE)
    v = qkv[:, qw + kw :].astype(bf16).reshape(seq_len, kv_heads, HEAD_SIZE)
    seg_row = segment_ids[0]
    places = jnp.arange(seq_len)
    allowed = (seg_row[:, None] == seg_row[None, :]) & (places[None, :] <= places[:, None]) & (
        live_row[None, :] > 0
    ) | (places[None, :] == places[:, None])
    scores = jnp.einsum("qkgd,skd->kgqs", q, k, preferred_element_type=f32) * scale
    scores = jnp.where(allowed[None, None], scores, negative)
    top_score = jnp.max(scores, -1, keepdims=True)
    exp_scores = jnp.exp(scores - top_score)
    probs = exp_scores / jnp.sum(exp_scores, -1, keepdims=True)
    probs_low = probs.astype(bf16)
    attn_out = (
        jnp.einsum("kgqs,skd->qkgd", probs_low, v, preferred_element_type=f32)
        .astype(bf16)
        .reshape(seq_len, qw)
    )
    proj_part = dot_t(attn_out, out_w)
    theirs = lax.dynamic_slice_in_dim(proj_part, (1 - c.core) * half, half, 0)
    inputs_half = tokens.astype(f32)
    resid = inputs_half + (my_half(proj_part) + c.other(theirs))
    inv_two = lax.rsqrt(jnp.mean(resid * resid, -1, keepdims=True) + epsilon)
    normed_two = resid * inv_two
    hidden_moe = (normed_two * gain_two).astype(bf16)

    hm = jnp.concatenate(c.gather_group(hidden_moe), 0)
    logits = dot(hm, router_w)
    named = jnp.any(ids_group[:, :, None] == jnp.arange(EXPERTS)[None, None, :], 1)
    masked = jnp.where(named, logits, negative)
    shifted = jnp.where(named, jnp.exp(logits - jnp.max(masked, -1, keepdims=True)), 0.0)
    gates = shifted / jnp.sum(shifted, -1, keepdims=True)
    my_gates = lax.dynamic_slice_in_dim(gates, c.ep * local_experts, local_experts, 1)
    wide = jnp.repeat(my_gates, ff, axis=1)

    kept = []
    mixed = 0.0
    for gw, uw, dw in zip(gate_ws, up_ws, down_ws):
        a = dot(hm, gw)
        b = dot(hm, uw)
        sigma = jax.nn.sigmoid(a)
        h = (a * sigma * b).astype(bf16)
        hs = (h.astype(f32) * wide).astype(bf16)
        mixed = mixed + dot_t(hs, dw)
        kept.append((a, b, h, hs))
    mixed = mixed.reshape(GROUP, half, MODEL_WIDTH)
    mix = mixed[0]
    for j in range(1, GROUP):
        mix = mix + c.swap(mixed[j].astype(bf16), c.reps * j).astype(f32)
    result = resid + mix

    live = my_half(live_row).astype(f32)[:, None]
    differ = result - my_half(teacher).astype(f32)
    err_cols = jnp.sum(live * differ * differ, 0)
    grad_out = seq_len * c.n / live_total * live * differ
    go = jnp.concatenate(c.gather_group(grad_out.astype(bf16)), 0)

    grad_hm = 0.0
    grad_gates = 0.0
    low = []
    for (a, b, h, hs), gw, uw, dw in zip(kept, gate_ws, up_ws, down_ws):
        u = dot(go, dw)
        grad_gates = grad_gates + jnp.sum(
            (h.astype(f32) * u).reshape(GROUP * half, local_experts, ff), -1
        )
        gh = u * wide
        sigma = jax.nn.sigmoid(a)
        ga = (gh * b * sigma * (1.0 + a * (1.0 - sigma))).astype(bf16)
        gb = (gh * a * sigma).astype(bf16)
        grad_hm = grad_hm + dot_t(ga, gw) + dot_t(gb, uw)
        low.append((ga, gb))
    gg = jnp.zeros((GROUP * half, MISC), f32)
    gg = lax.dynamic_update_slice_in_dim(gg, grad_gates, c.ep * local_experts, 1)
    back = jnp.concatenate([grad_hm, gg], 1).reshape(GROUP, half, MODEL_WIDTH + MISC)
    back_sum = back[0]
    for j in range(1, GROUP):
        back_sum = back_sum + c.swap(back[j].astype(bf16), c.reps * j).astype(f32)

    weight_sums = []
    for own, other in (
        ((hm, low[0][0]), (hm, low[1][0])),
        ((hm, low[0][1]), (hm, low[1][1])),
        ((go, kept[0][3]), (go, kept[1][3])),
    ):
        away = dot_o(*other).astype(bf16)
        weight_sums.append(dot_o(*own) + c.other(away).astype(f32))
    gate_s = c.scatter_reps(weight_sums[0], False)
    up_s = c.scatter_reps(weight_sums[1], True)
    down_s = jnp.concatenate(
        [
            c.scatter_reps(weight_sums[2][:, : ew // 2], False),
            c.scatter_reps(weight_sums[2][:, ew // 2 :], True),
        ],
        2,
    )
    sums = jnp.concatenate([gate_s, up_s, down_s], 2)
    sums_low = sums.astype(bf16)
    parts = [c.block(sums, 0)] + [
        c.swap(c.block(sums_low, k), c.reps * k).astype(f32) for k in range(1, GROUP)
    ]
    finished = c.stack_group(parts)

    def expert_grad(j):
        g = finished[:, :, j * ew : (j + 1) * ew].transpose(1, 0, 2)
        return g.reshape(rows, EXPERTS, ff)

    grad_probs = back_sum[:, MODEL_WIDTH : MODEL_WIDTH + EXPERTS]
    gate_probs = gates[:half]
    grad_logits = (
        gate_probs * (grad_probs - jnp.sum(gate_probs * grad_probs, -1, keepdims=True))
    ).astype(bf16)
    grad_hidden = back_sum[:, :MODEL_WIDTH] + dot_t(grad_logits, router_w)
    router_part = dot_o(hidden_moe, grad_logits)
    gain_two_part = jnp.sum(grad_hidden * normed_two, 0)
    scaled_two = grad_hidden * gain_two
    grad_resid = grad_out + inv_two * (
        scaled_two - normed_two * jnp.mean(scaled_two * normed_two, -1, keepdims=True)
    )
    gy_half = grad_resid.astype(bf16)
    gy = join_rows(gy_half, c.other(gy_half))

    out_part = dot_o(gy, attn_out)
    grad_attn = dot(gy, out_w).astype(bf16).reshape(seq_len, kv_heads, per, HEAD_SIZE)
    gp = jnp.einsum("qkgd,skd->kgqs", grad_attn, v, preferred_element_type=f32)
    gs = (probs * (gp - jnp.sum(probs * gp, -1, keepdims=True))).astype(bf16)
    gq = jnp.einsum("kgqs,skd->qkgd", gs, k, preferred_element_type=f32) * scale
    gk = jnp.einsum("kgqs,qkgd->skd", gs, q, preferred_element_type=f32) * scale
    gv = jnp.einsum("kgqs,qkgd->skd", probs_low, grad_attn, preferred_element_type=f32)
    gqk = jnp.concatenate([gq.reshape(seq_len, qw), gk.reshape(seq_len, kw)], 1)
    gqk = gqk * cosine - swap_halves(gqk) * sine
    gqkv = jnp.concatenate([gqk.astype(bf16), gv.astype(bf16).reshape(seq_len, kw)], 1)
    ghn_part = dot_t(gqkv, proj_w)
    ghn_low = ghn_part.astype(bf16)
    ghn = my_half(ghn_part) + c.other(
        lax.dynamic_slice_in_dim(ghn_low, (1 - c.core) * half, half, 0)
    ).astype(f32)
    proj_part_grad = dot_o(attention_hidden, gqkv)
    normed_half = my_half(normed_one)
    gain_one_part = jnp.sum(ghn * normed_half, 0)
    scaled_one = ghn * gain_one
    grad_input = grad_resid + my_half(inv_one) * (
        scaled_one - normed_half * jnp.mean(scaled_one * normed_half, -1, keepdims=True)
    )

    err_rows = jnp.sum(err_cols.reshape(MODEL_WIDTH // rows, rows), 0)
    misc_part = jnp.concatenate(
        [
            router_part,
            gain_one_part[:, None],
            gain_two_part[:, None],
            jnp.tile(err_rows, c.n)[:, None],
            jnp.zeros((MODEL_WIDTH, MISC - EXPERTS - 3), f32),
        ],
        1,
    )
    back_w = jnp.concatenate([proj_part_grad, out_part, misc_part], 1)
    mid = (back_w.shape[1] // 256) * 128
    attn_s = jnp.concatenate(
        [c.scatter_reps(back_w[:, :mid], False), c.scatter_reps(back_w[:, mid:], True)], 2
    )
    attn_low = attn_s.astype(bf16)
    own_w = c.block(attn_s, 0)
    for k_ in range(1, GROUP):
        own_w = own_w + c.swap(c.block(attn_low, k_), c.reps * k_).astype(f32)
    misc_own = own_w[:, pw + qw :]
    misc_own = misc_own + c.other(misc_own)
    loss = jnp.sum(misc_own[:, EXPERTS + 2]) / (2.0 * MODEL_WIDTH * live_total)

    return (
        loss,
        result.astype(bf16),
        grad_input.astype(bf16),
        misc_own[:, EXPERTS],
        own_w[:, :qw],
        own_w[:, qw : qw + kw],
        own_w[:, qw + kw : pw],
        own_w[:, pw : pw + qw],
        misc_own[:, EXPERTS + 1],
        misc_own[:, :EXPERTS],
        expert_grad(0),
        expert_grad(1),
        expert_grad(2),
    )


def solution(mesh):
    placed = (
        P(("dp", "tensor"), None),
        P("dp", None),
        P("dp", None),
        P("dp", None),
        P("dp", None),
        P("dp"),
        P("dp", "tensor"),
        P("dp", "tensor"),
        P("dp", "tensor"),
        P("dp", "tensor"),
        P("dp"),
        P("dp", None),
        P("dp", None, "tensor"),
        P("dp", None, "tensor"),
        P("dp", None, "tensor"),
    )
    return jax.shard_map(
        shards,
        mesh=mesh,
        in_specs=placed,
        out_specs=(
            P(),
            P(("dp", "tensor"), None),
            P(("dp", "tensor"), None),
            P("dp"),
            P("dp", "tensor"),
            P("dp", "tensor"),
            P("dp", "tensor"),
            P("dp", "tensor"),
            P("dp"),
            P("dp", None),
            P("dp", None, "tensor"),
            P("dp", None, "tensor"),
            P("dp", None, "tensor"),
        ),
        check_vma=False,
    )
```
